32 devices in a mesh: dp: 4 (over y, x), seq: 8 (over z, core).
Axes of the slice: x: 2, y: 2, z: 4, core: 2. Of those that a mesh axis runs over, the one named last changes fastest.
Arguments:
- tokens: bfloat16 [4, 2048, 1024], P('dp', 'seq'), may hold values from -6 to 6
- out_grad: bfloat16 [4, 2048, 1024], P('dp', 'seq'), may hold values from -6 to 6
- doc_ids: int32 [4, 2048], P('dp', 'seq'), may hold values from 0 to 15, never falling along the last dimension, each value on 1 to 1024 neighbouring positions
- expert_picks: int32 [4, 2048, 8], P('dp', 'seq'), may hold values from 0 to 15, all different within a row; in each aligned block of 256 rows (0 to 255, 256 to 511, ..., all dimensions but the last counted through in order) at most 192 rows name the same one
- w_query: float32 [1024, 1024], P('dp'), may hold values from -0.625 to 0.625
- key_weight_matrix: float32 [1024, 512], P('dp'), may hold values from -0.625 to 0.625
- value_weight_matrix: float32 [1024, 512], P('dp'), may hold values from -0.1875 to 0.1875
- w_out: float32 [1024, 1024], P('dp'), may hold values from -6 to 6
- w_router: float32 [1024, 16], P('dp'), may hold values from -0.09375 to 0.09375
- gain_attn: float32 [1024], P('dp'), may hold values from 0.5 to 1.5
- gain_moe: float32 [1024], P('dp'), may hold values from 0.5 to 1.5
- expert_in: float32 [16, 1024, 1024], P('seq', 'dp'), may hold values from -0.1875 to 0.1875
- expert_out: float32 [16, 1024, 512], P('seq', 'dp'), may hold values from -5 to 5
Outputs:
- output: bfloat16 [4, 2048, 1024], P('dp', 'seq')
- input_grad: bfloat16 [4, 2048, 1024], P('dp', 'seq')
- grad_w_query: float32 [1024, 1024], P(('dp', 'seq'))
- grad_w_key: float32 [1024, 512], P(('dp', 'seq'))
- grad_w_value: float32 [1024, 512], P(('dp', 'seq'))
- grad_w_out: float32 [1024, 1024], P(('dp', 'seq'))
- grad_w_router: float32 [1024, 16], P(('dp', 'seq'))
- grad_gain_attn: float32 [1024], P(('dp', 'seq'))
- grad_gain_moe: float32 [1024], P(('dp', 'seq'))
- grad_expert_in: float32 [16, 1024, 1024], P('seq', 'dp')
- grad_expert_out: float32 [16, 1024, 512], P('seq', 'dp')
The draws below stay inside these ranges and needn't reach their ends.
Inputs may be any that keep to these rules, and one draw needn't show every extreme that they name: `doc_ids`: within each sequence segment numbers never fall; a segment has 1 to 1024 positions, one exactly that many. `expert_picks`: each token names 8 different experts. Among the 256 tokens of one device (aligned blocks of a sequence) no expert is named more than 192 times, a bound that some block reaches.
All inputs are finite; a program needn't handle non-finite values.
Results may differ from the reference program's by a relative error of at most 0.019.
The reference program's roundings to bfloat16 on the way count: a program that leaves them out, or rounds other values in their place, can miss the bound.
Values may be sent and summed in bfloat16 or wider, within the bound.
A program may use at most 192 MiB of HBM per device.

```python
import math
import jax
import jax.numpy as jnp
import numpy as np
from jax import lax

MODEL_DIM = 1024
QUERY_HEADS = 16
KEY_VALUE_HEADS = 8
HEAD_SIZE = 64
FFE = 512
TOP = 8
TOK_DEV = 256
EXPERTS = 16
SEQUENCE_TOKENS = 2048
SEQS = 4
CAP = 192
NDOCS = 16
N_SEQ = 8


def levels(stream_key, extent, split, least, high):
    def one(axis_at, shards_of):
        draws = jax.random.uniform(jax.random.fold_in(jax.random.fold_in(stream_key, 6), axis_at), (shards_of,), jnp.float32, least / len(split), high / len(split))
        return jnp.repeat(jnp.exp(draws), extent[axis_at] // shards_of).reshape((-1,) + (1,) * (len(extent) - axis_at - 1))

    factor_of = one(*split[0])
    for cut in split[1:]:
        factor_of = factor_of * one(*cut)
    return factor_of


def profile(number_of, total, reach, slope):
    weights = [(1 << 20) // math.isqrt(grade ** slope) + 1 for grade in range(2, number_of + 1)]
    surplus, counts = total - reach - (number_of - 1), [1] * (number_of - 1)
    while surplus > 0:
        movable = [i for i in range(number_of - 1) if counts[i] < reach]
        pool, remaining = sum([weights[i] for i in movable]), surplus
        for i in movable:
            extra = min(reach - counts[i], max(1, remaining * weights[i] // pool), surplus)
            counts[i] = counts[i] + extra
            surplus = surplus - extra
    return np.array([reach] + counts)


def uneven(key, count, total, limit, slope):
    if count == 2:
        one = jax.random.randint(key, (), max(1, total - limit), min(limit, total - 1) + 1)
        return jnp.stack([one, total - one])
    lengths = jnp.asarray(profile(count, total, limit, slope), jnp.int32)
    couples = (count - 1) // 2
    source_of, receiver = lengths[1:1 + 2 * couples:2], lengths[2:2 + 2 * couples:2]
    slack = jnp.minimum(source_of - 1, limit - receiver)
    moved = jax.random.randint(jax.random.fold_in(key, 1), (couples,), 0, 1 << 20) % (slack + 1)
    lengths = lengths.at[1:1 + 2 * couples:2].set(source_of - moved).at[2:2 + 2 * couples:2].set(receiver + moved)
    return lengths[jax.random.permutation(jax.random.fold_in(key, 2), count)]


def routed_block(own_key, own, number, rows, number_of, top, limit, skew):
    order = jax.random.permutation(own_key, number_of)
    heavy_load, ordinary = load_shares(number_of, rows * top, limit, skew, True), load_shares(number_of, rows * top, limit, skew, False)
    places = jnp.arange(number_of)

    def named(lengths, offset_by):
        used = int((lengths > 0).sum())
        fixed = max(1, used // 4)
        shifted = fixed + (places - fixed + offset_by * (used - fixed)) % max(1, number_of - fixed)
        return jnp.zeros((number_of,), jnp.int32).at[order[jnp.where(places < fixed, places, shifted)]].set(jnp.asarray(lengths, jnp.int32))

    lengths = jnp.where(number % 4 == 0, named(heavy_load, number // 4), named(ordinary, number - number // 4 - 1))
    mixed = jax.random.permutation(jax.random.fold_in(own, 3), number_of)
    source_of, receiver = mixed[0:number_of // 2 * 2:2], mixed[1:number_of // 2 * 2:2]
    slack = jnp.minimum(lengths[source_of] - 1, limit - lengths[receiver]) // 2
    slack = jnp.where((source_of == order[0]) | (receiver == order[0]) | (lengths[receiver] == 0), 0, jnp.maximum(slack, 0))
    shifted = jax.random.randint(jax.random.fold_in(own, 4), (number_of // 2,), 0, 1 << 20) % (slack + 1)
    lengths = lengths.at[source_of].add(-shifted).at[receiver].add(shifted)
    members = jnp.searchsorted(jnp.cumsum(lengths), jnp.arange(rows * top), side="right").astype(jnp.int32)
    table = members.reshape(top, rows).T
    table = table[jax.random.permutation(jax.random.fold_in(own, 1), rows)]
    offset_by = jax.random.randint(jax.random.fold_in(own, 2), (rows, 1), 0, top)
    return jnp.take_along_axis(table, (jnp.arange(top)[None, :] + offset_by) % top, axis=1)


def load_shares(count, total, most, slope, full):
    weights = [(1 << 20) // math.isqrt(standing ** slope) + 1 for standing in range(1, count + 1)]
    largest = most if full else min(most, max(-(-total // count), total * weights[0] // sum(weights)))
    least = 1 if total - largest >= count - 1 else 0
    given, spare = [largest] + [least] * (count - 1), total - largest - least * (count - 1)
    while spare > 0:
        free = [i for i in range(1, count) if given[i] < largest] or [i for i in range(1, count) if given[i] < most]
        mass, budget = sum([weights[i] for i in free]), spare
        for i in free:
            more = min(most - given[i], max(1, budget * weights[i] // mass), spare)
            given[i] = given[i] + more
            spare = spare - more
    return np.array(given)


def bell_draw(stream_key, dims, deviation, reach, cuts=(), kind=jnp.bfloat16):
    array = deviation * jax.random.normal(stream_key, dims, jnp.float32)
    if cuts:
        array = array * levels(stream_key, dims, cuts, -0.22, 0.18)
    return jnp.clip(array, -reach, reach).astype(kind)


def setup_inputs(seed: int = 0) -> dict:
    streams_of = jax.random.split(jax.random.key(seed), 14)
    tokens = bell_draw(streams_of[0], (SEQS, SEQUENCE_TOKENS, MODEL_DIM), 1.0, 6.0, ((0, 4), (1, 8)))
    out_grad = bell_draw(streams_of[1], (SEQS, SEQUENCE_TOKENS, MODEL_DIM), 1.0, 6.0, ((0, 4), (1, 8)))
    doc_ids = jax.vmap(lambda own: jnp.searchsorted(jnp.cumsum(uneven(own, NDOCS, SEQUENCE_TOKENS, SEQUENCE_TOKENS // 2, 2)), jnp.arange(SEQUENCE_TOKENS), side="right"))(jax.random.split(streams_of[2], SEQS)).reshape((SEQS, SEQUENCE_TOKENS)).astype(jnp.int32)
    expert_picks_keys = jax.random.split(jax.random.fold_in(streams_of[3], 1), SEQS * SEQUENCE_TOKENS // TOK_DEV)
    expert_picks_turns = jax.random.permutation(jax.random.fold_in(streams_of[3], 3), SEQS * SEQUENCE_TOKENS // TOK_DEV)
    expert_picks = jax.vmap(lambda own, number: routed_block(jax.random.fold_in(streams_of[3], 2), own, number, TOK_DEV, EXPERTS, TOP, CAP, 1))(expert_picks_keys, expert_picks_turns).reshape((SEQS, SEQUENCE_TOKENS, TOP))
    w_query = bell_draw(streams_of[4], (MODEL_DIM, QUERY_HEADS * HEAD_SIZE), (3.5 * MODEL_DIM ** -0.5), 0.625, ((0, 4),), jnp.float32)
    key_weight_matrix = bell_draw(streams_of[5], (MODEL_DIM, KEY_VALUE_HEADS * HEAD_SIZE), (3.5 * MODEL_DIM ** -0.5), 0.625, ((0, 4),), jnp.float32)
    value_weight_matrix = bell_draw(streams_of[6], (MODEL_DIM, KEY_VALUE_HEADS * HEAD_SIZE), MODEL_DIM ** -0.5, 0.1875, ((0, 4),), jnp.float32)
    w_out = bell_draw(streams_of[7], (QUERY_HEADS * HEAD_SIZE, MODEL_DIM), (30 * (QUERY_HEADS * HEAD_SIZE) ** -0.5), 6.0, ((0, 4),), jnp.float32)
    w_router = bell_draw(streams_of[8], (MODEL_DIM, EXPERTS), (0.5 * MODEL_DIM ** -0.5), 0.09375, ((0, 4),), jnp.float32)
    gain_attn = jnp.clip(1.0 + 0.1 * jax.random.normal(streams_of[9], (MODEL_DIM,), jnp.float32), 0.5, 1.5)
    gain_moe = jnp.clip(1.0 + 0.1 * jax.random.normal(streams_of[10], (MODEL_DIM,), jnp.float32), 0.5, 1.5)
    expert_in = bell_draw(streams_of[11], (EXPERTS, MODEL_DIM, 2 * FFE), MODEL_DIM ** -0.5, 0.1875, ((0, 8), (1, 4)), jnp.float32)
    expert_out = bell_draw(streams_of[12], (EXPERTS, MODEL_DIM, FFE), (20 * FFE ** -0.5), 5.0, ((0, 8), (1, 4)), jnp.float32)
    return dict(tokens=tokens, out_grad=out_grad, doc_ids=doc_ids, expert_picks=expert_picks, w_query=w_query, key_weight_matrix=key_weight_matrix, value_weight_matrix=value_weight_matrix, w_out=w_out, w_router=w_router, gain_attn=gain_attn, gain_moe=gain_moe, expert_in=expert_in, expert_out=expert_out)


att_mult = 0.015625
res_mult = 0.22
norm_eps = 1e-06
rope_theta = 10000.0
highest_precision = lax.Precision.HIGHEST

@jax.custom_vjp
def lower_precision(v):
    return lax.optimization_barrier(v.astype(jnp.bfloat16)).astype(jnp.float32)

@jax.custom_vjp
def lower_backward(v):
    return v

def low_keep(v):
    return (lower_precision(v), None)

def low_pass(kept, grad):
    return (grad,)

def back_keep(v):
    return (v, None)

def back_low(kept, grad):
    return (lower_precision(grad),)
lower_precision.defvjp(low_keep, low_pass)
lower_backward.defvjp(back_keep, back_low)

def rms_scale(values, gain_vec):
    return values * lax.rsqrt(lax.optimization_barrier(jnp.mean(values * values, axis=-1, keepdims=True)) + norm_eps) * gain_vec

def rope_tables(length_count, head_size):
    half_size = head_size // 2
    frequency = rope_theta ** (-jnp.arange(half_size, dtype=jnp.float32) * 2.0 / head_size)
    angles = jnp.arange(length_count, dtype=jnp.float32)[:, None] * frequency[None, :]
    return (jnp.cos(angles), jnp.sin(angles))

def apply_rotary(values, cosine_table, sinusoid_table):
    half_size = values.shape[-1] // 2
    first_half = values[..., :half_size]
    second_half = values[..., half_size:]
    cos_b = cosine_table[:, None, :]
    sin_b = sinusoid_table[:, None, :]
    return jnp.concatenate([first_half * cos_b - second_half * sin_b, second_half * cos_b + first_half * sin_b], axis=-1)

def slot_ranks(chosen):
    flat_hot = (chosen.reshape(N_SEQ, TOK_DEV * TOP)[:, :, None] == jnp.arange(EXPERTS, dtype=jnp.int32)[None, None, :]).astype(jnp.int32)
    ranks = lax.optimization_barrier(jnp.sum((jnp.cumsum(flat_hot, axis=1) - 1) * flat_hot, axis=2))
    offsets = (jnp.arange(N_SEQ, dtype=jnp.int32) * CAP)[:, None]
    return (ranks + offsets).astype(jnp.int32).reshape(SEQUENCE_TOKENS, TOP)

def attention(queries, keys_rep, values_rep, seq_docs):
    block_rows = min(512, SEQUENCE_TOKENS)
    block_count = SEQUENCE_TOKENS // block_rows
    key_positions = jnp.arange(SEQUENCE_TOKENS, dtype=jnp.int32)

    def one_block(item):
        query_block, doc_block, row_positions = item
        raw_scores = jnp.einsum('qhd,khd->hqk', query_block, keys_rep, precision=highest_precision) * att_mult
        allowed = (doc_block[:, None] == seq_docs[None, :]) & (row_positions[:, None] >= key_positions[None, :])
        scores = lower_backward(jnp.where(allowed[None], raw_scores, -1e+30))
        prob_rows = lower_precision(jax.nn.softmax(scores, axis=-1))
        return jnp.einsum('hqk,khd->qhd', prob_rows, values_rep, precision=highest_precision)
    outputs = lax.map(jax.checkpoint(one_block), (queries.reshape(block_count, block_rows, QUERY_HEADS, HEAD_SIZE), seq_docs.reshape(block_count, block_rows), key_positions.reshape(block_count, block_rows)))
    return outputs.reshape(SEQUENCE_TOKENS, QUERY_HEADS * HEAD_SIZE)

def layer(resid_in, w_query, key_weight_matrix, value_weight_matrix, w_out, w_router, gain_attn, gain_moe, expert_in, expert_out, seq_docs, chosen, slot_index):
    query_group_width = QUERY_HEADS // KEY_VALUE_HEADS
    attention_normed_input = lower_precision(rms_scale(resid_in, lower_precision(gain_attn)))
    query_lin = lower_backward(jnp.dot(attention_normed_input, lower_precision(w_query), precision=highest_precision)).reshape(SEQUENCE_TOKENS, QUERY_HEADS, HEAD_SIZE)
    key_linear = lower_backward(jnp.dot(attention_normed_input, lower_precision(key_weight_matrix), precision=highest_precision)).reshape(SEQUENCE_TOKENS, KEY_VALUE_HEADS, HEAD_SIZE)
    value_linear = lower_backward(jnp.dot(attention_normed_input, lower_precision(value_weight_matrix), precision=highest_precision)).reshape(SEQUENCE_TOKENS, KEY_VALUE_HEADS, HEAD_SIZE)
    cosine_table, sinusoid_table = rope_tables(SEQUENCE_TOKENS, HEAD_SIZE)
    queries = lower_precision(lower_backward(apply_rotary(query_lin, cosine_table, sinusoid_table)))
    keys_rep = lower_precision(lower_backward(jnp.repeat(apply_rotary(key_linear, cosine_table, sinusoid_table), query_group_width, axis=1)))
    values_rep = lower_precision(lower_backward(jnp.repeat(value_linear, query_group_width, axis=1)))
    attended = lower_precision(lower_backward(attention(queries, keys_rep, values_rep, seq_docs)))
    attn_branch = lower_backward(jnp.dot(attended, lower_precision(w_out), precision=highest_precision))
    mid_resid = resid_in + res_mult * attn_branch
    normed_m = lower_precision(rms_scale(mid_resid, lower_precision(gain_moe)))
    logits = lower_backward(jnp.dot(normed_m, lower_precision(w_router), precision=highest_precision))
    gate_probs = jax.nn.softmax(jnp.take_along_axis(logits, chosen, axis=1), axis=-1)
    spread_rows = jnp.broadcast_to(normed_m[:, None, :], (SEQUENCE_TOKENS, TOP, MODEL_DIM))
    expert_rows = lower_backward(jnp.zeros((EXPERTS, N_SEQ * CAP, MODEL_DIM), jnp.float32).at[chosen, slot_index].add(spread_rows))

    def one_expert(item):
        rows_in, weight_in, weight_out = item
        gate_up = lower_backward(jnp.dot(rows_in, lower_precision(weight_in), precision=highest_precision))
        hidden = lower_precision(jax.nn.silu(gate_up[:, :FFE]) * gate_up[:, FFE:])
        return lower_precision(lower_backward(jnp.dot(hidden, lower_precision(weight_out).T, precision=highest_precision)))
    expert_res = lax.map(jax.checkpoint(one_expert), (expert_rows, expert_in, expert_out))
    picked = expert_res[chosen, slot_index]
    moe_branch = lax.optimization_barrier(jnp.sum(gate_probs[:, :, None] * picked, axis=1))
    return mid_resid + res_mult * moe_branch

def reference(tokens, out_grad, doc_ids, expert_picks, w_query, key_weight_matrix, value_weight_matrix, w_out, w_router, gain_attn, gain_moe, expert_in, expert_out):
    weights = (w_query, key_weight_matrix, value_weight_matrix, w_out, w_router, gain_attn, gain_moe, expert_in, expert_out)
    grad_start = tuple((jnp.zeros_like(weight) for weight in weights))

    def one_sequence(grad_sums, item):
        token_rows, cot_rows, seq_docs, chosen = item
        slot_index = slot_ranks(chosen)

        def run_layer(resid_in, *params):
            return layer(resid_in, *params, seq_docs, chosen, slot_index)
        result, pull_back = jax.vjp(run_layer, token_rows.astype(jnp.float32), *weights)
        grads_all = pull_back(cot_rows.astype(jnp.float32))
        grad_sums = tuple((total_sum + grad_part for total_sum, grad_part in zip(grad_sums, grads_all[1:])))
        return (grad_sums, (result.astype(jnp.bfloat16), grads_all[0].astype(jnp.bfloat16)))
    grad_sums, (output, input_grad) = lax.scan(one_sequence, grad_start, (tokens, out_grad, doc_ids, expert_picks))
    return (output, input_grad, grad_sums[0], grad_sums[1], grad_sums[2], grad_sums[3], grad_sums[4], grad_sums[5], grad_sums[6], grad_sums[7], grad_sums[8])
```

```python
import jax
import jax.numpy as jnp
from jax import lax
from jax.experimental import pallas as pl
from jax.experimental.pallas import tpu as pltpu
from jax.sharding import PartitionSpec as P

MESH = pl.DeviceIdType.MESH


def _block(ref, j, cut):
    if cut is None:
        return ref.at[j]
    return ref.at[:, pl.ds(pl.multiple_of(j * cut, cut), cut)]


def exchange(collective_id, ops):
    axes = tuple(dict.fromkeys(axis for _, axis, _, _ in ops))
    size = {axis: lax.axis_size(axis) for axis in axes}
    out_shapes, out_specs, scratch, places = [], [], [], []
    for kind, axis, x, cut in ops:
        count = size[axis]
        out_spec = pl.BlockSpec(memory_space=pl.ANY)
        extra = []
        if kind == "gather":
            shape, dtype, copies = (count,) + x.shape, x.dtype, count - 1
        elif kind == "swap":
            copies, dtype = count - 1, x.dtype
            if cut is None:
                shape = x.shape
            elif cut[0] == "in":
                shape = (count, x.shape[0], cut[1])
            else:
                shape = (x.shape[1], count * cut[1])
        else:
            chips = count // 2
            shape, dtype, copies = x.shape[1:], jnp.float32, 2 * chips - 1
            out_spec = pl.BlockSpec(memory_space=pltpu.VMEM)
            extra = [
                pltpu.VMEM((chips,) + x.shape[1:], x.dtype),
                pltpu.VMEM((chips,) + x.shape[1:], x.dtype),
                pltpu.VMEM((chips,) + x.shape[1:], x.dtype),
                pltpu.VMEM((chips,) + x.shape[1:], x.dtype),
                pltpu.SemaphoreType.DMA((chips,)),
            ]
        out_shapes.append(jax.ShapeDtypeStruct(shape, dtype))
        out_specs.append(out_spec)
        places.append((len(scratch), len(extra)))
        scratch += [
            pltpu.SemaphoreType.DMA((copies,)),
            pltpu.SemaphoreType.DMA((copies,)),
            pltpu.SemaphoreType.DMA,
        ] + extra

    def kernel(*refs):
        ins, outs, work = refs[: len(ops)], refs[len(ops) : 2 * len(ops)], refs[2 * len(ops) :]
        me = {axis: lax.axis_index(axis) for axis in axes}
        barrier = pltpu.get_barrier_semaphore()
        for axis in axes:
            for k in range(1, size[axis]):
                pl.semaphore_signal(
                    barrier,
                    inc=1,
                    device_id={axis: lax.rem(me[axis] + k, size[axis])},
                    device_id_type=MESH,
                )
        pl.semaphore_wait(barrier, sum(size[axis] - 1 for axis in axes))

        def remote(axis, src, dst, send, recv, to):
            return pltpu.make_async_remote_copy(
                src_ref=src,
                dst_ref=dst,
                send_sem=send,
                recv_sem=recv,
                device_id={axis: to},
                device_id_type=MESH,
            )

        second, third = [], []
        for (kind, axis, _, cut), x, o, (at, extra) in zip(ops, ins, outs, places):
            send, recv, local = work[at : at + 3]
            count, my = size[axis], me[axis]
            if kind == "swap":
                into = cut[1] if cut is not None and cut[0] == "out" else None
                outof = cut[1] if cut is not None and cut[0] == "in" else None
                own = pltpu.make_async_copy(_block(x, my, outof), _block(o, my, into), local)
                own.start()
                third.append(own.wait)
                for k in range(1, count):
                    to = lax.rem(my + k, count)
                    copy = remote(
                        axis,
                        _block(x, to, outof),
                        _block(o, my, into),
                        send.at[k - 1],
                        recv.at[k - 1],
                        to,
                    )
                    copy.start()
                    frm = lax.rem(my + count - k, count)
                    arrive = remote(
                        axis,
                        _block(x, to, outof),
                        _block(o, frm, into),
                        send.at[k - 1],
                        recv.at[k - 1],
                        to,
                    )
                    third.append(copy.wait_send)
                    third.append(arrive.wait_recv)
            elif kind == "gather" and axis == "dp":
                own = pltpu.make_async_copy(x, o.at[my], local)
                own.start()
                third.append(own.wait)
                for k in range(1, count):
                    to = lax.rem(my + k, count)
                    frm = lax.rem(my + count - k, count)
                    copy = remote(axis, x, o.at[my], send.at[k - 1], recv.at[k - 1], to)
                    copy.start()
                    third.append(copy.wait_send)
                    third.append(
                        remote(
                            axis, x, o.at[frm], send.at[k - 1], recv.at[k - 1], to
                        ).wait_recv
                    )
            elif kind == "gather":
                chips = count // 2
                chip, core = my // 2, lax.rem(my, 2)
                sibling = my + 1 - 2 * core
                own = pltpu.make_async_copy(x, o.at[my], local)
                own.start()
                third.append(own.wait)
                for k in range(1, chips):
                    to = lax.rem(chip + k, chips) * 2 + core
                    copy = remote(axis, x, o.at[my], send.at[k], recv.at[k], to)
                    copy.start()
                    third.append(copy.wait_send)
                copy = remote(axis, x, o.at[my], send.at[0], recv.at[0], sibling)
                copy.start()
                third.append(copy.wait_send)
                third.append(
                    remote(
                        axis, x, o.at[sibling], send.at[0], recv.at[0], sibling
                    ).wait_recv
                )

                def forward(
                    k, axis=axis, x=x, o=o, send=send, recv=recv, chips=chips, chip=chip, core=core, sibling=sibling
                ):
                    frm = lax.rem(chip + chips - k, chips) * 2
                    remote(
                        axis, x, o.at[frm + core], send.at[k], recv.at[k], sibling
                    ).wait_recv()
                    slot = chips - 1 + k
                    copy = remote(
                        axis,
                        o.at[frm + core],
                        o.at[frm + core],
                        send.at[slot],
                        recv.at[slot],
                        sibling,
                    )
                    copy.start()
                    third.append(copy.wait_send)
                    third.append(
                        remote(
                            axis,
                            x,
                            o.at[frm + 1 - core],
                            send.at[slot],
                            recv.at[slot],
                            sibling,
                        ).wait_recv
                    )

                for k in range(1, chips):
                    second.append((k, lambda k=k, forward=forward: forward(k)))
            else:
                chips = count // 2
                chip, core = my // 2, lax.rem(my, 2)
                sibling = my + 1 - 2 * core
                mine, theirs, pre, far, loads = work[at + 3 : at + 3 + extra]
                order = [k % chips for k in range(1, chips + 1)]
                for k in order:
                    to = lax.rem(chip + k, chips)
                    remote(
                        axis,
                        x.at[2 * to + 1 - core],
                        theirs.at[k],
                        send.at[k],
                        recv.at[k],
                        sibling,
                    ).start()
                    pltpu.make_async_copy(x.at[2 * to + core], mine.at[k], loads.at[k]).start()

                def fold(k, last, axis=axis, x=x, o=o, send=send, recv=recv, chips=chips, chip=chip, core=core, sibling=sibling, mine=mine, theirs=theirs, pre=pre, far=far, loads=loads):
                    to = lax.rem(chip + k, chips)
                    give = remote(
                        axis,
                        x.at[2 * to + 1 - core],
                        theirs.at[k],
                        send.at[k],
                        recv.at[k],
                        sibling,
                    )
                    give.wait_recv()
                    third.append(give.wait_send)
                    pltpu.make_async_copy(
                        x.at[2 * to + core], mine.at[k], loads.at[k]
                    ).wait()
                    both = mine[k].astype(jnp.float32) + theirs[k].astype(jnp.float32)
                    if not last:
                        pre[k] = both.astype(pre.dtype)
                        copy = remote(
                            axis,
                            pre.at[k],
                            far.at[k],
                            send.at[chips - 1 + k],
                            recv.at[chips - 1 + k],
                            to * 2 + core,
                        )
                        copy.start()
                        third.append(copy.wait_send)
                    else:
                        o[...] = both

                for k in order:
                    second.append((k or chips, lambda k=k, fold=fold: fold(k, k == 0)))

                def total(k, axis=axis, o=o, send=send, recv=recv, chips=chips, pre=pre, far=far, core=core, chip=chip):
                    remote(
                        axis,
                        pre.at[k],
                        far.at[k],
                        send.at[chips - 1 + k],
                        recv.at[chips - 1 + k],
                        lax.rem(chip + k, chips) * 2 + core,
                    ).wait_recv()
                    o[...] += far[k].astype(jnp.float32)

                for k in range(1, chips):
                    second.append((chips + k, lambda k=k, total=total: total(k)))
        for _, run in sorted(second, key=lambda item: item[0]):
            run()
        for wait in third:
            wait()

    return pl.pallas_call(
        kernel,
        name=f"exchange{collective_id}",
        out_shape=out_shapes,
        in_specs=[pl.BlockSpec(memory_space=pl.ANY)] * len(ops),
        out_specs=out_specs,
        scratch_shapes=scratch,
        compiler_params=pltpu.CompilerParams(
            collective_id=collective_id, has_side_effects=True, vmem_limit_bytes=48 << 20
        ),
    )(*[x for _, _, x, _ in ops])

QUERY_HEADS = 16
KEY_VALUE_HEADS = 8
HEAD_SIZE = 64
FFE = 512
TOP = 8

att_mult = 0.015625
res_mult = 0.22
norm_eps = 1e-06
rope_theta = 10000.0
LANES = 128
bf16 = jnp.bfloat16
f32 = jnp.float32
HEADS_LANES = 128


def dot_nt(a, b):
    return lax.dot_general(a, b, (((1,), (1,)), ((), ())), preferred_element_type=f32)


def dot_nn(a, b):
    return lax.dot_general(a, b, (((1,), (0,)), ((), ())), preferred_element_type=f32)


def dot_tn(a, b):
    return lax.dot_general(a, b, (((0,), (0,)), ((), ())), preferred_element_type=f32)


def turn(x):
    half = HEAD_SIZE // 2
    lane = lax.broadcasted_iota(jnp.int32, x.shape, 1)
    width = x.shape[1]
    return jnp.where(
        lax.rem(lane, HEAD_SIZE) < half, pltpu.roll(x, width - half, 1), pltpu.roll(x, half, 1)
    )


def rope_tables(length):
    half = HEAD_SIZE // 2
    frequency = rope_theta ** (-jnp.arange(half, dtype=f32) * 2.0 / HEAD_SIZE)
    angles = jnp.arange(length, dtype=jnp.int32).astype(f32)[:, None] * frequency[None, :]
    cos, sin = jnp.cos(angles), jnp.sin(angles)
    repeat = LANES // HEAD_SIZE
    return (
        jnp.concatenate([cos, cos] * repeat, axis=1),
        jnp.concatenate([-sin, sin] * repeat, axis=1),
    )


def stack_heads(x, heads):
    return jnp.concatenate(
        [x[:, h * HEAD_SIZE : (h + 1) * HEAD_SIZE] for h in range(heads)], axis=0
    )


def attend_forward(tok_all, w_own, gain, cos, sin, start, heads):
    blocks, rows, width = tok_all.shape
    length = blocks * rows
    cols = heads * rows
    first = start.reshape(blocks, rows)[:, 0] // rows
    start_rows = jnp.tile(start.reshape(blocks, 1, rows), (1, 1, heads))
    out_width = heads * HEAD_SIZE

    def kernel(first_ref, tok, w, gain_ref, cos_ref, sin_ref, start_ref, na_ref, q_ref, kv_ref, att_ref, ot_ref, lse_ref, k_scr, vt_scr):
        i = pl.program_id(0)
        x = tok[0].astype(f32)
        scale = lax.rsqrt(jnp.mean(x * x, axis=-1, keepdims=True) + norm_eps)
        na = (x * scale * gain_ref[...].astype(f32)).astype(bf16)
        na_ref[0] = na
        qkv = dot_nn(na, w[...])
        c, s = cos_ref[0], sin_ref[0]
        q, kv = qkv[:, :HEADS_LANES], qkv[:, HEADS_LANES:]
        q = (q * c + turn(q) * s).astype(bf16)
        lane = lax.broadcasted_iota(jnp.int32, kv.shape, 1)
        kv = jnp.where(lane < HEAD_SIZE, kv * c + turn(kv) * s, kv).astype(bf16)
        q_ref[0] = q
        kv_ref[0] = kv
        k_scr[i] = kv[:, :HEAD_SIZE]
        vt_scr[i] = kv.astype(f32).T[HEAD_SIZE:].astype(bf16)
        q2 = stack_heads(q, heads)
        start_row = start_ref[0]
        query = i * rows + lax.rem(lax.broadcasted_iota(jnp.int32, (1, cols), 1), rows)
        key_iota = lax.broadcasted_iota(jnp.int32, (rows, cols), 0)

        def step(j, carry):
            top, total, ot = carry
            scores = dot_nt(k_scr[j], q2) * att_mult
            key = key_iota + j * rows
            scores = jnp.where((key >= start_row) & (key <= query), scores, -1e30)
            new_top = jnp.maximum(top, jnp.max(scores, axis=0, keepdims=True))
            p = jnp.exp(scores - new_top)
            keep = jnp.exp(top - new_top)
            total = total * keep + jnp.sum(p, axis=0, keepdims=True)
            ot = ot * keep + dot_nn(vt_scr[j], p.astype(bf16))
            return new_top, total, ot

        top, total, ot = lax.fori_loop(
            first_ref[i],
            i + 1,
            step,
            (
                jnp.full((1, cols), -1e30, f32),
                jnp.zeros((1, cols), f32),
                jnp.zeros((HEAD_SIZE, cols), f32),
            ),
        )
        ot = ot / total
        ot_ref[0] = ot
        lse_ref[0] = top + jnp.log(total)
        out = ot.T
        att_ref[0] = jnp.concatenate(
            [out[h * rows : (h + 1) * rows] for h in range(heads)], axis=1
        ).astype(bf16)

    def block(shape):
        return pl.BlockSpec((1,) + shape, lambda i, _: (i, 0, 0))

    def whole(shape):
        return pl.BlockSpec(shape, lambda i, _: (0,) * len(shape))

    grid_spec = pltpu.PrefetchScalarGridSpec(
        num_scalar_prefetch=1,
        grid=(blocks,),
        in_specs=[
            block((rows, width)),
            whole(w_own.shape),
            whole((1, width)),
            block((rows, LANES)),
            block((rows, LANES)),
            block((1, cols)),
        ],
        out_specs=[
            block((rows, width)),
            block((rows, HEADS_LANES)),
            block((rows, LANES)),
            block((rows, out_width)),
            block((HEAD_SIZE, cols)),
            block((1, cols)),
        ],
        scratch_shapes=[
            pltpu.VMEM((blocks, rows, HEAD_SIZE), bf16),
            pltpu.VMEM((blocks, HEAD_SIZE, rows), bf16),
        ],
    )
    return pl.pallas_call(
        kernel,
        name="attend_forward",
        grid_spec=grid_spec,
        out_shape=[
            jax.ShapeDtypeStruct((blocks, rows, width), bf16),
            jax.ShapeDtypeStruct((blocks, rows, HEADS_LANES), bf16),
            jax.ShapeDtypeStruct((blocks, rows, LANES), bf16),
            jax.ShapeDtypeStruct((blocks, rows, out_width), bf16),
            jax.ShapeDtypeStruct((blocks, HEAD_SIZE, cols), f32),
            jax.ShapeDtypeStruct((blocks, 1, cols), f32),
        ],
        cost_estimate=pl.CostEstimate(
            flops=2 * length * width * 256 + 2 * length * length * cols // rows * 128,
            bytes_accessed=2 * length * width * 4,
            transcendentals=length * length,
        ),
        compiler_params=pltpu.CompilerParams(
            dimension_semantics=("arbitrary",), vmem_limit_bytes=40 << 20
        ),
    )(
        first,
        tok_all,
        w_own,
        gain,
        cos.reshape(blocks, rows, LANES),
        sin.reshape(blocks, rows, LANES),
        start_rows,
    )


def attend_backward(q_all, kv_all, cot, ot, lse, cos, sin, start, heads):
    blocks, rows, _ = q_all.shape
    length = blocks * rows
    cols = heads * rows
    first = start.reshape(blocks, rows)[:, 0] // rows
    start_rows = jnp.tile(start.reshape(blocks, 1, rows), (1, 1, heads))

    def kernel(first_ref, q_ref, kv_ref, do_ref, ot_ref, lse_ref, cos_ref, sin_ref, start_ref, out_ref, dk_scr, dv_scr, dq_scr):
        i = pl.program_id(0)

        @pl.when(i == 0)
        def _():
            dk_scr[...] = jnp.zeros_like(dk_scr)
            dv_scr[...] = jnp.zeros_like(dv_scr)

        q2 = stack_heads(q_ref[0], heads)
        do2 = stack_heads(do_ref[0], heads)
        delta = jnp.sum(do2.astype(f32).T * ot_ref[0], axis=0, keepdims=True)
        log_total = lse_ref[0]
        start_row = start_ref[0]
        query = i * rows + lax.rem(lax.broadcasted_iota(jnp.int32, (1, cols), 1), rows)
        key_iota = lax.broadcasted_iota(jnp.int32, (rows, cols), 0)
        dq_scr[...] = jnp.zeros_like(dq_scr)

        @pl.loop(first_ref[i], i + 1)
        def _(j):
            kv = kv_ref[j]
            k, v = kv[:, :HEAD_SIZE], kv[:, HEAD_SIZE:]
            scores = dot_nt(k, q2) * att_mult
            key = key_iota + j * rows
            p = jnp.where(
                (key >= start_row) & (key <= query), jnp.exp(scores - log_total), 0.0
            )
            ds = (p * (dot_nt(v, do2) - delta)).astype(bf16)
            dv_scr[j] += dot_nn(p.astype(bf16), do2)
            dk_scr[j] += dot_nn(ds, q2)
            dq_scr[...] += dot_tn(ds, k)

        def rope_back(x, c, s):
            return (x * c - turn(x) * s).astype(bf16)

        dq = dq_scr[...] * att_mult
        dq = [dq[h * rows : (h + 1) * rows] for h in range(heads)]
        if heads * HEAD_SIZE < HEADS_LANES:
            dq.append(jnp.zeros((rows, HEADS_LANES - heads * HEAD_SIZE), f32))
        dq = jnp.concatenate(dq, axis=1).astype(bf16).astype(f32)
        out_ref[i, :, :HEADS_LANES] = rope_back(dq, cos_ref[i], sin_ref[i])

        @pl.when(i == blocks - 1)
        def _():
            @pl.loop(0, blocks)
            def _(j):
                kv = jnp.concatenate([dk_scr[j] * att_mult, dv_scr[j]], axis=1)
                lane = lax.broadcasted_iota(jnp.int32, kv.shape, 1)
                out_ref[j, :, HEADS_LANES:] = jnp.where(
                    lane < HEAD_SIZE, kv * cos_ref[j] - turn(kv) * sin_ref[j], kv
                ).astype(bf16)

    def block(shape):
        return pl.BlockSpec((1,) + shape, lambda i, _: (i, 0, 0))

    def whole(shape):
        return pl.BlockSpec(shape, lambda i, _: (0,) * len(shape))

    grid_spec = pltpu.PrefetchScalarGridSpec(
        num_scalar_prefetch=1,
        grid=(blocks,),
        in_specs=[
            block((rows, HEADS_LANES)),
            whole((blocks, rows, LANES)),
            block((rows, heads * HEAD_SIZE)),
            block((HEAD_SIZE, cols)),
            block((1, cols)),
            whole((blocks, rows, LANES)),
            whole((blocks, rows, LANES)),
            block((1, cols)),
        ],
        out_specs=whole((blocks, rows, HEADS_LANES + LANES)),
        scratch_shapes=[
            pltpu.VMEM((blocks, rows, HEAD_SIZE), f32),
            pltpu.VMEM((blocks, rows, HEAD_SIZE), f32),
            pltpu.VMEM((cols, HEAD_SIZE), f32),
        ],
    )
    return pl.pallas_call(
        kernel,
        name="attend_backward",
        grid_spec=grid_spec,
        out_shape=jax.ShapeDtypeStruct((blocks, rows, HEADS_LANES + LANES), bf16),
        cost_estimate=pl.CostEstimate(
            flops=5 * length * length * cols // rows * 128,
            bytes_accessed=2 * length * 1024,
            transcendentals=length * length,
        ),
        compiler_params=pltpu.CompilerParams(
            dimension_semantics=("arbitrary",), vmem_limit_bytes=48 << 20
        ),
    )(
        first,
        q_all,
        kv_all,
        cot,
        ot,
        lse,
        cos.reshape(blocks, rows, LANES),
        sin.reshape(blocks, rows, LANES),
        start_rows,
    )


def rms_parts(values):
    return lax.rsqrt(jnp.mean(values * values, axis=-1, keepdims=True) + norm_eps)


def rms_pull(values, scale, gain, cot):
    weighted = cot * gain
    pulled = scale * weighted - values * (scale * scale * scale) * jnp.mean(
        weighted * values, axis=-1, keepdims=True
    )
    return pulled, jnp.sum(cot * values * scale, axis=0)


def on_device(
    tokens,
    out_grad,
    doc_ids,
    expert_picks,
    w_query,
    key_weight_matrix,
    value_weight_matrix,
    w_out,
    w_router,
    gain_attn,
    gain_moe,
    expert_in,
    expert_out,
):
    devices, parts = lax.axis_size("seq"), lax.axis_size("dp")
    me = lax.axis_index("seq")
    rows, width = tokens.shape[1:]
    length = rows * devices
    experts = w_router.shape[1]
    own_experts = expert_in.shape[0]
    heads = QUERY_HEADS // devices
    group = QUERY_HEADS // KEY_VALUE_HEADS
    share = max(1, group // heads)
    q_width = heads * HEAD_SIZE
    w_rows = w_query.shape[0]

    wq = w_query.astype(bf16).reshape(w_rows, devices, q_width)
    wq = jnp.pad(wq, ((0, 0), (0, 0), (0, HEADS_LANES - q_width)))
    wk = key_weight_matrix.astype(bf16).reshape(w_rows, KEY_VALUE_HEADS, HEAD_SIZE)
    wv = value_weight_matrix.astype(bf16).reshape(w_rows, KEY_VALUE_HEADS, HEAD_SIZE)
    wkv = jnp.repeat(jnp.concatenate([wk, wv], axis=2), share, axis=1)
    w_cols = HEADS_LANES + LANES
    w_all = jnp.concatenate([wq, wkv], axis=2).reshape(w_rows, devices * w_cols)
    w_own = lax.dynamic_slice_in_dim(w_all, me * w_cols, w_cols, 1)
    misc = jnp.concatenate(
        [w_router, gain_attn[:, None], gain_moe[:, None]], axis=1
    ).astype(bf16)
    misc = jnp.pad(misc, ((0, 0), (0, LANES - experts - 2)))
    ints = jnp.concatenate([expert_picks[0].T, doc_ids], axis=0)
    ints = jnp.pad(ints, ((0, 16 - TOP - 1), (0, 0)))

    out_grad_all = lax.all_gather(out_grad[0], "seq", axis=0, tiled=True)
    expert_in_full = lax.all_gather(expert_in.astype(bf16), "dp", axis=1, tiled=True)
    expert_out_full = lax.all_gather(expert_out.astype(bf16), "dp", axis=1, tiled=True)
    w_full = lax.all_gather(w_all, "dp", axis=0, tiled=True)

    tok_all, ints_all, w_own_all, wo_full, misc_full = exchange(
        0,
        [
            ("gather", "seq", tokens[0], None),
            ("gather", "seq", ints, None),
            ("gather", "dp", w_own, None),
            ("gather", "dp", w_out.astype(bf16), None),
            ("gather", "dp", misc, None),
        ],
    )
    w_own_all = w_own_all.reshape(width, w_cols)
    wo_full = wo_full.reshape(width, width)
    misc_full = misc_full.reshape(width, LANES)
    router_full = misc_full[:, :experts]
    gain_a = misc_full[:, experts]
    gain_m = misc_full[:, experts + 1].astype(f32)
    docs = ints_all[:, TOP].reshape(length)
    picks = ints_all[:, :TOP].transpose(1, 0, 2).reshape(TOP, length)
    start = jnp.sum((docs[:, None] < docs[None, :]).astype(jnp.int32), axis=0)
    cos, sin = rope_tables(length)

    normed_a, q_all, kv_all, attended_own, ot, lse = attend_forward(
        tok_all, w_own_all, gain_a[None], cos, sin, start, heads
    )
    wide = q_width % LANES == 0
    (attended,) = exchange(
        1, [("swap", "seq", attended_own, ("out", q_width) if wide else None)]
    )
    if not wide:
        attended = attended.transpose(1, 0, 2).reshape(rows, devices * q_width)

    resid = tokens[0].astype(f32)
    mid = resid + res_mult * dot_nn(attended, wo_full)
    mid_scale = rms_parts(mid)
    normed_m = (mid * mid_scale * gain_m).astype(bf16)
    (moe_all,) = exchange(2, [("gather", "seq", normed_m, None)])
    moe_all = moe_all.reshape(length, width)

    logits = lax.dot_general(
        router_full, moe_all, (((0,), (1,)), ((), ())), preferred_element_type=f32
    )
    chosen = jnp.any(
        picks[:, None, :] == jnp.arange(experts, dtype=jnp.int32)[None, :, None], axis=0
    )
    logits = jnp.where(chosen, logits, -jnp.inf)
    gates = jnp.exp(logits - jnp.max(logits, axis=0, keepdims=True))
    gates = gates / jnp.sum(gates, axis=0, keepdims=True)
    own_gates = lax.dynamic_slice_in_dim(gates, me * own_experts, own_experts, 0)

    out_cot = out_grad_all.astype(f32) * res_mult
    branch = jnp.zeros((length, width), f32)
    moe_cot = jnp.zeros((length, width), f32)
    gate_cots, grads_in, grads_out = [], [], []
    for e in range(own_experts):
        gate = own_gates[e][:, None]
        lin = dot_nn(moe_all, expert_in_full[e])
        gate_lin, up_lin = lin[:, :FFE], lin[:, FFE:]
        sig = jax.nn.sigmoid(gate_lin)
        silu = gate_lin * sig
        hidden = (silu * up_lin).astype(bf16)
        res = dot_nt(hidden, expert_out_full[e]).astype(bf16).astype(f32)
        branch = branch + gate * res
        gate_cots.append(jnp.sum(out_cot * res, axis=1))
        slot = (gate * out_cot).astype(bf16)
        hidden_cot = dot_nn(slot, expert_out_full[e])
        grads_out.append(dot_tn(slot, hidden).astype(bf16))
        lin_cot = jnp.concatenate(
            [hidden_cot * up_lin * (sig * (1 + gate_lin * (1 - sig))), hidden_cot * silu], axis=1
        ).astype(bf16)
        grads_in.append(dot_tn(moe_all, lin_cot).astype(bf16))
        moe_cot = moe_cot + dot_nt(lin_cot, expert_in_full[e]).astype(bf16).astype(f32)
    gate_cot = jnp.pad(
        jnp.stack(gate_cots).reshape(own_experts, devices, rows).transpose(1, 0, 2),
        ((0, 0), (0, 8 - own_experts), (0, 0)),
    )
    moe_sum, branch_sum, gate_cot = exchange(
        3,
        [
            ("sum", "seq", moe_cot.astype(bf16).reshape(devices, rows, width), None),
            ("sum", "seq", branch.astype(bf16).reshape(devices, rows, width), None),
            ("swap", "seq", gate_cot, None),
        ],
    )
    grads_in = jnp.stack(grads_in).reshape(own_experts, parts, w_rows, 2 * FFE)
    grads_out = jnp.stack(grads_out).reshape(own_experts, parts, w_rows, FFE)
    grads_in = lax.all_to_all(grads_in, "dp", split_axis=1, concat_axis=1)
    grads_out = lax.all_to_all(grads_out, "dp", split_axis=1, concat_axis=1)
    grad_e_in = jnp.sum(grads_in.astype(f32), axis=1)
    grad_e_out = jnp.sum(grads_out.astype(f32), axis=1)

    output = (mid + res_mult * branch_sum).astype(bf16)[None]
    gate_cot = gate_cot[:, :own_experts].reshape(experts, rows)
    my_gates = lax.dynamic_slice_in_dim(gates, me * rows, rows, 1)
    pick_cot = my_gates * (gate_cot - jnp.sum(my_gates * gate_cot, axis=0, keepdims=True))
    logit_cot = pick_cot.astype(bf16)
    grad_router = dot_nn(logit_cot, normed_m).T
    normed_m_cot = moe_sum + lax.dot_general(
        logit_cot, router_full, (((0,), (1,)), ((), ())), preferred_element_type=f32
    )
    pulled, grad_gain_m = rms_pull(mid, mid_scale, gain_m, normed_m_cot)
    mid_cot = out_grad[0].astype(f32) + pulled
    branch_cot = (res_mult * mid_cot).astype(bf16)
    grad_wo = dot_tn(attended, branch_cot)
    attended_cot = dot_nt(branch_cot, wo_full).astype(bf16)
    if not wide:
        attended_cot = attended_cot.reshape(rows, devices, q_width).transpose(1, 0, 2)
    (heads_cot,) = exchange(
        4, [("swap", "seq", attended_cot, ("in", q_width) if wide else None)]
    )
    qkv_cot = attend_backward(q_all, kv_all, heads_cot, ot, lse, cos, sin, start, heads)
    grad_qkv = dot_tn(
        normed_a.reshape(length, width), qkv_cot.reshape(length, w_cols)
    ).astype(bf16)
    token_pack = jnp.concatenate(
        [
            grad_wo,
            grad_router,
            grad_gain_m[:, None],
            jnp.zeros((width, LANES - experts - 1), f32),
        ],
        axis=1,
    ).astype(bf16)
    pack_cols = width + LANES
    qkv_cot_tok, grad_qkv, token_pack = exchange(
        5,
        [
            ("swap", "seq", qkv_cot, ("out", w_cols)),
            ("swap", "dp", grad_qkv.reshape(parts, w_rows, w_cols), None),
            ("swap", "dp", token_pack.reshape(parts, w_rows, pack_cols), None),
        ],
    )
    normed_a_cot = dot_nt(qkv_cot_tok, w_full)
    grad_qkv = jnp.sum(grad_qkv.astype(f32), axis=0).astype(bf16)
    token_pack = jnp.sum(token_pack.astype(f32), axis=0).astype(bf16)
    out_rows = w_rows // devices
    grad_qkv, token_pack = exchange(
        6,
        [
            ("swap", "seq", grad_qkv.reshape(devices, out_rows, w_cols), None),
            ("swap", "seq", token_pack.reshape(devices, out_rows, pack_cols), None),
        ],
    )
    resid_scale = rms_parts(resid)
    weighted = normed_a_cot * gain_a.astype(f32)
    input_grad = (
        mid_cot
        + resid_scale * weighted
        - resid
        * (resid_scale * resid_scale * resid_scale)
        * jnp.mean(weighted * resid, axis=-1, keepdims=True)
    ).astype(bf16)[None]

    grad_qkv = grad_qkv.astype(f32)
    grad_wq = grad_qkv[:, :, :q_width].transpose(1, 0, 2).reshape(out_rows, devices * q_width)

    def per_head(part):
        part = part.reshape(devices // share, share, out_rows, HEAD_SIZE).sum(axis=1)
        return part.transpose(1, 0, 2).reshape(out_rows, KEY_VALUE_HEADS * HEAD_SIZE)

    grad_wk = per_head(grad_qkv[:, :, HEADS_LANES : HEADS_LANES + HEAD_SIZE])
    grad_wv = per_head(grad_qkv[:, :, HEADS_LANES + HEAD_SIZE :])
    token_pack = jnp.sum(token_pack.astype(f32), axis=0)
    grad_wo = token_pack[:, :width]
    grad_router = token_pack[:, width : width + experts]
    grad_gain_m = token_pack[:, width + experts]

    def own_rows(weight):
        return lax.dynamic_slice_in_dim(weight, me * out_rows, out_rows, 0).astype(bf16).astype(f32)

    grad_gain_a = (
        jnp.sum(own_rows(w_query) * grad_wq, axis=1)
        + jnp.sum(own_rows(key_weight_matrix) * grad_wk, axis=1)
        + jnp.sum(own_rows(value_weight_matrix) * grad_wv, axis=1)
    ) / own_rows(gain_attn)
    return (
        output,
        input_grad,
        grad_wq,
        grad_wk,
        grad_wv,
        grad_wo,
        grad_router,
        grad_gain_a,
        grad_gain_m,
        grad_e_in,
        grad_e_out,
    )


def solution(mesh):
    return jax.shard_map(
        on_device,
        mesh=mesh,
        in_specs=(
            P("dp", "seq", None),
            P("dp", "seq", None),
            P("dp", "seq"),
            P("dp", "seq", None),
            P("dp", None),
            P("dp", None),
            P("dp", None),
            P("dp", None),
            P("dp", None),
            P("dp"),
            P("dp"),
            P("seq", "dp", None),
            P("seq", "dp", None),
        ),
        out_specs=(
            P("dp", "seq", None),
            P("dp", "seq", None),
            P(("dp", "seq"), None),
            P(("dp", "seq"), None),
            P(("dp", "seq"), None),
            P(("dp", "seq"), None),
            P(("dp", "seq"), None),
            P(("dp", "seq")),
            P(("dp", "seq")),
            P("seq", "dp", None),
            P("seq", "dp", None),
        ),
        check_vma=False,
    )
```

```python
import functools

import jax
import jax.numpy as jnp
from jax import lax
from jax.experimental import pallas as pl
from jax.experimental.pallas import tpu as pltpu
from jax.sharding import PartitionSpec as P

MESH = pl.DeviceIdType.MESH


def _block(ref, j, cut):
    if cut is None:
        return ref.at[j]
    return ref.at[:, pl.ds(pl.multiple_of(j * cut, cut), cut)]


def exchange(collective_id, ops):
    axes = tuple(dict.fromkeys(axis for _, axis, _, _ in ops))
    size = {axis: lax.axis_size(axis) for axis in axes}
    out_shapes, out_specs, scratch, places = [], [], [], []
    for kind, axis, x, cut in ops:
        count = size[axis]
        out_spec = pl.BlockSpec(memory_space=pl.ANY)
        extra = []
        if kind == "gather":
            shape, dtype = (count,) + x.shape, x.dtype
            copies = count - 1 if axis == "dp" else 3 + 4 * (count // 2 - 1)
        elif kind == "swap":
            copies, dtype = count - 1, x.dtype
            if cut is None:
                shape = x.shape
            elif cut[0] == "in":
                shape = (count, x.shape[0], cut[1])
            else:
                shape = (x.shape[1], count * cut[1])
        else:
            chips = count // 2
            shape, dtype, copies = x.shape[1:], jnp.float32, 2 * chips - 1
            out_spec = pl.BlockSpec(memory_space=pltpu.VMEM)
            extra = [
                pltpu.VMEM((chips,) + x.shape[1:], x.dtype),
                pltpu.VMEM((chips,) + x.shape[1:], x.dtype),
                pltpu.VMEM((chips,) + x.shape[1:], x.dtype),
                pltpu.VMEM((chips,) + x.shape[1:], x.dtype),
                pltpu.SemaphoreType.DMA((chips,)),
            ]
        out_shapes.append(jax.ShapeDtypeStruct(shape, dtype))
        out_specs.append(out_spec)
        places.append((len(scratch), len(extra)))
        scratch += [
            pltpu.SemaphoreType.DMA((copies,)),
            pltpu.SemaphoreType.DMA((max(copies, count),)),
            pltpu.SemaphoreType.DMA,
        ] + extra

    def kernel(*refs):
        ins, outs, work = refs[: len(ops)], refs[len(ops) : 2 * len(ops)], refs[2 * len(ops) :]
        me = {axis: lax.axis_index(axis) for axis in axes}
        barrier = pltpu.get_barrier_semaphore()
        for axis in axes:
            for k in range(1, size[axis]):
                pl.semaphore_signal(
                    barrier,
                    inc=1,
                    device_id={axis: lax.rem(me[axis] + k, size[axis])},
                    device_id_type=MESH,
                )
        pl.semaphore_wait(barrier, sum(size[axis] - 1 for axis in axes))

        def remote(axis, src, dst, send, recv, to):
            return pltpu.make_async_remote_copy(
                src_ref=src,
                dst_ref=dst,
                send_sem=send,
                recv_sem=recv,
                device_id={axis: to},
                device_id_type=MESH,
            )

        second, third = [], []
        for (kind, axis, _, cut), x, o, (at, extra) in zip(ops, ins, outs, places):
            send, recv, local = work[at : at + 3]
            count, my = size[axis], me[axis]
            if kind == "swap":
                into = cut[1] if cut is not None and cut[0] == "out" else None
                outof = cut[1] if cut is not None and cut[0] == "in" else None
                own = pltpu.make_async_copy(_block(x, my, outof), _block(o, my, into), local)
                own.start()
                third.append(own.wait)
                for k in range(1, count):
                    to = lax.rem(my + k, count)
                    copy = remote(
                        axis,
                        _block(x, to, outof),
                        _block(o, my, into),
                        send.at[k - 1],
                        recv.at[k - 1],
                        to,
                    )
                    copy.start()
                    frm = lax.rem(my + count - k, count)
                    arrive = remote(
                        axis,
                        _block(x, to, outof),
                        _block(o, frm, into),
                        send.at[k - 1],
                        recv.at[k - 1],
                        to,
                    )
                    third.append(copy.wait_send)
                    third.append(arrive.wait_recv)
            elif kind == "gather" and axis == "dp":
                own = pltpu.make_async_copy(x, o.at[my], local)
                own.start()
                third.append(own.wait)
                for k in range(1, count):
                    to = lax.rem(my + k, count)
                    frm = lax.rem(my + count - k, count)
                    copy = remote(axis, x, o.at[my], send.at[k - 1], recv.at[k - 1], to)
                    copy.start()
                    third.append(copy.wait_send)
                    third.append(
                        remote(
                            axis, x, o.at[frm], send.at[k - 1], recv.at[k - 1], to
                        ).wait_recv
                    )
            elif kind == "gather":
                chips = count // 2
                chip, core = my // 2, lax.rem(my, 2)
                sibling = my + 1 - 2 * core
                own = pltpu.make_async_copy(x, o.at[my], local)
                own.start()
                third.append(own.wait)

                def line(src, b, slot, to, axis=axis, o=o, send=send, recv=recv, core=core):
                    return remote(
                        axis, src, o.at[2 * b + core], send.at[slot], recv.at[b], to
                    )

                def across(src, b, slot, half, axis=axis, o=o, send=send, recv=recv, chips=chips, sibling=sibling):
                    return remote(
                        axis, src, o.at[2 * b + half], send.at[slot], recv.at[chips + b], sibling
                    )

                def guarded(where, act):
                    pl.when(where)(act)

                for slot, where, to in ((0, chip > 0, my - 2), (1, chip < chips - 1, my + 2)):
                    copy = line(x, chip, slot, to)
                    guarded(where, copy.start)
                    third.append(functools.partial(guarded, where, copy.wait_send))
                copy = across(x, chip, 2, core)
                copy.start()
                third.append(copy.wait_send)
                third.append(across(x, chip, 2, 1 - core).wait_recv)

                def hop(k, side, chips=chips, chip=chip, core=core, my=my, x=x, o=o, line=line, across=across):
                    b = chip + side * k
                    there = (b >= 0) & (b < chips)
                    onward = there & ((chip - side >= 0) & (chip - side < chips))
                    slot = 3 + (k - 1) * 4 + (side + 1)
                    spot = o.at[2 * b + core]
                    further = line(spot, b, slot, my - 2 * side)
                    over = across(spot, b, slot + 1, core)

                    @pl.when(there)
                    def _():
                        line(x, b, slot, my).wait_recv()
                        over.start()

                    guarded(onward, further.start)
                    third.append(functools.partial(guarded, onward, further.wait_send))
                    third.append(functools.partial(guarded, there, over.wait_send))
                    third.append(
                        functools.partial(
                            guarded, there, across(x, b, slot + 1, 1 - core).wait_recv
                        )
                    )

                for k in range(1, chips):
                    for side in (-1, 1):
                        second.append((k, functools.partial(hop, k, side)))
            else:
                chips = count // 2
                chip, core = my // 2, lax.rem(my, 2)
                sibling = my + 1 - 2 * core
                mine, theirs, pre, far, loads = work[at + 3 : at + 3 + extra]
                order = [k % chips for k in range(1, chips + 1)]
                for k in order:
                    to = lax.rem(chip + k, chips)
                    remote(
                        axis,
                        x.at[2 * to + 1 - core],
                        theirs.at[k],
                        send.at[k],
                        recv.at[k],
                        sibling,
                    ).start()
                    pltpu.make_async_copy(x.at[2 * to + core], mine.at[k], loads.at[k]).start()

                def fold(k, last, axis=axis, x=x, o=o, send=send, recv=recv, chips=chips, chip=chip, core=core, sibling=sibling, mine=mine, theirs=theirs, pre=pre, far=far, loads=loads):
                    to = lax.rem(chip + k, chips)
                    give = remote(
                        axis,
                        x.at[2 * to + 1 - core],
                        theirs.at[k],
                        send.at[k],
                        recv.at[k],
                        sibling,
                    )
                    give.wait_recv()
                    third.append(give.wait_send)
                    pltpu.make_async_copy(
                        x.at[2 * to + core], mine.at[k], loads.at[k]
                    ).wait()
                    both = mine[k].astype(jnp.float32) + theirs[k].astype(jnp.float32)
                    if not last:
                        pre[k] = both.astype(pre.dtype)
                        copy = remote(
                            axis,
                            pre.at[k],
                            far.at[k],
                            send.at[chips - 1 + k],
                            recv.at[chips - 1 + k],
                            to * 2 + core,
                        )
                        copy.start()
                        third.append(copy.wait_send)
                    else:
                        o[...] = both

                for k in order:
                    second.append((k or chips, lambda k=k, fold=fold: fold(k, k == 0)))

                def total(k, axis=axis, o=o, send=send, recv=recv, chips=chips, pre=pre, far=far, core=core, chip=chip):
                    remote(
                        axis,
                        pre.at[k],
                        far.at[k],
                        send.at[chips - 1 + k],
                        recv.at[chips - 1 + k],
                        lax.rem(chip + k, chips) * 2 + core,
                    ).wait_recv()
                    o[...] += far[k].astype(jnp.float32)

                for k in range(1, chips):
                    second.append((chips + k, lambda k=k, total=total: total(k)))
        for _, run in sorted(second, key=lambda item: item[0]):
            run()
        for wait in third:
            wait()

    return pl.pallas_call(
        kernel,
        name=f"exchange{collective_id}",
        out_shape=out_shapes,
        in_specs=[pl.BlockSpec(memory_space=pl.ANY)] * len(ops),
        out_specs=out_specs,
        scratch_shapes=scratch,
        compiler_params=pltpu.CompilerParams(
            collective_id=collective_id, has_side_effects=True, vmem_limit_bytes=48 << 20
        ),
    )(*[x for _, _, x, _ in ops])

QUERY_HEADS = 16
KEY_VALUE_HEADS = 8
HEAD_SIZE = 64
FFE = 512
TOP = 8

att_mult = 0.015625
res_mult = 0.22
norm_eps = 1e-06
rope_theta = 10000.0
LANES = 128
bf16 = jnp.bfloat16
f32 = jnp.float32
HEADS_LANES = 128


def dot_nt(a, b):
    return lax.dot_general(a, b, (((1,), (1,)), ((), ())), preferred_element_type=f32)


def dot_nn(a, b):
    return lax.dot_general(a, b, (((1,), (0,)), ((), ())), preferred_element_type=f32)


def dot_tn(a, b):
    return lax.dot_general(a, b, (((0,), (0,)), ((), ())), preferred_element_type=f32)


def turn(x):
    half = HEAD_SIZE // 2
    lane = lax.broadcasted_iota(jnp.int32, x.shape, 1)
    width = x.shape[1]
    return jnp.where(
        lax.rem(lane, HEAD_SIZE) < half, pltpu.roll(x, width - half, 1), pltpu.roll(x, half, 1)
    )


def rope_tables(length):
    half = HEAD_SIZE // 2
    frequency = rope_theta ** (-jnp.arange(half, dtype=f32) * 2.0 / HEAD_SIZE)
    angles = jnp.arange(length, dtype=jnp.int32).astype(f32)[:, None] * frequency[None, :]
    cos, sin = jnp.cos(angles), jnp.sin(angles)
    repeat = LANES // HEAD_SIZE
    return (
        jnp.concatenate([cos, cos] * repeat, axis=1),
        jnp.concatenate([-sin, sin] * repeat, axis=1),
    )


def stack_heads(x, heads):
    return jnp.concatenate(
        [x[:, h * HEAD_SIZE : (h + 1) * HEAD_SIZE] for h in range(heads)], axis=0
    )


def attend_forward(tok_all, w_own, gain, cos, sin, start, heads):
    blocks, rows, width = tok_all.shape
    length = blocks * rows
    cols = heads * rows
    first = start.reshape(blocks, rows)[:, 0] // rows
    start_rows = jnp.tile(start.reshape(blocks, 1, rows), (1, 1, heads))
    out_width = heads * HEAD_SIZE

    def kernel(first_ref, tok, w, gain_ref, cos_ref, sin_ref, start_ref, na_ref, q_ref, kv_ref, att_ref, ot_ref, lse_ref, k_scr, vt_scr):
        i = pl.program_id(0)
        x = tok[0].astype(f32)
        scale = lax.rsqrt(jnp.mean(x * x, axis=-1, keepdims=True) + norm_eps)
        na = (x * scale * gain_ref[...].astype(f32)).astype(bf16)
        na_ref[0] = na
        qkv = dot_nn(na, w[...])
        c, s = cos_ref[0], sin_ref[0]
        q, kv = qkv[:, :HEADS_LANES], qkv[:, HEADS_LANES:]
        q = (q * c + turn(q) * s).astype(bf16)
        lane = lax.broadcasted_iota(jnp.int32, kv.shape, 1)
        kv = jnp.where(lane < HEAD_SIZE, kv * c + turn(kv) * s, kv).astype(bf16)
        q_ref[0] = q
        kv_ref[0] = kv
        k_scr[i] = kv[:, :HEAD_SIZE]
        vt_scr[i] = kv.astype(f32).T[HEAD_SIZE:].astype(bf16)
        q2 = stack_heads(q, heads)
        start_row = start_ref[0]
        query = i * rows + lax.rem(lax.broadcasted_iota(jnp.int32, (1, cols), 1), rows)
        key_iota = lax.broadcasted_iota(jnp.int32, (rows, cols), 0)

        def step(j, carry):
            top, total, ot = carry
            scores = dot_nt(k_scr[j], q2) * att_mult
            key = key_iota + j * rows
            scores = jnp.where((key >= start_row) & (key <= query), scores, -1e30)
            new_top = jnp.maximum(top, jnp.max(scores, axis=0, keepdims=True))
            p = jnp.exp(scores - new_top)
            keep = jnp.exp(top - new_top)
            total = total * keep + jnp.sum(p, axis=0, keepdims=True)
            ot = ot * keep + dot_nn(vt_scr[j], p.astype(bf16))
            return new_top, total, ot

        top, total, ot = lax.fori_loop(
            first_ref[i],
            i + 1,
            step,
            (
                jnp.full((1, cols), -1e30, f32),
                jnp.zeros((1, cols), f32),
                jnp.zeros((HEAD_SIZE, cols), f32),
            ),
        )
        ot = ot / total
        ot_ref[0] = ot
        lse_ref[0] = top + jnp.log(total)
        out = ot.T
        att_ref[0] = jnp.concatenate(
            [out[h * rows : (h + 1) * rows] for h in range(heads)], axis=1
        ).astype(bf16)

    def block(shape):
        return pl.BlockSpec((1,) + shape, lambda i, _: (i, 0, 0))

    def whole(shape):
        return pl.BlockSpec(shape, lambda i, _: (0,) * len(shape))

    grid_spec = pltpu.PrefetchScalarGridSpec(
        num_scalar_prefetch=1,
        grid=(blocks,),
        in_specs=[
            block((rows, width)),
            whole(w_own.shape),
            whole((1, width)),
            block((rows, LANES)),
            block((rows, LANES)),
            block((1, cols)),
        ],
        out_specs=[
            block((rows, width)),
            block((rows, HEADS_LANES)),
            block((rows, LANES)),
            block((rows, out_width)),
            block((HEAD_SIZE, cols)),
            block((1, cols)),
        ],
        scratch_shapes=[
            pltpu.VMEM((blocks, rows, HEAD_SIZE), bf16),
            pltpu.VMEM((blocks, HEAD_SIZE, rows), bf16),
        ],
    )
    return pl.pallas_call(
        kernel,
        name="attend_forward",
        grid_spec=grid_spec,
        out_shape=[
            jax.ShapeDtypeStruct((blocks, rows, width), bf16),
            jax.ShapeDtypeStruct((blocks, rows, HEADS_LANES), bf16),
            jax.ShapeDtypeStruct((blocks, rows, LANES), bf16),
            jax.ShapeDtypeStruct((blocks, rows, out_width), bf16),
            jax.ShapeDtypeStruct((blocks, HEAD_SIZE, cols), f32),
            jax.ShapeDtypeStruct((blocks, 1, cols), f32),
        ],
        cost_estimate=pl.CostEstimate(
            flops=2 * length * width * 256 + 2 * length * length * cols // rows * 128,
            bytes_accessed=2 * length * width * 4,
            transcendentals=length * length,
        ),
        compiler_params=pltpu.CompilerParams(
            dimension_semantics=("arbitrary",), vmem_limit_bytes=40 << 20
        ),
    )(
        first,
        tok_all,
        w_own,
        gain,
        cos.reshape(blocks, rows, LANES),
        sin.reshape(blocks, rows, LANES),
        start_rows,
    )


def attend_backward(q_all, kv_all, cot, ot, lse, cos, sin, start, heads):
    blocks, rows, _ = q_all.shape
    length = blocks * rows
    cols = heads * rows
    first = start.reshape(blocks, rows)[:, 0] // rows
    start_rows = jnp.tile(start.reshape(blocks, 1, rows), (1, 1, heads))

    def kernel(first_ref, q_ref, kv_ref, do_ref, ot_ref, lse_ref, cos_ref, sin_ref, start_ref, out_ref, dk_scr, dv_scr, dq_scr):
        i = pl.program_id(0)

        @pl.when(i == 0)
        def _():
            dk_scr[...] = jnp.zeros_like(dk_scr)
            dv_scr[...] = jnp.zeros_like(dv_scr)

        q2 = stack_heads(q_ref[0], heads)
        do2 = stack_heads(do_ref[0], heads)
        delta = jnp.sum(do2.astype(f32).T * ot_ref[0], axis=0, keepdims=True)
        log_total = lse_ref[0]
        start_row = start_ref[0]
        query = i * rows + lax.rem(lax.broadcasted_iota(jnp.int32, (1, cols), 1), rows)
        key_iota = lax.broadcasted_iota(jnp.int32, (rows, cols), 0)
        dq_scr[...] = jnp.zeros_like(dq_scr)

        @pl.loop(first_ref[i], i + 1)
        def _(j):
            kv = kv_ref[j]
            k, v = kv[:, :HEAD_SIZE], kv[:, HEAD_SIZE:]
            scores = dot_nt(k, q2) * att_mult
            key = key_iota + j * rows
            p = jnp.where(
                (key >= start_row) & (key <= query), jnp.exp(scores - log_total), 0.0
            )
            ds = (p * (dot_nt(v, do2) - delta)).astype(bf16)
            dv_scr[j] += dot_nn(p.astype(bf16), do2)
            dk_scr[j] += dot_nn(ds, q2)
            dq_scr[...] += dot_tn(ds, k)

        def rope_back(x, c, s):
            return (x * c - turn(x) * s).astype(bf16)

        dq = dq_scr[...] * att_mult
        dq = [dq[h * rows : (h + 1) * rows] for h in range(heads)]
        if heads * HEAD_SIZE < HEADS_LANES:
            dq.append(jnp.zeros((rows, HEADS_LANES - heads * HEAD_SIZE), f32))
        dq = jnp.concatenate(dq, axis=1).astype(bf16).astype(f32)
        out_ref[i, :, :HEADS_LANES] = rope_back(dq, cos_ref[i], sin_ref[i])

        @pl.when(i == blocks - 1)
        def _():
            @pl.loop(0, blocks)
            def _(j):
                kv = jnp.concatenate([dk_scr[j] * att_mult, dv_scr[j]], axis=1)
                lane = lax.broadcasted_iota(jnp.int32, kv.shape, 1)
                out_ref[j, :, HEADS_LANES:] = jnp.where(
                    lane < HEAD_SIZE, kv * cos_ref[j] - turn(kv) * sin_ref[j], kv
                ).astype(bf16)

    def block(shape):
        return pl.BlockSpec((1,) + shape, lambda i, _: (i, 0, 0))

    def whole(shape):
        return pl.BlockSpec(shape, lambda i, _: (0,) * len(shape))

    grid_spec = pltpu.PrefetchScalarGridSpec(
        num_scalar_prefetch=1,
        grid=(blocks,),
        in_specs=[
            block((rows, HEADS_LANES)),
            whole((blocks, rows, LANES)),
            block((rows, heads * HEAD_SIZE)),
            block((HEAD_SIZE, cols)),
            block((1, cols)),
            whole((blocks, rows, LANES)),
            whole((blocks, rows, LANES)),
            block((1, cols)),
        ],
        out_specs=whole((blocks, rows, HEADS_LANES + LANES)),
        scratch_shapes=[
            pltpu.VMEM((blocks, rows, HEAD_SIZE), f32),
            pltpu.VMEM((blocks, rows, HEAD_SIZE), f32),
            pltpu.VMEM((cols, HEAD_SIZE), f32),
        ],
    )
    return pl.pallas_call(
        kernel,
        name="attend_backward",
        grid_spec=grid_spec,
        out_shape=jax.ShapeDtypeStruct((blocks, rows, HEADS_LANES + LANES), bf16),
        cost_estimate=pl.CostEstimate(
            flops=5 * length * length * cols // rows * 128,
            bytes_accessed=2 * length * 1024,
            transcendentals=length * length,
        ),
        compiler_params=pltpu.CompilerParams(
            dimension_semantics=("arbitrary",), vmem_limit_bytes=48 << 20
        ),
    )(
        first,
        q_all,
        kv_all,
        cot,
        ot,
        lse,
        cos.reshape(blocks, rows, LANES),
        sin.reshape(blocks, rows, LANES),
        start_rows,
    )


def moe_exchange(collective_id, normed, cots, mask, router, w_in, w_out, parts):
    devices = lax.axis_size("seq")
    chips = devices // 2
    rows, width = normed.shape
    own_experts = w_in.shape[0]

    def order(chip, k):
        near = jnp.minimum(chip, chips - 1 - chip)
        step = (k + 1) // 2
        both = jnp.where(lax.rem(k, 2) == 1, chip - step, chip + step)
        return jnp.where(
            k <= 2 * near, both, jnp.where(chip <= chips - 1 - chip, k, chips - 1 - k)
        )

    def kernel(*refs):
        x_in, g_in = refs[0], refs[1 : 1 + chips]
        mask_ref, router_ref, win_in, wout_in = refs[1 + chips : 5 + chips]
        (lin_out, slot_out, hid_out, n_sum, gate_out, gin_out, gout_out) = refs[
            5 + chips : 12 + chips
        ]
        y_outs = refs[12 + chips : 12 + 2 * chips]
        (
            x_all, g_all, win, wout, y_acc, n_acc, gate_acc, gate_stage,
            n_mine, n_far, n_give, n_theirs, y_mine, y_give, y_theirs, y_pre,
            lin_st, slot_st, hid_st, gin, gout, hid_ld,
            local, line_send, line_recv, sib_send, sib_recv, g_local, g_send, g_recv,
            n_send, n_recv, y_send, y_recv, far_send, far_recv, gate_send, gate_recv,
            st_sem, y_sem, ld_sem, w_sem, wg_sem,
        ) = refs[12 + 2 * chips :]
        me = lax.axis_index("seq")
        chip, core = me // 2, lax.rem(me, 2)
        sibling = me + 1 - 2 * core
        win_copy = pltpu.make_async_copy(win_in, win, w_sem.at[0])
        wout_copy = pltpu.make_async_copy(wout_in, wout, w_sem.at[1])
        win_copy.start()
        wout_copy.start()
        barrier = pltpu.get_barrier_semaphore()
        for k in range(1, devices):
            pl.semaphore_signal(
                barrier, inc=1, device_id={"seq": lax.rem(me + k, devices)}, device_id_type=MESH
            )
        pl.semaphore_wait(barrier, devices - 1)

        def remote(src, dst, send, recv, to):
            return pltpu.make_async_remote_copy(
                src_ref=src,
                dst_ref=dst,
                send_sem=send,
                recv_sem=recv,
                device_id={"seq": to},
                device_id_type=MESH,
            )

        def own_left():
            return remote(x_in, x_all.at[me], line_send.at[0], line_recv.at[chip], me - 2)

        def own_right():
            return remote(x_in, x_all.at[me], line_send.at[1], line_recv.at[chip], me + 2)

        def pass_on(b, k, to):
            place = x_all.at[2 * b + core]
            return remote(place, place, line_send.at[1 + k], line_recv.at[b], to)

        def to_sibling(b, k):
            place = x_all.at[2 * b + core]
            return remote(place, place, sib_send.at[k], sib_recv.at[b], sibling)

        def own_to_sibling():
            return remote(x_in, x_all.at[me], sib_send.at[0], sib_recv.at[chip], sibling)

        def cot_to_sibling(k):
            b = lax.rem(chip + chips - k, chips)
            return remote(
                g_in[k], g_all.at[2 * b + core], g_send.at[k], g_recv.at[b], sibling
            )

        def cot_local(k):
            b = lax.rem(chip + chips - k, chips)
            return pltpu.make_async_copy(g_in[k], g_all.at[2 * b + core], g_local.at[k])

        @pl.when(chip > 0)
        def _():
            own_left().start()

        @pl.when(chip < chips - 1)
        def _():
            own_right().start()

        own_to_sibling().start()
        own = pltpu.make_async_copy(x_in, x_all.at[me], local)
        own.start()
        for k in range(chips):
            cot_to_sibling(k).start()
            cot_local(k).start()
        own.wait()
        for k in range(chips):
            cot_local(k).wait()
        win_copy.wait()
        wout_copy.wait()

        def gate_copy(block):
            return remote(
                gate_stage.at[block],
                gate_out.at[me],
                gate_send.at[block],
                gate_recv.at[me],
                block,
            )

        def n_copy(p):
            return remote(n_give.at[p], n_theirs.at[p], n_send.at[p], n_recv.at[p], sibling)

        def y_copy(p):
            return remote(y_give.at[p], y_theirs.at[p], y_send.at[p], y_recv.at[p], sibling)

        def y_leave(p, k):
            return pltpu.make_async_copy(y_pre.at[p], y_outs[k], y_sem.at[p])

        def stage_copies(e, block):
            return [
                pltpu.make_async_copy(lin_st.at[e], lin_out.at[e, block], st_sem.at[0, e]),
                pltpu.make_async_copy(slot_st.at[e], slot_out.at[e, block], st_sem.at[1, e]),
                pltpu.make_async_copy(hid_st.at[e], hid_out.at[e, block], st_sem.at[2, e]),
            ]

        def far_copy(b):
            return remote(
                n_mine.at[b], n_far.at[chip], far_send.at[b], far_recv.at[chip], 2 * b + core
            )

        def fold(k):
            b, p = order(chip, k), lax.rem(k, 2)
            n_copy(p).wait_recv()
            both = n_mine[b].astype(f32) + n_theirs[p].astype(f32)

            @pl.when(b == chip)
            def _():
                n_sum[...] = both

            @pl.when(b != chip)
            def _():
                n_mine[b] = both.astype(bf16)
                far_copy(b).start()

            @pl.when(k > 1)
            def _():
                y_leave(p, 0).wait()

            y_copy(p).wait_recv()
            y_pre[p] = (y_mine[...].astype(f32) + y_theirs[p].astype(f32)).astype(bf16)
            away = lax.rem(b - chip + chips, chips)
            for r in range(chips):

                @pl.when(away == r)
                def _(r=r):
                    y_leave(p, r).start()

        def compute(block, before):
            x = x_all[block]
            there = mask_ref[block] > 0
            logits = jnp.where(there, dot_nn(x, router_ref[...]), -1e30)
            gates = jnp.where(
                there, jnp.exp(logits - jnp.max(logits, axis=1, keepdims=True)), 0.0
            )
            gates = gates / jnp.sum(gates, axis=1, keepdims=True)
            lane = lax.broadcasted_iota(jnp.int32, gates.shape, 1)
            y_acc[...] = jnp.zeros_like(y_acc)
            n_acc[...] = jnp.zeros_like(n_acc)
            gate_acc[...] = jnp.zeros_like(gate_acc)

            @pl.loop(0, own_experts)
            def _(e):
                gate = jnp.sum(
                    jnp.where(lane == me * own_experts + e, gates, 0.0), axis=1, keepdims=True
                )
                lin = dot_nn(x_all[block], win[e])
                gate_lin, up_lin = lin[:, :FFE], lin[:, FFE:]
                sig = 1.0 / (1.0 + jnp.exp(-gate_lin))
                silu = gate_lin * sig
                hidden = (silu * up_lin).astype(bf16)

                @pl.when(before)
                def _():
                    for copy in stage_copies(e, block):
                        copy.wait()

                hid_st[e] = hidden
                res = dot_nt(hidden, wout[e]).astype(bf16).astype(f32)
                y_acc[...] += gate * res
                cot = g_all[block].astype(f32) * res_mult
                gate_acc[...] += jnp.where(
                    lane == e, jnp.sum(cot * res, axis=1, keepdims=True), 0.0
                )
                slot = (gate * cot).astype(bf16)
                slot_st[e] = slot
                hidden_cot = dot_nn(slot, wout[e])
                lin_cot = jnp.concatenate(
                    [
                        hidden_cot * up_lin * (sig * (1.0 + gate_lin * (1.0 - sig))),
                        hidden_cot * silu,
                    ],
                    axis=1,
                ).astype(bf16)
                lin_st[e] = lin_cot
                for copy in stage_copies(e, block):
                    copy.start()
                n_acc[...] += dot_nt(lin_cot, win[e]).astype(bf16).astype(f32)

            gate_stage[block] = gate_acc[...].T[:8]

            @pl.when(block != me)
            def _():
                gate_copy(block).start()

            @pl.when(block == me)
            def _():
                gate_out[block] = gate_stage[block]

        @pl.loop(0, chips)
        def _(k):
            b = order(chip, k)

            @pl.when(k > 0)
            def _():
                pass_on(b, k, sibling).wait_recv()
                to_sibling(b, k).start()

                @pl.when((b < chip) & (chip < chips - 1))
                def _():
                    pass_on(b, k, me + 2).start()

                @pl.when((b > chip) & (chip > 0))
                def _():
                    pass_on(b, k, me - 2).start()

            remote(
                x_in, x_all.at[2 * b + 1 - core], sib_send.at[0], sib_recv.at[b], sibling
            ).wait_recv()
            remote(
                x_in, g_all.at[2 * b + 1 - core], g_send.at[0], g_recv.at[b], sibling
            ).wait_recv()

            @pl.loop(0, 2)
            def _(h):
                compute(2 * b + lax.rem(core + 1 + h, 2), (k > 0) | (h > 0))

                @pl.when(h == 0)
                def _():
                    p = lax.rem(k, 2)

                    @pl.when(k > 0)
                    def _():
                        fold(k - 1)

                    @pl.when(k > 1)
                    def _():
                        n_copy(p).wait_send()
                        y_copy(p).wait_send()

                    n_give[p] = n_acc[...].astype(bf16)
                    y_give[p] = y_acc[...].astype(bf16)
                    n_copy(p).start()
                    y_copy(p).start()

                @pl.when(h == 1)
                def _():
                    n_mine[b] = n_acc[...].astype(bf16)
                    y_mine[...] = y_acc[...].astype(bf16)

        @pl.loop(chips - 1, chips)
        def _(k):
            fold(k)

        for e in range(own_experts):
            for copy in stage_copies(e, 0):
                copy.wait()

        def loads(t, p):
            e, b = lax.rem(t, own_experts), t // own_experts
            pair = pl.ds(2 * b, 2)
            return [
                pltpu.make_async_copy(
                    lin_out.at[e, pair], g_all.at[pl.ds(4 * p, 2)], ld_sem.at[0, p]
                ),
                pltpu.make_async_copy(
                    slot_out.at[e, pair], g_all.at[pl.ds(4 * p + 2, 2)], ld_sem.at[1, p]
                ),
                pltpu.make_async_copy(hid_out.at[e, pair], hid_ld.at[p], ld_sem.at[2, p]),
            ]

        for copy in loads(jnp.int32(0), 0):
            copy.start()
        gin[...] = jnp.zeros_like(gin)
        gout[...] = jnp.zeros_like(gout)

        @pl.loop(0, chips * own_experts)
        def _(t):
            p = lax.rem(t, 2)
            for copy in loads(t, p):
                copy.wait()

            @pl.when(t + 1 < chips * own_experts)
            def _():
                for copy in loads(t + 1, 1 - p):
                    copy.start()

            e, b = lax.rem(t, own_experts), t // own_experts
            x = x_all[pl.ds(2 * b, 2)].reshape(2 * rows, width)
            lin_cot = g_all[pl.ds(4 * p, 2)].reshape(2 * rows, width)
            gin[e] += dot_tn(x, lin_cot)
            slot = g_all[pl.ds(4 * p + 2, 2)].reshape(2 * rows, width)
            gout[e] += dot_tn(slot, hid_ld[p].reshape(2 * rows, FFE))

        @pl.loop(1, chips)
        def _(k):
            b = order(chip, k)
            to_sibling(b, k).wait_send()

            @pl.when((b < chip) & (chip < chips - 1))
            def _():
                pass_on(b, k, me + 2).wait_send()

            @pl.when((b > chip) & (chip > 0))
            def _():
                pass_on(b, k, me - 2).wait_send()

        own_to_sibling().wait_send()

        @pl.when(chip > 0)
        def _():
            own_left().wait_send()

        @pl.when(chip < chips - 1)
        def _():
            own_right().wait_send()

        part_rows = width // parts
        leaving = []
        for e in range(own_experts):
            for j in range(width // rows):
                i = e * (width // rows) + j
                x_all[i] = gin[e, j * rows : (j + 1) * rows].astype(bf16)
                g_all[i, :, :FFE] = gout[e, j * rows : (j + 1) * rows].astype(bf16)
                for q in range(rows // part_rows):
                    here = pl.ds(q * part_rows, part_rows)
                    part = (j * rows + q * part_rows) // part_rows
                    at = 2 * len(leaving)
                    leaving.append(
                        (
                            pltpu.make_async_copy(
                                x_all.at[i, here], gin_out.at[part, e], wg_sem.at[at]
                            ),
                            pltpu.make_async_copy(
                                g_all.at[i, here, pl.ds(0, FFE)],
                                gout_out.at[part, e],
                                wg_sem.at[at + 1],
                            ),
                        )
                    )
                    for copy in leaving[-1]:
                        copy.start()

        @pl.loop(1, chips)
        def _(k):
            b = order(chip, k)
            remote(
                n_mine.at[b], n_far.at[b], far_send.at[b], far_recv.at[b], 2 * b + core
            ).wait_recv()
            n_sum[...] += n_far[b].astype(f32)
            far_copy(b).wait_send()

        @pl.loop(1, devices)
        def _(k):
            block = lax.rem(me + k, devices)
            remote(
                gate_stage.at[block],
                gate_out.at[block],
                gate_send.at[block],
                gate_recv.at[block],
                block,
            ).wait_recv()
            gate_copy(block).wait_send()

        for p in range(2):
            n_copy(p).wait_send()
            y_copy(p).wait_send()
            y_leave(p, 0).wait()
        for pair in leaving:
            for copy in pair:
                copy.wait()

        for k in range(chips):
            cot_to_sibling(k).wait_send()

    hbm = pl.BlockSpec(memory_space=pl.ANY)
    vmem = pl.BlockSpec(memory_space=pltpu.VMEM)
    block = (rows, width)
    dma = pltpu.SemaphoreType.DMA
    flops = 9 * own_experts * 2 * devices * rows * width * FFE // 1
    return pl.pallas_call(
        kernel,
        name="moe_exchange",
        out_shape=[
            jax.ShapeDtypeStruct((own_experts, devices, rows, 2 * FFE), bf16),
            jax.ShapeDtypeStruct((own_experts, devices) + block, bf16),
            jax.ShapeDtypeStruct((own_experts, devices, rows, FFE), bf16),
            jax.ShapeDtypeStruct(block, f32),
            jax.ShapeDtypeStruct((devices, 8, rows), f32),
            jax.ShapeDtypeStruct((parts, own_experts, width // parts, 2 * FFE), bf16),
            jax.ShapeDtypeStruct((parts, own_experts, width // parts, FFE), bf16),
        ]
        + [jax.ShapeDtypeStruct(block, bf16)] * chips,
        in_specs=[hbm] * (1 + chips) + [vmem] * 2 + [hbm] * 2,
        out_specs=[hbm] * 3 + [vmem] * 2 + [hbm] * (2 + chips),
        scratch_shapes=[
            pltpu.VMEM((devices,) + block, bf16),
            pltpu.VMEM((devices,) + block, bf16),
            pltpu.VMEM(w_in.shape, bf16),
            pltpu.VMEM(w_out.shape, bf16),
            pltpu.VMEM(block, f32),
            pltpu.VMEM(block, f32),
            pltpu.VMEM((rows, LANES), f32),
            pltpu.VMEM((devices, 8, rows), f32),
            pltpu.VMEM((chips,) + block, bf16),
            pltpu.VMEM((chips,) + block, bf16),
            pltpu.VMEM((2,) + block, bf16),
            pltpu.VMEM((2,) + block, bf16),
            pltpu.VMEM(block, bf16),
            pltpu.VMEM((2,) + block, bf16),
            pltpu.VMEM((2,) + block, bf16),
            pltpu.VMEM((2,) + block, bf16),
            pltpu.VMEM((own_experts, rows, 2 * FFE), bf16),
            pltpu.VMEM((own_experts,) + block, bf16),
            pltpu.VMEM((own_experts, rows, FFE), bf16),
            pltpu.VMEM((own_experts, width, 2 * FFE), f32),
            pltpu.VMEM((own_experts, width, FFE), f32),
            pltpu.VMEM((2, 2, rows, FFE), bf16),
        ]
        + [dma]
        + [
            dma((count,))
            for count in (
                chips + 1, chips, chips, chips, chips, chips, chips,
                2, 2, 2, 2, chips, chips, devices, devices,
            )
        ]
        + [
            dma((3, own_experts)),
            dma((2,)),
            dma((3, 2)),
            dma((2,)),
            dma((2 * own_experts * max(parts, width // rows),)),
        ],
        cost_estimate=pl.CostEstimate(
            flops=flops, bytes_accessed=40 << 20, transcendentals=devices * rows * FFE * 2
        ),
        compiler_params=pltpu.CompilerParams(
            collective_id=collective_id, has_side_effects=True, vmem_limit_bytes=62 << 20
        ),
    )(normed, *cots, mask, router, w_in, w_out)


def rms_parts(values):
    return lax.rsqrt(jnp.mean(values * values, axis=-1, keepdims=True) + norm_eps)


def rms_pull(values, scale, gain, cot):
    weighted = cot * gain
    pulled = scale * weighted - values * (scale * scale * scale) * jnp.mean(
        weighted * values, axis=-1, keepdims=True
    )
    return pulled, jnp.sum(cot * values * scale, axis=0)


def on_device(
    tokens,
    out_grad,
    doc_ids,
    expert_picks,
    w_query,
    key_weight_matrix,
    value_weight_matrix,
    w_out,
    w_router,
    gain_attn,
    gain_moe,
    expert_in,
    expert_out,
):
    devices, parts = lax.axis_size("seq"), lax.axis_size("dp")
    me = lax.axis_index("seq")
    rows, width = tokens.shape[1:]
    length = rows * devices
    experts = w_router.shape[1]
    own_experts = expert_in.shape[0]
    heads = QUERY_HEADS // devices
    group = QUERY_HEADS // KEY_VALUE_HEADS
    share = max(1, group // heads)
    q_width = heads * HEAD_SIZE
    w_rows = w_query.shape[0]

    wq = w_query.astype(bf16).reshape(w_rows, devices, q_width)
    wq = jnp.pad(wq, ((0, 0), (0, 0), (0, HEADS_LANES - q_width)))
    wk = key_weight_matrix.astype(bf16).reshape(w_rows, KEY_VALUE_HEADS, HEAD_SIZE)
    wv = value_weight_matrix.astype(bf16).reshape(w_rows, KEY_VALUE_HEADS, HEAD_SIZE)
    wkv = jnp.repeat(jnp.concatenate([wk, wv], axis=2), share, axis=1)
    w_cols = HEADS_LANES + LANES
    w_all = jnp.concatenate([wq, wkv], axis=2).reshape(w_rows, devices * w_cols)
    w_own = lax.dynamic_slice_in_dim(w_all, me * w_cols, w_cols, 1)
    misc = jnp.concatenate(
        [w_router, gain_attn[:, None], gain_moe[:, None]], axis=1
    ).astype(bf16)
    misc = jnp.pad(misc, ((0, 0), (0, LANES - experts - 2)))
    ints = jnp.concatenate([expert_picks[0].T, doc_ids], axis=0)
    ints = jnp.pad(ints, ((0, 16 - TOP - 1), (0, 0)))

    expert_in_full = lax.all_gather(expert_in.astype(bf16), "dp", axis=1, tiled=True)
    expert_out_full = lax.all_gather(expert_out.astype(bf16), "dp", axis=1, tiled=True)
    w_full = lax.all_gather(w_all, "dp", axis=0, tiled=True)

    tok_all, ints_all, w_own_all, wo_full, misc_full = exchange(
        0,
        [
            ("gather", "seq", tokens[0], None),
            ("gather", "seq", ints, None),
            ("gather", "dp", w_own, None),
            ("gather", "dp", w_out.astype(bf16), None),
            ("gather", "dp", misc, None),
        ],
    )
    held, tok_all = lax.optimization_barrier((out_grad[0], tok_all))
    chips = devices // 2
    cots = [held] + [
        lax.ppermute(held, "seq", [(i, (i + 2 * k) % devices) for i in range(devices)])
        for k in range(1, chips)
    ]
    w_own_all = w_own_all.reshape(width, w_cols)
    wo_full = wo_full.reshape(width, width)
    misc_full = misc_full.reshape(width, LANES)
    router_full = jnp.where(jnp.arange(LANES)[None, :] < experts, misc_full, 0)
    gain_a = misc_full[:, experts]
    gain_m = misc_full[:, experts + 1].astype(f32)
    docs = ints_all[:, TOP].reshape(length)
    chosen = jnp.any(
        ints_all[:, :TOP, :, None] == jnp.arange(LANES, dtype=jnp.int32), axis=1
    ).astype(bf16)
    start = jnp.sum((docs[:, None] < docs[None, :]).astype(jnp.int32), axis=0)
    cos, sin = rope_tables(length)

    normed_a, q_all, kv_all, attended_own, ot, lse = attend_forward(
        tok_all, w_own_all, gain_a[None], cos, sin, start, heads
    )
    wide = q_width % LANES == 0
    (attended,) = exchange(
        1, [("swap", "seq", attended_own, ("out", q_width) if wide else None)]
    )
    if not wide:
        attended = attended.transpose(1, 0, 2).reshape(rows, devices * q_width)

    resid = tokens[0].astype(f32)
    mid = resid + res_mult * dot_nn(attended, wo_full)
    mid_scale = rms_parts(mid)
    normed_m = (mid * mid_scale * gain_m).astype(bf16)
    (_, _, _, moe_sum, gate_cot, grads_in, grads_out, *branches) = moe_exchange(
        2, normed_m, cots, chosen, router_full, expert_in_full, expert_out_full, parts
    )
    branches = [branches[0]] + [
        lax.ppermute(
            branches[k], "seq", [(i, (i + 2 * k) % devices) for i in range(devices)]
        )
        for k in range(1, chips)
    ]
    grads_in = lax.all_to_all(grads_in, "dp", split_axis=0, concat_axis=0)
    grads_out = lax.all_to_all(grads_out, "dp", split_axis=0, concat_axis=0)
    gate_cot = gate_cot[:, :own_experts].reshape(experts, rows)
    logits = lax.dot_general(
        router_full[:, :experts], normed_m, (((0,), (1,)), ((), ())), preferred_element_type=f32
    )
    my_chosen = jnp.any(
        expert_picks[0].T[:, None, :] == jnp.arange(experts, dtype=jnp.int32)[None, :, None], axis=0
    )
    logits = jnp.where(my_chosen, logits, -jnp.inf)
    my_gates = jnp.exp(logits - jnp.max(logits, axis=0, keepdims=True))
    my_gates = my_gates / jnp.sum(my_gates, axis=0, keepdims=True)
    pick_cot = my_gates * (gate_cot - jnp.sum(my_gates * gate_cot, axis=0, keepdims=True))
    logit_cot = pick_cot.astype(bf16)
    grad_router = dot_nn(logit_cot, normed_m).T
    normed_m_cot = moe_sum + lax.dot_general(
        logit_cot, router_full[:, :experts], (((0,), (1,)), ((), ())), preferred_element_type=f32
    )
    pulled, grad_gain_m = rms_pull(mid, mid_scale, gain_m, normed_m_cot)
    mid_cot = out_grad[0].astype(f32) + pulled
    branch_cot = (res_mult * mid_cot).astype(bf16)
    grad_wo = dot_tn(attended, branch_cot)
    attended_cot = dot_nt(branch_cot, wo_full).astype(bf16)
    if not wide:
        attended_cot = attended_cot.reshape(rows, devices, q_width).transpose(1, 0, 2)
    (heads_cot,) = exchange(
        4, [("swap", "seq", attended_cot, ("in", q_width) if wide else None)]
    )
    qkv_cot = attend_backward(q_all, kv_all, heads_cot, ot, lse, cos, sin, start, heads)
    grad_qkv = dot_tn(
        normed_a.reshape(length, width), qkv_cot.reshape(length, w_cols)
    ).astype(bf16)
    token_pack = jnp.concatenate(
        [
            grad_wo,
            grad_router,
            grad_gain_m[:, None],
            jnp.zeros((width, LANES - experts - 1), f32),
        ],
        axis=1,
    ).astype(bf16)
    pack_cols = width + LANES
    qkv_cot_tok, grad_qkv, token_pack = exchange(
        5,
        [
            ("swap", "seq", qkv_cot, ("out", w_cols)),
            ("swap", "dp", grad_qkv.reshape(parts, w_rows, w_cols), None),
            ("swap", "dp", token_pack.reshape(parts, w_rows, pack_cols), None),
        ],
    )
    normed_a_cot = dot_nt(qkv_cot_tok, w_full)
    grad_qkv = jnp.sum(grad_qkv.astype(f32), axis=0).astype(bf16)
    token_pack = jnp.sum(token_pack.astype(f32), axis=0).astype(bf16)
    out_rows = w_rows // devices
    grad_qkv, token_pack = exchange(
        6,
        [
            ("swap", "seq", grad_qkv.reshape(devices, out_rows, w_cols), None),
            ("swap", "seq", token_pack.reshape(devices, out_rows, pack_cols), None),
        ],
    )
    (grad_qkv, token_pack), branches, grads_in, grads_out = lax.optimization_barrier(
        ((grad_qkv, token_pack), branches, grads_in, grads_out)
    )
    branch_sum = branches[0].astype(f32)
    for k in range(1, chips):
        branch_sum = branch_sum + branches[k].astype(f32)
    output = (mid + res_mult * branch_sum).astype(bf16)[None]
    grad_e_in = jnp.sum(grads_in.astype(f32), axis=0)
    grad_e_out = jnp.sum(grads_out.astype(f32), axis=0)
    resid_scale = rms_parts(resid)
    weighted = normed_a_cot * gain_a.astype(f32)
    input_grad = (
        mid_cot
        + resid_scale * weighted
        - resid
        * (resid_scale * resid_scale * resid_scale)
        * jnp.mean(weighted * resid, axis=-1, keepdims=True)
    ).astype(bf16)[None]

    grad_qkv = grad_qkv.astype(f32)
    grad_wq = grad_qkv[:, :, :q_width].transpose(1, 0, 2).reshape(out_rows, devices * q_width)

    def per_head(part):
        part = part.reshape(devices // share, share, out_rows, HEAD_SIZE).sum(axis=1)
        return part.transpose(1, 0, 2).reshape(out_rows, KEY_VALUE_HEADS * HEAD_SIZE)

    grad_wk = per_head(grad_qkv[:, :, HEADS_LANES : HEADS_LANES + HEAD_SIZE])
    grad_wv = per_head(grad_qkv[:, :, HEADS_LANES + HEAD_SIZE :])
    token_pack = jnp.sum(token_pack.astype(f32), axis=0)
    grad_wo = token_pack[:, :width]
    grad_router = token_pack[:, width : width + experts]
    grad_gain_m = token_pack[:, width + experts]

    def own_rows(weight):
        return lax.dynamic_slice_in_dim(weight, me * out_rows, out_rows, 0).astype(bf16).astype(f32)

    grad_gain_a = (
        jnp.sum(own_rows(w_query) * grad_wq, axis=1)
        + jnp.sum(own_rows(key_weight_matrix) * grad_wk, axis=1)
        + jnp.sum(own_rows(value_weight_matrix) * grad_wv, axis=1)
    ) / own_rows(gain_attn)
    return (
        output,
        input_grad,
        grad_wq,
        grad_wk,
        grad_wv,
        grad_wo,
        grad_router,
        grad_gain_a,
        grad_gain_m,
        grad_e_in,
        grad_e_out,
    )


def solution(mesh):
    return jax.shard_map(
        on_device,
        mesh=mesh,
        in_specs=(
            P("dp", "seq", None),
            P("dp", "seq", None),
            P("dp", "seq"),
            P("dp", "seq", None),
            P("dp", None),
            P("dp", None),
            P("dp", None),
            P("dp", None),
            P("dp", None),
            P("dp"),
            P("dp"),
            P("seq", "dp", None),
            P("seq", "dp", None),
        ),
        out_specs=(
            P("dp", "seq", None),
            P("dp", "seq", None),
            P(("dp", "seq"), None),
            P(("dp", "seq"), None),
            P(("dp", "seq"), None),
            P(("dp", "seq"), None),
            P(("dp", "seq"), None),
            P(("dp", "seq")),
            P(("dp", "seq")),
            P("seq", "dp", None),
            P("seq", "dp", None),
        ),
        check_vma=False,
    )
```

```python
import functools

import jax
import jax.numpy as jnp
import numpy as np
from jax import lax
from jax.experimental import pallas as pl
from jax.experimental.pallas import tpu as pltpu
from jax.sharding import PartitionSpec as P

MESH = pl.DeviceIdType.MESH
PIECES = 2


def _block(ref, j, cut):
    if cut is None:
        return ref.at[j]
    return ref.at[:, pl.ds(pl.multiple_of(j * cut, cut), cut)]


def exchange(collective_id, ops):
    axes = tuple(dict.fromkeys(axis for _, axis, _, _ in ops))
    size = {axis: lax.axis_size(axis) for axis in axes}
    out_shapes, out_specs, scratch, places = [], [], [], []
    for kind, axis, x, cut in ops:
        count = size[axis]
        out_spec = pl.BlockSpec(memory_space=pl.ANY)
        extra = []
        lead = (PIECES,) if kind == "gather" and axis == "seq" else ()
        if kind == "gather":
            shape, dtype = (count,) + x.shape, x.dtype
            copies = count - 1 if axis == "dp" else 3 + 4 * (count // 2 - 1)
        elif kind == "swap":
            copies, dtype = count - 1, x.dtype
            if cut is None:
                shape = x.shape
            elif cut[0] == "in":
                shape = (count, x.shape[0], cut[1])
            else:
                shape = (x.shape[1], count * cut[1])
        out_shapes.append(jax.ShapeDtypeStruct(shape, dtype))
        out_specs.append(out_spec)
        places.append((len(scratch), len(extra)))
        scratch += [
            pltpu.SemaphoreType.DMA(lead + (copies,)),
            pltpu.SemaphoreType.DMA(lead + (max(copies, count),)),
            pltpu.SemaphoreType.DMA,
        ] + extra

    def kernel(*refs):
        ins, outs, work = refs[: len(ops)], refs[len(ops) : 2 * len(ops)], refs[2 * len(ops) :]
        me = {axis: lax.axis_index(axis) for axis in axes}
        barrier = pltpu.get_barrier_semaphore()
        for axis in axes:
            for k in range(1, size[axis]):
                pl.semaphore_signal(
                    barrier,
                    inc=1,
                    device_id={axis: lax.rem(me[axis] + k, size[axis])},
                    device_id_type=MESH,
                )
        pl.semaphore_wait(barrier, sum(size[axis] - 1 for axis in axes))

        def remote(axis, src, dst, send, recv, to):
            return pltpu.make_async_remote_copy(
                src_ref=src,
                dst_ref=dst,
                send_sem=send,
                recv_sem=recv,
                device_id={axis: to},
                device_id_type=MESH,
            )

        second, third = [], []
        for (kind, axis, _, cut), x, o, (at, extra) in zip(ops, ins, outs, places):
            send, recv, local = work[at : at + 3]
            count, my = size[axis], me[axis]
            if kind == "swap":
                into = cut[1] if cut is not None and cut[0] == "out" else None
                outof = cut[1] if cut is not None and cut[0] == "in" else None
                own = pltpu.make_async_copy(_block(x, my, outof), _block(o, my, into), local)
                own.start()
                third.append(own.wait)
                for k in range(1, count):
                    to = lax.rem(my + k, count)
                    copy = remote(
                        axis,
                        _block(x, to, outof),
                        _block(o, my, into),
                        send.at[k - 1],
                        recv.at[k - 1],
                        to,
                    )
                    copy.start()
                    frm = lax.rem(my + count - k, count)
                    arrive = remote(
                        axis,
                        _block(x, to, outof),
                        _block(o, frm, into),
                        send.at[k - 1],
                        recv.at[k - 1],
                        to,
                    )
                    third.append(copy.wait_send)
                    third.append(arrive.wait_recv)
            elif kind == "gather" and axis == "dp":
                own = pltpu.make_async_copy(x, o.at[my], local)
                own.start()
                third.append(own.wait)
                for k in range(1, count):
                    to = lax.rem(my + k, count)
                    frm = lax.rem(my + count - k, count)
                    copy = remote(axis, x, o.at[my], send.at[k - 1], recv.at[k - 1], to)
                    copy.start()
                    third.append(copy.wait_send)
                    third.append(
                        remote(
                            axis, x, o.at[frm], send.at[k - 1], recv.at[k - 1], to
                        ).wait_recv
                    )
            elif kind == "gather":
                chips = count // 2
                chip, core = my // 2, lax.rem(my, 2)
                sibling = my + 1 - 2 * core
                own = pltpu.make_async_copy(x, o.at[my], local)
                own.start()
                third.append(own.wait)

                cuts = PIECES if x.shape[0] % (16 * PIECES) == 0 else 1
                size_of = x.shape[0] // cuts

                def cut_of(ref, i, size_of=size_of):
                    return ref.at[pl.ds(i * size_of, size_of)]

                def line(src, b, i, slot, to, axis=axis, o=o, send=send, recv=recv, core=core, cut_of=cut_of):
                    return remote(
                        axis, src, cut_of(o.at[2 * b + core], i), send.at[i, slot], recv.at[i, b], to
                    )

                def across(src, b, i, slot, half, axis=axis, o=o, send=send, recv=recv, chips=chips, sibling=sibling, cut_of=cut_of):
                    return remote(
                        axis,
                        src,
                        cut_of(o.at[2 * b + half], i),
                        send.at[i, slot],
                        recv.at[i, chips + b],
                        sibling,
                    )

                def guarded(where, act):
                    pl.when(where)(act)

                for i in range(cuts):
                    for slot, where, to in ((0, chip > 0, my - 2), (1, chip < chips - 1, my + 2)):
                        copy = line(cut_of(x, i), chip, i, slot, to)
                        guarded(where, copy.start)
                        third.append(functools.partial(guarded, where, copy.wait_send))
                for i in range(cuts):
                    copy = across(cut_of(x, i), chip, i, 2, core)
                    copy.start()
                    third.append(copy.wait_send)
                    third.append(across(cut_of(x, i), chip, i, 2, 1 - core).wait_recv)

                def hop(k, side, i, chips=chips, chip=chip, core=core, my=my, x=x, o=o, line=line, across=across, cut_of=cut_of):
                    b = chip + side * k
                    there = (b >= 0) & (b < chips)
                    onward = there & ((chip - side >= 0) & (chip - side < chips))
                    slot = 3 + (k - 1) * 4 + (side + 1)
                    spot = cut_of(o.at[2 * b + core], i)
                    further = line(spot, b, i, slot, my - 2 * side)
                    over = across(spot, b, i, slot + 1, core)
                    arrived = line(cut_of(x, i), b, i, slot, my)
                    brought = across(cut_of(x, i), b, i, slot + 1, 1 - core)

                    @pl.when(there)
                    def _():
                        arrived.wait_recv()

                    guarded(onward, further.start)
                    guarded(there, over.start)
                    third.append(functools.partial(guarded, onward, further.wait_send))
                    third.append(functools.partial(guarded, there, over.wait_send))
                    third.append(functools.partial(guarded, there, brought.wait_recv))

                for k in range(1, chips):
                    for i in range(cuts):
                        for side in (-1, 1):
                            second.append((k + i / cuts, functools.partial(hop, k, side, i)))
        for _, run in sorted(second, key=lambda item: item[0]):
            run()
        for wait in third:
            wait()

    return pl.pallas_call(
        kernel,
        name=f"exchange{collective_id}",
        out_shape=out_shapes,
        in_specs=[pl.BlockSpec(memory_space=pl.ANY)] * len(ops),
        out_specs=out_specs,
        scratch_shapes=scratch,
        compiler_params=pltpu.CompilerParams(
            collective_id=collective_id, has_side_effects=True, vmem_limit_bytes=48 << 20
        ),
    )(*[x for _, _, x, _ in ops])

QUERY_HEADS = 16
KEY_VALUE_HEADS = 8
HEAD_SIZE = 64
FFE = 512
TOP = 8

att_mult = 0.015625
res_mult = 0.22
norm_eps = 1e-06
rope_theta = 10000.0
LANES = 128
bf16 = jnp.bfloat16
f32 = jnp.float32
HEADS_LANES = 128


def dot_nt(a, b):
    return lax.dot_general(a, b, (((1,), (1,)), ((), ())), preferred_element_type=f32)


def dot_nn(a, b):
    return lax.dot_general(a, b, (((1,), (0,)), ((), ())), preferred_element_type=f32)


def dot_tn(a, b):
    return lax.dot_general(a, b, (((0,), (0,)), ((), ())), preferred_element_type=f32)


def turn(x):
    half = HEAD_SIZE // 2
    lane = lax.broadcasted_iota(jnp.int32, x.shape, 1)
    width = x.shape[1]
    return jnp.where(
        lax.rem(lane, HEAD_SIZE) < half, pltpu.roll(x, width - half, 1), pltpu.roll(x, half, 1)
    )


def rope_table(blocks, rows):
    half = HEAD_SIZE // 2
    frequency = np.float32(rope_theta) ** (
        -np.arange(half, dtype=np.float32) * np.float32(2.0) / np.float32(HEAD_SIZE)
    )
    angles = (frequency[:, None] * np.arange(blocks * rows, dtype=np.float32)[None, :]).astype(
        np.float32
    )
    table = np.concatenate([np.cos(angles), np.sin(angles)], axis=0).astype(np.float32)
    return jnp.asarray(table.reshape(HEAD_SIZE, blocks, rows).transpose(1, 0, 2))


def spread_table(table):
    half = HEAD_SIZE // 2
    turned = table.T
    cos, sin = turned[:, :half], turned[:, half:]
    return (
        jnp.concatenate([cos, cos] * (LANES // HEAD_SIZE), axis=1),
        jnp.concatenate([-sin, sin] * (LANES // HEAD_SIZE), axis=1),
    )


def across_lanes(row, lanes):
    return jnp.broadcast_to(row, (lanes, row.shape[1])).T


def first_blocks(docs):
    return jnp.sum(
        (docs[:, -1][:, None] < docs[:, 0][None, :]).astype(jnp.int32), axis=0
    )


def stack_heads(x, heads):
    return jnp.concatenate(
        [x[:, h * HEAD_SIZE : (h + 1) * HEAD_SIZE] for h in range(heads)], axis=0
    )


def attend_forward(tok_all, w_own, gain, table, docs, heads):
    blocks, rows, width = tok_all.shape
    length = blocks * rows
    cols = heads * rows
    first = first_blocks(docs)
    out_width = heads * HEAD_SIZE

    def kernel(first_ref, tok, w, gain_ref, table_ref, docs_ref, na_ref, q_ref, kv_ref, att_ref, ot_ref, lse_ref, k_scr, vt_scr, doc_scr):
        i = pl.program_id(0)
        x = tok[0].astype(f32)
        scale = lax.rsqrt(jnp.mean(x * x, axis=-1, keepdims=True) + norm_eps)
        na = (x * scale * gain_ref[...].astype(f32)).astype(bf16)
        na_ref[0] = na
        qkv = dot_nn(na, w[...])
        c, s = spread_table(table_ref[0])
        q, kv = qkv[:, :HEADS_LANES], qkv[:, HEADS_LANES:]
        q = (q * c + turn(q) * s).astype(bf16)
        lane = lax.broadcasted_iota(jnp.int32, kv.shape, 1)
        kv = jnp.where(lane < HEAD_SIZE, kv * c + turn(kv) * s, kv).astype(bf16)
        q_ref[0] = q
        kv_ref[0] = kv
        k_scr[i] = kv[:, :HEAD_SIZE]
        vt_scr[i] = kv.astype(f32).T[HEAD_SIZE:].astype(bf16)
        q2 = stack_heads(q, heads)
        doc_row = docs_ref[0].astype(f32)
        doc_scr[i] = across_lanes(doc_row, LANES)
        doc_query = jnp.concatenate([doc_row] * heads, axis=1)
        query = i * rows + lax.rem(lax.broadcasted_iota(jnp.int32, (1, cols), 1), rows)
        key_iota = lax.broadcasted_iota(jnp.int32, (rows, cols), 0)

        def step(j, carry):
            top, total, ot = carry
            scores = dot_nt(k_scr[j], q2) * att_mult
            key = key_iota + j * rows
            same = jnp.concatenate([doc_scr[j]] * (cols // LANES), axis=1) == doc_query
            scores = jnp.where(same & (key <= query), scores, -1e30)
            new_top = jnp.maximum(top, jnp.max(scores, axis=0, keepdims=True))
            p = jnp.exp(scores - new_top)
            keep = jnp.exp(top - new_top)
            total = total * keep + jnp.sum(p, axis=0, keepdims=True)
            ot = ot * keep + dot_nn(vt_scr[j], p.astype(bf16))
            return new_top, total, ot

        top, total, ot = lax.fori_loop(
            first_ref[i],
            i + 1,
            step,
            (
                jnp.full((1, cols), -1e30, f32),
                jnp.zeros((1, cols), f32),
                jnp.zeros((HEAD_SIZE, cols), f32),
            ),
        )
        ot = ot / total
        ot_ref[0] = ot
        lse_ref[0] = top + jnp.log(total)
        out = ot.T
        att_ref[0] = jnp.concatenate(
            [out[h * rows : (h + 1) * rows] for h in range(heads)], axis=1
        ).astype(bf16)

    def block(shape):
        return pl.BlockSpec((1,) + shape, lambda i, _: (i, 0, 0))

    def whole(shape):
        return pl.BlockSpec(shape, lambda i, _: (0,) * len(shape))

    grid_spec = pltpu.PrefetchScalarGridSpec(
        num_scalar_prefetch=1,
        grid=(blocks,),
        in_specs=[
            block((rows, width)),
            whole(w_own.shape),
            whole((1, width)),
            block((HEAD_SIZE, rows)),
            block((1, rows)),
        ],
        out_specs=[
            block((rows, width)),
            block((rows, HEADS_LANES)),
            block((rows, LANES)),
            block((rows, out_width)),
            block((HEAD_SIZE, cols)),
            block((1, cols)),
        ],
        scratch_shapes=[
            pltpu.VMEM((blocks, rows, HEAD_SIZE), bf16),
            pltpu.VMEM((blocks, HEAD_SIZE, rows), bf16),
            pltpu.VMEM((blocks, rows, LANES), f32),
        ],
    )
    return pl.pallas_call(
        kernel,
        name="attend_forward",
        grid_spec=grid_spec,
        out_shape=[
            jax.ShapeDtypeStruct((blocks, rows, width), bf16),
            jax.ShapeDtypeStruct((blocks, rows, HEADS_LANES), bf16),
            jax.ShapeDtypeStruct((blocks, rows, LANES), bf16),
            jax.ShapeDtypeStruct((blocks, rows, out_width), bf16),
            jax.ShapeDtypeStruct((blocks, HEAD_SIZE, cols), f32),
            jax.ShapeDtypeStruct((blocks, 1, cols), f32),
        ],
        cost_estimate=pl.CostEstimate(
            flops=2 * length * width * 256 + 2 * length * length * cols // rows * 128,
            bytes_accessed=2 * length * width * 4,
            transcendentals=length * length,
        ),
        compiler_params=pltpu.CompilerParams(
            dimension_semantics=("arbitrary",), vmem_limit_bytes=40 << 20
        ),
    )(
        first,
        tok_all,
        w_own,
        gain,
        table,
        docs[:, None],
    )


def attend_backward(q_all, kv_all, cot, ot, lse, table, docs, heads):
    blocks, rows, _ = q_all.shape
    length = blocks * rows
    cols = heads * rows
    first = first_blocks(docs)

    def kernel(first_ref, q_ref, kv_ref, do_ref, ot_ref, lse_ref, table_ref, docs_ref, out_ref, dk_scr, dv_scr, dq_scr, doc_scr):
        i = pl.program_id(0)

        @pl.when(i == 0)
        def _():
            dk_scr[...] = jnp.zeros_like(dk_scr)
            dv_scr[...] = jnp.zeros_like(dv_scr)

        q2 = stack_heads(q_ref[0], heads)
        do2 = stack_heads(do_ref[0], heads)
        delta = jnp.sum(do2.astype(f32).T * ot_ref[0], axis=0, keepdims=True)
        log_total = lse_ref[0]
        doc_row = docs_ref[0].astype(f32)
        doc_scr[i] = across_lanes(doc_row, LANES)
        doc_query = jnp.concatenate([doc_row] * heads, axis=1)
        query = i * rows + lax.rem(lax.broadcasted_iota(jnp.int32, (1, cols), 1), rows)
        key_iota = lax.broadcasted_iota(jnp.int32, (rows, cols), 0)
        dq_scr[...] = jnp.zeros_like(dq_scr)

        @pl.loop(first_ref[i], i + 1)
        def _(j):
            kv = kv_ref[j]
            k, v = kv[:, :HEAD_SIZE], kv[:, HEAD_SIZE:]
            scores = dot_nt(k, q2) * att_mult
            key = key_iota + j * rows
            same = jnp.concatenate([doc_scr[j]] * (cols // LANES), axis=1) == doc_query
            p = jnp.where(same & (key <= query), jnp.exp(scores - log_total), 0.0)
            ds = (p * (dot_nt(v, do2) - delta)).astype(bf16)
            dv_scr[j] += dot_nn(p.astype(bf16), do2)
            dk_scr[j] += dot_nn(ds, q2)
            dq_scr[...] += dot_tn(ds, k)

        def rope_back(x, c, s):
            return (x * c - turn(x) * s).astype(bf16)

        dq = dq_scr[...] * att_mult
        dq = [dq[h * rows : (h + 1) * rows] for h in range(heads)]
        if heads * HEAD_SIZE < HEADS_LANES:
            dq.append(jnp.zeros((rows, HEADS_LANES - heads * HEAD_SIZE), f32))
        dq = jnp.concatenate(dq, axis=1).astype(bf16).astype(f32)
        out_ref[i, :, :HEADS_LANES] = rope_back(dq, *spread_table(table_ref[i]))

        @pl.when(i == blocks - 1)
        def _():
            @pl.loop(0, blocks)
            def _(j):
                kv = jnp.concatenate([dk_scr[j] * att_mult, dv_scr[j]], axis=1)
                lane = lax.broadcasted_iota(jnp.int32, kv.shape, 1)
                c, s = spread_table(table_ref[j])
                out_ref[j, :, HEADS_LANES:] = jnp.where(
                    lane < HEAD_SIZE, kv * c - turn(kv) * s, kv
                ).astype(bf16)

    def block(shape):
        return pl.BlockSpec((1,) + shape, lambda i, _: (i, 0, 0))

    def whole(shape):
        return pl.BlockSpec(shape, lambda i, _: (0,) * len(shape))

    grid_spec = pltpu.PrefetchScalarGridSpec(
        num_scalar_prefetch=1,
        grid=(blocks,),
        in_specs=[
            block((rows, HEADS_LANES)),
            whole((blocks, rows, LANES)),
            block((rows, heads * HEAD_SIZE)),
            block((HEAD_SIZE, cols)),
            block((1, cols)),
            whole((blocks, HEAD_SIZE, rows)),
            block((1, rows)),
        ],
        out_specs=whole((blocks, rows, HEADS_LANES + LANES)),
        scratch_shapes=[
            pltpu.VMEM((blocks, rows, HEAD_SIZE), f32),
            pltpu.VMEM((blocks, rows, HEAD_SIZE), f32),
            pltpu.VMEM((cols, HEAD_SIZE), f32),
            pltpu.VMEM((blocks, rows, LANES), f32),
        ],
    )
    return pl.pallas_call(
        kernel,
        name="attend_backward",
        grid_spec=grid_spec,
        out_shape=jax.ShapeDtypeStruct((blocks, rows, HEADS_LANES + LANES), bf16),
        cost_estimate=pl.CostEstimate(
            flops=5 * length * length * cols // rows * 128,
            bytes_accessed=2 * length * 1024,
            transcendentals=length * length,
        ),
        compiler_params=pltpu.CompilerParams(
            dimension_semantics=("arbitrary",), vmem_limit_bytes=48 << 20
        ),
    )(
        first,
        q_all,
        kv_all,
        cot,
        ot,
        lse,
        table,
        docs[:, None],
    )


def moe_exchange(collective_id, normed, cots, mask, router, w_in, w_out, parts):
    devices = lax.axis_size("seq")
    chips = devices // 2
    rows, width = normed.shape
    own_experts = w_in.shape[0]

    def order(chip, k):
        left = chip < chips - 1 - chip
        longer = jnp.where(left, chips - 1 - chip, chip)
        near = jnp.where(left, chip + k, chip - k)
        return jnp.where(k <= longer, near, jnp.where(left, chips - 1 - k, k))

    def kernel(*refs):
        x_in, g_in = refs[0], refs[1 : 1 + chips]
        mask_ref, router_ref, win_in, wout_in = refs[1 + chips : 5 + chips]
        (lin_out, slot_out, hid_out, n_sum, gate_out, g_out) = refs[5 + chips : 11 + chips]
        y_outs = refs[11 + chips : 11 + 2 * chips]
        (
            x_all, g_all, win, wout, y_acc, n_acc, gate_acc, gate_stage,
            n_mine, n_far, n_give, n_theirs, y_mine, y_give, y_theirs, y_pre,
            lin_st, slot_st, hid_st, gin, gout, hid_ld,
            local, line_send, line_recv, sib_send, sib_recv, g_local, g_send, g_recv,
            n_send, n_recv, y_send, y_recv, far_send, far_recv, gate_send, gate_recv,
            st_sem, y_sem, ld_sem, w_sem, wg_sem,
        ) = refs[11 + 2 * chips :]
        me = lax.axis_index("seq")
        chip, core = me // 2, lax.rem(me, 2)
        sibling = me + 1 - 2 * core
        win_copy = pltpu.make_async_copy(win_in, win, w_sem.at[0])
        wout_copy = pltpu.make_async_copy(wout_in, wout, w_sem.at[1])
        win_copy.start()
        wout_copy.start()
        barrier = pltpu.get_barrier_semaphore()
        for k in range(1, devices):
            pl.semaphore_signal(
                barrier, inc=1, device_id={"seq": lax.rem(me + k, devices)}, device_id_type=MESH
            )
        pl.semaphore_wait(barrier, devices - 1)

        def remote(src, dst, send, recv, to):
            return pltpu.make_async_remote_copy(
                src_ref=src,
                dst_ref=dst,
                send_sem=send,
                recv_sem=recv,
                device_id={"seq": to},
                device_id_type=MESH,
            )

        half = rows // PIECES

        def piece(b, core_of, i):
            return x_all.at[2 * b + core_of, pl.ds(i * half, half)]

        def line(src, b, i, slot, to):
            return remote(
                src, piece(b, core, i), line_send.at[i, slot], line_recv.at[i, b], to
            )

        def across(src, b, core_of, i):
            return remote(
                src, piece(b, core_of, i), sib_send.at[i, b], sib_recv.at[i, b], sibling
            )

        def own_piece(i):
            return x_in.at[pl.ds(i * half, half)]

        def pass_on(b, i, to):
            return line(piece(b, core, i), b, i, 2 + b, to)

        def to_sibling(b, i):
            return across(piece(b, core, i), b, core, i)

        def own_sends(act):
            for i in range(PIECES):

                @pl.when(chip > 0)
                def _(i=i):
                    act(line(own_piece(i), chip, i, 0, me - 2))

                @pl.when(chip < chips - 1)
                def _(i=i):
                    act(line(own_piece(i), chip, i, 1, me + 2))

            for i in range(PIECES):
                act(across(own_piece(i), chip, core, i))

        def cot_to_sibling(k):
            b = lax.rem(chip + chips - k, chips)
            return remote(
                g_in[k], g_all.at[2 * b + core], g_send.at[k], g_recv.at[b], sibling
            )

        def cot_local(k):
            b = lax.rem(chip + chips - k, chips)
            return pltpu.make_async_copy(g_in[k], g_all.at[2 * b + core], g_local.at[k])

        own_sends(lambda copy: copy.start())
        own = pltpu.make_async_copy(x_in, x_all.at[me], local)
        own.start()
        for k in range(chips):
            cot_to_sibling(k).start()
            cot_local(k).start()
        own.wait()
        for k in range(chips):
            cot_local(k).wait()
        win_copy.wait()
        wout_copy.wait()

        def gate_copy(block):
            return remote(
                gate_stage.at[block],
                gate_out.at[me],
                gate_send.at[block],
                gate_recv.at[me],
                block,
            )

        def n_copy(p):
            return remote(n_give.at[p], n_theirs.at[p], n_send.at[p], n_recv.at[p], sibling)

        def y_copy(p):
            return remote(y_give.at[p], y_theirs.at[p], y_send.at[p], y_recv.at[p], sibling)

        def y_leave(p, k):
            return pltpu.make_async_copy(y_pre.at[p], y_outs[k], y_sem.at[p])

        def stage_copies(e, block):
            return [
                pltpu.make_async_copy(lin_st.at[e], lin_out.at[e, block], st_sem.at[0, e]),
                pltpu.make_async_copy(slot_st.at[e], slot_out.at[e, block], st_sem.at[1, e]),
                pltpu.make_async_copy(hid_st.at[e], hid_out.at[e, block], st_sem.at[2, e]),
            ]

        def far_copy(b):
            return remote(
                n_mine.at[b], n_far.at[chip], far_send.at[b], far_recv.at[chip], 2 * b + core
            )

        def fold(k):
            b, p = order(chip, k), lax.rem(k, 2)
            n_copy(p).wait_recv()
            both = n_mine[b].astype(f32) + n_theirs[p].astype(f32)

            @pl.when(b == chip)
            def _():
                n_sum[...] = both

            @pl.when(b != chip)
            def _():
                n_mine[b] = both.astype(bf16)
                far_copy(b).start()

            @pl.when(k > 1)
            def _():
                y_leave(p, 0).wait()

            y_copy(p).wait_recv()
            y_pre[p] = (y_mine[...].astype(f32) + y_theirs[p].astype(f32)).astype(bf16)
            away = lax.rem(b - chip + chips, chips)
            for r in range(chips):

                @pl.when(away == r)
                def _(r=r):
                    y_leave(p, r).start()

        def compute(block, before):
            x = x_all[block]
            there = mask_ref[block] > 0
            logits = jnp.where(there, dot_nn(x, router_ref[...]), -1e30)
            gates = jnp.where(
                there, jnp.exp(logits - jnp.max(logits, axis=1, keepdims=True)), 0.0
            )
            gates = gates / jnp.sum(gates, axis=1, keepdims=True)
            lane = lax.broadcasted_iota(jnp.int32, gates.shape, 1)
            y_acc[...] = jnp.zeros_like(y_acc)
            n_acc[...] = jnp.zeros_like(n_acc)
            gate_acc[...] = jnp.zeros_like(gate_acc)

            @pl.loop(0, own_experts)
            def _(e):
                gate = jnp.sum(
                    jnp.where(lane == me * own_experts + e, gates, 0.0), axis=1, keepdims=True
                )
                lin = dot_nn(x_all[block], win[e])
                gate_lin, up_lin = lin[:, :FFE], lin[:, FFE:]
                sig = 1.0 / (1.0 + jnp.exp(-gate_lin))
                silu = gate_lin * sig
                hidden = (silu * up_lin).astype(bf16)

                @pl.when(before)
                def _():
                    for copy in stage_copies(e, block):
                        copy.wait()

                hid_st[e] = hidden
                res = dot_nt(hidden, wout[e]).astype(bf16).astype(f32)
                y_acc[...] += gate * res
                cot = g_all[block].astype(f32) * res_mult
                gate_acc[...] += jnp.where(
                    lane == e, jnp.sum(cot * res, axis=1, keepdims=True), 0.0
                )
                slot = (gate * cot).astype(bf16)
                slot_st[e] = slot
                hidden_cot = dot_nn(slot, wout[e])
                lin_cot = jnp.concatenate(
                    [
                        hidden_cot * up_lin * (sig * (1.0 + gate_lin * (1.0 - sig))),
                        hidden_cot * silu,
                    ],
                    axis=1,
                ).astype(bf16)
                lin_st[e] = lin_cot
                for copy in stage_copies(e, block):
                    copy.start()
                n_acc[...] += dot_nt(lin_cot, win[e]).astype(bf16).astype(f32)

            gate_stage[block] = gate_acc[...].T[:8]

            @pl.when(block != me)
            def _():
                gate_copy(block).start()

            @pl.when(block == me)
            def _():
                gate_out[block] = gate_stage[block]

        @pl.loop(0, chips)
        def _(k):
            b = order(chip, k)

            for side in (-1, 1):
                away = chip + side * k

                for i in range(PIECES):

                    @pl.when((k > 0) & (away >= 0) & (away < chips))
                    def _(side=side, away=away, i=i):
                        pass_on(away, i, me).wait_recv()
                        to_sibling(away, i).start()

                        @pl.when((chip - side >= 0) & (chip - side < chips))
                        def _():
                            pass_on(away, i, me - 2 * side).start()

            for i in range(PIECES):
                across(own_piece(i), b, 1 - core, i).wait_recv()
            remote(
                x_in, g_all.at[2 * b + 1 - core], g_send.at[0], g_recv.at[b], sibling
            ).wait_recv()

            @pl.loop(0, 2)
            def _(h):
                compute(2 * b + lax.rem(core + 1 + h, 2), (k > 0) | (h > 0))

                @pl.when(h == 0)
                def _():
                    p = lax.rem(k, 2)

                    @pl.when(k > 0)
                    def _():
                        fold(k - 1)

                    @pl.when(k > 1)
                    def _():
                        n_copy(p).wait_send()
                        y_copy(p).wait_send()

                    n_give[p] = n_acc[...].astype(bf16)
                    y_give[p] = y_acc[...].astype(bf16)
                    n_copy(p).start()
                    y_copy(p).start()

                @pl.when(h == 1)
                def _():
                    n_mine[b] = n_acc[...].astype(bf16)
                    y_mine[...] = y_acc[...].astype(bf16)

        @pl.loop(chips - 1, chips)
        def _(k):
            fold(k)

        for e in range(own_experts):
            for copy in stage_copies(e, 0):
                copy.wait()

        def loads(t, p):
            e, b = lax.rem(t, own_experts), t // own_experts
            pair = pl.ds(2 * b, 2)
            return [
                pltpu.make_async_copy(
                    lin_out.at[e, pair], g_all.at[pl.ds(4 * p, 2)], ld_sem.at[0, p]
                ),
                pltpu.make_async_copy(
                    slot_out.at[e, pair], g_all.at[pl.ds(4 * p + 2, 2)], ld_sem.at[1, p]
                ),
                pltpu.make_async_copy(hid_out.at[e, pair], hid_ld.at[p], ld_sem.at[2, p]),
            ]

        for copy in loads(jnp.int32(0), 0):
            copy.start()
        gin[...] = jnp.zeros_like(gin)
        gout[...] = jnp.zeros_like(gout)

        @pl.loop(0, chips * own_experts)
        def _(t):
            p = lax.rem(t, 2)
            for copy in loads(t, p):
                copy.wait()

            @pl.when(t + 1 < chips * own_experts)
            def _():
                for copy in loads(t + 1, 1 - p):
                    copy.start()

            e, b = lax.rem(t, own_experts), t // own_experts
            x = x_all[pl.ds(2 * b, 2)].reshape(2 * rows, width)
            lin_cot = g_all[pl.ds(4 * p, 2)].reshape(2 * rows, width)
            gin[e] += dot_tn(x, lin_cot)
            slot = g_all[pl.ds(4 * p + 2, 2)].reshape(2 * rows, width)
            gout[e] += dot_tn(slot, hid_ld[p].reshape(2 * rows, FFE))

        @pl.loop(1, chips)
        def _(k):
            for side in (-1, 1):
                away = chip + side * k

                for i in range(PIECES):

                    @pl.when((away >= 0) & (away < chips))
                    def _(side=side, away=away, i=i):
                        to_sibling(away, i).wait_send()

                        @pl.when((chip - side >= 0) & (chip - side < chips))
                        def _():
                            pass_on(away, i, me - 2 * side).wait_send()

        own_sends(lambda copy: copy.wait_send())

        part_rows = width // parts
        leaving = []
        for e in range(own_experts):
            for j in range(width // rows):
                i = e * (width // rows) + j
                x_all[i] = gin[e, j * rows : (j + 1) * rows].astype(bf16)
                g_all[i, :, :FFE] = gout[e, j * rows : (j + 1) * rows].astype(bf16)
                for q in range(rows // part_rows):
                    here = pl.ds(q * part_rows, part_rows)
                    part = (j * rows + q * part_rows) // part_rows
                    at = 2 * len(leaving)
                    leaving.append(
                        (
                            pltpu.make_async_copy(
                                x_all.at[i, here], g_out.at[part, e, :, pl.ds(0, 2 * FFE)], wg_sem.at[at]
                            ),
                            pltpu.make_async_copy(
                                g_all.at[i, here, pl.ds(0, FFE)],
                                g_out.at[part, e, :, pl.ds(2 * FFE, FFE)],
                                wg_sem.at[at + 1],
                            ),
                        )
                    )
                    for copy in leaving[-1]:
                        copy.start()

        @pl.loop(1, chips)
        def _(k):
            b = order(chip, k)
            remote(
                n_mine.at[b], n_far.at[b], far_send.at[b], far_recv.at[b], 2 * b + core
            ).wait_recv()
            n_sum[...] += n_far[b].astype(f32)
            far_copy(b).wait_send()

        @pl.loop(1, devices)
        def _(k):
            block = lax.rem(me + k, devices)
            remote(
                gate_stage.at[block],
                gate_out.at[block],
                gate_send.at[block],
                gate_recv.at[block],
                block,
            ).wait_recv()
            gate_copy(block).wait_send()

        for p in range(2):
            n_copy(p).wait_send()
            y_copy(p).wait_send()
            y_leave(p, 0).wait()
        for pair in leaving:
            for copy in pair:
                copy.wait()

        for k in range(chips):
            cot_to_sibling(k).wait_send()

    hbm = pl.BlockSpec(memory_space=pl.ANY)
    vmem = pl.BlockSpec(memory_space=pltpu.VMEM)
    block = (rows, width)
    dma = pltpu.SemaphoreType.DMA
    flops = 9 * own_experts * 2 * devices * rows * width * FFE // 1
    return pl.pallas_call(
        kernel,
        name="moe_exchange",
        out_shape=[
            jax.ShapeDtypeStruct((own_experts, devices, rows, 2 * FFE), bf16),
            jax.ShapeDtypeStruct((own_experts, devices) + block, bf16),
            jax.ShapeDtypeStruct((own_experts, devices, rows, FFE), bf16),
            jax.ShapeDtypeStruct(block, f32),
            jax.ShapeDtypeStruct((devices, 8, rows), f32),
            jax.ShapeDtypeStruct((parts, own_experts, width // parts, 3 * FFE), bf16),
        ]
        + [jax.ShapeDtypeStruct(block, bf16)] * chips,
        in_specs=[hbm] * (1 + chips) + [vmem] * 2 + [hbm] * 2,
        out_specs=[hbm] * 3 + [vmem] * 2 + [hbm] * (1 + chips),
        scratch_shapes=[
            pltpu.VMEM((devices,) + block, bf16),
            pltpu.VMEM((devices,) + block, bf16),
            pltpu.VMEM(w_in.shape, bf16),
            pltpu.VMEM(w_out.shape, bf16),
            pltpu.VMEM(block, f32),
            pltpu.VMEM(block, f32),
            pltpu.VMEM((rows, LANES), f32),
            pltpu.VMEM((devices, 8, rows), f32),
            pltpu.VMEM((chips,) + block, bf16),
            pltpu.VMEM((chips,) + block, bf16),
            pltpu.VMEM((2,) + block, bf16),
            pltpu.VMEM((2,) + block, bf16),
            pltpu.VMEM(block, bf16),
            pltpu.VMEM((2,) + block, bf16),
            pltpu.VMEM((2,) + block, bf16),
            pltpu.VMEM((2,) + block, bf16),
            pltpu.VMEM((own_experts, rows, 2 * FFE), bf16),
            pltpu.VMEM((own_experts,) + block, bf16),
            pltpu.VMEM((own_experts, rows, FFE), bf16),
            pltpu.VMEM((own_experts, width, 2 * FFE), f32),
            pltpu.VMEM((own_experts, width, FFE), f32),
            pltpu.VMEM((2, 2, rows, FFE), bf16),
        ]
        + [dma]
        + [
            dma(count)
            for count in (
                (PIECES, chips + 2), (PIECES, chips), (PIECES, chips), (PIECES, chips),
                (chips,), (chips,), (chips,), (2,), (2,), (2,), (2,),
                (chips,), (chips,), (devices,), (devices,),
            )
        ]
        + [
            dma((3, own_experts)),
            dma((2,)),
            dma((3, 2)),
            dma((2,)),
            dma((2 * own_experts * max(parts, width // rows),)),
        ],
        cost_estimate=pl.CostEstimate(
            flops=flops, bytes_accessed=40 << 20, transcendentals=devices * rows * FFE * 2
        ),
        compiler_params=pltpu.CompilerParams(
            collective_id=collective_id, has_side_effects=True, vmem_limit_bytes=62 << 20
        ),
    )(normed, *cots, mask, router, w_in, w_out)


def rms_parts(values):
    return lax.rsqrt(jnp.mean(values * values, axis=-1, keepdims=True) + norm_eps)


def rms_pull(values, scale, gain, cot):
    weighted = cot * gain
    pulled = scale * weighted - values * (scale * scale * scale) * jnp.mean(
        weighted * values, axis=-1, keepdims=True
    )
    return pulled, jnp.sum(cot * values * scale, axis=0)


def on_device(
    tokens,
    out_grad,
    doc_ids,
    expert_picks,
    w_query,
    key_weight_matrix,
    value_weight_matrix,
    w_out,
    w_router,
    gain_attn,
    gain_moe,
    expert_in,
    expert_out,
):
    devices, parts = lax.axis_size("seq"), lax.axis_size("dp")
    me = lax.axis_index("seq")
    rows, width = tokens.shape[1:]
    length = rows * devices
    experts = w_router.shape[1]
    own_experts = expert_in.shape[0]
    heads = QUERY_HEADS // devices
    group = QUERY_HEADS // KEY_VALUE_HEADS
    share = max(1, group // heads)
    q_width = heads * HEAD_SIZE
    w_rows = w_query.shape[0]

    wq = w_query.astype(bf16).reshape(w_rows, devices, q_width)
    wq = jnp.pad(wq, ((0, 0), (0, 0), (0, HEADS_LANES - q_width)))
    wk = key_weight_matrix.astype(bf16).reshape(w_rows, KEY_VALUE_HEADS, HEAD_SIZE)
    wv = value_weight_matrix.astype(bf16).reshape(w_rows, KEY_VALUE_HEADS, HEAD_SIZE)
    wkv = jnp.repeat(jnp.concatenate([wk, wv], axis=2), share, axis=1)
    w_cols = HEADS_LANES + LANES
    w_all = jnp.concatenate([wq, wkv], axis=2).reshape(w_rows, devices * w_cols)
    w_own = lax.dynamic_slice_in_dim(w_all, me * w_cols, w_cols, 1)
    misc = jnp.concatenate(
        [w_router, gain_attn[:, None], gain_moe[:, None]], axis=1
    ).astype(bf16)
    misc = jnp.pad(misc, ((0, 0), (0, LANES - experts - 2)))
    mask = jnp.any(
        expert_picks[0][:, :, None] == jnp.arange(LANES, dtype=jnp.int32), axis=1
    ).astype(bf16)
    doc_rows = jnp.broadcast_to(doc_ids, (8, rows))

    expert_in_full = lax.all_gather(expert_in.astype(bf16), "dp", axis=1, tiled=True)
    expert_out_full = lax.all_gather(expert_out.astype(bf16), "dp", axis=1, tiled=True)
    w_full = lax.all_gather(w_all, "dp", axis=0, tiled=True)

    tok_all, doc_all, mask_all, w_own_all, wo_full, misc_full = exchange(
        0,
        [
            ("gather", "seq", tokens[0], None),
            ("gather", "seq", doc_rows, None),
            ("gather", "seq", mask, None),
            ("gather", "dp", w_own, None),
            ("gather", "dp", w_out.astype(bf16), None),
            ("gather", "dp", misc, None),
        ],
    )
    held, tok_all = lax.optimization_barrier((out_grad[0], tok_all))
    chips = devices // 2
    cots = [held] + [
        lax.ppermute(held, "seq", [(i, (i + 2 * k) % devices) for i in range(devices)])
        for k in range(1, chips)
    ]
    w_own_all = w_own_all.reshape(width, w_cols)
    wo_full = wo_full.reshape(width, width)
    misc_full = misc_full.reshape(width, LANES)
    gain_a = misc_full[:, experts]
    gain_m = misc_full[:, experts + 1].astype(f32)
    docs = doc_all[:, 0]
    table = rope_table(devices, rows)

    normed_a, q_all, kv_all, attended_own, ot, lse = attend_forward(
        tok_all, w_own_all, gain_a[None], table, docs, heads
    )
    wide = q_width % LANES == 0
    (attended,) = exchange(
        1, [("swap", "seq", attended_own, ("out", q_width) if wide else None)]
    )
    if not wide:
        attended = attended.transpose(1, 0, 2).reshape(rows, devices * q_width)

    resid = tokens[0].astype(f32)
    mid = resid + res_mult * dot_nn(attended, wo_full)
    mid_scale = rms_parts(mid)
    normed_m = (mid * mid_scale * gain_m).astype(bf16)
    (_, _, _, moe_sum, gate_cot, e_grads, *branches) = moe_exchange(
        2, normed_m, cots, mask_all, misc_full, expert_in_full, expert_out_full, parts
    )
    branches = [branches[0]] + [
        lax.ppermute(
            branches[k], "seq", [(i, (i + 2 * k) % devices) for i in range(devices)]
        )
        for k in range(1, chips)
    ]
    e_grads = lax.all_to_all(e_grads, "dp", split_axis=0, concat_axis=0)
    gate_cot = gate_cot[:, :own_experts].reshape(experts, rows)
    logits = lax.dot_general(
        misc_full[:, :experts], normed_m, (((0,), (1,)), ((), ())), preferred_element_type=f32
    )
    logits = jnp.where(mask[:, :experts].T > 0, logits, -jnp.inf)
    my_gates = jnp.exp(logits - jnp.max(logits, axis=0, keepdims=True))
    my_gates = my_gates / jnp.sum(my_gates, axis=0, keepdims=True)
    pick_cot = my_gates * (gate_cot - jnp.sum(my_gates * gate_cot, axis=0, keepdims=True))
    logit_cot = pick_cot.astype(bf16)
    grad_router = dot_nn(logit_cot, normed_m).T
    normed_m_cot = moe_sum + lax.dot_general(
        logit_cot, misc_full[:, :experts], (((0,), (1,)), ((), ())), preferred_element_type=f32
    )
    pulled, grad_gain_m = rms_pull(mid, mid_scale, gain_m, normed_m_cot)
    mid_cot = out_grad[0].astype(f32) + pulled
    branch_cot = (res_mult * mid_cot).astype(bf16)
    grad_wo = dot_tn(attended, branch_cot)
    attended_cot = dot_nt(branch_cot, wo_full).astype(bf16)
    if not wide:
        attended_cot = attended_cot.reshape(rows, devices, q_width).transpose(1, 0, 2)
    (heads_cot,) = exchange(
        4, [("swap", "seq", attended_cot, ("in", q_width) if wide else None)]
    )
    qkv_cot = attend_backward(q_all, kv_all, heads_cot, ot, lse, table, docs, heads)
    qkv_cot, branches = lax.optimization_barrier((qkv_cot, branches))
    grad_qkv = dot_tn(
        normed_a.reshape(length, width), qkv_cot.reshape(length, w_cols)
    ).astype(bf16)
    router_pack = jnp.concatenate(
        [grad_router, grad_gain_m[:, None], jnp.zeros((width, LANES - experts - 1), f32)], axis=1
    ).astype(bf16)
    qkv_cot_tok, grad_qkv, grad_wo, router_pack = exchange(
        5,
        [
            ("swap", "seq", qkv_cot, ("out", w_cols)),
            ("swap", "dp", grad_qkv.reshape(parts, w_rows, w_cols), None),
            ("swap", "dp", grad_wo.astype(bf16).reshape(parts, w_rows, width), None),
            ("swap", "dp", router_pack.reshape(parts, w_rows, LANES), None),
        ],
    )
    normed_a_cot = dot_nt(qkv_cot_tok, w_full)
    grad_qkv = jnp.sum(grad_qkv.astype(f32), axis=0).astype(bf16)
    grad_wo = jnp.sum(grad_wo.astype(f32), axis=0).astype(bf16)
    router_pack = jnp.sum(router_pack.astype(f32), axis=0).astype(bf16)
    out_rows = w_rows // devices
    grad_qkv, grad_wo, router_pack = exchange(
        6,
        [
            ("swap", "seq", grad_qkv.reshape(devices, out_rows, w_cols), None),
            ("swap", "seq", grad_wo.reshape(devices, out_rows, width), None),
            ("swap", "seq", router_pack.reshape(devices, out_rows, LANES), None),
        ],
    )
    grad_wo, e_grads = lax.optimization_barrier((grad_wo, e_grads))
    branch_sum = branches[0].astype(f32)
    for k in range(1, chips):
        branch_sum = branch_sum + branches[k].astype(f32)
    output = (mid + res_mult * branch_sum).astype(bf16)[None]
    e_grads = jnp.sum(e_grads.astype(f32), axis=0)
    grad_e_in, grad_e_out = e_grads[:, :, : 2 * FFE], e_grads[:, :, 2 * FFE :]
    resid_scale = rms_parts(resid)
    weighted = normed_a_cot * gain_a.astype(f32)
    input_grad = (
        mid_cot
        + resid_scale * weighted
        - resid
        * (resid_scale * resid_scale * resid_scale)
        * jnp.mean(weighted * resid, axis=-1, keepdims=True)
    ).astype(bf16)[None]

    grad_qkv = grad_qkv.astype(f32)
    grad_wq = grad_qkv[:, :, :q_width].transpose(1, 0, 2).reshape(out_rows, devices * q_width)

    def per_head(part):
        part = part.reshape(devices // share, share, out_rows, HEAD_SIZE).sum(axis=1)
        return part.transpose(1, 0, 2).reshape(out_rows, KEY_VALUE_HEADS * HEAD_SIZE)

    grad_wk = per_head(grad_qkv[:, :, HEADS_LANES : HEADS_LANES + HEAD_SIZE])
    grad_wv = per_head(grad_qkv[:, :, HEADS_LANES + HEAD_SIZE :])
    grad_wo = jnp.sum(grad_wo.astype(f32), axis=0)
    router_pack = jnp.sum(router_pack.astype(f32), axis=0)
    grad_router = router_pack[:, :experts]
    grad_gain_m = router_pack[:, experts]

    def own_rows(weight):
        return lax.dynamic_slice_in_dim(weight, me * out_rows, out_rows, 0).astype(bf16).astype(f32)

    grad_gain_a = (
        jnp.sum(own_rows(w_query) * grad_wq, axis=1)
        + jnp.sum(own_rows(key_weight_matrix) * grad_wk, axis=1)
        + jnp.sum(own_rows(value_weight_matrix) * grad_wv, axis=1)
    ) / own_rows(gain_attn)
    return (
        output,
        input_grad,
        grad_wq,
        grad_wk,
        grad_wv,
        grad_wo,
        grad_router,
        grad_gain_a,
        grad_gain_m,
        grad_e_in,
        grad_e_out,
    )


def solution(mesh):
    return jax.shard_map(
        on_device,
        mesh=mesh,
        in_specs=(
            P("dp", "seq", None),
            P("dp", "seq", None),
            P("dp", "seq"),
            P("dp", "seq", None),
            P("dp", None),
            P("dp", None),
            P("dp", None),
            P("dp", None),
            P("dp", None),
            P("dp"),
            P("dp"),
            P("seq", "dp", None),
            P("seq", "dp", None),
        ),
        out_specs=(
            P("dp", "seq", None),
            P("dp", "seq", None),
            P(("dp", "seq"), None),
            P(("dp", "seq"), None),
            P(("dp", "seq"), None),
            P(("dp", "seq"), None),
            P(("dp", "seq"), None),
            P(("dp", "seq")),
            P(("dp", "seq")),
            P("seq", "dp", None),
            P("seq", "dp", None),
        ),
        check_vma=False,
    )
```

```python
import functools

import jax
import jax.numpy as jnp
import numpy as np
from jax import lax
from jax.experimental import pallas as pl
from jax.experimental.pallas import tpu as pltpu
from jax.sharding import PartitionSpec as P

MESH = pl.DeviceIdType.MESH
PIECES = 2


def _block(ref, j, cut):
    if cut is None:
        return ref.at[j]
    return ref.at[:, pl.ds(pl.multiple_of(j * cut, cut), cut)]


def exchange(collective_id, ops):
    axes = tuple(dict.fromkeys(axis for _, axis, _, _ in ops))
    size = {axis: lax.axis_size(axis) for axis in axes}
    out_shapes, out_specs, scratch, places = [], [], [], []
    for kind, axis, x, cut in ops:
        count = size[axis]
        out_spec = pl.BlockSpec(memory_space=pl.ANY)
        extra = []
        lead = (PIECES,) if kind == "gather" and axis == "seq" else ()
        if kind == "share":
            shape, dtype, copies = (count,) + x.shape, x.dtype, 2 * (count - 1)
        elif kind == "gather":
            shape, dtype = (count,) + x.shape, x.dtype
            copies = count - 1 if axis == "dp" else 3 + 4 * (count // 2 - 1)
        elif kind == "swap":
            copies, dtype = count - 1, x.dtype
            if cut is None:
                shape = x.shape
            elif cut[0] == "in":
                shape = (count, x.shape[0], cut[1])
            else:
                shape = (x.shape[1], count * cut[1])
        out_shapes.append(jax.ShapeDtypeStruct(shape, dtype))
        out_specs.append(out_spec)
        places.append((len(scratch), len(extra)))
        scratch += [
            pltpu.SemaphoreType.DMA(lead + (copies,)),
            pltpu.SemaphoreType.DMA(lead + (max(copies, count),)),
            pltpu.SemaphoreType.DMA,
        ] + extra

    def kernel(*refs):
        ins, outs, work = refs[: len(ops)], refs[len(ops) : 2 * len(ops)], refs[2 * len(ops) :]
        me = {axis: lax.axis_index(axis) for axis in axes}
        barrier = pltpu.get_barrier_semaphore()
        for axis in axes:
            for k in range(1, size[axis]):
                pl.semaphore_signal(
                    barrier,
                    inc=1,
                    device_id={axis: lax.rem(me[axis] + k, size[axis])},
                    device_id_type=MESH,
                )
        pl.semaphore_wait(barrier, sum(size[axis] - 1 for axis in axes))

        def remote(axis, src, dst, send, recv, to):
            return pltpu.make_async_remote_copy(
                src_ref=src,
                dst_ref=dst,
                send_sem=send,
                recv_sem=recv,
                device_id={axis: to},
                device_id_type=MESH,
            )

        second, third = [], []
        for (kind, axis, _, cut), x, o, (at, extra) in zip(ops, ins, outs, places):
            send, recv, local = work[at : at + 3]
            count, my = size[axis], me[axis]
            if kind == "swap":
                into = cut[1] if cut is not None and cut[0] == "out" else None
                outof = cut[1] if cut is not None and cut[0] == "in" else None
                own = pltpu.make_async_copy(_block(x, my, outof), _block(o, my, into), local)
                own.start()
                third.append(own.wait)
                for k in range(1, count):
                    to = lax.rem(my + k, count)
                    copy = remote(
                        axis,
                        _block(x, to, outof),
                        _block(o, my, into),
                        send.at[k - 1],
                        recv.at[k - 1],
                        to,
                    )
                    copy.start()
                    frm = lax.rem(my + count - k, count)
                    arrive = remote(
                        axis,
                        _block(x, to, outof),
                        _block(o, frm, into),
                        send.at[k - 1],
                        recv.at[k - 1],
                        to,
                    )
                    third.append(copy.wait_send)
                    third.append(arrive.wait_recv)
            elif kind == "gather" and axis == "dp":
                own = pltpu.make_async_copy(x, o.at[my], local)
                own.start()
                third.append(own.wait)
                for k in range(1, count):
                    to = lax.rem(my + k, count)
                    frm = lax.rem(my + count - k, count)
                    copy = remote(axis, x, o.at[my], send.at[k - 1], recv.at[k - 1], to)
                    copy.start()
                    third.append(copy.wait_send)
                    third.append(
                        remote(
                            axis, x, o.at[frm], send.at[k - 1], recv.at[k - 1], to
                        ).wait_recv
                    )
            elif kind == "share":
                seq, half = me["seq"], x.shape[0] // 2
                core = lax.rem(seq, 2)
                sibling = seq + 1 - 2 * core
                own = pltpu.make_async_copy(x, o.at[my], local)
                own.start()
                third.append(own.wait)

                def side_of(ref, which, half=half):
                    return ref.at[pl.ds(which * half, half)]

                def relay(k, axis=axis, x=x, o=o, send=send, recv=recv, count=count, my=my, core=core, sibling=sibling, side_of=side_of):
                    to = lax.rem(my + k, count)
                    frm = lax.rem(my + count - k, count)
                    remote(
                        axis,
                        side_of(x, core),
                        side_of(o.at[frm], core),
                        send.at[k - 1],
                        recv.at[k - 1],
                        to,
                    ).wait_recv()
                    slot = count - 2 + k
                    spot = side_of(o.at[frm], core)
                    over = remote("seq", spot, spot, send.at[slot], recv.at[slot], sibling)
                    over.start()
                    third.append(over.wait_send)
                    third.append(
                        remote(
                            "seq",
                            spot,
                            side_of(o.at[frm], 1 - core),
                            send.at[slot],
                            recv.at[slot],
                            sibling,
                        ).wait_recv
                    )

                for k in range(1, count):
                    to = lax.rem(my + k, count)
                    copy = remote(
                        axis,
                        side_of(x, core),
                        side_of(o.at[my], core),
                        send.at[k - 1],
                        recv.at[k - 1],
                        to,
                    )
                    copy.start()
                    third.append(copy.wait_send)
                    second.append((k + 0.75, functools.partial(relay, k)))
            elif kind == "gather":
                chips = count // 2
                chip, core = my // 2, lax.rem(my, 2)
                sibling = my + 1 - 2 * core
                own = pltpu.make_async_copy(x, o.at[my], local)
                own.start()
                third.append(own.wait)

                cuts = PIECES if x.shape[0] % (16 * PIECES) == 0 else 1
                size_of = x.shape[0] // cuts

                def cut_of(ref, i, size_of=size_of):
                    return ref.at[pl.ds(i * size_of, size_of)]

                def line(src, b, i, slot, to, axis=axis, o=o, send=send, recv=recv, core=core, cut_of=cut_of):
                    return remote(
                        axis, src, cut_of(o.at[2 * b + core], i), send.at[i, slot], recv.at[i, b], to
                    )

                def across(src, b, i, slot, half, axis=axis, o=o, send=send, recv=recv, chips=chips, sibling=sibling, cut_of=cut_of):
                    return remote(
                        axis,
                        src,
                        cut_of(o.at[2 * b + half], i),
                        send.at[i, slot],
                        recv.at[i, chips + b],
                        sibling,
                    )

                def guarded(where, act):
                    pl.when(where)(act)

                for i in range(cuts):
                    for slot, where, to in ((0, chip > 0, my - 2), (1, chip < chips - 1, my + 2)):
                        copy = line(cut_of(x, i), chip, i, slot, to)
                        guarded(where, copy.start)
                        third.append(functools.partial(guarded, where, copy.wait_send))
                for i in range(cuts):
                    copy = across(cut_of(x, i), chip, i, 2, core)
                    copy.start()
                    third.append(copy.wait_send)
                    third.append(across(cut_of(x, i), chip, i, 2, 1 - core).wait_recv)

                def hop(k, side, i, chips=chips, chip=chip, core=core, my=my, x=x, o=o, line=line, across=across, cut_of=cut_of):
                    b = chip + side * k
                    there = (b >= 0) & (b < chips)
                    onward = there & ((chip - side >= 0) & (chip - side < chips))
                    slot = 3 + (k - 1) * 4 + (side + 1)
                    spot = cut_of(o.at[2 * b + core], i)
                    further = line(spot, b, i, slot, my - 2 * side)
                    over = across(spot, b, i, slot + 1, core)
                    arrived = line(cut_of(x, i), b, i, slot, my)
                    brought = across(cut_of(x, i), b, i, slot + 1, 1 - core)

                    @pl.when(there)
                    def _():
                        arrived.wait_recv()

                    guarded(onward, further.start)
                    guarded(there, over.start)
                    third.append(functools.partial(guarded, onward, further.wait_send))
                    third.append(functools.partial(guarded, there, over.wait_send))
                    third.append(functools.partial(guarded, there, brought.wait_recv))

                for k in range(1, chips):
                    for i in range(cuts):
                        for side in (-1, 1):
                            second.append((k + i / cuts, functools.partial(hop, k, side, i)))
        for _, run in sorted(second, key=lambda item: item[0]):
            run()
        for wait in third:
            wait()

    return pl.pallas_call(
        kernel,
        name=f"exchange{collective_id}",
        out_shape=out_shapes,
        in_specs=[pl.BlockSpec(memory_space=pl.ANY)] * len(ops),
        out_specs=out_specs,
        scratch_shapes=scratch,
        compiler_params=pltpu.CompilerParams(
            collective_id=collective_id, has_side_effects=True, vmem_limit_bytes=48 << 20
        ),
    )(*[x for _, _, x, _ in ops])

QUERY_HEADS = 16
KEY_VALUE_HEADS = 8
HEAD_SIZE = 64
FFE = 512
TOP = 8

att_mult = 0.015625
res_mult = 0.22
norm_eps = 1e-06
rope_theta = 10000.0
LANES = 128
bf16 = jnp.bfloat16
f32 = jnp.float32
HEADS_LANES = 128


def dot_nt(a, b):
    return lax.dot_general(a, b, (((1,), (1,)), ((), ())), preferred_element_type=f32)


def dot_nn(a, b):
    return lax.dot_general(a, b, (((1,), (0,)), ((), ())), preferred_element_type=f32)


def dot_tn(a, b):
    return lax.dot_general(a, b, (((0,), (0,)), ((), ())), preferred_element_type=f32)


def turn(x):
    half = HEAD_SIZE // 2
    lane = lax.broadcasted_iota(jnp.int32, x.shape, 1)
    width = x.shape[1]
    return jnp.where(
        lax.rem(lane, HEAD_SIZE) < half, pltpu.roll(x, width - half, 1), pltpu.roll(x, half, 1)
    )


def rope_table(blocks, rows):
    half = HEAD_SIZE // 2
    frequency = np.float32(rope_theta) ** (
        -np.arange(half, dtype=np.float32) * np.float32(2.0) / np.float32(HEAD_SIZE)
    )
    angles = (frequency[:, None] * np.arange(blocks * rows, dtype=np.float32)[None, :]).astype(
        np.float32
    )
    table = np.concatenate([np.cos(angles), np.sin(angles)], axis=0).astype(np.float32)
    return jnp.asarray(table.reshape(HEAD_SIZE, blocks, rows).transpose(1, 0, 2))


def spread_table(table):
    half = HEAD_SIZE // 2
    turned = table.T
    cos, sin = turned[:, :half], turned[:, half:]
    return (
        jnp.concatenate([cos, cos] * (LANES // HEAD_SIZE), axis=1),
        jnp.concatenate([-sin, sin] * (LANES // HEAD_SIZE), axis=1),
    )


def across_lanes(row, lanes):
    return jnp.broadcast_to(row, (lanes, row.shape[1])).T


def first_blocks(docs):
    return jnp.sum(
        (docs[:, -1][:, None] < docs[:, 0][None, :]).astype(jnp.int32), axis=0
    )


def stack_heads(x, heads):
    return jnp.concatenate(
        [x[:, h * HEAD_SIZE : (h + 1) * HEAD_SIZE] for h in range(heads)], axis=0
    )


def attend_forward(tok_all, w_own, gain, table, docs, heads):
    blocks, rows, width = tok_all.shape
    length = blocks * rows
    cols = heads * rows
    first = first_blocks(docs)
    out_width = heads * HEAD_SIZE

    def kernel(first_ref, tok, w, gain_ref, table_ref, docs_ref, na_ref, q_ref, kv_ref, att_ref, ot_ref, lse_ref, k_scr, vt_scr, doc_scr):
        i = pl.program_id(0)
        x = tok[0].astype(f32)
        scale = lax.rsqrt(jnp.mean(x * x, axis=-1, keepdims=True) + norm_eps)
        na = (x * scale * gain_ref[...].astype(f32)).astype(bf16)
        na_ref[0] = na
        qkv = dot_nn(na, w[...])
        c, s = spread_table(table_ref[0])
        q, kv = qkv[:, :HEADS_LANES], qkv[:, HEADS_LANES:]
        q = (q * c + turn(q) * s).astype(bf16)
        lane = lax.broadcasted_iota(jnp.int32, kv.shape, 1)
        kv = jnp.where(lane < HEAD_SIZE, kv * c + turn(kv) * s, kv).astype(bf16)
        q_ref[0] = q
        kv_ref[0] = kv
        k_scr[i] = kv[:, :HEAD_SIZE]
        vt_scr[i] = kv.astype(f32).T[HEAD_SIZE:].astype(bf16)
        q2 = stack_heads(q, heads)
        doc_row = docs_ref[0].astype(f32)
        doc_scr[i] = across_lanes(doc_row, LANES)
        doc_query = jnp.concatenate([doc_row] * heads, axis=1)
        query = i * rows + lax.rem(lax.broadcasted_iota(jnp.int32, (1, cols), 1), rows)
        key_iota = lax.broadcasted_iota(jnp.int32, (rows, cols), 0)

        def step(j, carry):
            top, total, ot = carry
            scores = dot_nt(k_scr[j], q2) * att_mult
            key = key_iota + j * rows
            same = jnp.concatenate([doc_scr[j]] * (cols // LANES), axis=1) == doc_query
            scores = jnp.where(same & (key <= query), scores, -1e30)
            new_top = jnp.maximum(top, jnp.max(scores, axis=0, keepdims=True))
            p = jnp.exp(scores - new_top)
            keep = jnp.exp(top - new_top)
            total = total * keep + jnp.sum(p, axis=0, keepdims=True)
            ot = ot * keep + dot_nn(vt_scr[j], p.astype(bf16))
            return new_top, total, ot

        top, total, ot = lax.fori_loop(
            first_ref[i],
            i + 1,
            step,
            (
                jnp.full((1, cols), -1e30, f32),
                jnp.zeros((1, cols), f32),
                jnp.zeros((HEAD_SIZE, cols), f32),
            ),
        )
        ot = ot / total
        ot_ref[0] = ot
        lse_ref[0] = top + jnp.log(total)
        out = ot.T
        att_ref[0] = jnp.concatenate(
            [out[h * rows : (h + 1) * rows] for h in range(heads)], axis=1
        ).astype(bf16)

    def block(shape):
        return pl.BlockSpec((1,) + shape, lambda i, _: (i, 0, 0))

    def whole(shape):
        return pl.BlockSpec(shape, lambda i, _: (0,) * len(shape))

    grid_spec = pltpu.PrefetchScalarGridSpec(
        num_scalar_prefetch=1,
        grid=(blocks,),
        in_specs=[
            block((rows, width)),
            whole(w_own.shape),
            whole((1, width)),
            block((HEAD_SIZE, rows)),
            block((1, rows)),
        ],
        out_specs=[
            block((rows, width)),
            block((rows, HEADS_LANES)),
            block((rows, LANES)),
            block((rows, out_width)),
            block((HEAD_SIZE, cols)),
            block((1, cols)),
        ],
        scratch_shapes=[
            pltpu.VMEM((blocks, rows, HEAD_SIZE), bf16),
            pltpu.VMEM((blocks, HEAD_SIZE, rows), bf16),
            pltpu.VMEM((blocks, rows, LANES), f32),
        ],
    )
    return pl.pallas_call(
        kernel,
        name="attend_forward",
        grid_spec=grid_spec,
        out_shape=[
            jax.ShapeDtypeStruct((blocks, rows, width), bf16),
            jax.ShapeDtypeStruct((blocks, rows, HEADS_LANES), bf16),
            jax.ShapeDtypeStruct((blocks, rows, LANES), bf16),
            jax.ShapeDtypeStruct((blocks, rows, out_width), bf16),
            jax.ShapeDtypeStruct((blocks, HEAD_SIZE, cols), f32),
            jax.ShapeDtypeStruct((blocks, 1, cols), f32),
        ],
        cost_estimate=pl.CostEstimate(
            flops=2 * length * width * 256 + 2 * length * length * cols // rows * 128,
            bytes_accessed=2 * length * width * 4,
            transcendentals=length * length,
        ),
        compiler_params=pltpu.CompilerParams(
            dimension_semantics=("arbitrary",), vmem_limit_bytes=40 << 20
        ),
    )(
        first,
        tok_all,
        w_own,
        gain,
        table,
        docs[:, None],
    )


def attend_backward(q_all, kv_all, cot, ot, lse, table, docs, heads):
    blocks, rows, _ = q_all.shape
    length = blocks * rows
    cols = heads * rows
    first = first_blocks(docs)

    def kernel(first_ref, q_ref, kv_ref, do_ref, ot_ref, lse_ref, table_ref, docs_ref, out_ref, dk_scr, dv_scr, dq_scr, doc_scr):
        i = pl.program_id(0)

        @pl.when(i == 0)
        def _():
            dk_scr[...] = jnp.zeros_like(dk_scr)
            dv_scr[...] = jnp.zeros_like(dv_scr)

        q2 = stack_heads(q_ref[0], heads)
        do2 = stack_heads(do_ref[0], heads)
        delta = jnp.sum(do2.astype(f32).T * ot_ref[0], axis=0, keepdims=True)
        log_total = lse_ref[0]
        doc_row = docs_ref[0].astype(f32)
        doc_scr[i] = across_lanes(doc_row, LANES)
        doc_query = jnp.concatenate([doc_row] * heads, axis=1)
        query = i * rows + lax.rem(lax.broadcasted_iota(jnp.int32, (1, cols), 1), rows)
        key_iota = lax.broadcasted_iota(jnp.int32, (rows, cols), 0)
        dq_scr[...] = jnp.zeros_like(dq_scr)

        @pl.loop(first_ref[i], i + 1)
        def _(j):
            kv = kv_ref[j]
            k, v = kv[:, :HEAD_SIZE], kv[:, HEAD_SIZE:]
            scores = dot_nt(k, q2) * att_mult
            key = key_iota + j * rows
            same = jnp.concatenate([doc_scr[j]] * (cols // LANES), axis=1) == doc_query
            p = jnp.where(same & (key <= query), jnp.exp(scores - log_total), 0.0)
            ds = (p * (dot_nt(v, do2) - delta)).astype(bf16)
            dv_scr[j] += dot_nn(p.astype(bf16), do2)
            dk_scr[j] += dot_nn(ds, q2)
            dq_scr[...] += dot_tn(ds, k)

        def rope_back(x, c, s):
            return (x * c - turn(x) * s).astype(bf16)

        dq = dq_scr[...] * att_mult
        dq = [dq[h * rows : (h + 1) * rows] for h in range(heads)]
        if heads * HEAD_SIZE < HEADS_LANES:
            dq.append(jnp.zeros((rows, HEADS_LANES - heads * HEAD_SIZE), f32))
        dq = jnp.concatenate(dq, axis=1).astype(bf16).astype(f32)
        out_ref[i, :, :HEADS_LANES] = rope_back(dq, *spread_table(table_ref[i]))

        @pl.when(i == blocks - 1)
        def _():
            @pl.loop(0, blocks)
            def _(j):
                kv = jnp.concatenate([dk_scr[j] * att_mult, dv_scr[j]], axis=1)
                lane = lax.broadcasted_iota(jnp.int32, kv.shape, 1)
                c, s = spread_table(table_ref[j])
                out_ref[j, :, HEADS_LANES:] = jnp.where(
                    lane < HEAD_SIZE, kv * c - turn(kv) * s, kv
                ).astype(bf16)

    def block(shape):
        return pl.BlockSpec((1,) + shape, lambda i, _: (i, 0, 0))

    def whole(shape):
        return pl.BlockSpec(shape, lambda i, _: (0,) * len(shape))

    grid_spec = pltpu.PrefetchScalarGridSpec(
        num_scalar_prefetch=1,
        grid=(blocks,),
        in_specs=[
            block((rows, HEADS_LANES)),
            whole((blocks, rows, LANES)),
            block((rows, heads * HEAD_SIZE)),
            block((HEAD_SIZE, cols)),
            block((1, cols)),
            whole((blocks, HEAD_SIZE, rows)),
            block((1, rows)),
        ],
        out_specs=whole((blocks, rows, HEADS_LANES + LANES)),
        scratch_shapes=[
            pltpu.VMEM((blocks, rows, HEAD_SIZE), f32),
            pltpu.VMEM((blocks, rows, HEAD_SIZE), f32),
            pltpu.VMEM((cols, HEAD_SIZE), f32),
            pltpu.VMEM((blocks, rows, LANES), f32),
        ],
    )
    return pl.pallas_call(
        kernel,
        name="attend_backward",
        grid_spec=grid_spec,
        out_shape=jax.ShapeDtypeStruct((blocks, rows, HEADS_LANES + LANES), bf16),
        cost_estimate=pl.CostEstimate(
            flops=5 * length * length * cols // rows * 128,
            bytes_accessed=2 * length * 1024,
            transcendentals=length * length,
        ),
        compiler_params=pltpu.CompilerParams(
            dimension_semantics=("arbitrary",), vmem_limit_bytes=48 << 20
        ),
    )(
        first,
        q_all,
        kv_all,
        cot,
        ot,
        lse,
        table,
        docs[:, None],
    )


def moe_exchange(collective_id, normed, cots, mask, router, w_in, w_out, parts):
    devices = lax.axis_size("seq")
    chips = devices // 2
    rows, width = normed.shape
    own_experts = w_in.shape[0]

    def order(chip, k):
        left = chip < chips - 1 - chip
        longer = jnp.where(left, chips - 1 - chip, chip)
        near = jnp.where(left, chip + k, chip - k)
        return jnp.where(k <= longer, near, jnp.where(left, chips - 1 - k, k))

    def kernel(*refs):
        x_in, g_in = refs[0], refs[1 : 1 + chips]
        mask_ref, router_ref, win_in, wout_in = refs[1 + chips : 5 + chips]
        (lin_out, slot_out, hid_out, n_sum, gate_out, g_out) = refs[5 + chips : 11 + chips]
        y_outs = refs[11 + chips : 11 + 2 * chips]
        (
            x_all, g_all, win, wout, y_acc, n_acc, gate_acc, gate_stage,
            n_mine, n_far, n_give, n_theirs, y_mine, y_give, y_theirs, y_pre,
            lin_st, slot_st, hid_st, gin, gout, hid_ld,
            local, line_send, line_recv, sib_send, sib_recv, g_local, g_send, g_recv,
            n_send, n_recv, y_send, y_recv, far_send, far_recv, gate_send, gate_recv,
            st_sem, y_sem, ld_sem, w_sem, wg_sem,
        ) = refs[11 + 2 * chips :]
        me = lax.axis_index("seq")
        chip, core = me // 2, lax.rem(me, 2)
        sibling = me + 1 - 2 * core
        win_copy = pltpu.make_async_copy(win_in, win, w_sem.at[0])
        wout_copy = pltpu.make_async_copy(wout_in, wout, w_sem.at[1])
        win_copy.start()
        wout_copy.start()
        barrier = pltpu.get_barrier_semaphore()
        for k in range(1, devices):
            pl.semaphore_signal(
                barrier, inc=1, device_id={"seq": lax.rem(me + k, devices)}, device_id_type=MESH
            )
        pl.semaphore_wait(barrier, devices - 1)

        def remote(src, dst, send, recv, to):
            return pltpu.make_async_remote_copy(
                src_ref=src,
                dst_ref=dst,
                send_sem=send,
                recv_sem=recv,
                device_id={"seq": to},
                device_id_type=MESH,
            )

        half = rows // PIECES

        def piece(b, core_of, i):
            return x_all.at[2 * b + core_of, pl.ds(i * half, half)]

        def line(src, b, i, slot, to):
            return remote(
                src, piece(b, core, i), line_send.at[i, slot], line_recv.at[i, b], to
            )

        def across(src, b, core_of, i):
            return remote(
                src, piece(b, core_of, i), sib_send.at[i, b], sib_recv.at[i, b], sibling
            )

        def own_piece(i):
            return x_in.at[pl.ds(i * half, half)]

        def pass_on(b, i, to):
            return line(piece(b, core, i), b, i, 2 + b, to)

        def to_sibling(b, i):
            return across(piece(b, core, i), b, core, i)

        def own_sends(act):
            for i in range(PIECES):

                @pl.when(chip > 0)
                def _(i=i):
                    act(line(own_piece(i), chip, i, 0, me - 2))

                @pl.when(chip < chips - 1)
                def _(i=i):
                    act(line(own_piece(i), chip, i, 1, me + 2))

            for i in range(PIECES):
                act(across(own_piece(i), chip, core, i))

        def cot_to_sibling(k):
            b = lax.rem(chip + chips - k, chips)
            return remote(
                g_in[k], g_all.at[2 * b + core], g_send.at[k], g_recv.at[b], sibling
            )

        def cot_local(k):
            b = lax.rem(chip + chips - k, chips)
            return pltpu.make_async_copy(g_in[k], g_all.at[2 * b + core], g_local.at[k])

        own_sends(lambda copy: copy.start())
        own = pltpu.make_async_copy(x_in, x_all.at[me], local)
        own.start()
        for k in range(chips):
            cot_to_sibling(k).start()
            cot_local(k).start()
        own.wait()
        for k in range(chips):
            cot_local(k).wait()
        win_copy.wait()
        wout_copy.wait()

        def gate_copy(block):
            return remote(
                gate_stage.at[block],
                gate_out.at[me],
                gate_send.at[block],
                gate_recv.at[me],
                block,
            )

        def n_copy(p):
            return remote(n_give.at[p], n_theirs.at[p], n_send.at[p], n_recv.at[p], sibling)

        def y_copy(p):
            return remote(y_give.at[p], y_theirs.at[p], y_send.at[p], y_recv.at[p], sibling)

        def y_leave(p, k):
            return pltpu.make_async_copy(y_pre.at[p], y_outs[k], y_sem.at[p])

        def stage_copies(e, block):
            return [
                pltpu.make_async_copy(lin_st.at[e], lin_out.at[e, block], st_sem.at[0, e]),
                pltpu.make_async_copy(slot_st.at[e], slot_out.at[e, block], st_sem.at[1, e]),
                pltpu.make_async_copy(hid_st.at[e], hid_out.at[e, block], st_sem.at[2, e]),
            ]

        def far_copy(b):
            return remote(
                n_mine.at[b], n_far.at[chip], far_send.at[b], far_recv.at[chip], 2 * b + core
            )

        def fold(k):
            b, p = order(chip, k), lax.rem(k, 2)
            n_copy(p).wait_recv()
            both = n_mine[b].astype(f32) + n_theirs[p].astype(f32)

            @pl.when(b == chip)
            def _():
                n_sum[...] = both

            @pl.when(b != chip)
            def _():
                n_mine[b] = both.astype(bf16)
                far_copy(b).start()

            @pl.when(k > 1)
            def _():
                y_leave(p, 0).wait()

            y_copy(p).wait_recv()
            y_pre[p] = (y_mine[...].astype(f32) + y_theirs[p].astype(f32)).astype(bf16)
            away = lax.rem(b - chip + chips, chips)
            for r in range(chips):

                @pl.when(away == r)
                def _(r=r):
                    y_leave(p, r).start()

        def compute(block, before):
            x = x_all[block]
            there = mask_ref[block] > 0
            logits = jnp.where(there, dot_nn(x, router_ref[...]), -1e30)
            gates = jnp.where(
                there, jnp.exp(logits - jnp.max(logits, axis=1, keepdims=True)), 0.0
            )
            gates = gates / jnp.sum(gates, axis=1, keepdims=True)
            lane = lax.broadcasted_iota(jnp.int32, gates.shape, 1)
            y_acc[...] = jnp.zeros_like(y_acc)
            n_acc[...] = jnp.zeros_like(n_acc)
            gate_acc[...] = jnp.zeros_like(gate_acc)

            @pl.loop(0, own_experts)
            def _(e):
                gate = jnp.sum(
                    jnp.where(lane == me * own_experts + e, gates, 0.0), axis=1, keepdims=True
                )
                lin = dot_nn(x_all[block], win[e])
                gate_lin, up_lin = lin[:, :FFE], lin[:, FFE:]
                sig = 1.0 / (1.0 + jnp.exp(-gate_lin))
                silu = gate_lin * sig
                hidden = (silu * up_lin).astype(bf16)

                @pl.when(before)
                def _():
                    for copy in stage_copies(e, block):
                        copy.wait()

                hid_st[e] = hidden
                res = dot_nt(hidden, wout[e]).astype(bf16).astype(f32)
                y_acc[...] += gate * res
                cot = g_all[block].astype(f32) * res_mult
                gate_acc[...] += jnp.where(
                    lane == e, jnp.sum(cot * res, axis=1, keepdims=True), 0.0
                )
                slot = (gate * cot).astype(bf16)
                slot_st[e] = slot
                hidden_cot = dot_nn(slot, wout[e])
                lin_cot = jnp.concatenate(
                    [
                        hidden_cot * up_lin * (sig * (1.0 + gate_lin * (1.0 - sig))),
                        hidden_cot * silu,
                    ],
                    axis=1,
                ).astype(bf16)
                lin_st[e] = lin_cot
                for copy in stage_copies(e, block):
                    copy.start()
                n_acc[...] += dot_nt(lin_cot, win[e]).astype(bf16).astype(f32)

            gate_stage[block] = gate_acc[...].T[:8]

            @pl.when(block != me)
            def _():
                gate_copy(block).start()

            @pl.when(block == me)
            def _():
                gate_out[block] = gate_stage[block]

        @pl.loop(0, chips)
        def _(k):
            b = order(chip, k)

            for side in (-1, 1):
                away = chip + side * k

                for i in range(PIECES):

                    @pl.when((k > 0) & (away >= 0) & (away < chips))
                    def _(side=side, away=away, i=i):
                        pass_on(away, i, me).wait_recv()
                        to_sibling(away, i).start()

                        @pl.when((chip - side >= 0) & (chip - side < chips))
                        def _():
                            pass_on(away, i, me - 2 * side).start()

            for i in range(PIECES):
                across(own_piece(i), b, 1 - core, i).wait_recv()
            remote(
                x_in, g_all.at[2 * b + 1 - core], g_send.at[0], g_recv.at[b], sibling
            ).wait_recv()

            @pl.loop(0, 2)
            def _(h):
                compute(2 * b + lax.rem(core + 1 + h, 2), (k > 0) | (h > 0))

                @pl.when(h == 0)
                def _():
                    p = lax.rem(k, 2)

                    @pl.when(k > 0)
                    def _():
                        fold(k - 1)

                    @pl.when(k > 1)
                    def _():
                        n_copy(p).wait_send()
                        y_copy(p).wait_send()

                    n_give[p] = n_acc[...].astype(bf16)
                    y_give[p] = y_acc[...].astype(bf16)
                    n_copy(p).start()
                    y_copy(p).start()

                @pl.when(h == 1)
                def _():
                    n_mine[b] = n_acc[...].astype(bf16)
                    y_mine[...] = y_acc[...].astype(bf16)

        @pl.loop(chips - 1, chips)
        def _(k):
            fold(k)

        for e in range(own_experts):
            for copy in stage_copies(e, 0):
                copy.wait()

        def loads(t, p):
            e, b = lax.rem(t, own_experts), t // own_experts
            pair = pl.ds(2 * b, 2)
            return [
                pltpu.make_async_copy(
                    lin_out.at[e, pair], g_all.at[pl.ds(4 * p, 2)], ld_sem.at[0, p]
                ),
                pltpu.make_async_copy(
                    slot_out.at[e, pair], g_all.at[pl.ds(4 * p + 2, 2)], ld_sem.at[1, p]
                ),
                pltpu.make_async_copy(hid_out.at[e, pair], hid_ld.at[p], ld_sem.at[2, p]),
            ]

        for copy in loads(jnp.int32(0), 0):
            copy.start()
        gin[...] = jnp.zeros_like(gin)
        gout[...] = jnp.zeros_like(gout)

        @pl.loop(0, chips * own_experts)
        def _(t):
            p = lax.rem(t, 2)
            for copy in loads(t, p):
                copy.wait()

            @pl.when(t + 1 < chips * own_experts)
            def _():
                for copy in loads(t + 1, 1 - p):
                    copy.start()

            e, b = lax.rem(t, own_experts), t // own_experts
            x = x_all[pl.ds(2 * b, 2)].reshape(2 * rows, width)
            lin_cot = g_all[pl.ds(4 * p, 2)].reshape(2 * rows, width)
            gin[e] += dot_tn(x, lin_cot)
            slot = g_all[pl.ds(4 * p + 2, 2)].reshape(2 * rows, width)
            gout[e] += dot_tn(slot, hid_ld[p].reshape(2 * rows, FFE))

        @pl.loop(1, chips)
        def _(k):
            for side in (-1, 1):
                away = chip + side * k

                for i in range(PIECES):

                    @pl.when((away >= 0) & (away < chips))
                    def _(side=side, away=away, i=i):
                        to_sibling(away, i).wait_send()

                        @pl.when((chip - side >= 0) & (chip - side < chips))
                        def _():
                            pass_on(away, i, me - 2 * side).wait_send()

        own_sends(lambda copy: copy.wait_send())

        part_rows = width // parts
        leaving = []
        for e in range(own_experts):
            for j in range(width // rows):
                i = e * (width // rows) + j
                x_all[i] = gin[e, j * rows : (j + 1) * rows].astype(bf16)
                g_all[i, :, :FFE] = gout[e, j * rows : (j + 1) * rows].astype(bf16)
                for q in range(rows // part_rows):
                    here = pl.ds(q * part_rows, part_rows)
                    part = (j * rows + q * part_rows) // part_rows
                    at = 2 * len(leaving)
                    leaving.append(
                        (
                            pltpu.make_async_copy(
                                x_all.at[i, here], g_out.at[part, e, :, pl.ds(0, 2 * FFE)], wg_sem.at[at]
                            ),
                            pltpu.make_async_copy(
                                g_all.at[i, here, pl.ds(0, FFE)],
                                g_out.at[part, e, :, pl.ds(2 * FFE, FFE)],
                                wg_sem.at[at + 1],
                            ),
                        )
                    )
                    for copy in leaving[-1]:
                        copy.start()

        @pl.loop(1, chips)
        def _(k):
            b = order(chip, k)
            remote(
                n_mine.at[b], n_far.at[b], far_send.at[b], far_recv.at[b], 2 * b + core
            ).wait_recv()
            n_sum[...] += n_far[b].astype(f32)
            far_copy(b).wait_send()

        @pl.loop(1, devices)
        def _(k):
            block = lax.rem(me + k, devices)
            remote(
                gate_stage.at[block],
                gate_out.at[block],
                gate_send.at[block],
                gate_recv.at[block],
                block,
            ).wait_recv()
            gate_copy(block).wait_send()

        for p in range(2):
            n_copy(p).wait_send()
            y_copy(p).wait_send()
            y_leave(p, 0).wait()
        for pair in leaving:
            for copy in pair:
                copy.wait()

        for k in range(chips):
            cot_to_sibling(k).wait_send()

    hbm = pl.BlockSpec(memory_space=pl.ANY)
    vmem = pl.BlockSpec(memory_space=pltpu.VMEM)
    block = (rows, width)
    dma = pltpu.SemaphoreType.DMA
    flops = 9 * own_experts * 2 * devices * rows * width * FFE // 1
    return pl.pallas_call(
        kernel,
        name="moe_exchange",
        out_shape=[
            jax.ShapeDtypeStruct((own_experts, devices, rows, 2 * FFE), bf16),
            jax.ShapeDtypeStruct((own_experts, devices) + block, bf16),
            jax.ShapeDtypeStruct((own_experts, devices, rows, FFE), bf16),
            jax.ShapeDtypeStruct(block, f32),
            jax.ShapeDtypeStruct((devices, 8, rows), f32),
            jax.ShapeDtypeStruct((parts, own_experts, width // parts, 3 * FFE), bf16),
        ]
        + [jax.ShapeDtypeStruct(block, bf16)] * chips,
        in_specs=[hbm] * (1 + chips) + [vmem] * 2 + [hbm] * 2,
        out_specs=[hbm] * 3 + [vmem] * 2 + [hbm] * (1 + chips),
        scratch_shapes=[
            pltpu.VMEM((devices,) + block, bf16),
            pltpu.VMEM((devices,) + block, bf16),
            pltpu.VMEM(w_in.shape, bf16),
            pltpu.VMEM(w_out.shape, bf16),
            pltpu.VMEM(block, f32),
            pltpu.VMEM(block, f32),
            pltpu.VMEM((rows, LANES), f32),
            pltpu.VMEM((devices, 8, rows), f32),
            pltpu.VMEM((chips,) + block, bf16),
            pltpu.VMEM((chips,) + block, bf16),
            pltpu.VMEM((2,) + block, bf16),
            pltpu.VMEM((2,) + block, bf16),
            pltpu.VMEM(block, bf16),
            pltpu.VMEM((2,) + block, bf16),
            pltpu.VMEM((2,) + block, bf16),
            pltpu.VMEM((2,) + block, bf16),
            pltpu.VMEM((own_experts, rows, 2 * FFE), bf16),
            pltpu.VMEM((own_experts,) + block, bf16),
            pltpu.VMEM((own_experts, rows, FFE), bf16),
            pltpu.VMEM((own_experts, width, 2 * FFE), f32),
            pltpu.VMEM((own_experts, width, FFE), f32),
            pltpu.VMEM((2, 2, rows, FFE), bf16),
        ]
        + [dma]
        + [
            dma(count)
            for count in (
                (PIECES, chips + 2), (PIECES, chips), (PIECES, chips), (PIECES, chips),
                (chips,), (chips,), (chips,), (2,), (2,), (2,), (2,),
                (chips,), (chips,), (devices,), (devices,),
            )
        ]
        + [
            dma((3, own_experts)),
            dma((2,)),
            dma((3, 2)),
            dma((2,)),
            dma((2 * own_experts * max(parts, width // rows),)),
        ],
        cost_estimate=pl.CostEstimate(
            flops=flops, bytes_accessed=40 << 20, transcendentals=devices * rows * FFE * 2
        ),
        compiler_params=pltpu.CompilerParams(
            collective_id=collective_id, has_side_effects=True, vmem_limit_bytes=62 << 20
        ),
    )(normed, *cots, mask, router, w_in, w_out)


def final_exchange(
    collective_id, qkv_cot, grad_qkv, token_grads, w_full, tokens, mid_cot, gain, mid, branches
):
    devices, parts = lax.axis_size("seq"), lax.axis_size("dp")
    chips = devices // 2
    _, rows, cols = qkv_cot.shape
    width = tokens.shape[1]
    out_rows = grad_qkv.shape[2]
    count = len(token_grads)
    wides = [x.shape[3] for x in token_grads]
    token_grads = [x.reshape(parts, chips, 2, out_rows, x.shape[3]) for x in token_grads]

    def kernel(*refs):
        qkv_in, gq_in = refs[:2]
        gt_in = refs[2 : 2 + count]
        w_in, tok_ref, mid_cot_ref, gain_ref, mid_ref = refs[2 + count : 7 + count]
        y_refs = refs[7 + count : 7 + count + chips]
        refs = refs[7 + count + chips :]
        in_grad, output, gq_out = refs[:3]
        gt_out = refs[3 : 3 + count]
        refs = refs[3 + count :]
        (
            qkv_tok, w_all, nac, gq_recv, gq_sum,
            q_send, q_recv, local, w_sem, gq_send, gq_rsem, gqz_send, gqz_recv, gq_local,
        ) = refs[:14]
        work = [refs[14 + 11 * i : 25 + 11 * i] for i in range(count)]
        me, my = lax.axis_index("seq"), lax.axis_index("dp")
        chip, core = me // 2, lax.rem(me, 2)
        sibling = me + 1 - 2 * core
        w_copy = pltpu.make_async_copy(w_in, w_all, w_sem)
        w_copy.start()
        barrier = pltpu.get_barrier_semaphore()
        for axis, index, size in (("seq", me, devices), ("dp", my, parts)):
            for k in range(1, size):
                pl.semaphore_signal(
                    barrier,
                    inc=1,
                    device_id={axis: lax.rem(index + k, size)},
                    device_id_type=MESH,
                )
        pl.semaphore_wait(barrier, devices + parts - 2)

        def remote(axis, src, dst, send, recv, to):
            return pltpu.make_async_remote_copy(
                src_ref=src,
                dst_ref=dst,
                send_sem=send,
                recv_sem=recv,
                device_id={axis: to},
                device_id_type=MESH,
            )

        sent = []

        def columns(j):
            return qkv_tok.at[:, pl.ds(pl.multiple_of(j * cols, cols), cols)]

        for x, w in zip(gt_in, work):
            mine, theirs, far, near, last, sems, dp_send, dp_recv, z_send, z_recv, _ = w
            copy = remote(
                "seq", x.at[:, :, 1 - core], theirs, sems.at[0], sems.at[1], sibling
            )
            copy.start()
            sent.append(copy)
            pltpu.make_async_copy(x.at[:, :, core], mine, sems.at[2]).start()
        for k in range(1, parts):
            to = lax.rem(my + k, parts)
            copy = remote(
                "dp", gq_in.at[to], gq_recv.at[my], gq_send.at[k - 1], gq_rsem.at[k - 1], to
            )
            copy.start()
            sent.append(copy)
        own_q = pltpu.make_async_copy(gq_in.at[my], gq_recv.at[my], gq_local)
        own_q.start()
        own = pltpu.make_async_copy(qkv_in.at[me], columns(me), local)
        own.start()
        for k in range(1, devices):
            to = lax.rem(me + k, devices)
            copy = remote(
                "seq", qkv_in.at[to], columns(me), q_send.at[k - 1], q_recv.at[k - 1], to
            )
            copy.start()
            sent.append(copy)

        for x, w in zip(gt_in, work):
            mine, theirs, far, near, last, sems, dp_send, dp_recv, z_send, z_recv, _ = w
            remote("seq", x.at[:, :, core], theirs, sems.at[0], sems.at[1], sibling).wait_recv()
            pltpu.make_async_copy(x.at[:, :, core], mine, sems.at[2]).wait()
            mine[...] = (mine[...].astype(f32) + theirs[...].astype(f32)).astype(bf16)
            for k in range(1, parts):
                to = lax.rem(my + k, parts)
                copy = remote(
                    "dp", mine.at[to], far.at[k - 1], dp_send.at[k - 1], dp_recv.at[k - 1], to
                )
                copy.start()
                sent.append(copy)

        total = y_refs[0][...].astype(f32)
        for k in range(1, chips):
            total = total + y_refs[k][...].astype(f32)
        output[...] = (mid_ref[...] + res_mult * total).astype(bf16)

        own_q.wait()
        for k in range(1, parts):
            frm = lax.rem(my + parts - k, parts)
            remote(
                "dp", gq_in.at[frm], gq_recv.at[frm], gq_send.at[k - 1], gq_rsem.at[k - 1], frm
            ).wait_recv()
        summed = gq_recv[0].astype(f32)
        for p in range(1, parts):
            summed = summed + gq_recv[p].astype(f32)
        gq_sum[...] = summed.astype(bf16)
        own_z = pltpu.make_async_copy(gq_sum.at[me], gq_out.at[me], gq_local)
        own_z.start()
        for k in range(1, devices):
            to = lax.rem(me + k, devices)
            copy = remote(
                "seq", gq_sum.at[to], gq_out.at[me], gqz_send.at[k - 1], gqz_recv.at[k - 1], to
            )
            copy.start()
            sent.append(copy)
        for w in work:
            mine, theirs, far, near, last, sems, dp_send, dp_recv, z_send, z_recv, _ = w
            summed = mine[my].astype(f32)
            for k in range(1, parts):
                remote(
                    "dp", mine.at[0], far.at[k - 1], dp_send.at[k - 1], dp_recv.at[k - 1], my
                ).wait_recv()
                summed = summed + far[k - 1].astype(f32)
            near[...] = summed.astype(bf16)
            for k in range(1, chips):
                to = lax.rem(chip + k, chips)
                copy = remote(
                    "seq",
                    near.at[to],
                    last.at[k - 1],
                    z_send.at[k - 1],
                    z_recv.at[k - 1],
                    2 * to + core,
                )
                copy.start()
                sent.append(copy)

        own.wait()
        w_copy.wait()
        for k in range(1, devices):
            frm = lax.rem(me + devices - k, devices)
            remote(
                "seq", qkv_in.at[frm], columns(frm), q_send.at[k - 1], q_recv.at[k - 1], frm
            ).wait_recv()

        @pl.loop(0, width // 256)
        def _(j):
            at = pl.multiple_of(j * 256, 256)
            nac[:, pl.ds(at, 256)] = dot_nt(qkv_tok[...], w_all[pl.ds(at, 256), :])

        resid = tok_ref[...].astype(f32)
        scale = lax.rsqrt(jnp.mean(resid * resid, axis=-1, keepdims=True) + norm_eps)
        weighted = nac[...] * gain_ref[...].astype(f32)
        in_grad[...] = (
            mid_cot_ref[...]
            + scale * weighted
            - resid
            * (scale * scale * scale)
            * jnp.mean(weighted * resid, axis=-1, keepdims=True)
        ).astype(bf16)

        for o, w in zip(gt_out, work):
            mine, theirs, far, near, last, sems, dp_send, dp_recv, z_send, z_recv, _ = w
            summed = near[chip].astype(f32)
            for k in range(1, chips):
                remote(
                    "seq", near.at[0], last.at[k - 1], z_send.at[k - 1], z_recv.at[k - 1], me
                ).wait_recv()
                summed = summed + last[k - 1].astype(f32)
            o[...] = summed
        own_z.wait()
        for k in range(1, devices):
            frm = lax.rem(me + devices - k, devices)
            remote(
                "seq", gq_sum.at[frm], gq_out.at[frm], gqz_send.at[k - 1], gqz_recv.at[k - 1], frm
            ).wait_recv()
        for copy in sent:
            copy.wait_send()

    hbm = pl.BlockSpec(memory_space=pl.ANY)
    vmem = pl.BlockSpec(memory_space=pltpu.VMEM)
    dma = pltpu.SemaphoreType.DMA
    scratch = [
        pltpu.VMEM((rows, devices * cols), bf16),
        pltpu.VMEM(w_full.shape, bf16),
        pltpu.VMEM((rows, width), f32),
        pltpu.VMEM(grad_qkv.shape, bf16),
        pltpu.VMEM(grad_qkv.shape[1:], bf16),
        dma((devices - 1,)),
        dma((devices - 1,)),
        dma,
        dma,
        dma((parts - 1,)),
        dma((parts - 1,)),
        dma((devices - 1,)),
        dma((devices - 1,)),
        dma,
    ]
    for wide in wides:
        piece = (out_rows, wide)
        scratch += [
            pltpu.VMEM((parts, chips) + piece, bf16),
            pltpu.VMEM((parts, chips) + piece, bf16),
            pltpu.VMEM((parts - 1, chips) + piece, bf16),
            pltpu.VMEM((chips,) + piece, bf16),
            pltpu.VMEM((chips - 1,) + piece, bf16),
            dma((3,)),
            dma((parts - 1,)),
            dma((parts - 1,)),
            dma((chips - 1,)),
            dma((chips - 1,)),
            dma,
        ]
    return pl.pallas_call(
        kernel,
        name="final_exchange",
        out_shape=[
            jax.ShapeDtypeStruct((rows, width), bf16),
            jax.ShapeDtypeStruct((rows, width), bf16),
            jax.ShapeDtypeStruct(grad_qkv.shape[1:], bf16),
        ]
        + [jax.ShapeDtypeStruct((out_rows, wide), f32) for wide in wides],
        in_specs=[hbm] * (3 + count) + [vmem] * (4 + chips),
        out_specs=[vmem] * (3 + count),
        scratch_shapes=scratch,
        compiler_params=pltpu.CompilerParams(
            collective_id=collective_id, has_side_effects=True, vmem_limit_bytes=48 << 20
        ),
    )(qkv_cot, grad_qkv, *token_grads, w_full, tokens, mid_cot, gain, mid, *branches)


def rms_parts(values):
    return lax.rsqrt(jnp.mean(values * values, axis=-1, keepdims=True) + norm_eps)


def rms_pull(values, scale, gain, cot):
    weighted = cot * gain
    pulled = scale * weighted - values * (scale * scale * scale) * jnp.mean(
        weighted * values, axis=-1, keepdims=True
    )
    return pulled, jnp.sum(cot * values * scale, axis=0)


def on_device(
    tokens,
    out_grad,
    doc_ids,
    expert_picks,
    w_query,
    key_weight_matrix,
    value_weight_matrix,
    w_out,
    w_router,
    gain_attn,
    gain_moe,
    expert_in,
    expert_out,
):
    devices, parts = lax.axis_size("seq"), lax.axis_size("dp")
    me = lax.axis_index("seq")
    rows, width = tokens.shape[1:]
    length = rows * devices
    experts = w_router.shape[1]
    own_experts = expert_in.shape[0]
    heads = QUERY_HEADS // devices
    group = QUERY_HEADS // KEY_VALUE_HEADS
    share = max(1, group // heads)
    q_width = heads * HEAD_SIZE
    w_rows = w_query.shape[0]

    wq = w_query.astype(bf16).reshape(w_rows, devices, q_width)
    wq = jnp.pad(wq, ((0, 0), (0, 0), (0, HEADS_LANES - q_width)))
    wk = key_weight_matrix.astype(bf16).reshape(w_rows, KEY_VALUE_HEADS, HEAD_SIZE)
    wv = value_weight_matrix.astype(bf16).reshape(w_rows, KEY_VALUE_HEADS, HEAD_SIZE)
    wkv = jnp.repeat(jnp.concatenate([wk, wv], axis=2), share, axis=1)
    w_cols = HEADS_LANES + LANES
    w_all = jnp.concatenate([wq, wkv], axis=2).reshape(w_rows, devices * w_cols)
    w_own = lax.dynamic_slice_in_dim(w_all, me * w_cols, w_cols, 1)
    misc = jnp.concatenate(
        [w_router, gain_attn[:, None], gain_moe[:, None]], axis=1
    ).astype(bf16)
    misc = jnp.pad(misc, ((0, 0), (0, LANES - experts - 2)))
    mask = jnp.any(
        expert_picks[0][:, :, None] == jnp.arange(LANES, dtype=jnp.int32), axis=1
    ).astype(bf16)
    doc_rows = jnp.broadcast_to(doc_ids, (8, rows))

    expert_in_full = lax.all_gather(expert_in.astype(bf16), "dp", axis=1, tiled=True)
    expert_out_full = lax.all_gather(expert_out.astype(bf16), "dp", axis=1, tiled=True)
    w_full = lax.all_gather(w_all, "dp", axis=0, tiled=True)

    chips = devices // 2

    def shift(x, k):
        return lax.ppermute(x, "seq", [(i, (i + 2 * k) % devices) for i in range(devices)])

    held = out_grad[0]
    early = shift(held, 1)
    tok_all, doc_all, mask_all, w_own_all, wo_full, misc_full = exchange(
        0,
        [
            ("gather", "seq", tokens[0], None),
            ("gather", "seq", doc_rows, None),
            ("gather", "seq", mask, None),
            ("gather", "dp", w_own, None),
            ("share", "dp", w_out.astype(bf16), None),
            ("share", "dp", misc, None),
        ],
    )
    tok_all, held, early = lax.optimization_barrier((tok_all, held, early))
    cots = [held, early] + [shift(held, k) for k in range(2, chips)]
    w_own_all = w_own_all.reshape(width, w_cols)
    wo_full = wo_full.reshape(width, width)
    misc_full = misc_full.reshape(width, LANES)
    gain_a = misc_full[:, experts]
    gain_m = misc_full[:, experts + 1].astype(f32)
    docs = doc_all[:, 0]
    table = rope_table(devices, rows)

    normed_a, q_all, kv_all, attended_own, ot, lse = attend_forward(
        tok_all, w_own_all, gain_a[None], table, docs, heads
    )
    wide = q_width % LANES == 0
    (attended,) = exchange(
        1, [("swap", "seq", attended_own, ("out", q_width) if wide else None)]
    )
    if not wide:
        attended = attended.transpose(1, 0, 2).reshape(rows, devices * q_width)

    resid = tokens[0].astype(f32)
    mid = resid + res_mult * dot_nn(attended, wo_full)
    mid_scale = rms_parts(mid)
    normed_m = (mid * mid_scale * gain_m).astype(bf16)
    (_, _, _, moe_sum, gate_cot, e_grads, *branches) = moe_exchange(
        2, normed_m, cots, mask_all, misc_full, expert_in_full, expert_out_full, parts
    )
    middle = chips // 2
    branches[middle] = shift(branches[middle], middle)
    e_grads = lax.all_to_all(e_grads, "dp", split_axis=0, concat_axis=0)
    gate_cot = gate_cot[:, :own_experts].reshape(experts, rows)
    logits = lax.dot_general(
        misc_full[:, :experts], normed_m, (((0,), (1,)), ((), ())), preferred_element_type=f32
    )
    logits = jnp.where(mask[:, :experts].T > 0, logits, -jnp.inf)
    my_gates = jnp.exp(logits - jnp.max(logits, axis=0, keepdims=True))
    my_gates = my_gates / jnp.sum(my_gates, axis=0, keepdims=True)
    pick_cot = my_gates * (gate_cot - jnp.sum(my_gates * gate_cot, axis=0, keepdims=True))
    logit_cot = pick_cot.astype(bf16)
    grad_router = dot_nn(logit_cot, normed_m).T
    normed_m_cot = moe_sum + lax.dot_general(
        logit_cot, misc_full[:, :experts], (((0,), (1,)), ((), ())), preferred_element_type=f32
    )
    pulled, grad_gain_m = rms_pull(mid, mid_scale, gain_m, normed_m_cot)
    mid_cot = out_grad[0].astype(f32) + pulled
    branch_cot = (res_mult * mid_cot).astype(bf16)
    grad_wo = dot_tn(attended, branch_cot)
    attended_cot = dot_nt(branch_cot, wo_full).astype(bf16)
    if not wide:
        attended_cot = attended_cot.reshape(rows, devices, q_width).transpose(1, 0, 2)
    (heads_cot,) = exchange(
        4, [("swap", "seq", attended_cot, ("in", q_width) if wide else None)]
    )
    others = [k for k in range(1, chips) if k != middle]
    heads_cot, later = lax.optimization_barrier((heads_cot, [branches[k] for k in others]))
    for k, branch in zip(others, later):
        branches[k] = shift(branch, k)
    qkv_cot = attend_backward(q_all, kv_all, heads_cot, ot, lse, table, docs, heads)
    qkv_cot, branches = lax.optimization_barrier((qkv_cot, branches))
    grad_qkv = dot_tn(
        normed_a.reshape(length, width), qkv_cot.reshape(length, w_cols)
    ).astype(bf16)
    router_pack = jnp.concatenate(
        [grad_router, grad_gain_m[:, None], jnp.zeros((width, LANES - experts - 1), f32)], axis=1
    ).astype(bf16)
    out_rows = w_rows // devices
    input_grad, output, grad_qkv, grad_wo, router_pack = final_exchange(
        5,
        qkv_cot,
        grad_qkv.reshape(parts, devices, out_rows, w_cols),
        [
            grad_wo.astype(bf16).reshape(parts, devices, out_rows, width),
            router_pack.reshape(parts, devices, out_rows, LANES),
        ],
        w_full,
        tokens[0],
        mid_cot,
        gain_a[None],
        mid,
        branches,
    )
    input_grad, output = input_grad[None], output[None]
    grad_e_in = jnp.sum(e_grads[..., : 2 * FFE].astype(f32), axis=0)
    grad_e_out = jnp.sum(e_grads[..., 2 * FFE :].astype(f32), axis=0)

    grad_qkv = grad_qkv.astype(f32)
    grad_wq = grad_qkv[:, :, :q_width].transpose(1, 0, 2).reshape(out_rows, devices * q_width)

    def per_head(part):
        part = part.reshape(devices // share, share, out_rows, HEAD_SIZE).sum(axis=1)
        return part.transpose(1, 0, 2).reshape(out_rows, KEY_VALUE_HEADS * HEAD_SIZE)

    grad_wk = per_head(grad_qkv[:, :, HEADS_LANES : HEADS_LANES + HEAD_SIZE])
    grad_wv = per_head(grad_qkv[:, :, HEADS_LANES + HEAD_SIZE :])
    grad_router = router_pack[:, :experts]
    grad_gain_m = router_pack[:, experts]

    def own_rows(weight):
        return lax.dynamic_slice_in_dim(weight, me * out_rows, out_rows, 0).astype(bf16).astype(f32)

    grad_gain_a = (
        jnp.sum(own_rows(w_query) * grad_wq, axis=1)
        + jnp.sum(own_rows(key_weight_matrix) * grad_wk, axis=1)
        + jnp.sum(own_rows(value_weight_matrix) * grad_wv, axis=1)
    ) / own_rows(gain_attn)
    return (
        output,
        input_grad,
        grad_wq,
        grad_wk,
        grad_wv,
        grad_wo,
        grad_router,
        grad_gain_a,
        grad_gain_m,
        grad_e_in,
        grad_e_out,
    )


def solution(mesh):
    return jax.shard_map(
        on_device,
        mesh=mesh,
        in_specs=(
            P("dp", "seq", None),
            P("dp", "seq", None),
            P("dp", "seq"),
            P("dp", "seq", None),
            P("dp", None),
            P("dp", None),
            P("dp", None),
            P("dp", None),
            P("dp", None),
            P("dp"),
            P("dp"),
            P("seq", "dp", None),
            P("seq", "dp", None),
        ),
        out_specs=(
            P("dp", "seq", None),
            P("dp", "seq", None),
            P(("dp", "seq"), None),
            P(("dp", "seq"), None),
            P(("dp", "seq"), None),
            P(("dp", "seq"), None),
            P(("dp", "seq"), None),
            P(("dp", "seq")),
            P(("dp", "seq")),
            P("seq", "dp", None),
            P("seq", "dp", None),
        ),
        check_vma=False,
    )
```

```python
import functools

import jax
import jax.numpy as jnp
import numpy as np
from jax import lax
from jax.experimental import pallas as pl
from jax.experimental.pallas import tpu as pltpu
from jax.sharding import PartitionSpec as P

MESH = pl.DeviceIdType.MESH
PIECES = 2


def _block(ref, j, cut):
    if cut is None:
        return ref.at[j]
    return ref.at[:, pl.ds(pl.multiple_of(j * cut, cut), cut)]


def exchange(collective_id, ops, prepare=None, given=(), work=(), made=None, keep=None):
    axes = tuple(dict.fromkeys(axis for _, axis, _, _ in ops))
    size = {axis: lax.axis_size(axis) for axis in axes}
    out_shapes, out_specs, scratch, places = [], [], [], []
    for kind, axis, x, cut in ops:
        count = size[axis]
        out_spec = pl.BlockSpec(memory_space=pl.ANY)
        extra = []
        lead = (PIECES,) if kind == "gather" and axis == "seq" else ()
        if kind == "shift":
            shape, dtype, copies = x.shape, x.dtype, 1
        elif kind == "share":
            shape, dtype, copies = (count,) + x.shape, x.dtype, 2 * (count - 1)
        elif kind == "gather":
            shape, dtype = (count,) + x.shape, x.dtype
            copies = count - 1 if axis == "dp" else 3 + 4 * (count // 2 - 1)
        elif kind == "swap":
            copies, dtype = count - 1, x.dtype
            if cut is None:
                shape = x.shape
            elif cut[0] == "in":
                shape = (count, x.shape[0], cut[1])
            else:
                shape = (x.shape[1], count * cut[1])
        out_shapes.append(jax.ShapeDtypeStruct(shape, dtype))
        out_specs.append(out_spec)
        places.append((len(scratch), len(extra)))
        scratch += [
            pltpu.SemaphoreType.DMA(lead + (copies,)),
            pltpu.SemaphoreType.DMA(lead + (max(copies, count),)),
            pltpu.SemaphoreType.DMA,
        ] + extra

    early = [x for _, _, x, cut in ops if not isinstance(cut, int)]
    own_scratch = len(scratch)

    def kernel(*refs):
        ins, refs = list(refs[: len(early)]), refs[len(early) :]
        extra_in, refs = refs[: len(given)], refs[len(given) :]
        outs, refs = refs[: len(ops)], refs[len(ops) :]
        if keep is not None:
            kept, refs = refs[0], refs[1:]
        work, extra_work = refs[:own_scratch], refs[own_scratch:]
        ins += [None] * (len(ops) - len(early))
        me = {axis: lax.axis_index(axis) for axis in axes}
        barrier = pltpu.get_barrier_semaphore()
        for axis in axes:
            for k in range(1, size[axis]):
                pl.semaphore_signal(
                    barrier,
                    inc=1,
                    device_id={axis: lax.rem(me[axis] + k, size[axis])},
                    device_id_type=MESH,
                )
        pl.semaphore_wait(barrier, sum(size[axis] - 1 for axis in axes))

        def remote(axis, src, dst, send, recv, to):
            return pltpu.make_async_remote_copy(
                src_ref=src,
                dst_ref=dst,
                send_sem=send,
                recv_sem=recv,
                device_id={axis: to},
                device_id_type=MESH,
            )

        second, third = [], []
        for (kind, axis, _, cut), x, o, (at, extra) in zip(ops, ins, outs, places):
            if isinstance(cut, int):
                if x is None and cut == 0:
                    all_refs = list(extra_in) + list(extra_work[:-1])
                    prepare(all_refs)
                    late = made(all_refs)
                    leave = pltpu.make_async_copy(all_refs[keep[1]], kept, extra_work[-1])
                    leave.start()
                    third.append(leave.wait)
                x, cut = late[cut], None
            send, recv, local = work[at : at + 3]
            count, my = size[axis], me[axis]
            if kind == "swap":
                into = cut[1] if cut is not None and cut[0] == "out" else None
                outof = cut[1] if cut is not None and cut[0] == "in" else None
                own = pltpu.make_async_copy(_block(x, my, outof), _block(o, my, into), local)
                own.start()
                third.append(own.wait)
                for k in range(1, count):
                    to = lax.rem(my + k, count)
                    copy = remote(
                        axis,
                        _block(x, to, outof),
                        _block(o, my, into),
                        send.at[k - 1],
                        recv.at[k - 1],
                        to,
                    )
                    copy.start()
                    frm = lax.rem(my + count - k, count)
                    arrive = remote(
                        axis,
                        _block(x, to, outof),
                        _block(o, frm, into),
                        send.at[k - 1],
                        recv.at[k - 1],
                        to,
                    )
                    third.append(copy.wait_send)
                    third.append(arrive.wait_recv)
            elif kind == "gather" and axis == "dp":
                own = pltpu.make_async_copy(x, o.at[my], local)
                own.start()
                third.append(own.wait)
                for k in range(1, count):
                    to = lax.rem(my + k, count)
                    frm = lax.rem(my + count - k, count)
                    copy = remote(axis, x, o.at[my], send.at[k - 1], recv.at[k - 1], to)
                    copy.start()
                    third.append(copy.wait_send)
                    third.append(
                        remote(
                            axis, x, o.at[frm], send.at[k - 1], recv.at[k - 1], to
                        ).wait_recv
                    )
            elif kind == "shift":
                copy = remote(
                    axis, x, o, send.at[0], recv.at[0], lax.rem(my + 2 * (count // 4), count)
                )
                second.append((count // 4 + 0.9, copy.start))
                third.append(copy.wait)
            elif kind == "share":
                seq, half = me["seq"], x.shape[0] // 2
                core = lax.rem(seq, 2)
                sibling = seq + 1 - 2 * core
                own = pltpu.make_async_copy(x, o.at[my], local)
                own.start()
                third.append(own.wait)

                def side_of(ref, which, half=half):
                    return ref.at[pl.ds(which * half, half)]

                def relay(k, axis=axis, x=x, o=o, send=send, recv=recv, count=count, my=my, core=core, sibling=sibling, side_of=side_of):
                    to = lax.rem(my + k, count)
                    frm = lax.rem(my + count - k, count)
                    remote(
                        axis,
                        side_of(x, core),
                        side_of(o.at[frm], core),
                        send.at[k - 1],
                        recv.at[k - 1],
                        to,
                    ).wait_recv()
                    slot = count - 2 + k
                    spot = side_of(o.at[frm], core)
                    over = remote("seq", spot, spot, send.at[slot], recv.at[slot], sibling)
                    over.start()
                    third.append(over.wait_send)
                    third.append(
                        remote(
                            "seq",
                            spot,
                            side_of(o.at[frm], 1 - core),
                            send.at[slot],
                            recv.at[slot],
                            sibling,
                        ).wait_recv
                    )

                for k in range(1, count):
                    to = lax.rem(my + k, count)
                    copy = remote(
                        axis,
                        side_of(x, core),
                        side_of(o.at[my], core),
                        send.at[k - 1],
                        recv.at[k - 1],
                        to,
                    )
                    copy.start()
                    third.append(copy.wait_send)
                    second.append((k + 0.75, functools.partial(relay, k)))
            elif kind == "gather":
                chips = count // 2
                chip, core = my // 2, lax.rem(my, 2)
                sibling = my + 1 - 2 * core
                own = pltpu.make_async_copy(x, o.at[my], local)
                own.start()
                third.append(own.wait)

                cuts = PIECES if x.shape[0] % (16 * PIECES) == 0 else 1
                size_of = x.shape[0] // cuts

                def cut_of(ref, i, size_of=size_of):
                    return ref.at[pl.ds(i * size_of, size_of)]

                def line(src, b, i, slot, to, axis=axis, o=o, send=send, recv=recv, core=core, cut_of=cut_of):
                    return remote(
                        axis, src, cut_of(o.at[2 * b + core], i), send.at[i, slot], recv.at[i, b], to
                    )

                def across(src, b, i, slot, half, axis=axis, o=o, send=send, recv=recv, chips=chips, sibling=sibling, cut_of=cut_of):
                    return remote(
                        axis,
                        src,
                        cut_of(o.at[2 * b + half], i),
                        send.at[i, slot],
                        recv.at[i, chips + b],
                        sibling,
                    )

                def guarded(where, act):
                    pl.when(where)(act)

                for i in range(cuts):
                    for slot, where, to in ((0, chip > 0, my - 2), (1, chip < chips - 1, my + 2)):
                        copy = line(cut_of(x, i), chip, i, slot, to)
                        guarded(where, copy.start)
                        third.append(functools.partial(guarded, where, copy.wait_send))
                for i in range(cuts):
                    copy = across(cut_of(x, i), chip, i, 2, core)
                    copy.start()
                    third.append(copy.wait_send)
                    third.append(across(cut_of(x, i), chip, i, 2, 1 - core).wait_recv)

                def hop(k, side, i, chips=chips, chip=chip, core=core, my=my, x=x, o=o, line=line, across=across, cut_of=cut_of):
                    b = chip + side * k
                    there = (b >= 0) & (b < chips)
                    onward = there & ((chip - side >= 0) & (chip - side < chips))
                    slot = 3 + (k - 1) * 4 + (side + 1)
                    spot = cut_of(o.at[2 * b + core], i)
                    further = line(spot, b, i, slot, my - 2 * side)
                    over = across(spot, b, i, slot + 1, core)
                    arrived = line(cut_of(x, i), b, i, slot, my)
                    brought = across(cut_of(x, i), b, i, slot + 1, 1 - core)

                    @pl.when(there)
                    def _():
                        arrived.wait_recv()

                    guarded(onward, further.start)
                    guarded(there, over.start)
                    third.append(functools.partial(guarded, onward, further.wait_send))
                    third.append(functools.partial(guarded, there, over.wait_send))
                    third.append(functools.partial(guarded, there, brought.wait_recv))

                for k in range(1, chips):
                    for i in range(cuts):
                        for side in (-1, 1):
                            second.append((k + i / cuts, functools.partial(hop, k, side, i)))
        for _, run in sorted(second, key=lambda item: item[0]):
            run()
        for wait in third:
            wait()

    return pl.pallas_call(
        kernel,
        name=f"exchange{collective_id}",
        out_shape=out_shapes + ([] if keep is None else [keep[0]]),
        in_specs=[pl.BlockSpec(memory_space=pl.ANY)] * (len(early) + len(given)),
        out_specs=out_specs + ([] if keep is None else [pl.BlockSpec(memory_space=pl.ANY)]),
        scratch_shapes=scratch
        + list(work)
        + ([] if keep is None else [pltpu.SemaphoreType.DMA]),
        compiler_params=pltpu.CompilerParams(
            collective_id=collective_id, has_side_effects=True, vmem_limit_bytes=60 << 20
        ),
    )(*early, *given)

QUERY_HEADS = 16
KEY_VALUE_HEADS = 8
HEAD_SIZE = 64
FFE = 512
TOP = 8

att_mult = 0.015625
res_mult = 0.22
norm_eps = 1e-06
rope_theta = 10000.0
LANES = 128
bf16 = jnp.bfloat16
f32 = jnp.float32
HEADS_LANES = 128


def dot_nt(a, b):
    return lax.dot_general(a, b, (((1,), (1,)), ((), ())), preferred_element_type=f32)


def dot_nn(a, b):
    return lax.dot_general(a, b, (((1,), (0,)), ((), ())), preferred_element_type=f32)


def dot_tn(a, b):
    return lax.dot_general(a, b, (((0,), (0,)), ((), ())), preferred_element_type=f32)


def turn(x):
    half = HEAD_SIZE // 2
    lane = lax.broadcasted_iota(jnp.int32, x.shape, 1)
    width = x.shape[1]
    return jnp.where(
        lax.rem(lane, HEAD_SIZE) < half, pltpu.roll(x, width - half, 1), pltpu.roll(x, half, 1)
    )


def rope_table(blocks, rows):
    half = HEAD_SIZE // 2
    frequency = np.float32(rope_theta) ** (
        -np.arange(half, dtype=np.float32) * np.float32(2.0) / np.float32(HEAD_SIZE)
    )
    angles = (frequency[:, None] * np.arange(blocks * rows, dtype=np.float32)[None, :]).astype(
        np.float32
    )
    table = np.concatenate([np.cos(angles), np.sin(angles)], axis=0).astype(np.float32)
    return jnp.asarray(table.reshape(HEAD_SIZE, blocks, rows).transpose(1, 0, 2))


def spread_table(table):
    half = HEAD_SIZE // 2
    turned = table.T
    cos, sin = turned[:, :half], turned[:, half:]
    return (
        jnp.concatenate([cos, cos] * (LANES // HEAD_SIZE), axis=1),
        jnp.concatenate([-sin, sin] * (LANES // HEAD_SIZE), axis=1),
    )


def across_lanes(row, lanes):
    return jnp.broadcast_to(row, (lanes, row.shape[1])).T


def first_blocks(docs):
    return jnp.sum(
        (docs[:, -1][:, None] < docs[:, 0][None, :]).astype(jnp.int32), axis=0
    )


def stack_heads(x, heads):
    return jnp.concatenate(
        [x[:, h * HEAD_SIZE : (h + 1) * HEAD_SIZE] for h in range(heads)], axis=0
    )


def attend_forward(tok_all, w_own, gain, table, docs, heads):
    blocks, rows, width = tok_all.shape
    length = blocks * rows
    cols = heads * rows
    first = first_blocks(docs)
    out_width = heads * HEAD_SIZE

    def kernel(first_ref, tok, w, gain_ref, table_ref, docs_ref, na_ref, q_ref, kv_ref, att_ref, ot_ref, lse_ref, k_scr, vt_scr, doc_scr):
        i = pl.program_id(0)
        x = tok[0].astype(f32)
        scale = lax.rsqrt(jnp.mean(x * x, axis=-1, keepdims=True) + norm_eps)
        na = (x * scale * gain_ref[...].astype(f32)).astype(bf16)
        na_ref[0] = na
        qkv = dot_nn(na, w[...])
        c, s = spread_table(table_ref[0])
        q, kv = qkv[:, :HEADS_LANES], qkv[:, HEADS_LANES:]
        q = (q * c + turn(q) * s).astype(bf16)
        lane = lax.broadcasted_iota(jnp.int32, kv.shape, 1)
        kv = jnp.where(lane < HEAD_SIZE, kv * c + turn(kv) * s, kv).astype(bf16)
        q_ref[0] = q
        kv_ref[0] = kv
        k_scr[i] = kv[:, :HEAD_SIZE]
        vt_scr[i] = kv.astype(f32).T[HEAD_SIZE:].astype(bf16)
        q2 = stack_heads(q, heads)
        doc_row = docs_ref[0].astype(f32)
        doc_scr[i] = across_lanes(doc_row, LANES)
        doc_query = jnp.concatenate([doc_row] * heads, axis=1)
        query = i * rows + lax.rem(lax.broadcasted_iota(jnp.int32, (1, cols), 1), rows)
        key_iota = lax.broadcasted_iota(jnp.int32, (rows, cols), 0)

        def step(j, carry):
            top, total, ot = carry
            scores = dot_nt(k_scr[j], q2) * att_mult
            key = key_iota + j * rows
            same = jnp.concatenate([doc_scr[j]] * (cols // LANES), axis=1) == doc_query
            scores = jnp.where(same & (key <= query), scores, -1e30)
            new_top = jnp.maximum(top, jnp.max(scores, axis=0, keepdims=True))
            p = jnp.exp(scores - new_top)
            keep = jnp.exp(top - new_top)
            total = total * keep + jnp.sum(p, axis=0, keepdims=True)
            ot = ot * keep + dot_nn(vt_scr[j], p.astype(bf16))
            return new_top, total, ot

        top, total, ot = lax.fori_loop(
            first_ref[i],
            i + 1,
            step,
            (
                jnp.full((1, cols), -1e30, f32),
                jnp.zeros((1, cols), f32),
                jnp.zeros((HEAD_SIZE, cols), f32),
            ),
        )
        ot = ot / total
        ot_ref[0] = ot
        lse_ref[0] = top + jnp.log(total)
        out = ot.T
        att_ref[0] = jnp.concatenate(
            [out[h * rows : (h + 1) * rows] for h in range(heads)], axis=1
        ).astype(bf16)

    def block(shape):
        return pl.BlockSpec((1,) + shape, lambda i, _: (i, 0, 0))

    def whole(shape):
        return pl.BlockSpec(shape, lambda i, _: (0,) * len(shape))

    grid_spec = pltpu.PrefetchScalarGridSpec(
        num_scalar_prefetch=1,
        grid=(blocks,),
        in_specs=[
            block((rows, width)),
            whole(w_own.shape),
            whole((1, width)),
            block((HEAD_SIZE, rows)),
            block((1, rows)),
        ],
        out_specs=[
            block((rows, width)),
            block((rows, HEADS_LANES)),
            block((rows, LANES)),
            block((rows, out_width)),
            block((HEAD_SIZE, cols)),
            block((1, cols)),
        ],
        scratch_shapes=[
            pltpu.VMEM((blocks, rows, HEAD_SIZE), bf16),
            pltpu.VMEM((blocks, HEAD_SIZE, rows), bf16),
            pltpu.VMEM((blocks, rows, LANES), f32),
        ],
    )
    return pl.pallas_call(
        kernel,
        name="attend_forward",
        grid_spec=grid_spec,
        out_shape=[
            jax.ShapeDtypeStruct((blocks, rows, width), bf16),
            jax.ShapeDtypeStruct((blocks, rows, HEADS_LANES), bf16),
            jax.ShapeDtypeStruct((blocks, rows, LANES), bf16),
            jax.ShapeDtypeStruct((blocks, rows, out_width), bf16),
            jax.ShapeDtypeStruct((blocks, HEAD_SIZE, cols), f32),
            jax.ShapeDtypeStruct((blocks, 1, cols), f32),
        ],
        cost_estimate=pl.CostEstimate(
            flops=2 * length * width * 256 + 2 * length * length * cols // rows * 128,
            bytes_accessed=2 * length * width * 4,
            transcendentals=length * length,
        ),
        compiler_params=pltpu.CompilerParams(
            dimension_semantics=("arbitrary",), vmem_limit_bytes=60 << 20
        ),
    )(
        first,
        tok_all,
        w_own,
        gain,
        table,
        docs[:, None],
    )


def attend_backward(q_all, kv_all, cot, ot, lse, table, docs, heads, normed):
    blocks, rows, _ = q_all.shape
    length = blocks * rows
    cols = heads * rows
    first = first_blocks(docs)

    def kernel(first_ref, q_ref, kv_ref, do_ref, ot_ref, lse_ref, table_ref, docs_ref, normed_in, out_ref, grad_ref, dk_scr, dv_scr, dq_scr, doc_scr, normed_all, grad_scr, sem):
        i = pl.program_id(0)

        @pl.when(i == 0)
        def _():
            pltpu.make_async_copy(normed_in, normed_all, sem).start()
            dk_scr[...] = jnp.zeros_like(dk_scr)
            dv_scr[...] = jnp.zeros_like(dv_scr)

        q2 = stack_heads(q_ref[0], heads)
        do2 = stack_heads(do_ref[0], heads)
        delta = jnp.sum(do2.astype(f32).T * ot_ref[0], axis=0, keepdims=True)
        log_total = lse_ref[0]
        doc_row = docs_ref[0].astype(f32)
        doc_scr[i] = across_lanes(doc_row, LANES)
        doc_query = jnp.concatenate([doc_row] * heads, axis=1)
        query = i * rows + lax.rem(lax.broadcasted_iota(jnp.int32, (1, cols), 1), rows)
        key_iota = lax.broadcasted_iota(jnp.int32, (rows, cols), 0)
        dq_scr[...] = jnp.zeros_like(dq_scr)

        @pl.loop(first_ref[i], i + 1)
        def _(j):
            kv = kv_ref[j]
            k, v = kv[:, :HEAD_SIZE], kv[:, HEAD_SIZE:]
            scores = dot_nt(k, q2) * att_mult
            key = key_iota + j * rows
            same = jnp.concatenate([doc_scr[j]] * (cols // LANES), axis=1) == doc_query
            p = jnp.where(same & (key <= query), jnp.exp(scores - log_total), 0.0)
            ds = (p * (dot_nt(v, do2) - delta)).astype(bf16)
            dv_scr[j] += dot_nn(p.astype(bf16), do2)
            dk_scr[j] += dot_nn(ds, q2)
            dq_scr[...] += dot_tn(ds, k)

        def rope_back(x, c, s):
            return (x * c - turn(x) * s).astype(bf16)

        dq = dq_scr[...] * att_mult
        dq = [dq[h * rows : (h + 1) * rows] for h in range(heads)]
        if heads * HEAD_SIZE < HEADS_LANES:
            dq.append(jnp.zeros((rows, HEADS_LANES - heads * HEAD_SIZE), f32))
        dq = jnp.concatenate(dq, axis=1).astype(bf16).astype(f32)
        out_ref[i, :, :HEADS_LANES] = rope_back(dq, *spread_table(table_ref[i]))

        @pl.when(i == blocks - 1)
        def _():
            pltpu.make_async_copy(normed_in, normed_all, sem).wait()
            grad_scr[...] = jnp.zeros_like(grad_scr)

            @pl.loop(0, blocks)
            def _(j):
                kv = jnp.concatenate([dk_scr[j] * att_mult, dv_scr[j]], axis=1)
                lane = lax.broadcasted_iota(jnp.int32, kv.shape, 1)
                c, s = spread_table(table_ref[j])
                kv = jnp.where(lane < HEAD_SIZE, kv * c - turn(kv) * s, kv).astype(bf16)
                out_ref[j, :, HEADS_LANES:] = kv
                grad_scr[...] += dot_tn(normed_all[j], out_ref[j])

            grad_ref[...] = grad_scr[...].astype(bf16)

    def block(shape):
        return pl.BlockSpec((1,) + shape, lambda i, _: (i, 0, 0))

    def whole(shape):
        return pl.BlockSpec(shape, lambda i, _: (0,) * len(shape))

    grid_spec = pltpu.PrefetchScalarGridSpec(
        num_scalar_prefetch=1,
        grid=(blocks,),
        in_specs=[
            block((rows, HEADS_LANES)),
            whole((blocks, rows, LANES)),
            block((rows, heads * HEAD_SIZE)),
            block((HEAD_SIZE, cols)),
            block((1, cols)),
            whole((blocks, HEAD_SIZE, rows)),
            block((1, rows)),
            pl.BlockSpec(memory_space=pl.ANY),
        ],
        out_specs=[
            whole((blocks, rows, HEADS_LANES + LANES)),
            whole((normed.shape[2], HEADS_LANES + LANES)),
        ],
        scratch_shapes=[
            pltpu.VMEM((blocks, rows, HEAD_SIZE), f32),
            pltpu.VMEM((blocks, rows, HEAD_SIZE), f32),
            pltpu.VMEM((cols, HEAD_SIZE), f32),
            pltpu.VMEM((blocks, rows, LANES), f32),
            pltpu.VMEM(normed.shape, bf16),
            pltpu.VMEM((normed.shape[2], HEADS_LANES + LANES), f32),
            pltpu.SemaphoreType.DMA,
        ],
    )
    return pl.pallas_call(
        kernel,
        name="attend_backward",
        grid_spec=grid_spec,
        out_shape=[
            jax.ShapeDtypeStruct((blocks, rows, HEADS_LANES + LANES), bf16),
            jax.ShapeDtypeStruct((normed.shape[2], HEADS_LANES + LANES), bf16),
        ],
        cost_estimate=pl.CostEstimate(
            flops=5 * length * length * cols // rows * 128,
            bytes_accessed=2 * length * 1024,
            transcendentals=length * length,
        ),
        compiler_params=pltpu.CompilerParams(
            dimension_semantics=("arbitrary",), vmem_limit_bytes=60 << 20
        ),
    )(
        first,
        q_all,
        kv_all,
        cot,
        ot,
        lse,
        table,
        docs[:, None],
        normed,
    )


def moe_exchange(collective_id, normed, cots, mask, router, w_in, w_out, parts):
    devices = lax.axis_size("seq")
    chips = devices // 2
    rows, width = normed.shape
    own_experts = w_in.shape[0]
    gate_rows = devices * own_experts

    def order(chip, k):
        left = chip < chips - 1 - chip
        longer = jnp.where(left, chips - 1 - chip, chip)
        near = jnp.where(left, chip + k, chip - k)
        return jnp.where(k <= longer, near, jnp.where(left, chips - 1 - k, k))

    def kernel(*refs):
        x_in, g_in = refs[0], refs[1 : 1 + chips]
        mask_ref, router_ref, win_in, wout_in = refs[1 + chips : 5 + chips]
        (lin_out, slot_out, hid_out, n_sum, gate_out, g_out) = refs[5 + chips : 11 + chips]
        y_outs = refs[11 + chips : 12 + chips + chips // 2]
        (
            x_all, g_all, win, wout, y_acc, n_acc, gate_acc, gate_stage,
            n_mine, n_far, n_give, n_theirs, y_give, y_theirs, y_pre, y_in,
            lin_st, slot_st, hid_st, gin, gout, hid_ld,
            local, line_send, line_recv, sib_send, sib_recv, g_local, g_send, g_recv,
            n_send, n_recv, y_send, y_recv, far_send, far_recv, gate_send, gate_recv,
            st_sem, y_sem, ld_sem, w_sem, wg_sem, hand_send, hand_recv,
        ) = refs[12 + chips + chips // 2 :]
        me = lax.axis_index("seq")
        chip, core = me // 2, lax.rem(me, 2)
        sibling = me + 1 - 2 * core
        win_copy = pltpu.make_async_copy(win_in, win, w_sem.at[0])
        wout_copy = pltpu.make_async_copy(wout_in, wout, w_sem.at[1])
        win_copy.start()
        wout_copy.start()
        barrier = pltpu.get_barrier_semaphore()
        for k in range(1, devices):
            pl.semaphore_signal(
                barrier, inc=1, device_id={"seq": lax.rem(me + k, devices)}, device_id_type=MESH
            )
        pl.semaphore_wait(barrier, devices - 1)

        def remote(src, dst, send, recv, to):
            return pltpu.make_async_remote_copy(
                src_ref=src,
                dst_ref=dst,
                send_sem=send,
                recv_sem=recv,
                device_id={"seq": to},
                device_id_type=MESH,
            )

        half = rows // PIECES

        def piece(b, core_of, i):
            return x_all.at[2 * b + core_of, pl.ds(i * half, half)]

        def line(src, b, i, slot, to):
            return remote(
                src, piece(b, core, i), line_send.at[i, slot], line_recv.at[i, b], to
            )

        def across(src, b, core_of, i):
            return remote(
                src, piece(b, core_of, i), sib_send.at[i, b], sib_recv.at[i, b], sibling
            )

        def own_piece(i):
            return x_in.at[pl.ds(i * half, half)]

        def pass_on(b, i, to):
            return line(piece(b, core, i), b, i, 2 + b, to)

        def to_sibling(b, i):
            return across(piece(b, core, i), b, core, i)

        def own_sends(act):
            for i in range(PIECES):

                @pl.when(chip > 0)
                def _(i=i):
                    act(line(own_piece(i), chip, i, 0, me - 2))

                @pl.when(chip < chips - 1)
                def _(i=i):
                    act(line(own_piece(i), chip, i, 1, me + 2))

            for i in range(PIECES):
                act(across(own_piece(i), chip, core, i))

        def cot_to_sibling(k):
            b = lax.rem(chip + chips - k, chips)
            return remote(
                g_in[k], g_all.at[2 * b + core], g_send.at[k], g_recv.at[b], sibling
            )

        def cot_local(k):
            b = lax.rem(chip + chips - k, chips)
            return pltpu.make_async_copy(g_in[k], g_all.at[2 * b + core], g_local.at[k])

        own_sends(lambda copy: copy.start())
        own = pltpu.make_async_copy(x_in, x_all.at[me], local)
        own.start()
        for k in range(chips):
            cot_to_sibling(k).start()
            cot_local(k).start()
        own.wait()
        for k in range(chips):
            cot_local(k).wait()
        win_copy.wait()
        wout_copy.wait()

        def gate_copy(block):
            return remote(
                gate_stage.at[block],
                gate_out.at[me],
                gate_send.at[block],
                gate_recv.at[me],
                block,
            )

        def n_copy(p):
            return remote(n_give, n_theirs.at[p], n_send.at[p], n_recv.at[p], sibling)

        def y_copy(p):
            return remote(y_give, y_theirs.at[p], y_send.at[p], y_recv.at[p], sibling)

        pairs = chips // 2
        pair = chip // 2
        mate = chip + 1 - 2 * lax.rem(chip, 2)

        def y_leave(b, k):
            return pltpu.make_async_copy(y_pre.at[b], y_outs[k], y_sem.at[k])

        def y_hand(b):
            far = lax.rem(b // 2 + pairs - pair, pairs) - 1
            return remote(
                y_pre.at[b], y_in.at[far], hand_send.at[far], hand_recv.at[far], 2 * mate + core
            )

        def stage_copies(e, block):
            return [
                pltpu.make_async_copy(lin_st.at[e], lin_out.at[e, block], st_sem.at[0, e]),
                pltpu.make_async_copy(slot_st.at[e], slot_out.at[e, block], st_sem.at[1, e]),
                pltpu.make_async_copy(hid_st.at[e], hid_out.at[e, block], st_sem.at[2, e]),
            ]

        def far_copy(b):
            return remote(
                n_mine.at[b], n_far.at[chip], far_send.at[b], far_recv.at[chip], 2 * b + core
            )

        def fold(k):
            b, p = order(chip, k), lax.rem(k, 2)
            n_copy(p).wait_recv()
            both = n_acc[...].astype(bf16).astype(f32) + n_theirs[p].astype(f32)

            @pl.when(b == chip)
            def _():
                n_sum[...] = both

            @pl.when(b != chip)
            def _():
                n_mine[b] = both.astype(bf16)
                far_copy(b).start()

            y_copy(p).wait_recv()
            y_pre[b] = (y_acc[...] + y_theirs[p].astype(f32)).astype(bf16)

            @pl.when(b == chip)
            def _():
                y_leave(b, 0).start()

            @pl.when(b == mate)
            def _():
                y_leave(b, 1).start()

            @pl.when((b != mate) & (lax.rem(b + chip, 2) == 1))
            def _():
                y_hand(b).start()

        def compute(block, before):
            x = x_all[block]
            there = mask_ref[block] > 0
            logits = jnp.where(there, dot_nn(x, router_ref[...]), -1e30)
            gates = jnp.where(
                there, jnp.exp(logits - jnp.max(logits, axis=1, keepdims=True)), 0.0
            )
            gates = gates / jnp.sum(gates, axis=1, keepdims=True)
            lane = lax.broadcasted_iota(jnp.int32, gates.shape, 1)
            y_acc[...] = jnp.zeros_like(y_acc)
            n_acc[...] = jnp.zeros_like(n_acc)
            gate_acc[...] = jnp.zeros_like(gate_acc)

            @pl.loop(0, own_experts)
            def _(e):
                gate = jnp.sum(
                    jnp.where(lane == me * own_experts + e, gates, 0.0), axis=1, keepdims=True
                )
                lin = dot_nn(x_all[block], win[e])
                gate_lin, up_lin = lin[:, :FFE], lin[:, FFE:]
                sig = 0.5 + 0.5 * jnp.tanh(0.5 * gate_lin)
                silu = gate_lin * sig
                hidden = (silu * up_lin).astype(bf16)

                @pl.when(before)
                def _():
                    for copy in stage_copies(e, block):
                        copy.wait()

                hid_st[e] = hidden
                res = dot_nt(hidden, wout[e]).astype(bf16).astype(f32)
                y_acc[...] += gate * res
                cot = g_all[block].astype(f32) * res_mult
                gate_acc[...] += jnp.where(
                    lane == me * own_experts + e, jnp.sum(cot * res, axis=1, keepdims=True), 0.0
                )
                slot = (gate * cot).astype(bf16)
                slot_st[e] = slot
                hidden_cot = dot_nn(slot, wout[e])
                lin_cot = jnp.concatenate(
                    [
                        hidden_cot * up_lin * (sig * (1.0 + gate_lin * (1.0 - sig))),
                        hidden_cot * silu,
                    ],
                    axis=1,
                ).astype(bf16)
                lin_st[e] = lin_cot
                for copy in stage_copies(e, block):
                    copy.start()
                n_acc[...] += dot_nt(lin_cot, win[e]).astype(bf16).astype(f32)

            gate_stage[block] = gate_acc[...].T[:gate_rows]

            @pl.when(block != me)
            def _():
                gate_copy(block).start()

            @pl.when(block == me)
            def _():
                gate_out[block] = gate_stage[block]

        @pl.loop(0, chips)
        def _(k):
            b = order(chip, k)

            for side in (-1, 1):
                away = chip + side * k

                for i in range(PIECES):

                    @pl.when((k > 0) & (away >= 0) & (away < chips))
                    def _(side=side, away=away, i=i):
                        pass_on(away, i, me).wait_recv()
                        to_sibling(away, i).start()

                        @pl.when((chip - side >= 0) & (chip - side < chips))
                        def _():
                            pass_on(away, i, me - 2 * side).start()

            for i in range(PIECES):
                across(own_piece(i), b, 1 - core, i).wait_recv()
            remote(
                x_in, g_all.at[2 * b + 1 - core], g_send.at[0], g_recv.at[b], sibling
            ).wait_recv()

            @pl.loop(0, 2)
            def _(h):
                compute(2 * b + lax.rem(core + 1 + h, 2), (k > 0) | (h > 0))

                @pl.when(h == 0)
                def _():
                    p = lax.rem(k, 2)

                    @pl.when(k > 0)
                    def _():
                        n_copy(1 - p).wait_send()
                        y_copy(1 - p).wait_send()

                    n_give[...] = n_acc[...].astype(bf16)
                    y_give[...] = y_acc[...].astype(bf16)
                    n_copy(p).start()
                    y_copy(p).start()

                @pl.when(h == 1)
                def _():
                    fold(k)

        for e in range(own_experts):
            for copy in stage_copies(e, 0):
                copy.wait()

        def loads(t, p):
            e, b = lax.rem(t, own_experts), t // own_experts
            pair = pl.ds(2 * b, 2)
            return [
                pltpu.make_async_copy(
                    lin_out.at[e, pair], g_all.at[pl.ds(4 * p, 2)], ld_sem.at[0, p]
                ),
                pltpu.make_async_copy(
                    slot_out.at[e, pair], g_all.at[pl.ds(4 * p + 2, 2)], ld_sem.at[1, p]
                ),
                pltpu.make_async_copy(hid_out.at[e, pair], hid_ld.at[p], ld_sem.at[2, p]),
            ]

        for copy in loads(jnp.int32(0), 0):
            copy.start()
        gin[...] = jnp.zeros_like(gin)
        gout[...] = jnp.zeros_like(gout)

        @pl.loop(0, chips * own_experts)
        def _(t):
            p = lax.rem(t, 2)
            for copy in loads(t, p):
                copy.wait()

            @pl.when(t + 1 < chips * own_experts)
            def _():
                for copy in loads(t + 1, 1 - p):
                    copy.start()

            e, b = lax.rem(t, own_experts), t // own_experts
            x = x_all[pl.ds(2 * b, 2)].reshape(2 * rows, width)
            lin_cot = g_all[pl.ds(4 * p, 2)].reshape(2 * rows, width)
            gin[e] += dot_tn(x, lin_cot)
            slot = g_all[pl.ds(4 * p + 2, 2)].reshape(2 * rows, width)
            gout[e] += dot_tn(slot, hid_ld[p].reshape(2 * rows, FFE))

        @pl.loop(1, chips)
        def _(k):
            for side in (-1, 1):
                away = chip + side * k

                for i in range(PIECES):

                    @pl.when((away >= 0) & (away < chips))
                    def _(side=side, away=away, i=i):
                        to_sibling(away, i).wait_send()

                        @pl.when((chip - side >= 0) & (chip - side < chips))
                        def _():
                            pass_on(away, i, me - 2 * side).wait_send()

        own_sends(lambda copy: copy.wait_send())

        def keep_of(j):
            return 2 * lax.rem(pair + 1 + j, pairs) + lax.rem(chip, 2)

        for j in range(pairs - 1):
            b = keep_of(j)
            y_hand(b).wait_recv()
            y_pre[b] = (y_pre[b].astype(f32) + y_in[j].astype(f32)).astype(bf16)
            y_leave(b, 2 + j).start()

        part_rows = width // parts
        leaving = []
        for e in range(own_experts):
            for j in range(width // rows):
                i = e * (width // rows) + j
                x_all[i] = gin[e, j * rows : (j + 1) * rows].astype(bf16)
                g_all[i, :, :FFE] = gout[e, j * rows : (j + 1) * rows].astype(bf16)
                for q in range(rows // part_rows):
                    here = pl.ds(q * part_rows, part_rows)
                    part = (j * rows + q * part_rows) // part_rows
                    at = 2 * len(leaving)
                    leaving.append(
                        (
                            pltpu.make_async_copy(
                                x_all.at[i, here],
                                g_out.at[part, e, :, pl.ds(0, 2 * FFE)],
                                wg_sem.at[at],
                            ),
                            pltpu.make_async_copy(
                                g_all.at[i, here, pl.ds(0, FFE)],
                                g_out.at[part, e, :, pl.ds(2 * FFE, FFE)],
                                wg_sem.at[at + 1],
                            ),
                        )
                    )
                    for copy in leaving[-1]:
                        copy.start()

        @pl.loop(1, chips)
        def _(k):
            b = order(chip, k)
            remote(
                n_mine.at[b], n_far.at[b], far_send.at[b], far_recv.at[b], 2 * b + core
            ).wait_recv()
            n_sum[...] += n_far[b].astype(f32)
            far_copy(b).wait_send()

        @pl.loop(1, devices)
        def _(k):
            block = lax.rem(me + k, devices)
            remote(
                gate_stage.at[block],
                gate_out.at[block],
                gate_send.at[block],
                gate_recv.at[block],
                block,
            ).wait_recv()
            gate_copy(block).wait_send()

        n_copy((chips - 1) % 2).wait_send()
        y_copy((chips - 1) % 2).wait_send()
        for both in leaving:
            for copy in both:
                copy.wait()
        y_leave(chip, 0).wait()
        y_leave(mate, 1).wait()
        for j in range(pairs - 1):
            y_leave(keep_of(j), 2 + j).wait()
            y_hand(keep_of(j) + mate - chip).wait_send()

        for k in range(chips):
            cot_to_sibling(k).wait_send()

    hbm = pl.BlockSpec(memory_space=pl.ANY)
    vmem = pl.BlockSpec(memory_space=pltpu.VMEM)
    block = (rows, width)
    dma = pltpu.SemaphoreType.DMA
    flops = 9 * own_experts * 2 * devices * rows * width * FFE // 1
    return pl.pallas_call(
        kernel,
        name="moe_exchange",
        out_shape=[
            jax.ShapeDtypeStruct((own_experts, devices, rows, 2 * FFE), bf16),
            jax.ShapeDtypeStruct((own_experts, devices) + block, bf16),
            jax.ShapeDtypeStruct((own_experts, devices, rows, FFE), bf16),
            jax.ShapeDtypeStruct(block, f32),
            jax.ShapeDtypeStruct((devices, gate_rows, rows), f32),
            jax.ShapeDtypeStruct((parts, own_experts, width // parts, 3 * FFE), bf16),
        ]
        + [jax.ShapeDtypeStruct(block, bf16)] * (1 + chips // 2),
        in_specs=[hbm] * (1 + chips) + [vmem] * 2 + [hbm] * 2,
        out_specs=[hbm] * 3 + [vmem] * 2 + [hbm] * (2 + chips // 2),
        scratch_shapes=[
            pltpu.VMEM((devices,) + block, bf16),
            pltpu.VMEM((devices,) + block, bf16),
            pltpu.VMEM(w_in.shape, bf16),
            pltpu.VMEM(w_out.shape, bf16),
            pltpu.VMEM(block, f32),
            pltpu.VMEM(block, f32),
            pltpu.VMEM((rows, LANES), f32),
            pltpu.VMEM((devices, gate_rows, rows), f32),
            pltpu.VMEM((chips,) + block, bf16),
            pltpu.VMEM((chips,) + block, bf16),
            pltpu.VMEM(block, bf16),
            pltpu.VMEM((2,) + block, bf16),
            pltpu.VMEM(block, bf16),
            pltpu.VMEM((2,) + block, bf16),
            pltpu.VMEM((chips,) + block, bf16),
            pltpu.VMEM((chips // 2 - 1,) + block, bf16),
            pltpu.VMEM((own_experts, rows, 2 * FFE), bf16),
            pltpu.VMEM((own_experts,) + block, bf16),
            pltpu.VMEM((own_experts, rows, FFE), bf16),
            pltpu.VMEM((own_experts, width, 2 * FFE), f32),
            pltpu.VMEM((own_experts, width, FFE), f32),
            pltpu.VMEM((2, 2, rows, FFE), bf16),
        ]
        + [dma]
        + [
            dma(count)
            for count in (
                (PIECES, chips + 2), (PIECES, chips), (PIECES, chips), (PIECES, chips),
                (chips,), (chips,), (chips,), (2,), (2,), (2,), (2,),
                (chips,), (chips,), (devices,), (devices,),
            )
        ]
        + [
            dma((3, own_experts)),
            dma((1 + chips // 2,)),
            dma((3, 2)),
            dma((2,)),
            dma((2 * own_experts * max(parts, width // rows),)),
            dma((chips // 2 - 1,)),
            dma((chips // 2 - 1,)),
        ],
        cost_estimate=pl.CostEstimate(
            flops=flops, bytes_accessed=40 << 20, transcendentals=devices * rows * FFE * 2
        ),
        compiler_params=pltpu.CompilerParams(
            collective_id=collective_id, has_side_effects=True, vmem_limit_bytes=63 << 20
        ),
    )(normed, *cots, mask, router, w_in, w_out)


class Links:
    def __init__(self, axes):
        self.size = {axis: lax.axis_size(axis) for axis in axes}
        self.me = {axis: lax.axis_index(axis) for axis in axes}

    def barrier(self):
        sem = pltpu.get_barrier_semaphore()
        for axis, size in self.size.items():
            for k in range(1, size):
                pl.semaphore_signal(
                    sem,
                    inc=1,
                    device_id={axis: lax.rem(self.me[axis] + k, size)},
                    device_id_type=MESH,
                )
        pl.semaphore_wait(sem, sum(size - 1 for size in self.size.values()))

    def copy(self, axis, src, dst, send, recv, to):
        return pltpu.make_async_remote_copy(
            src_ref=src,
            dst_ref=dst,
            send_sem=send,
            recv_sem=recv,
            device_id={axis: to},
            device_id_type=MESH,
        )

    def swap_start(self, axis, src, dst, send, recv, local):
        me, size = self.me[axis], self.size[axis]
        pltpu.make_async_copy(src.at[me], dst.at[me], local).start()
        for k in range(1, size):
            to = lax.rem(me + k, size)
            self.copy(axis, src.at[to], dst.at[me], send.at[k - 1], recv.at[k - 1], to).start()

    def swap_wait(self, axis, src, dst, send, recv, local):
        me, size = self.me[axis], self.size[axis]
        pltpu.make_async_copy(src.at[me], dst.at[me], local).wait()
        for k in range(1, size):
            frm = lax.rem(me + size - k, size)
            self.copy(axis, src.at[frm], dst.at[frm], send.at[k - 1], recv.at[k - 1], frm).wait()


def loads(pairs, sems):
    copies = [
        pltpu.make_async_copy(src, dst, sems.at[i]) for i, (src, dst) in enumerate(pairs)
    ]
    for copy in copies:
        copy.start()
    return copies


def staged(arrays):
    return [pltpu.VMEM(x.shape, x.dtype) for x in arrays]


def swap_sems(size):
    dma = pltpu.SemaphoreType.DMA
    return [dma((size - 1,)), dma((size - 1,)), dma]


def attended_exchange(collective_id, attended_own, tokens, w_out, gain):
    devices, rows, cols = attended_own.shape
    width = tokens.shape[1]

    ins = [tokens, w_out, gain]
    outs = [
        jax.ShapeDtypeStruct((rows, width), bf16),
        jax.ShapeDtypeStruct((rows, width), f32),
        jax.ShapeDtypeStruct((rows, width), bf16),
    ]

    def kernel(att_in, *refs):
        given, results = refs[:3], refs[3:6]
        tok, w_all, gain_ref = refs[6:9]
        att_ref, mid_ref, norm_ref, got, in_sem, out_sem, *sems = refs[9:]
        links = Links(("seq",))
        arriving = loads(list(zip(given, (tok, w_all, gain_ref))), in_sem)
        links.barrier()
        links.swap_start("seq", att_in, got, *sems)
        for copy in arriving:
            copy.wait()
        links.swap_wait("seq", att_in, got, *sems)
        attended = jnp.concatenate([got[j] for j in range(devices)], axis=1)
        att_ref[...] = attended
        mid = tok[...].astype(f32) + res_mult * dot_nn(attended, w_all[...])
        mid_ref[...] = mid
        scale = lax.rsqrt(jnp.mean(mid * mid, axis=-1, keepdims=True) + norm_eps)
        norm_ref[...] = (mid * scale * gain_ref[...].astype(f32)).astype(bf16)
        for copy in loads(list(zip((att_ref, mid_ref, norm_ref), results)), out_sem):
            copy.wait()

    hbm = pl.BlockSpec(memory_space=pl.ANY)
    dma = pltpu.SemaphoreType.DMA
    return pl.pallas_call(
        kernel,
        name="attended_exchange",
        out_shape=outs,
        in_specs=[hbm] * 4,
        out_specs=[hbm] * 3,
        scratch_shapes=staged(ins)
        + staged(outs)
        + [pltpu.VMEM(attended_own.shape, bf16), dma((3,)), dma((3,))]
        + swap_sems(devices),
        compiler_params=pltpu.CompilerParams(
            collective_id=collective_id, has_side_effects=True, vmem_limit_bytes=60 << 20
        ),
    )(attended_own, *ins)


def middle_exchange(
    collective_id, moe_sum, gate_cot, normed, router, mask, mid, out_grad, gain, w_out, attended, cols
):
    devices, gate_rows, rows = gate_cot.shape
    width = normed.shape[1]
    experts = gate_rows

    ins = [moe_sum, gate_cot, normed, router, mask, mid, out_grad, gain, w_out, attended]
    outs = [
        jax.ShapeDtypeStruct((width, LANES), bf16),
        jax.ShapeDtypeStruct((rows, width), f32),
        jax.ShapeDtypeStruct((width, width), bf16),
    ]

    def kernel(*refs):
        given, heads_out, results, refs = refs[:10], refs[10], refs[11:14], refs[14:]
        (
            moe_ref, gate_ref, norm_ref, router_ref, mask_ref, mid_ref, cot_ref, gain_ref, w_all, att_ref,
            pack_out, mid_cot_out, wo_out, give, in_sem, out_sem, *sems,
        ) = refs
        links = Links(("seq",))
        arriving = loads(list(zip(given, refs[:10])), in_sem)
        links.barrier()
        for copy in arriving:
            copy.wait()
        there = mask_ref[...] > 0
        logits = jnp.where(there, dot_nn(norm_ref[...], router_ref[...]), -1e30)
        gates = jnp.where(
            there, jnp.exp(logits - jnp.max(logits, axis=1, keepdims=True)), 0.0
        )
        gates = gates / jnp.sum(gates, axis=1, keepdims=True)
        gate = gate_ref[0]
        for j in range(1, devices):
            gate = gate + gate_ref[j]
        gate = jnp.concatenate([gate, jnp.zeros((LANES - gate_rows, rows), f32)], axis=0).T
        pick_cot = gates * (gate - jnp.sum(gates * gate, axis=1, keepdims=True))
        logit_cot = pick_cot.astype(bf16)
        cot = moe_ref[...] + dot_nt(logit_cot, router_ref[...])
        mid = mid_ref[...]
        scale = lax.rsqrt(jnp.mean(mid * mid, axis=-1, keepdims=True) + norm_eps)
        gain_grad = jnp.sum(cot * mid * scale, axis=0, keepdims=True)
        weighted = cot * gain_ref[...].astype(f32)
        mid_cot = (
            cot_ref[...].astype(f32)
            + scale * weighted
            - mid * (scale * scale * scale) * jnp.mean(weighted * mid, axis=-1, keepdims=True)
        )
        mid_cot_out[...] = mid_cot
        branch_cot = (res_mult * mid_cot).astype(bf16)
        attended_cot = dot_nt(branch_cot, w_all[...]).astype(bf16)
        for j in range(devices):
            give[j] = attended_cot[:, j * cols : (j + 1) * cols]
        links.swap_start("seq", give, heads_out, *sems)
        wo_out[...] = dot_tn(att_ref[...], branch_cot).astype(bf16)
        pack = dot_tn(norm_ref[...], logit_cot)
        lane = lax.broadcasted_iota(jnp.int32, pack.shape, 1)
        pack_out[...] = jnp.where(
            lane == experts, jnp.broadcast_to(gain_grad, (LANES, width)).T, pack
        ).astype(bf16)
        for copy in loads(list(zip((pack_out, mid_cot_out, wo_out), results)), out_sem):
            copy.wait()
        links.swap_wait("seq", give, heads_out, *sems)

    hbm = pl.BlockSpec(memory_space=pl.ANY)
    dma = pltpu.SemaphoreType.DMA
    return pl.pallas_call(
        kernel,
        name="middle_exchange",
        out_shape=[jax.ShapeDtypeStruct((devices, rows, cols), bf16)] + outs,
        in_specs=[hbm] * 10,
        out_specs=[hbm] * 4,
        scratch_shapes=staged(ins)
        + staged(outs)
        + [pltpu.VMEM((devices, rows, cols), bf16), dma((10,)), dma((3,))]
        + swap_sems(devices),
        compiler_params=pltpu.CompilerParams(
            collective_id=collective_id, has_side_effects=True, vmem_limit_bytes=60 << 20
        ),
    )(*ins)


def finish(e_grads, grad_qkv, grad_wo, pack, input_grad, output, weights, gain, heads, experts):
    parts, own_experts, e_rows, e_cols = e_grads.shape
    devices, out_rows, _ = grad_qkv.shape
    q_width = heads * HEAD_SIZE
    share = devices // KEY_VALUE_HEADS if devices > KEY_VALUE_HEADS else 1
    steps = 8
    chunk = e_rows // steps
    me = lax.axis_index("seq").astype(jnp.int32).reshape(1)

    def kernel(
        me_ref, e_ref, qkv_ref, wo_ref, pack_ref, in_ref, out_ref, wq, wk, wv, gain_ref,
        e_in, e_out, gq, gk, gv, gwo, grouter, ggain_m, ggain_a, in_grad, output_ref,
    ):
        total = e_ref[0].astype(f32)
        for p in range(1, parts):
            total = total + e_ref[p].astype(f32)
        e_in[...] = total[:, :, : 2 * FFE]
        e_out[...] = total[:, :, 2 * FFE :]

        @pl.when(pl.program_id(0) == 0)
        def _():
            blocks = [qkv_ref[j].astype(f32) for j in range(devices)]

            def per_head(first):
                heads_of = []
                for j in range(KEY_VALUE_HEADS):
                    part = blocks[j * share][:, first : first + HEAD_SIZE]
                    for i in range(1, share):
                        part = part + blocks[j * share + i][:, first : first + HEAD_SIZE]
                    heads_of.append(part)
                return jnp.concatenate(heads_of, axis=1)

            grad_q = jnp.concatenate([b[:, :q_width] for b in blocks], axis=1)
            grad_k = per_head(HEADS_LANES)
            grad_v = per_head(HEADS_LANES + HEAD_SIZE)
            gq[...], gk[...], gv[...] = grad_q, grad_k, grad_v

            def rounded(ref):
                return ref[...].astype(bf16).astype(f32)

            def row(column):
                return jnp.broadcast_to(column, (out_rows, LANES)).T[:1]

            gain_grad = (
                jnp.sum(rounded(wq) * grad_q, axis=1, keepdims=True)
                + jnp.sum(rounded(wk) * grad_k, axis=1, keepdims=True)
                + jnp.sum(rounded(wv) * grad_v, axis=1, keepdims=True)
            )
            own = lax.broadcasted_iota(jnp.int32, (devices, 1), 0) == me_ref[0]
            own_gain = jnp.sum(jnp.where(own, rounded(gain_ref), 0.0), axis=0, keepdims=True)
            ggain_a[...] = row(gain_grad) / own_gain
            gwo[...] = wo_ref[...]
            grouter[...] = pack_ref[:, :experts]
            ggain_m[...] = row(pack_ref[:, experts : experts + 1])
            in_grad[...] = in_ref[...]
            output_ref[...] = out_ref[...]

    def whole(x):
        return pl.BlockSpec(x.shape, lambda i, _: (0,) * len(x.shape))

    def own_rows(x):
        return pl.BlockSpec((out_rows, x.shape[1]), lambda i, me_ref: (me_ref[0], 0))

    def shape(*dims, dtype=f32):
        return jax.ShapeDtypeStruct(dims, dtype)

    rest = [grad_qkv, grad_wo, pack, input_grad, output]
    kv_width = KEY_VALUE_HEADS * HEAD_SIZE
    small = [
        shape(out_rows, devices * q_width),
        shape(out_rows, kv_width),
        shape(out_rows, kv_width),
        shape(*grad_wo.shape),
        shape(out_rows, experts),
        shape(1, out_rows),
        shape(1, out_rows),
        shape(*input_grad.shape, dtype=bf16),
        shape(*output.shape, dtype=bf16),
    ]
    return pl.pallas_call(
        kernel,
        name="finish",
        grid_spec=pltpu.PrefetchScalarGridSpec(
            num_scalar_prefetch=1,
            grid=(steps,),
            in_specs=[pl.BlockSpec((parts, own_experts, chunk, e_cols), lambda i, _: (0, 0, i, 0))]
            + [whole(x) for x in rest]
            + [own_rows(x) for x in weights]
            + [whole(gain)],
            out_specs=[
                pl.BlockSpec((own_experts, chunk, 2 * FFE), lambda i, _: (0, i, 0)),
                pl.BlockSpec((own_experts, chunk, FFE), lambda i, _: (0, i, 0)),
            ]
            + [whole(x) for x in small],
        ),
        out_shape=[
            shape(own_experts, e_rows, 2 * FFE),
            shape(own_experts, e_rows, FFE),
        ]
        + small,
        cost_estimate=pl.CostEstimate(flops=0, bytes_accessed=8 << 20, transcendentals=0),
        compiler_params=pltpu.CompilerParams(
            dimension_semantics=("arbitrary",), vmem_limit_bytes=48 << 20
        ),
    )(me, e_grads, *rest, *weights, gain)


def first_exchange(collective_id, tokens, out_grad, docs, mask, misc, w_query, w_key, w_value, w_out):
    devices, parts = lax.axis_size("seq"), lax.axis_size("dp")
    w_rows, width = w_out.shape
    heads = QUERY_HEADS // devices
    q_width = heads * HEAD_SIZE
    group = QUERY_HEADS // KEY_VALUE_HEADS
    w_cols = HEADS_LANES + LANES
    weights = [w_query, w_key, w_value, w_out]

    def prepare(refs):
        given, (wq, wk, wv, wo, w_all, wo_low, sem) = refs[:4], refs[4:]
        for copy in loads(list(zip(given, (wq, wk, wv, wo))), sem):
            copy.wait()
        wo_low[...] = wo[...].astype(bf16)
        for s in range(devices):
            kv = s * heads // group * HEAD_SIZE
            pieces = [wq[:, s * q_width : (s + 1) * q_width]]
            if q_width < HEADS_LANES:
                pieces.append(jnp.zeros((w_rows, HEADS_LANES - q_width), f32))
            pieces += [wk[:, kv : kv + HEAD_SIZE], wv[:, kv : kv + HEAD_SIZE]]
            w_all[s] = jnp.concatenate(pieces, axis=1).astype(bf16)

    return exchange(
        collective_id,
        [
            ("gather", "seq", tokens, None),
            ("gather", "seq", docs, None),
            ("gather", "seq", mask, None),
            ("shift", "seq", out_grad, None),
            ("share", "dp", misc, None),
            ("gather", "dp", jax.ShapeDtypeStruct((w_rows, w_cols), bf16), 0),
            ("share", "dp", jax.ShapeDtypeStruct((w_rows, width), bf16), 1),
        ],
        prepare=prepare,
        given=weights,
        work=staged(weights)
        + [
            pltpu.VMEM((devices, w_rows, w_cols), bf16),
            pltpu.VMEM((w_rows, width), bf16),
            pltpu.SemaphoreType.DMA((4,)),
        ],
        made=lambda refs: (refs[8].at[lax.axis_index("seq")], refs[9]),
        keep=(jax.ShapeDtypeStruct((devices, w_rows, w_cols), bf16), 8),
    )


def final_exchange(
    collective_id, qkv_cot, grad_qkv, token_grads, w_full, tokens, mid_cot, gain, mid, branches
):
    devices, parts = lax.axis_size("seq"), lax.axis_size("dp")
    chips = devices // 2
    _, rows, cols = qkv_cot.shape
    width = tokens.shape[1]
    out_rows = grad_qkv.shape[2]
    count = len(token_grads)
    wides = [x.shape[3] for x in token_grads]
    token_grads = [x.reshape(parts, chips, 2, out_rows, x.shape[3]) for x in token_grads]

    ins = [w_full, tokens, mid_cot, gain, mid, *branches]

    def kernel(*refs):
        qkv_in, gq_in = refs[:2]
        gt_in = refs[2 : 2 + count]
        given = refs[2 + count : 2 + count + len(ins)]
        refs = refs[2 + count + len(ins) :]
        in_grad_out, output_out, gq_out = refs[:3]
        gt_out = refs[3 : 3 + count]
        refs = refs[3 + count :]
        (
            qkv_tok, nac, gq_recv, gq_sum,
            q_send, q_recv, local, gq_send, gq_rsem, gqz_send, gqz_recv, gq_local,
        ) = refs[:12]
        work = [refs[12 + 11 * i : 23 + 11 * i] for i in range(count)]
        refs = refs[12 + 11 * count :]
        local_ins, (in_grad, output, in_sem, out_sem) = refs[: len(ins)], refs[len(ins) :]
        w_all, tok_ref, mid_cot_ref, gain_ref, mid_ref, *y_refs = local_ins
        me, my = lax.axis_index("seq"), lax.axis_index("dp")
        chip, core = me // 2, lax.rem(me, 2)
        sibling = me + 1 - 2 * core
        arriving = loads(list(zip(given, local_ins)), in_sem)
        barrier = pltpu.get_barrier_semaphore()
        for axis, index, size in (("seq", me, devices), ("dp", my, parts)):
            for k in range(1, size):
                pl.semaphore_signal(
                    barrier,
                    inc=1,
                    device_id={axis: lax.rem(index + k, size)},
                    device_id_type=MESH,
                )
        pl.semaphore_wait(barrier, devices + parts - 2)

        def remote(axis, src, dst, send, recv, to):
            return pltpu.make_async_remote_copy(
                src_ref=src,
                dst_ref=dst,
                send_sem=send,
                recv_sem=recv,
                device_id={axis: to},
                device_id_type=MESH,
            )

        sent = []

        def columns(j):
            return qkv_tok.at[:, pl.ds(pl.multiple_of(j * cols, cols), cols)]

        for x, w in zip(gt_in, work):
            mine, theirs, far, near, last, sems, dp_send, dp_recv, z_send, z_recv, _ = w
            copy = remote(
                "seq", x.at[:, :, 1 - core], theirs, sems.at[0], sems.at[1], sibling
            )
            copy.start()
            sent.append(copy)
            pltpu.make_async_copy(x.at[:, :, core], mine, sems.at[2]).start()
        for k in range(1, parts):
            to = lax.rem(my + k, parts)
            copy = remote(
                "dp", gq_in.at[to], gq_recv.at[my], gq_send.at[k - 1], gq_rsem.at[k - 1], to
            )
            copy.start()
            sent.append(copy)
        own_q = pltpu.make_async_copy(gq_in.at[my], gq_recv.at[my], gq_local)
        own_q.start()
        own = pltpu.make_async_copy(qkv_in.at[me], columns(me), local)
        own.start()
        for k in range(1, devices):
            to = lax.rem(me + k, devices)
            copy = remote(
                "seq", qkv_in.at[to], columns(me), q_send.at[k - 1], q_recv.at[k - 1], to
            )
            copy.start()
            sent.append(copy)

        for x, w in zip(gt_in, work):
            mine, theirs, far, near, last, sems, dp_send, dp_recv, z_send, z_recv, _ = w
            remote("seq", x.at[:, :, core], theirs, sems.at[0], sems.at[1], sibling).wait_recv()
            pltpu.make_async_copy(x.at[:, :, core], mine, sems.at[2]).wait()
            mine[...] = (mine[...].astype(f32) + theirs[...].astype(f32)).astype(bf16)
            for k in range(1, parts):
                to = lax.rem(my + k, parts)
                copy = remote(
                    "dp", mine.at[to], far.at[k - 1], dp_send.at[k - 1], dp_recv.at[k - 1], to
                )
                copy.start()
                sent.append(copy)

        for copy in arriving:
            copy.wait()
        total = y_refs[0][...].astype(f32)
        for k in range(1, len(branches)):
            total = total + y_refs[k][...].astype(f32)
        output[...] = (mid_ref[...] + res_mult * total).astype(bf16)
        leaving = [pltpu.make_async_copy(output, output_out, out_sem.at[0])]
        leaving[0].start()

        own_q.wait()
        for k in range(1, parts):
            frm = lax.rem(my + parts - k, parts)
            remote(
                "dp", gq_in.at[frm], gq_recv.at[frm], gq_send.at[k - 1], gq_rsem.at[k - 1], frm
            ).wait_recv()
        summed = gq_recv[0].astype(f32)
        for p in range(1, parts):
            summed = summed + gq_recv[p].astype(f32)
        gq_sum[...] = summed.astype(bf16)
        own_z = pltpu.make_async_copy(gq_sum.at[me], gq_out.at[me], gq_local)
        own_z.start()
        for k in range(1, devices):
            to = lax.rem(me + k, devices)
            copy = remote(
                "seq", gq_sum.at[to], gq_out.at[me], gqz_send.at[k - 1], gqz_recv.at[k - 1], to
            )
            copy.start()
            sent.append(copy)
        for w in work:
            mine, theirs, far, near, last, sems, dp_send, dp_recv, z_send, z_recv, _ = w
            summed = mine[my].astype(f32)
            for k in range(1, parts):
                remote(
                    "dp", mine.at[0], far.at[k - 1], dp_send.at[k - 1], dp_recv.at[k - 1], my
                ).wait_recv()
                summed = summed + far[k - 1].astype(f32)
            near[...] = summed.astype(bf16)
            for k in range(1, chips):
                to = lax.rem(chip + k, chips)
                copy = remote(
                    "seq",
                    near.at[to],
                    last.at[k - 1],
                    z_send.at[k - 1],
                    z_recv.at[k - 1],
                    2 * to + core,
                )
                copy.start()
                sent.append(copy)

        for k in range(devices):
            frm = lax.rem(me + devices - k, devices)
            if k == 0:
                own.wait()
            else:
                remote(
                    "seq", qkv_in.at[frm], columns(frm), q_send.at[k - 1], q_recv.at[k - 1], frm
                ).wait_recv()
            part = dot_nt(columns(frm)[...], w_all[frm])
            nac[...] = part if k == 0 else nac[...] + part

        resid = tok_ref[...].astype(f32)
        scale = lax.rsqrt(jnp.mean(resid * resid, axis=-1, keepdims=True) + norm_eps)
        weighted = nac[...] * gain_ref[...].astype(f32)
        in_grad[...] = (
            mid_cot_ref[...]
            + scale * weighted
            - resid
            * (scale * scale * scale)
            * jnp.mean(weighted * resid, axis=-1, keepdims=True)
        ).astype(bf16)

        leaving.append(pltpu.make_async_copy(in_grad, in_grad_out, out_sem.at[1]))
        leaving[1].start()
        for o, w in zip(gt_out, work):
            mine, theirs, far, near, last, sems, dp_send, dp_recv, z_send, z_recv, _ = w
            summed = near[chip].astype(f32)
            for k in range(1, chips):
                remote(
                    "seq", near.at[0], last.at[k - 1], z_send.at[k - 1], z_recv.at[k - 1], me
                ).wait_recv()
                summed = summed + last[k - 1].astype(f32)
            o[...] = summed
        own_z.wait()
        for k in range(1, devices):
            frm = lax.rem(me + devices - k, devices)
            remote(
                "seq", gq_sum.at[frm], gq_out.at[frm], gqz_send.at[k - 1], gqz_recv.at[k - 1], frm
            ).wait_recv()
        for copy in sent:
            copy.wait_send()
        for copy in leaving:
            copy.wait()

    hbm = pl.BlockSpec(memory_space=pl.ANY)
    vmem = pl.BlockSpec(memory_space=pltpu.VMEM)
    dma = pltpu.SemaphoreType.DMA
    scratch = [
        pltpu.VMEM((rows, devices * cols), bf16),
        pltpu.VMEM((rows, width), f32),
        pltpu.VMEM(grad_qkv.shape, bf16),
        pltpu.VMEM(grad_qkv.shape[1:], bf16),
        dma((devices - 1,)),
        dma((devices - 1,)),
        dma,
        dma((parts - 1,)),
        dma((parts - 1,)),
        dma((devices - 1,)),
        dma((devices - 1,)),
        dma,
    ]
    for wide in wides:
        piece = (out_rows, wide)
        scratch += [
            pltpu.VMEM((parts, chips) + piece, bf16),
            pltpu.VMEM((parts, chips) + piece, bf16),
            pltpu.VMEM((parts - 1, chips) + piece, bf16),
            pltpu.VMEM((chips,) + piece, bf16),
            pltpu.VMEM((chips - 1,) + piece, bf16),
            dma((3,)),
            dma((parts - 1,)),
            dma((parts - 1,)),
            dma((chips - 1,)),
            dma((chips - 1,)),
            dma,
        ]
    scratch += staged(ins) + [
        pltpu.VMEM((rows, width), bf16),
        pltpu.VMEM((rows, width), bf16),
        dma((len(ins),)),
        dma((2,)),
    ]
    return pl.pallas_call(
        kernel,
        name="final_exchange",
        out_shape=[
            jax.ShapeDtypeStruct((rows, width), bf16),
            jax.ShapeDtypeStruct((rows, width), bf16),
            jax.ShapeDtypeStruct(grad_qkv.shape[1:], bf16),
        ]
        + [jax.ShapeDtypeStruct((out_rows, wide), f32) for wide in wides],
        in_specs=[hbm] * (2 + count + len(ins)),
        out_specs=[hbm] * 3 + [vmem] * count,
        scratch_shapes=scratch,
        compiler_params=pltpu.CompilerParams(
            collective_id=collective_id, has_side_effects=True, vmem_limit_bytes=60 << 20
        ),
    )(qkv_cot, grad_qkv, *token_grads, *ins)


def on_device(
    tokens,
    out_grad,
    doc_ids,
    expert_picks,
    w_query,
    key_weight_matrix,
    value_weight_matrix,
    w_out,
    w_router,
    gain_attn,
    gain_moe,
    expert_in,
    expert_out,
):
    devices, parts = lax.axis_size("seq"), lax.axis_size("dp")
    me = lax.axis_index("seq")
    rows, width = tokens.shape[1:]
    length = rows * devices
    experts = w_router.shape[1]
    heads = QUERY_HEADS // devices
    group = QUERY_HEADS // KEY_VALUE_HEADS
    q_width = heads * HEAD_SIZE
    w_rows = w_query.shape[0]

    w_cols = HEADS_LANES + LANES
    misc = jnp.concatenate(
        [w_router, gain_attn[:, None], gain_moe[:, None]], axis=1
    ).astype(bf16)
    misc = jnp.pad(misc, ((0, 0), (0, LANES - experts - 2)))
    mask = jnp.any(
        expert_picks[0][:, :, None] == jnp.arange(LANES, dtype=jnp.int32), axis=1
    ).astype(bf16)
    doc_rows = jnp.broadcast_to(doc_ids, (8, rows))

    expert_in_full = lax.all_gather(expert_in.astype(bf16), "dp", axis=1, tiled=True)
    expert_out_full = lax.all_gather(expert_out.astype(bf16), "dp", axis=1, tiled=True)
    chips = devices // 2

    def shift(x, k):
        return lax.ppermute(x, "seq", [(i, (i + 2 * k) % devices) for i in range(devices)])

    tok_all, doc_all, mask_all, middle_cot, misc_full, w_own_all, wo_full, w_all = first_exchange(
        0,
        tokens[0],
        out_grad[0],
        doc_rows,
        mask,
        misc,
        w_query,
        key_weight_matrix,
        value_weight_matrix,
        w_out,
    )
    w_full = lax.all_gather(w_all, "dp", axis=1, tiled=True)
    held, tok_all = lax.optimization_barrier((out_grad[0], tok_all))
    cots = [held] + [
        middle_cot if k == chips // 2 else shift(held, k) for k in range(1, chips)
    ]
    w_own_all = w_own_all.reshape(width, w_cols)
    wo_full = wo_full.reshape(width, width)
    misc_full = misc_full.reshape(width, LANES)
    gain_a = misc_full[:, experts]
    gain_m = misc_full[:, experts + 1]
    docs = doc_all[:, 0]
    table = rope_table(devices, rows)

    normed_a, q_all, kv_all, attended_own, ot, lse = attend_forward(
        tok_all, w_own_all, gain_a[None], table, docs, heads
    )
    attended, mid, normed_m = attended_exchange(
        1, attended_own, tokens[0], wo_full, gain_m[None]
    )
    (_, _, _, moe_sum, gate_cot, e_grads, *branches) = moe_exchange(
        2, normed_m, cots, mask_all, misc_full, expert_in_full, expert_out_full, parts
    )
    e_grads = lax.all_to_all(e_grads, "dp", split_axis=0, concat_axis=0)
    heads_cot, router_pack, mid_cot, grad_wo = middle_exchange(
        4, moe_sum, gate_cot, normed_m, misc_full, mask, mid, out_grad[0], gain_m[None],
        wo_full, attended, q_width,
    )
    heads_cot, branches = lax.optimization_barrier((heads_cot, branches))
    branches = [
        branches[0],
        lax.ppermute(branches[1], "seq", [(i, i ^ 2) for i in range(devices)]),
    ] + [shift(branches[1 + k], 2 * k) for k in range(1, chips // 2)]
    qkv_cot, grad_qkv = attend_backward(
        q_all, kv_all, heads_cot, ot, lse, table, docs, heads, normed_a
    )
    qkv_cot, branches = lax.optimization_barrier((qkv_cot, branches))
    out_rows = w_rows // devices
    input_grad, output, grad_qkv, grad_wo, router_pack = final_exchange(
        5,
        qkv_cot,
        grad_qkv.reshape(parts, devices, out_rows, w_cols),
        [
            grad_wo.reshape(parts, devices, out_rows, width),
            router_pack.reshape(parts, devices, out_rows, LANES),
        ],
        w_full,
        tokens[0],
        mid_cot,
        gain_a[None],
        mid,
        branches,
    )

    (
        grad_e_in, grad_e_out, grad_wq, grad_wk, grad_wv, grad_wo, grad_router, grad_gain_m,
        grad_gain_a, input_grad, output,
    ) = finish(
        e_grads,
        grad_qkv,
        grad_wo,
        router_pack,
        input_grad,
        output,
        [w_query, key_weight_matrix, value_weight_matrix],
        gain_attn.reshape(devices, out_rows),
        heads,
        experts,
    )
    input_grad, output = input_grad[None], output[None]
    grad_gain_a = grad_gain_a.reshape(out_rows)
    grad_gain_m = grad_gain_m.reshape(out_rows)
    return (
        output,
        input_grad,
        grad_wq,
        grad_wk,
        grad_wv,
        grad_wo,
        grad_router,
        grad_gain_a,
        grad_gain_m,
        grad_e_in,
        grad_e_out,
    )


def solution(mesh):
    return jax.shard_map(
        on_device,
        mesh=mesh,
        in_specs=(
            P("dp", "seq", None),
            P("dp", "seq", None),
            P("dp", "seq"),
            P("dp", "seq", None),
            P("dp", None),
            P("dp", None),
            P("dp", None),
            P("dp", None),
            P("dp", None),
            P("dp"),
            P("dp"),
            P("seq", "dp", None),
            P("seq", "dp", None),
        ),
        out_specs=(
            P("dp", "seq", None),
            P("dp", "seq", None),
            P(("dp", "seq"), None),
            P(("dp", "seq"), None),
            P(("dp", "seq"), None),
            P(("dp", "seq"), None),
            P(("dp", "seq"), None),
            P(("dp", "seq")),
            P(("dp", "seq")),
            P("seq", "dp", None),
            P("seq", "dp", None),
        ),
        check_vma=False,
    )
```

```python
import functools

import jax
import jax.numpy as jnp
import numpy as np
from jax import lax
from jax.experimental import pallas as pl
from jax.experimental.pallas import tpu as pltpu
from jax.sharding import PartitionSpec as P

MESH = pl.DeviceIdType.MESH
PIECES = 2


def _block(ref, j, cut):
    if cut is None:
        return ref.at[j]
    return ref.at[:, pl.ds(pl.multiple_of(j * cut, cut), cut)]


def exchange(collective_id, ops, prepare=None, given=(), work=(), made=None, keep=None):
    axes = tuple(dict.fromkeys(axis for _, axis, _, _ in ops))
    size = {axis: lax.axis_size(axis) for axis in axes}
    out_shapes, out_specs, scratch, places = [], [], [], []
    for kind, axis, x, cut in ops:
        count = size[axis]
        out_spec = pl.BlockSpec(memory_space=pl.ANY)
        extra = []
        lead = (PIECES,) if kind == "gather" and axis == "seq" else ()
        if kind == "shift":
            shape, dtype, copies = x.shape, x.dtype, 1
        elif kind == "share":
            shape, dtype, copies = (count,) + x.shape, x.dtype, 2 * (count - 1)
        elif kind == "gather":
            shape, dtype = (count,) + x.shape, x.dtype
            copies = count - 1 if axis == "dp" else 3 + 4 * (count // 2 - 1)
        elif kind == "swap":
            copies, dtype = count - 1, x.dtype
            if cut is None:
                shape = x.shape
            elif cut[0] == "in":
                shape = (count, x.shape[0], cut[1])
            else:
                shape = (x.shape[1], count * cut[1])
        out_shapes.append(jax.ShapeDtypeStruct(shape, dtype))
        out_specs.append(out_spec)
        places.append((len(scratch), len(extra)))
        scratch += [
            pltpu.SemaphoreType.DMA(lead + (copies,)),
            pltpu.SemaphoreType.DMA(lead + (max(copies, count),)),
            pltpu.SemaphoreType.DMA,
        ] + extra

    early = [x for _, _, x, cut in ops if not isinstance(cut, int)]
    own_scratch = len(scratch)

    def kernel(*refs):
        ins, refs = list(refs[: len(early)]), refs[len(early) :]
        extra_in, refs = refs[: len(given)], refs[len(given) :]
        outs, refs = refs[: len(ops)], refs[len(ops) :]
        if keep is not None:
            kept, refs = refs[0], refs[1:]
        work, extra_work = refs[:own_scratch], refs[own_scratch:]
        ins += [None] * (len(ops) - len(early))
        me = {axis: lax.axis_index(axis) for axis in axes}
        barrier = pltpu.get_barrier_semaphore()
        for axis in axes:
            for k in range(1, size[axis]):
                pl.semaphore_signal(
                    barrier,
                    inc=1,
                    device_id={axis: lax.rem(me[axis] + k, size[axis])},
                    device_id_type=MESH,
                )
        pl.semaphore_wait(barrier, sum(size[axis] - 1 for axis in axes))

        def remote(axis, src, dst, send, recv, to):
            return pltpu.make_async_remote_copy(
                src_ref=src,
                dst_ref=dst,
                send_sem=send,
                recv_sem=recv,
                device_id={axis: to},
                device_id_type=MESH,
            )

        second, third = [], []
        for (kind, axis, _, cut), x, o, (at, extra) in zip(ops, ins, outs, places):
            if isinstance(cut, int):
                if x is None and cut == 0:
                    all_refs = list(extra_in) + list(extra_work[:-1])
                    prepare(all_refs)
                    late = made(all_refs)
                    leave = pltpu.make_async_copy(all_refs[keep[1]], kept, extra_work[-1])
                    leave.start()
                    third.append(leave.wait)
                x, cut = late[cut], None
            send, recv, local = work[at : at + 3]
            count, my = size[axis], me[axis]
            if kind == "swap":
                into = cut[1] if cut is not None and cut[0] == "out" else None
                outof = cut[1] if cut is not None and cut[0] == "in" else None
                own = pltpu.make_async_copy(_block(x, my, outof), _block(o, my, into), local)
                own.start()
                third.append(own.wait)
                for k in range(1, count):
                    to = lax.rem(my + k, count)
                    copy = remote(
                        axis,
                        _block(x, to, outof),
                        _block(o, my, into),
                        send.at[k - 1],
                        recv.at[k - 1],
                        to,
                    )
                    copy.start()
                    frm = lax.rem(my + count - k, count)
                    arrive = remote(
                        axis,
                        _block(x, to, outof),
                        _block(o, frm, into),
                        send.at[k - 1],
                        recv.at[k - 1],
                        to,
                    )
                    third.append(copy.wait_send)
                    third.append(arrive.wait_recv)
            elif kind == "gather" and axis == "dp":
                own = pltpu.make_async_copy(x, o.at[my], local)
                own.start()
                third.append(own.wait)
                for k in range(1, count):
                    to = lax.rem(my + k, count)
                    frm = lax.rem(my + count - k, count)
                    copy = remote(axis, x, o.at[my], send.at[k - 1], recv.at[k - 1], to)
                    copy.start()
                    third.append(copy.wait_send)
                    third.append(
                        remote(
                            axis, x, o.at[frm], send.at[k - 1], recv.at[k - 1], to
                        ).wait_recv
                    )
            elif kind == "shift":
                copy = remote(
                    axis, x, o, send.at[0], recv.at[0], lax.rem(my + 2 * (count // 4), count)
                )
                second.append((count // 4 + 0.9, copy.start))
                third.append(copy.wait)
            elif kind == "share":
                seq, half = me["seq"], x.shape[0] // 2
                core = lax.rem(seq, 2)
                sibling = seq + 1 - 2 * core
                own = pltpu.make_async_copy(x, o.at[my], local)
                own.start()
                third.append(own.wait)

                def side_of(ref, which, half=half):
                    return ref.at[pl.ds(which * half, half)]

                def relay(k, axis=axis, x=x, o=o, send=send, recv=recv, count=count, my=my, core=core, sibling=sibling, side_of=side_of):
                    to = lax.rem(my + k, count)
                    frm = lax.rem(my + count - k, count)
                    remote(
                        axis,
                        side_of(x, core),
                        side_of(o.at[frm], core),
                        send.at[k - 1],
                        recv.at[k - 1],
                        to,
                    ).wait_recv()
                    slot = count - 2 + k
                    spot = side_of(o.at[frm], core)
                    over = remote("seq", spot, spot, send.at[slot], recv.at[slot], sibling)
                    over.start()
                    third.append(over.wait_send)
                    third.append(
                        remote(
                            "seq",
                            spot,
                            side_of(o.at[frm], 1 - core),
                            send.at[slot],
                            recv.at[slot],
                            sibling,
                        ).wait_recv
                    )

                for k in range(1, count):
                    to = lax.rem(my + k, count)
                    copy = remote(
                        axis,
                        side_of(x, core),
                        side_of(o.at[my], core),
                        send.at[k - 1],
                        recv.at[k - 1],
                        to,
                    )
                    copy.start()
                    third.append(copy.wait_send)
                    second.append((k + 0.75, functools.partial(relay, k)))
            elif kind == "gather":
                chips = count // 2
                chip, core = my // 2, lax.rem(my, 2)
                sibling = my + 1 - 2 * core
                own = pltpu.make_async_copy(x, o.at[my], local)
                own.start()
                third.append(own.wait)

                cuts = PIECES if x.shape[0] % (16 * PIECES) == 0 else 1
                size_of = x.shape[0] // cuts

                def cut_of(ref, i, size_of=size_of):
                    return ref.at[pl.ds(i * size_of, size_of)]

                def line(src, b, i, slot, to, axis=axis, o=o, send=send, recv=recv, core=core, cut_of=cut_of):
                    return remote(
                        axis, src, cut_of(o.at[2 * b + core], i), send.at[i, slot], recv.at[i, b], to
                    )

                def across(src, b, i, slot, half, axis=axis, o=o, send=send, recv=recv, chips=chips, sibling=sibling, cut_of=cut_of):
                    return remote(
                        axis,
                        src,
                        cut_of(o.at[2 * b + half], i),
                        send.at[i, slot],
                        recv.at[i, chips + b],
                        sibling,
                    )

                def guarded(where, act):
                    pl.when(where)(act)

                for i in range(cuts):
                    for slot, where, to in ((0, chip > 0, my - 2), (1, chip < chips - 1, my + 2)):
                        copy = line(cut_of(x, i), chip, i, slot, to)
                        guarded(where, copy.start)
                        third.append(functools.partial(guarded, where, copy.wait_send))
                for i in range(cuts):
                    copy = across(cut_of(x, i), chip, i, 2, core)
                    copy.start()
                    third.append(copy.wait_send)
                    third.append(across(cut_of(x, i), chip, i, 2, 1 - core).wait_recv)

                def hop(k, side, i, chips=chips, chip=chip, core=core, my=my, x=x, o=o, line=line, across=across, cut_of=cut_of):
                    b = chip + side * k
                    there = (b >= 0) & (b < chips)
                    onward = there & ((chip - side >= 0) & (chip - side < chips))
                    slot = 3 + (k - 1) * 4 + (side + 1)
                    spot = cut_of(o.at[2 * b + core], i)
                    further = line(spot, b, i, slot, my - 2 * side)
                    over = across(spot, b, i, slot + 1, core)
                    arrived = line(cut_of(x, i), b, i, slot, my)
                    brought = across(cut_of(x, i), b, i, slot + 1, 1 - core)

                    @pl.when(there)
                    def _():
                        arrived.wait_recv()

                    guarded(onward, further.start)
                    guarded(there, over.start)
                    third.append(functools.partial(guarded, onward, further.wait_send))
                    third.append(functools.partial(guarded, there, over.wait_send))
                    third.append(functools.partial(guarded, there, brought.wait_recv))

                for k in range(1, chips):
                    for i in range(cuts):
                        for side in (-1, 1):
                            second.append((k + i / cuts, functools.partial(hop, k, side, i)))
        for _, run in sorted(second, key=lambda item: item[0]):
            run()
        for wait in third:
            wait()

    return pl.pallas_call(
        kernel,
        name=f"exchange{collective_id}",
        out_shape=out_shapes + ([] if keep is None else [keep[0]]),
        in_specs=[pl.BlockSpec(memory_space=pl.ANY)] * (len(early) + len(given)),
        out_specs=out_specs + ([] if keep is None else [pl.BlockSpec(memory_space=pl.ANY)]),
        scratch_shapes=scratch
        + list(work)
        + ([] if keep is None else [pltpu.SemaphoreType.DMA]),
        compiler_params=pltpu.CompilerParams(
            collective_id=collective_id, has_side_effects=True, vmem_limit_bytes=60 << 20
        ),
    )(*early, *given)

QUERY_HEADS = 16
KEY_VALUE_HEADS = 8
HEAD_SIZE = 64
FFE = 512
TOP = 8

att_mult = 0.015625
res_mult = 0.22
norm_eps = 1e-06
rope_theta = 10000.0
LANES = 128
bf16 = jnp.bfloat16
f32 = jnp.float32
HEADS_LANES = 128


def dot_nt(a, b):
    return lax.dot_general(a, b, (((1,), (1,)), ((), ())), preferred_element_type=f32)


def dot_nn(a, b):
    return lax.dot_general(a, b, (((1,), (0,)), ((), ())), preferred_element_type=f32)


def dot_tn(a, b):
    return lax.dot_general(a, b, (((0,), (0,)), ((), ())), preferred_element_type=f32)


def turn(x):
    half = HEAD_SIZE // 2
    lane = lax.broadcasted_iota(jnp.int32, x.shape, 1)
    width = x.shape[1]
    return jnp.where(
        lax.rem(lane, HEAD_SIZE) < half, pltpu.roll(x, width - half, 1), pltpu.roll(x, half, 1)
    )


def rope_table(blocks, rows):
    half = HEAD_SIZE // 2
    frequency = np.float32(rope_theta) ** (
        -np.arange(half, dtype=np.float32) * np.float32(2.0) / np.float32(HEAD_SIZE)
    )
    angles = (frequency[:, None] * np.arange(blocks * rows, dtype=np.float32)[None, :]).astype(
        np.float32
    )
    table = np.concatenate([np.cos(angles), np.sin(angles)], axis=0).astype(np.float32)
    return jnp.asarray(table.reshape(HEAD_SIZE, blocks, rows).transpose(1, 0, 2))


def spread_table(table):
    half = HEAD_SIZE // 2
    turned = table.T
    cos, sin = turned[:, :half], turned[:, half:]
    return (
        jnp.concatenate([cos, cos] * (LANES // HEAD_SIZE), axis=1),
        jnp.concatenate([-sin, sin] * (LANES // HEAD_SIZE), axis=1),
    )


def across_lanes(row, lanes):
    return jnp.broadcast_to(row, (lanes, row.shape[1])).T


def first_block(docs_ref, i):
    docs = docs_ref[:, 0, :].astype(f32)
    own = lax.broadcasted_iota(jnp.int32, docs.shape, 0) == i
    lane = lax.broadcasted_iota(jnp.int32, docs.shape, 1)
    start = jnp.sum(jnp.where(own & (lane == 0), docs, 0.0))
    ends = (lane == docs.shape[1] - 1) & (docs < start)
    return jnp.sum(jnp.where(ends, 1.0, 0.0)).astype(jnp.int32)


def stack_heads(x, heads):
    return jnp.concatenate(
        [x[:, h * HEAD_SIZE : (h + 1) * HEAD_SIZE] for h in range(heads)], axis=0
    )


def gain_row(ref, which):
    return jnp.concatenate(
        [ref[p, which : which + 1, :] for p in range(ref.shape[0])], axis=1
    ).astype(f32)


def attend_forward(tok_all, w_own, gain, table, docs, heads):
    blocks, rows, width = tok_all.shape
    length = blocks * rows
    cols = heads * rows
    out_width = heads * HEAD_SIZE

    def kernel(tok, w, gain_ref, table_ref, docs_ref, na_ref, q_ref, kv_ref, att_ref, ot_ref, lse_ref, k_scr, vt_scr, doc_scr):
        i = pl.program_id(0)
        x = tok[0].astype(f32)
        scale = lax.rsqrt(jnp.mean(x * x, axis=-1, keepdims=True) + norm_eps)
        na = (x * scale * gain_row(gain_ref, 0)).astype(bf16)
        na_ref[0] = na
        qkv = dot_nn(na, w[...])
        c, s = spread_table(table_ref[0])
        q, kv = qkv[:, :HEADS_LANES], qkv[:, HEADS_LANES:]
        q = (q * c + turn(q) * s).astype(bf16)
        lane = lax.broadcasted_iota(jnp.int32, kv.shape, 1)
        kv = jnp.where(lane < HEAD_SIZE, kv * c + turn(kv) * s, kv).astype(bf16)
        q_ref[0] = q
        kv_ref[0] = kv
        k_scr[i] = kv[:, :HEAD_SIZE]
        vt_scr[i] = kv.astype(f32).T[HEAD_SIZE:].astype(bf16)
        q2 = stack_heads(q, heads)
        doc_row = docs_ref[i, :1].astype(f32)
        doc_scr[i] = across_lanes(doc_row, LANES)
        doc_query = jnp.concatenate([doc_row] * heads, axis=1)
        query = i * rows + lax.rem(lax.broadcasted_iota(jnp.int32, (1, cols), 1), rows)
        key_iota = lax.broadcasted_iota(jnp.int32, (rows, cols), 0)

        def step(j, carry):
            top, total, ot = carry
            scores = dot_nt(k_scr[j], q2) * att_mult
            key = key_iota + j * rows
            same = jnp.concatenate([doc_scr[j]] * (cols // LANES), axis=1) == doc_query
            scores = jnp.where(same & (key <= query), scores, -1e30)
            new_top = jnp.maximum(top, jnp.max(scores, axis=0, keepdims=True))
            p = jnp.exp(scores - new_top)
            keep = jnp.exp(top - new_top)
            total = total * keep + jnp.sum(p, axis=0, keepdims=True)
            ot = ot * keep + dot_nn(vt_scr[j], p.astype(bf16))
            return new_top, total, ot

        top, total, ot = lax.fori_loop(
            first_block(docs_ref, i),
            i + 1,
            step,
            (
                jnp.full((1, cols), -1e30, f32),
                jnp.zeros((1, cols), f32),
                jnp.zeros((HEAD_SIZE, cols), f32),
            ),
        )
        ot = ot / total
        ot_ref[0] = ot
        lse_ref[0] = top + jnp.log(total)
        out = ot.T
        att_ref[0] = jnp.concatenate(
            [out[h * rows : (h + 1) * rows] for h in range(heads)], axis=1
        ).astype(bf16)

    def block(shape):
        return pl.BlockSpec((1,) + shape, lambda i: (i, 0, 0))

    def whole(shape):
        return pl.BlockSpec(shape, lambda i: (0,) * len(shape))

    grid_spec = pltpu.PrefetchScalarGridSpec(
        num_scalar_prefetch=0,
        grid=(blocks,),
        in_specs=[
            block((rows, width)),
            whole(w_own.shape),
            whole(gain.shape),
            block((HEAD_SIZE, rows)),
            whole(docs.shape),
        ],
        out_specs=[
            block((rows, width)),
            block((rows, HEADS_LANES)),
            block((rows, LANES)),
            block((rows, out_width)),
            block((HEAD_SIZE, cols)),
            block((1, cols)),
        ],
        scratch_shapes=[
            pltpu.VMEM((blocks, rows, HEAD_SIZE), bf16),
            pltpu.VMEM((blocks, HEAD_SIZE, rows), bf16),
            pltpu.VMEM((blocks, rows, LANES), f32),
        ],
    )
    return pl.pallas_call(
        kernel,
        name="attend_forward",
        grid_spec=grid_spec,
        out_shape=[
            jax.ShapeDtypeStruct((blocks, rows, width), bf16),
            jax.ShapeDtypeStruct((blocks, rows, HEADS_LANES), bf16),
            jax.ShapeDtypeStruct((blocks, rows, LANES), bf16),
            jax.ShapeDtypeStruct((blocks, rows, out_width), bf16),
            jax.ShapeDtypeStruct((blocks, HEAD_SIZE, cols), f32),
            jax.ShapeDtypeStruct((blocks, 1, cols), f32),
        ],
        cost_estimate=pl.CostEstimate(
            flops=2 * length * width * 256 + 2 * length * length * cols // rows * 128,
            bytes_accessed=2 * length * width * 4,
            transcendentals=length * length,
        ),
        compiler_params=pltpu.CompilerParams(
            dimension_semantics=("arbitrary",), vmem_limit_bytes=60 << 20
        ),
    )(
        tok_all,
        w_own,
        gain,
        table,
        docs,
    )


def attend_backward(q_all, kv_all, cot, ot, lse, table, docs, heads):
    blocks, rows, _ = q_all.shape
    length = blocks * rows
    cols = heads * rows

    def kernel(q_ref, kv_ref, do_ref, ot_ref, lse_ref, table_ref, docs_ref, out_ref, dk_scr, dv_scr, dq_scr, doc_scr):
        i = pl.program_id(0)

        @pl.when(i == 0)
        def _():
            dk_scr[...] = jnp.zeros_like(dk_scr)
            dv_scr[...] = jnp.zeros_like(dv_scr)

        q2 = stack_heads(q_ref[0], heads)
        do2 = stack_heads(do_ref[0], heads)
        delta = jnp.sum(do2.astype(f32).T * ot_ref[0], axis=0, keepdims=True)
        log_total = lse_ref[0]
        doc_row = docs_ref[i, :1].astype(f32)
        doc_scr[i] = across_lanes(doc_row, LANES)
        doc_query = jnp.concatenate([doc_row] * heads, axis=1)
        query = i * rows + lax.rem(lax.broadcasted_iota(jnp.int32, (1, cols), 1), rows)
        key_iota = lax.broadcasted_iota(jnp.int32, (rows, cols), 0)
        dq_scr[...] = jnp.zeros_like(dq_scr)

        @pl.loop(first_block(docs_ref, i), i + 1)
        def _(j):
            kv = kv_ref[j]
            k, v = kv[:, :HEAD_SIZE], kv[:, HEAD_SIZE:]
            scores = dot_nt(k, q2) * att_mult
            key = key_iota + j * rows
            same = jnp.concatenate([doc_scr[j]] * (cols // LANES), axis=1) == doc_query
            p = jnp.where(same & (key <= query), jnp.exp(scores - log_total), 0.0)
            ds = (p * (dot_nt(v, do2) - delta)).astype(bf16)
            dv_scr[j] += dot_nn(p.astype(bf16), do2)
            dk_scr[j] += dot_nn(ds, q2)
            dq_scr[...] += dot_tn(ds, k)

        def rope_back(x, c, s):
            return (x * c - turn(x) * s).astype(bf16)

        dq = dq_scr[...] * att_mult
        dq = [dq[h * rows : (h + 1) * rows] for h in range(heads)]
        if heads * HEAD_SIZE < HEADS_LANES:
            dq.append(jnp.zeros((rows, HEADS_LANES - heads * HEAD_SIZE), f32))
        dq = jnp.concatenate(dq, axis=1).astype(bf16).astype(f32)
        out_ref[i, :, :HEADS_LANES] = rope_back(dq, *spread_table(table_ref[i]))

        @pl.when(i == blocks - 1)
        def _():
            @pl.loop(0, blocks)
            def _(j):
                kv = jnp.concatenate([dk_scr[j] * att_mult, dv_scr[j]], axis=1)
                lane = lax.broadcasted_iota(jnp.int32, kv.shape, 1)
                c, s = spread_table(table_ref[j])
                kv = jnp.where(lane < HEAD_SIZE, kv * c - turn(kv) * s, kv).astype(bf16)
                out_ref[j, :, HEADS_LANES:] = kv

    def block(shape):
        return pl.BlockSpec((1,) + shape, lambda i: (i, 0, 0))

    def whole(shape):
        return pl.BlockSpec(shape, lambda i: (0,) * len(shape))

    grid_spec = pltpu.PrefetchScalarGridSpec(
        num_scalar_prefetch=0,
        grid=(blocks,),
        in_specs=[
            block((rows, HEADS_LANES)),
            whole((blocks, rows, LANES)),
            block((rows, heads * HEAD_SIZE)),
            block((HEAD_SIZE, cols)),
            block((1, cols)),
            whole((blocks, HEAD_SIZE, rows)),
            whole(docs.shape),
        ],
        out_specs=whole((blocks, rows, HEADS_LANES + LANES)),
        scratch_shapes=[
            pltpu.VMEM((blocks, rows, HEAD_SIZE), f32),
            pltpu.VMEM((blocks, rows, HEAD_SIZE), f32),
            pltpu.VMEM((cols, HEAD_SIZE), f32),
            pltpu.VMEM((blocks, rows, LANES), f32),
        ],
    )
    return pl.pallas_call(
        kernel,
        name="attend_backward",
        grid_spec=grid_spec,
        out_shape=jax.ShapeDtypeStruct((blocks, rows, HEADS_LANES + LANES), bf16),
        cost_estimate=pl.CostEstimate(
            flops=5 * length * length * cols // rows * 128,
            bytes_accessed=2 * length * 1024,
            transcendentals=length * length,
        ),
        compiler_params=pltpu.CompilerParams(
            dimension_semantics=("arbitrary",), vmem_limit_bytes=60 << 20
        ),
    )(
        q_all,
        kv_all,
        cot,
        ot,
        lse,
        table,
        docs,
    )


def moe_exchange(collective_id, normed, cots, mask, router, w_in, w_out):
    devices = lax.axis_size("seq")
    chips = devices // 2
    rows, width = normed.shape
    own_experts = w_in.shape[0]
    gate_rows = devices * own_experts

    def order(chip, k):
        left = chip < chips - 1 - chip
        longer = jnp.where(left, chips - 1 - chip, chip)
        near = jnp.where(left, chip + k, chip - k)
        return jnp.where(k <= longer, near, jnp.where(left, chips - 1 - k, k))

    def kernel(*refs):
        x_in, g_in = refs[0], refs[1 : 1 + chips]
        mask_ref, router_ref, win_in, wout_in = refs[1 + chips : 5 + chips]
        (lin_out, slot_out, hid_out, n_sum, gate_out, g_out) = refs[5 + chips : 11 + chips]
        y_outs = refs[11 + chips : 12 + chips + chips // 2]
        (
            x_all, g_all, win, wout, y_acc, n_acc, gate_acc, gate_stage,
            n_mine, n_far, n_give, n_theirs, y_give, y_theirs, y_pre, y_in,
            lin_st, slot_st, hid_st, gin, gout, hid_ld,
            local, line_send, line_recv, sib_send, sib_recv, g_local, g_send, g_recv,
            n_send, n_recv, y_send, y_recv, far_send, far_recv, gate_send, gate_recv,
            st_sem, y_sem, ld_sem, w_sem, wg_sem, hand_send, hand_recv,
        ) = refs[12 + chips + chips // 2 :]
        me = lax.axis_index("seq")
        chip, core = me // 2, lax.rem(me, 2)
        sibling = me + 1 - 2 * core
        win_copy = pltpu.make_async_copy(win_in, win, w_sem.at[0])
        wout_copy = pltpu.make_async_copy(wout_in, wout, w_sem.at[1])
        win_copy.start()
        wout_copy.start()
        barrier = pltpu.get_barrier_semaphore()
        for k in range(1, devices):
            pl.semaphore_signal(
                barrier, inc=1, device_id={"seq": lax.rem(me + k, devices)}, device_id_type=MESH
            )
        pl.semaphore_wait(barrier, devices - 1)

        def remote(src, dst, send, recv, to):
            return pltpu.make_async_remote_copy(
                src_ref=src,
                dst_ref=dst,
                send_sem=send,
                recv_sem=recv,
                device_id={"seq": to},
                device_id_type=MESH,
            )

        half = rows // PIECES

        def piece(b, core_of, i):
            return x_all.at[2 * b + core_of, pl.ds(i * half, half)]

        def line(src, b, i, slot, to):
            return remote(
                src, piece(b, core, i), line_send.at[i, slot], line_recv.at[i, b], to
            )

        def across(src, b, core_of, i):
            return remote(
                src, piece(b, core_of, i), sib_send.at[i, b], sib_recv.at[i, b], sibling
            )

        def own_piece(i):
            return x_in.at[pl.ds(i * half, half)]

        def pass_on(b, i, to):
            return line(piece(b, core, i), b, i, 2 + b, to)

        def to_sibling(b, i):
            return across(piece(b, core, i), b, core, i)

        def own_sends(act):
            for i in range(PIECES):

                @pl.when(chip > 0)
                def _(i=i):
                    act(line(own_piece(i), chip, i, 0, me - 2))

                @pl.when(chip < chips - 1)
                def _(i=i):
                    act(line(own_piece(i), chip, i, 1, me + 2))

            for i in range(PIECES):
                act(across(own_piece(i), chip, core, i))

        def cot_to_sibling(k):
            b = lax.rem(chip + chips - k, chips)
            return remote(
                g_in[k], g_all.at[2 * b + core], g_send.at[k], g_recv.at[b], sibling
            )

        def cot_local(k):
            b = lax.rem(chip + chips - k, chips)
            return pltpu.make_async_copy(g_in[k], g_all.at[2 * b + core], g_local.at[k])

        own_sends(lambda copy: copy.start())
        own = pltpu.make_async_copy(x_in, x_all.at[me], local)
        own.start()
        for k in range(chips):
            cot_to_sibling(k).start()
            cot_local(k).start()
        own.wait()
        for k in range(chips):
            cot_local(k).wait()
        win_copy.wait()
        wout_copy.wait()

        def gate_copy(block):
            return remote(
                gate_stage.at[block],
                gate_out.at[me],
                gate_send.at[block],
                gate_recv.at[me],
                block,
            )

        def n_copy(p):
            return remote(n_give, n_theirs.at[p], n_send.at[p], n_recv.at[p], sibling)

        def y_copy(p):
            return remote(y_give, y_theirs.at[p], y_send.at[p], y_recv.at[p], sibling)

        pairs = chips // 2
        pair = chip // 2
        mate = chip + 1 - 2 * lax.rem(chip, 2)

        def y_leave(b, k):
            return pltpu.make_async_copy(y_pre.at[b], y_outs[k], y_sem.at[k])

        def y_hand(b):
            far = lax.rem(b // 2 + pairs - pair, pairs) - 1
            return remote(
                y_pre.at[b], y_in.at[far], hand_send.at[far], hand_recv.at[far], 2 * mate + core
            )

        def stage_copies(e, block):
            return [
                pltpu.make_async_copy(lin_st.at[e], lin_out.at[e, block], st_sem.at[0, e]),
                pltpu.make_async_copy(slot_st.at[e], slot_out.at[e, block], st_sem.at[1, e]),
                pltpu.make_async_copy(hid_st.at[e], hid_out.at[e, block], st_sem.at[2, e]),
            ]

        def far_copy(b):
            return remote(
                n_mine.at[b], n_far.at[chip], far_send.at[b], far_recv.at[chip], 2 * b + core
            )

        def fold(k):
            b, p = order(chip, k), lax.rem(k, 2)
            n_copy(p).wait_recv()
            both = n_acc[...].astype(bf16).astype(f32) + n_theirs[p].astype(f32)

            @pl.when(b == chip)
            def _():
                n_sum[...] = both

            @pl.when(b != chip)
            def _():
                n_mine[b] = both.astype(bf16)
                far_copy(b).start()

            y_copy(p).wait_recv()
            y_pre[b] = (y_acc[...] + y_theirs[p].astype(f32)).astype(bf16)

            @pl.when(b == chip)
            def _():
                y_leave(b, 0).start()

            @pl.when(b == mate)
            def _():
                y_leave(b, 1).start()

            @pl.when((b != mate) & (lax.rem(b + chip, 2) == 1))
            def _():
                y_hand(b).start()

        def compute(block, before):
            x = x_all[block]
            there = mask_ref[block] > 0
            logits = jnp.where(there, dot_nn(x, router_ref[...]), -1e30)
            gates = jnp.where(
                there, jnp.exp(logits - jnp.max(logits, axis=1, keepdims=True)), 0.0
            )
            gates = gates / jnp.sum(gates, axis=1, keepdims=True)
            lane = lax.broadcasted_iota(jnp.int32, gates.shape, 1)
            y_acc[...] = jnp.zeros_like(y_acc)
            n_acc[...] = jnp.zeros_like(n_acc)
            gate_acc[...] = jnp.zeros_like(gate_acc)

            @pl.loop(0, own_experts)
            def _(e):
                gate = jnp.sum(
                    jnp.where(lane == me * own_experts + e, gates, 0.0), axis=1, keepdims=True
                )
                lin = dot_nn(x_all[block], win[e])
                gate_lin, up_lin = lin[:, :FFE], lin[:, FFE:]
                sig = 0.5 + 0.5 * jnp.tanh(0.5 * gate_lin)
                silu = gate_lin * sig
                hidden = (silu * up_lin).astype(bf16)

                @pl.when(before)
                def _():
                    for copy in stage_copies(e, block):
                        copy.wait()

                hid_st[e] = hidden
                res = dot_nt(hidden, wout[e]).astype(bf16).astype(f32)
                y_acc[...] += gate * res
                cot = g_all[block].astype(f32) * res_mult
                gate_acc[...] += jnp.where(
                    lane == me * own_experts + e, jnp.sum(cot * res, axis=1, keepdims=True), 0.0
                )
                slot = (gate * cot).astype(bf16)
                slot_st[e] = slot
                hidden_cot = dot_nn(slot, wout[e])
                lin_cot = jnp.concatenate(
                    [
                        hidden_cot * up_lin * (sig * (1.0 + gate_lin * (1.0 - sig))),
                        hidden_cot * silu,
                    ],
                    axis=1,
                ).astype(bf16)
                lin_st[e] = lin_cot
                for copy in stage_copies(e, block):
                    copy.start()
                n_acc[...] += dot_nt(lin_cot, win[e]).astype(bf16).astype(f32)

            gate_stage[block] = gate_acc[...].T[:gate_rows]

            @pl.when(block != me)
            def _():
                gate_copy(block).start()

            @pl.when(block == me)
            def _():
                gate_out[block] = gate_stage[block]

        def hop(k, i):
            for side in (-1, 1):
                away = chip + side * k

                @pl.when((k > 0) & (k < chips) & (away >= 0) & (away < chips))
                def _(side=side, away=away):
                    pass_on(away, i, me).wait_recv()

                    @pl.when((chip - side >= 0) & (chip - side < chips))
                    def _():
                        pass_on(away, i, me - 2 * side).start()

                    to_sibling(away, i).start()

        @pl.loop(0, chips)
        def _(k):
            b = order(chip, k)
            hop(k, 1)
            for i in range(PIECES):
                across(own_piece(i), b, 1 - core, i).wait_recv()
            remote(
                x_in, g_all.at[2 * b + 1 - core], g_send.at[0], g_recv.at[b], sibling
            ).wait_recv()

            @pl.loop(0, 2)
            def _(h):
                @pl.when(h == 1)
                def _():
                    hop(k + 1, 0)

                compute(2 * b + lax.rem(core + 1 + h, 2), (k > 0) | (h > 0))

                @pl.when(h == 0)
                def _():
                    p = lax.rem(k, 2)

                    @pl.when(k > 0)
                    def _():
                        n_copy(1 - p).wait_send()
                        y_copy(1 - p).wait_send()

                    n_give[...] = n_acc[...].astype(bf16)
                    y_give[...] = y_acc[...].astype(bf16)
                    n_copy(p).start()
                    y_copy(p).start()

                @pl.when(h == 1)
                def _():
                    fold(k)

        for e in range(own_experts):
            for copy in stage_copies(e, 0):
                copy.wait()

        def loads(t, p):
            e, b = lax.rem(t, own_experts), t // own_experts
            pair = pl.ds(2 * b, 2)
            return [
                pltpu.make_async_copy(
                    lin_out.at[e, pair], g_all.at[pl.ds(4 * p, 2)], ld_sem.at[0, p]
                ),
                pltpu.make_async_copy(
                    slot_out.at[e, pair], g_all.at[pl.ds(4 * p + 2, 2)], ld_sem.at[1, p]
                ),
                pltpu.make_async_copy(hid_out.at[e, pair], hid_ld.at[p], ld_sem.at[2, p]),
            ]

        for copy in loads(jnp.int32(0), 0):
            copy.start()
        gin[...] = jnp.zeros_like(gin)
        gout[...] = jnp.zeros_like(gout)

        @pl.loop(0, chips * own_experts)
        def _(t):
            p = lax.rem(t, 2)
            for copy in loads(t, p):
                copy.wait()

            @pl.when(t + 1 < chips * own_experts)
            def _():
                for copy in loads(t + 1, 1 - p):
                    copy.start()

            e, b = lax.rem(t, own_experts), t // own_experts
            x = x_all[pl.ds(2 * b, 2)].reshape(2 * rows, width)
            lin_cot = g_all[pl.ds(4 * p, 2)].reshape(2 * rows, width)
            gin[e] += dot_tn(x, lin_cot)
            slot = g_all[pl.ds(4 * p + 2, 2)].reshape(2 * rows, width)
            gout[e] += dot_tn(slot, hid_ld[p].reshape(2 * rows, FFE))

        @pl.loop(1, chips)
        def _(k):
            for side in (-1, 1):
                away = chip + side * k

                for i in range(PIECES):

                    @pl.when((away >= 0) & (away < chips))
                    def _(side=side, away=away, i=i):
                        to_sibling(away, i).wait_send()

                        @pl.when((chip - side >= 0) & (chip - side < chips))
                        def _():
                            pass_on(away, i, me - 2 * side).wait_send()

        own_sends(lambda copy: copy.wait_send())

        def keep_of(j):
            return 2 * lax.rem(pair + 1 + j, pairs) + lax.rem(chip, 2)

        for j in range(pairs - 1):
            b = keep_of(j)
            y_hand(b).wait_recv()
            y_pre[b] = (y_pre[b].astype(f32) + y_in[j].astype(f32)).astype(bf16)
            y_leave(b, 2 + j).start()

        leaving = []
        for e in range(own_experts):
            for j in range(width // rows):
                i = e * (width // rows) + j
                x_all[i] = gin[e, j * rows : (j + 1) * rows].astype(bf16)
                g_all[i, :, :FFE] = gout[e, j * rows : (j + 1) * rows].astype(bf16)
                at = 2 * len(leaving)
                here = pl.ds(j * rows, rows)
                leaving.append(
                    (
                        pltpu.make_async_copy(
                            x_all.at[i], g_out.at[e, here, pl.ds(0, 2 * FFE)], wg_sem.at[at]
                        ),
                        pltpu.make_async_copy(
                            g_all.at[i, :, pl.ds(0, FFE)],
                            g_out.at[e, here, pl.ds(2 * FFE, FFE)],
                            wg_sem.at[at + 1],
                        ),
                    )
                )
                for copy in leaving[-1]:
                    copy.start()

        @pl.loop(1, chips)
        def _(k):
            b = order(chip, k)
            remote(
                n_mine.at[b], n_far.at[b], far_send.at[b], far_recv.at[b], 2 * b + core
            ).wait_recv()
            n_sum[...] += n_far[b].astype(f32)
            far_copy(b).wait_send()

        @pl.loop(1, devices)
        def _(k):
            block = lax.rem(me + k, devices)
            remote(
                gate_stage.at[block],
                gate_out.at[block],
                gate_send.at[block],
                gate_recv.at[block],
                block,
            ).wait_recv()
            gate_copy(block).wait_send()

        n_copy((chips - 1) % 2).wait_send()
        y_copy((chips - 1) % 2).wait_send()
        for both in leaving:
            for copy in both:
                copy.wait()
        y_leave(chip, 0).wait()
        y_leave(mate, 1).wait()
        for j in range(pairs - 1):
            y_leave(keep_of(j), 2 + j).wait()
            y_hand(keep_of(j) + mate - chip).wait_send()

        for k in range(chips):
            cot_to_sibling(k).wait_send()

    hbm = pl.BlockSpec(memory_space=pl.ANY)
    vmem = pl.BlockSpec(memory_space=pltpu.VMEM)
    block = (rows, width)
    dma = pltpu.SemaphoreType.DMA
    flops = 9 * own_experts * 2 * devices * rows * width * FFE // 1
    return pl.pallas_call(
        kernel,
        name="moe_exchange",
        out_shape=[
            jax.ShapeDtypeStruct((own_experts, devices, rows, 2 * FFE), bf16),
            jax.ShapeDtypeStruct((own_experts, devices) + block, bf16),
            jax.ShapeDtypeStruct((own_experts, devices, rows, FFE), bf16),
            jax.ShapeDtypeStruct(block, f32),
            jax.ShapeDtypeStruct((devices, gate_rows, rows), f32),
            jax.ShapeDtypeStruct((own_experts, width, 3 * FFE), bf16),
        ]
        + [jax.ShapeDtypeStruct(block, bf16)] * (1 + chips // 2),
        in_specs=[hbm] * (1 + chips) + [vmem] * 2 + [hbm] * 2,
        out_specs=[hbm] * 3 + [vmem] * 2 + [hbm] * (2 + chips // 2),
        scratch_shapes=[
            pltpu.VMEM((devices,) + block, bf16),
            pltpu.VMEM((devices,) + block, bf16),
            pltpu.VMEM(w_in.shape, bf16),
            pltpu.VMEM(w_out.shape, bf16),
            pltpu.VMEM(block, f32),
            pltpu.VMEM(block, f32),
            pltpu.VMEM((rows, LANES), f32),
            pltpu.VMEM((devices, gate_rows, rows), f32),
            pltpu.VMEM((chips,) + block, bf16),
            pltpu.VMEM((chips,) + block, bf16),
            pltpu.VMEM(block, bf16),
            pltpu.VMEM((2,) + block, bf16),
            pltpu.VMEM(block, bf16),
            pltpu.VMEM((2,) + block, bf16),
            pltpu.VMEM((chips,) + block, bf16),
            pltpu.VMEM((chips // 2 - 1,) + block, bf16),
            pltpu.VMEM((own_experts, rows, 2 * FFE), bf16),
            pltpu.VMEM((own_experts,) + block, bf16),
            pltpu.VMEM((own_experts, rows, FFE), bf16),
            pltpu.VMEM((own_experts, width, 2 * FFE), f32),
            pltpu.VMEM((own_experts, width, FFE), f32),
            pltpu.VMEM((2, 2, rows, FFE), bf16),
        ]
        + [dma]
        + [
            dma(count)
            for count in (
                (PIECES, chips + 2), (PIECES, chips), (PIECES, chips), (PIECES, chips),
                (chips,), (chips,), (chips,), (2,), (2,), (2,), (2,),
                (chips,), (chips,), (devices,), (devices,),
            )
        ]
        + [
            dma((3, own_experts)),
            dma((1 + chips // 2,)),
            dma((3, 2)),
            dma((2,)),
            dma((2 * own_experts * (width // rows),)),
            dma((chips // 2 - 1,)),
            dma((chips // 2 - 1,)),
        ],
        cost_estimate=pl.CostEstimate(
            flops=flops, bytes_accessed=40 << 20, transcendentals=devices * rows * FFE * 2
        ),
        compiler_params=pltpu.CompilerParams(
            collective_id=collective_id, has_side_effects=True, vmem_limit_bytes=63 << 20
        ),
    )(normed, *cots, mask, router, w_in, w_out)


class Links:
    def __init__(self, axes):
        self.size = {axis: lax.axis_size(axis) for axis in axes}
        self.me = {axis: lax.axis_index(axis) for axis in axes}

    def barrier(self):
        sem = pltpu.get_barrier_semaphore()
        for axis, size in self.size.items():
            for k in range(1, size):
                pl.semaphore_signal(
                    sem,
                    inc=1,
                    device_id={axis: lax.rem(self.me[axis] + k, size)},
                    device_id_type=MESH,
                )
        pl.semaphore_wait(sem, sum(size - 1 for size in self.size.values()))

    def copy(self, axis, src, dst, send, recv, to):
        return pltpu.make_async_remote_copy(
            src_ref=src,
            dst_ref=dst,
            send_sem=send,
            recv_sem=recv,
            device_id={axis: to},
            device_id_type=MESH,
        )

    def swap_start(self, axis, src, dst, send, recv, local):
        me, size = self.me[axis], self.size[axis]
        pltpu.make_async_copy(src.at[me], dst.at[me], local).start()
        for k in range(1, size):
            to = lax.rem(me + k, size)
            self.copy(axis, src.at[to], dst.at[me], send.at[k - 1], recv.at[k - 1], to).start()

    def swap_wait(self, axis, src, dst, send, recv, local):
        me, size = self.me[axis], self.size[axis]
        pltpu.make_async_copy(src.at[me], dst.at[me], local).wait()
        for k in range(1, size):
            frm = lax.rem(me + size - k, size)
            self.copy(axis, src.at[frm], dst.at[frm], send.at[k - 1], recv.at[k - 1], frm).wait()


def loads(pairs, sems):
    copies = [
        pltpu.make_async_copy(src, dst, sems.at[i]) for i, (src, dst) in enumerate(pairs)
    ]
    for copy in copies:
        copy.start()
    return copies


def staged(arrays):
    return [pltpu.VMEM(x.shape, x.dtype) for x in arrays]


def swap_sems(size):
    dma = pltpu.SemaphoreType.DMA
    return [dma((size - 1,)), dma((size - 1,)), dma]


def attended_exchange(collective_id, attended_own, tokens, w_out, gain):
    devices, rows, cols = attended_own.shape
    width = tokens.shape[1]

    ins = [tokens, w_out, gain]
    outs = [
        jax.ShapeDtypeStruct((rows, width), bf16),
        jax.ShapeDtypeStruct((rows, width), f32),
        jax.ShapeDtypeStruct((rows, width), bf16),
    ]

    def kernel(att_in, *refs):
        given, results = refs[:3], refs[3:6]
        tok, w_all, gain_ref = refs[6:9]
        att_ref, mid_ref, norm_ref, got, in_sem, out_sem, *sems = refs[9:]
        links = Links(("seq",))
        arriving = loads(list(zip(given, (tok, w_all, gain_ref))), in_sem)
        links.barrier()
        links.swap_start("seq", att_in, got, *sems)
        for copy in arriving:
            copy.wait()
        links.swap_wait("seq", att_in, got, *sems)
        attended = jnp.concatenate([got[j] for j in range(devices)], axis=1)
        att_ref[...] = attended
        mid = tok[...].astype(f32) + res_mult * dot_nn(attended, w_all[...])
        mid_ref[...] = mid
        scale = lax.rsqrt(jnp.mean(mid * mid, axis=-1, keepdims=True) + norm_eps)
        norm_ref[...] = (mid * scale * gain_row(gain_ref, 1)).astype(bf16)
        for copy in loads(list(zip((att_ref, mid_ref, norm_ref), results)), out_sem):
            copy.wait()

    hbm = pl.BlockSpec(memory_space=pl.ANY)
    dma = pltpu.SemaphoreType.DMA
    return pl.pallas_call(
        kernel,
        name="attended_exchange",
        out_shape=outs,
        in_specs=[hbm] * 4,
        out_specs=[hbm] * 3,
        scratch_shapes=staged(ins)
        + staged(outs)
        + [pltpu.VMEM(attended_own.shape, bf16), dma((3,)), dma((3,))]
        + swap_sems(devices),
        compiler_params=pltpu.CompilerParams(
            collective_id=collective_id, has_side_effects=True, vmem_limit_bytes=60 << 20
        ),
    )(attended_own, *ins)


def middle_exchange(
    collective_id, moe_sum, gate_cot, normed, router, mask, mid, out_grad, gain, w_out, attended, cols
):
    devices, gate_rows, rows = gate_cot.shape
    width = normed.shape[1]
    experts = gate_rows

    ins = [moe_sum, gate_cot, normed, router, mask, mid, out_grad, gain, w_out, attended]
    outs = [
        jax.ShapeDtypeStruct((width, LANES), bf16),
        jax.ShapeDtypeStruct((rows, width), f32),
        jax.ShapeDtypeStruct((width, width), bf16),
    ]

    def kernel(*refs):
        given, heads_out, results, refs = refs[:10], refs[10], refs[11:14], refs[14:]
        (
            moe_ref, gate_ref, norm_ref, router_ref, mask_ref, mid_ref, cot_ref, gain_ref, w_all, att_ref,
            pack_out, mid_cot_out, wo_out, give, in_sem, out_sem, *sems,
        ) = refs
        links = Links(("seq",))
        arriving = loads(list(zip(given, refs[:10])), in_sem)
        links.barrier()
        for copy in arriving:
            copy.wait()
        there = mask_ref[...] > 0
        logits = jnp.where(there, dot_nn(norm_ref[...], router_ref[...]), -1e30)
        gates = jnp.where(
            there, jnp.exp(logits - jnp.max(logits, axis=1, keepdims=True)), 0.0
        )
        gates = gates / jnp.sum(gates, axis=1, keepdims=True)
        gate = gate_ref[0]
        for j in range(1, devices):
            gate = gate + gate_ref[j]
        gate = jnp.concatenate([gate, jnp.zeros((LANES - gate_rows, rows), f32)], axis=0).T
        pick_cot = gates * (gate - jnp.sum(gates * gate, axis=1, keepdims=True))
        logit_cot = pick_cot.astype(bf16)
        cot = moe_ref[...] + dot_nt(logit_cot, router_ref[...])
        mid = mid_ref[...]
        scale = lax.rsqrt(jnp.mean(mid * mid, axis=-1, keepdims=True) + norm_eps)
        gain_grad = jnp.sum(cot * mid * scale, axis=0, keepdims=True)
        weighted = cot * gain_row(gain_ref, 1)
        mid_cot = (
            cot_ref[...].astype(f32)
            + scale * weighted
            - mid * (scale * scale * scale) * jnp.mean(weighted * mid, axis=-1, keepdims=True)
        )
        mid_cot_out[...] = mid_cot
        branch_cot = (res_mult * mid_cot).astype(bf16)
        attended_cot = dot_nt(branch_cot, w_all[...]).astype(bf16)
        for j in range(devices):
            give[j] = attended_cot[:, j * cols : (j + 1) * cols]
        links.swap_start("seq", give, heads_out, *sems)
        wo_out[...] = dot_tn(att_ref[...], branch_cot).astype(bf16)
        pack = dot_tn(norm_ref[...], logit_cot)
        lane = lax.broadcasted_iota(jnp.int32, pack.shape, 1)
        pack_out[...] = jnp.where(
            lane == experts, jnp.broadcast_to(gain_grad, (LANES, width)).T, pack
        ).astype(bf16)
        for copy in loads(list(zip((pack_out, mid_cot_out, wo_out), results)), out_sem):
            copy.wait()
        links.swap_wait("seq", give, heads_out, *sems)

    hbm = pl.BlockSpec(memory_space=pl.ANY)
    dma = pltpu.SemaphoreType.DMA
    return pl.pallas_call(
        kernel,
        name="middle_exchange",
        out_shape=[jax.ShapeDtypeStruct((devices, rows, cols), bf16)] + outs,
        in_specs=[hbm] * 10,
        out_specs=[hbm] * 4,
        scratch_shapes=staged(ins)
        + staged(outs)
        + [pltpu.VMEM((devices, rows, cols), bf16), dma((10,)), dma((3,))]
        + swap_sems(devices),
        compiler_params=pltpu.CompilerParams(
            collective_id=collective_id, has_side_effects=True, vmem_limit_bytes=60 << 20
        ),
    )(*ins)


def finish(e_grads, grad_qkv, grad_wo, pack, input_grad, output, weights, gain, heads, experts):
    own_experts, e_rows, e_cols = e_grads.shape
    devices, out_rows, _ = grad_qkv.shape
    q_width = heads * HEAD_SIZE
    share = devices // KEY_VALUE_HEADS if devices > KEY_VALUE_HEADS else 1
    steps = 4
    chunk = e_rows // steps
    me = lax.axis_index("seq").astype(jnp.int32).reshape(1)

    def kernel(
        me_ref, e_ref, qkv_ref, wo_ref, pack_ref, in_ref, out_ref, wq, wk, wv, gain_ref,
        e_in, e_out, gq, gk, gv, gwo, grouter, ggain_m, ggain_a, in_grad, output_ref,
    ):
        e_in[...] = e_ref[:, :, : 2 * FFE].astype(f32)
        e_out[...] = e_ref[:, :, 2 * FFE :].astype(f32)

        @pl.when(pl.program_id(0) == 0)
        def _():
            blocks = [qkv_ref[j].astype(f32) for j in range(devices)]

            def per_head(first):
                heads_of = []
                for j in range(KEY_VALUE_HEADS):
                    part = blocks[j * share][:, first : first + HEAD_SIZE]
                    for i in range(1, share):
                        part = part + blocks[j * share + i][:, first : first + HEAD_SIZE]
                    heads_of.append(part)
                return jnp.concatenate(heads_of, axis=1)

            grad_q = jnp.concatenate([b[:, :q_width] for b in blocks], axis=1)
            grad_k = per_head(HEADS_LANES)
            grad_v = per_head(HEADS_LANES + HEAD_SIZE)
            gq[...], gk[...], gv[...] = grad_q, grad_k, grad_v

            def rounded(ref):
                return ref[...].astype(bf16).astype(f32)

            def row(column):
                return jnp.broadcast_to(column, (out_rows, LANES)).T[:1]

            gain_grad = (
                jnp.sum(rounded(wq) * grad_q, axis=1, keepdims=True)
                + jnp.sum(rounded(wk) * grad_k, axis=1, keepdims=True)
                + jnp.sum(rounded(wv) * grad_v, axis=1, keepdims=True)
            )
            own = lax.broadcasted_iota(jnp.int32, (devices, 1), 0) == me_ref[0]
            own_gain = jnp.sum(jnp.where(own, rounded(gain_ref), 0.0), axis=0, keepdims=True)
            ggain_a[...] = row(gain_grad) / own_gain
            gwo[...] = wo_ref[...]
            grouter[...] = pack_ref[:, :experts]
            ggain_m[...] = row(pack_ref[:, experts : experts + 1])
            in_grad[...] = in_ref[...]
            output_ref[...] = out_ref[...]

    def whole(x):
        return pl.BlockSpec(x.shape, lambda i, _: (0,) * len(x.shape))

    def own_rows(x):
        return pl.BlockSpec((out_rows, x.shape[1]), lambda i, me_ref: (me_ref[0], 0))

    def shape(*dims, dtype=f32):
        return jax.ShapeDtypeStruct(dims, dtype)

    rest = [grad_qkv, grad_wo, pack, input_grad, output]
    kv_width = KEY_VALUE_HEADS * HEAD_SIZE
    small = [
        shape(out_rows, devices * q_width),
        shape(out_rows, kv_width),
        shape(out_rows, kv_width),
        shape(*grad_wo.shape),
        shape(out_rows, experts),
        shape(1, out_rows),
        shape(1, out_rows),
        shape(*input_grad.shape, dtype=bf16),
        shape(*output.shape, dtype=bf16),
    ]
    return pl.pallas_call(
        kernel,
        name="finish",
        grid_spec=pltpu.PrefetchScalarGridSpec(
            num_scalar_prefetch=1,
            grid=(steps,),
            in_specs=[pl.BlockSpec((own_experts, chunk, e_cols), lambda i, _: (0, i, 0))]
            + [whole(x) for x in rest]
            + [own_rows(x) for x in weights]
            + [whole(gain)],
            out_specs=[
                pl.BlockSpec((own_experts, chunk, 2 * FFE), lambda i, _: (0, i, 0)),
                pl.BlockSpec((own_experts, chunk, FFE), lambda i, _: (0, i, 0)),
            ]
            + [whole(x) for x in small],
        ),
        out_shape=[
            shape(own_experts, e_rows, 2 * FFE),
            shape(own_experts, e_rows, FFE),
        ]
        + small,
        cost_estimate=pl.CostEstimate(flops=0, bytes_accessed=8 << 20, transcendentals=0),
        compiler_params=pltpu.CompilerParams(
            dimension_semantics=("arbitrary",), vmem_limit_bytes=60 << 20
        ),
    )(me, e_grads, *rest, *weights, gain)


def first_exchange(collective_id, tokens, out_grad, docs, mask, misc, gains, w_query, w_key, w_value, w_out):
    devices, parts = lax.axis_size("seq"), lax.axis_size("dp")
    w_rows, width = w_out.shape
    heads = QUERY_HEADS // devices
    q_width = heads * HEAD_SIZE
    group = QUERY_HEADS // KEY_VALUE_HEADS
    w_cols = HEADS_LANES + LANES
    weights = [w_query, w_key, w_value, w_out]

    def prepare(refs):
        given, (wq, wk, wv, wo, w_all, wo_low, sem) = refs[:4], refs[4:]
        for copy in loads(list(zip(given, (wq, wk, wv, wo))), sem):
            copy.wait()
        wo_low[...] = wo[...].astype(bf16)
        for s in range(devices):
            kv = s * heads // group * HEAD_SIZE
            pieces = [wq[:, s * q_width : (s + 1) * q_width]]
            if q_width < HEADS_LANES:
                pieces.append(jnp.zeros((w_rows, HEADS_LANES - q_width), f32))
            pieces += [wk[:, kv : kv + HEAD_SIZE], wv[:, kv : kv + HEAD_SIZE]]
            w_all[s] = jnp.concatenate(pieces, axis=1).astype(bf16)

    return exchange(
        collective_id,
        [
            ("gather", "seq", tokens, None),
            ("gather", "seq", docs, None),
            ("gather", "seq", mask, None),
            ("shift", "seq", out_grad, None),
            ("share", "dp", misc, None),
            ("gather", "dp", gains, None),
            ("gather", "dp", jax.ShapeDtypeStruct((w_rows, w_cols), bf16), 0),
            ("share", "dp", jax.ShapeDtypeStruct((w_rows, width), bf16), 1),
        ],
        prepare=prepare,
        given=weights,
        work=staged(weights)
        + [
            pltpu.VMEM((devices, w_rows, w_cols), bf16),
            pltpu.VMEM((w_rows, width), bf16),
            pltpu.SemaphoreType.DMA((4,)),
        ],
        made=lambda refs: (refs[8].at[lax.axis_index("seq")], refs[9]),
        keep=(jax.ShapeDtypeStruct((devices, w_rows, w_cols), bf16), 8),
    )


def prepare(expert_in, expert_out, picks, docs, w_router, gain_attn, gain_moe):
    own_experts, w_rows, _ = expert_in.shape
    rows, experts = picks.shape[0], w_router.shape[1]
    steps = 4
    chunk = w_rows // steps

    def kernel(
        e_in, e_out, picks_ref, docs_ref, router, gain_a, gain_m, in_low, out_low, mask, docs_out, misc, gains
    ):
        in_low[...] = e_in[...].astype(bf16)
        out_low[...] = e_out[...].astype(bf16)

        @pl.when(pl.program_id(0) == 0)
        def _():
            lane = lax.broadcasted_iota(jnp.int32, (rows, LANES), 1)
            chosen = picks_ref[:, :1] == lane
            for k in range(1, TOP):
                chosen = chosen | (picks_ref[:, k : k + 1] == lane)
            mask[...] = jnp.where(chosen, 1.0, 0.0).astype(bf16)
            docs_out[...] = jnp.broadcast_to(docs_ref[...], docs_out.shape)
            misc[...] = jnp.concatenate(
                [router[...], jnp.zeros((w_rows, LANES - experts), f32)], axis=1
            ).astype(bf16)
            upper = lax.broadcasted_iota(jnp.int32, (8, w_rows), 0) == 0
            gains[...] = jnp.where(upper, gain_a[...], gain_m[...]).astype(bf16)

    def whole(shape):
        return pl.BlockSpec(shape, lambda i: (0,) * len(shape))

    def part(x):
        return pl.BlockSpec((own_experts, chunk, x.shape[2]), lambda i: (0, i, 0))

    small = [picks, docs, w_router, gain_attn[None], gain_moe[None]]
    outs = [
        jax.ShapeDtypeStruct((rows, LANES), bf16),
        jax.ShapeDtypeStruct((8, rows), jnp.int32),
        jax.ShapeDtypeStruct((w_rows, LANES), bf16),
        jax.ShapeDtypeStruct((8, w_rows), bf16),
    ]
    return pl.pallas_call(
        kernel,
        name="prepare",
        grid=(steps,),
        out_shape=[jax.ShapeDtypeStruct(x.shape, bf16) for x in (expert_in, expert_out)] + outs,
        in_specs=[part(expert_in), part(expert_out)] + [whole(x.shape) for x in small],
        out_specs=[part(expert_in), part(expert_out)] + [whole(x.shape) for x in outs],
        compiler_params=pltpu.CompilerParams(
            dimension_semantics=("arbitrary",), vmem_limit_bytes=60 << 20
        ),
    )(expert_in, expert_out, *small)


def final_exchange(
    collective_id, qkv_cot, normed, token_grads, w_full, tokens, mid_cot, gain, mid, branches
):
    devices, parts = lax.axis_size("seq"), lax.axis_size("dp")
    chips = devices // 2
    _, rows, cols = qkv_cot.shape
    width = tokens.shape[1]
    out_rows = token_grads[0].shape[2]
    gq_shape = (parts, devices, out_rows, cols)
    count = len(token_grads)
    wides = [x.shape[3] for x in token_grads]
    token_grads = [x.reshape(parts, chips, 2, out_rows, x.shape[3]) for x in token_grads]

    ins = [w_full, normed, qkv_cot, tokens, mid_cot, gain, mid, *branches]

    def kernel(*refs):
        qkv_in = refs[0]
        gt_in = refs[1 : 1 + count]
        given = refs[1 + count : 1 + count + len(ins)]
        refs = refs[1 + count + len(ins) :]
        in_grad_out, output_out, gq_out = refs[:3]
        gt_out = refs[3 : 3 + count]
        refs = refs[3 + count :]
        (
            qkv_tok, nac, gq_in, grad, gq_recv, gq_sum,
            q_send, q_recv, local, gq_send, gq_rsem, gqz_send, gqz_recv, gq_local,
        ) = refs[:14]
        work = [refs[14 + 11 * i : 25 + 11 * i] for i in range(count)]
        refs = refs[14 + 11 * count :]
        local_ins, (in_grad, output, in_sem, out_sem) = refs[: len(ins)], refs[len(ins) :]
        w_all, normed_all, qkv_all, tok_ref, mid_cot_ref, gain_ref, mid_ref, *y_refs = local_ins
        me, my = lax.axis_index("seq"), lax.axis_index("dp")
        chip, core = me // 2, lax.rem(me, 2)
        sibling = me + 1 - 2 * core
        arriving = loads(list(zip(given, local_ins)), in_sem)
        barrier = pltpu.get_barrier_semaphore()
        for axis, index, size in (("seq", me, devices), ("dp", my, parts)):
            for k in range(1, size):
                pl.semaphore_signal(
                    barrier,
                    inc=1,
                    device_id={axis: lax.rem(index + k, size)},
                    device_id_type=MESH,
                )
        pl.semaphore_wait(barrier, devices + parts - 2)

        def remote(axis, src, dst, send, recv, to):
            return pltpu.make_async_remote_copy(
                src_ref=src,
                dst_ref=dst,
                send_sem=send,
                recv_sem=recv,
                device_id={axis: to},
                device_id_type=MESH,
            )

        sent = []

        def columns(j):
            return qkv_tok.at[:, pl.ds(pl.multiple_of(j * cols, cols), cols)]

        for x, w in zip(gt_in, work):
            mine, theirs, far, near, last, sems, dp_send, dp_recv, z_send, z_recv, _ = w
            copy = remote(
                "seq", x.at[:, :, 1 - core], theirs, sems.at[0], sems.at[1], sibling
            )
            copy.start()
            sent.append(copy)
            pltpu.make_async_copy(x.at[:, :, core], mine, sems.at[2]).start()
        own = pltpu.make_async_copy(qkv_in.at[me], columns(me), local)
        own.start()
        for k in range(1, devices):
            to = lax.rem(me + k, devices)
            copy = remote(
                "seq", qkv_in.at[to], columns(me), q_send.at[k - 1], q_recv.at[k - 1], to
            )
            copy.start()
            sent.append(copy)

        for x, w in zip(gt_in, work):
            mine, theirs, far, near, last, sems, dp_send, dp_recv, z_send, z_recv, _ = w
            remote("seq", x.at[:, :, core], theirs, sems.at[0], sems.at[1], sibling).wait_recv()
            pltpu.make_async_copy(x.at[:, :, core], mine, sems.at[2]).wait()
            mine[...] = (mine[...].astype(f32) + theirs[...].astype(f32)).astype(bf16)
            for k in range(1, parts):
                to = lax.rem(my + k, parts)
                copy = remote(
                    "dp", mine.at[to], far.at[k - 1], dp_send.at[k - 1], dp_recv.at[k - 1], to
                )
                copy.start()
                sent.append(copy)

        for copy in arriving:
            copy.wait()
        grad[...] = jnp.zeros_like(grad)

        @pl.loop(0, devices)
        def _(j):
            grad[...] += dot_tn(normed_all[j], qkv_all[j])

        gq_in[...] = grad[...].astype(bf16).reshape(gq_shape)
        for k in range(1, parts):
            to = lax.rem(my + k, parts)
            copy = remote(
                "dp", gq_in.at[to], gq_recv.at[my], gq_send.at[k - 1], gq_rsem.at[k - 1], to
            )
            copy.start()
            sent.append(copy)
        own_q = pltpu.make_async_copy(gq_in.at[my], gq_recv.at[my], gq_local)
        own_q.start()
        total = y_refs[0][...].astype(f32)
        for k in range(1, len(branches)):
            total = total + y_refs[k][...].astype(f32)
        output[...] = (mid_ref[...] + res_mult * total).astype(bf16)
        leaving = [pltpu.make_async_copy(output, output_out, out_sem.at[0])]
        leaving[0].start()

        own_q.wait()
        for k in range(1, parts):
            frm = lax.rem(my + parts - k, parts)
            remote(
                "dp", gq_in.at[frm], gq_recv.at[frm], gq_send.at[k - 1], gq_rsem.at[k - 1], frm
            ).wait_recv()
        summed = gq_recv[0].astype(f32)
        for p in range(1, parts):
            summed = summed + gq_recv[p].astype(f32)
        gq_sum[...] = summed.astype(bf16)
        own_z = pltpu.make_async_copy(gq_sum.at[me], gq_out.at[me], gq_local)
        own_z.start()
        for k in range(1, devices):
            to = lax.rem(me + k, devices)
            copy = remote(
                "seq", gq_sum.at[to], gq_out.at[me], gqz_send.at[k - 1], gqz_recv.at[k - 1], to
            )
            copy.start()
            sent.append(copy)
        for w in work:
            mine, theirs, far, near, last, sems, dp_send, dp_recv, z_send, z_recv, _ = w
            summed = mine[my].astype(f32)
            for k in range(1, parts):
                remote(
                    "dp", mine.at[0], far.at[k - 1], dp_send.at[k - 1], dp_recv.at[k - 1], my
                ).wait_recv()
                summed = summed + far[k - 1].astype(f32)
            near[...] = summed.astype(bf16)
            for k in range(1, chips):
                to = lax.rem(chip + k, chips)
                copy = remote(
                    "seq",
                    near.at[to],
                    last.at[k - 1],
                    z_send.at[k - 1],
                    z_recv.at[k - 1],
                    2 * to + core,
                )
                copy.start()
                sent.append(copy)

        for k in range(devices):
            frm = lax.rem(me + devices - k, devices)
            if k == 0:
                own.wait()
            else:
                remote(
                    "seq", qkv_in.at[frm], columns(frm), q_send.at[k - 1], q_recv.at[k - 1], frm
                ).wait_recv()
            part = dot_nt(columns(frm)[...], w_all[frm])
            nac[...] = part if k == 0 else nac[...] + part

        resid = tok_ref[...].astype(f32)
        scale = lax.rsqrt(jnp.mean(resid * resid, axis=-1, keepdims=True) + norm_eps)
        weighted = nac[...] * gain_row(gain_ref, 0)
        in_grad[...] = (
            mid_cot_ref[...]
            + scale * weighted
            - resid
            * (scale * scale * scale)
            * jnp.mean(weighted * resid, axis=-1, keepdims=True)
        ).astype(bf16)

        leaving.append(pltpu.make_async_copy(in_grad, in_grad_out, out_sem.at[1]))
        leaving[1].start()
        for o, w in zip(gt_out, work):
            mine, theirs, far, near, last, sems, dp_send, dp_recv, z_send, z_recv, _ = w
            summed = near[chip].astype(f32)
            for k in range(1, chips):
                remote(
                    "seq", near.at[0], last.at[k - 1], z_send.at[k - 1], z_recv.at[k - 1], me
                ).wait_recv()
                summed = summed + last[k - 1].astype(f32)
            o[...] = summed
        own_z.wait()
        for k in range(1, devices):
            frm = lax.rem(me + devices - k, devices)
            remote(
                "seq", gq_sum.at[frm], gq_out.at[frm], gqz_send.at[k - 1], gqz_recv.at[k - 1], frm
            ).wait_recv()
        for copy in sent:
            copy.wait_send()
        for copy in leaving:
            copy.wait()

    hbm = pl.BlockSpec(memory_space=pl.ANY)
    vmem = pl.BlockSpec(memory_space=pltpu.VMEM)
    dma = pltpu.SemaphoreType.DMA
    scratch = [
        pltpu.VMEM((rows, devices * cols), bf16),
        pltpu.VMEM((rows, width), f32),
        pltpu.VMEM(gq_shape, bf16),
        pltpu.VMEM((width, cols), f32),
        pltpu.VMEM(gq_shape, bf16),
        pltpu.VMEM(gq_shape[1:], bf16),
        dma((devices - 1,)),
        dma((devices - 1,)),
        dma,
        dma((parts - 1,)),
        dma((parts - 1,)),
        dma((devices - 1,)),
        dma((devices - 1,)),
        dma,
    ]
    for wide in wides:
        piece = (out_rows, wide)
        scratch += [
            pltpu.VMEM((parts, chips) + piece, bf16),
            pltpu.VMEM((parts, chips) + piece, bf16),
            pltpu.VMEM((parts - 1, chips) + piece, bf16),
            pltpu.VMEM((chips,) + piece, bf16),
            pltpu.VMEM((chips - 1,) + piece, bf16),
            dma((3,)),
            dma((parts - 1,)),
            dma((parts - 1,)),
            dma((chips - 1,)),
            dma((chips - 1,)),
            dma,
        ]
    scratch += staged(ins) + [
        pltpu.VMEM((rows, width), bf16),
        pltpu.VMEM((rows, width), bf16),
        dma((len(ins),)),
        dma((2,)),
    ]
    return pl.pallas_call(
        kernel,
        name="final_exchange",
        out_shape=[
            jax.ShapeDtypeStruct((rows, width), bf16),
            jax.ShapeDtypeStruct((rows, width), bf16),
            jax.ShapeDtypeStruct(gq_shape[1:], bf16),
        ]
        + [jax.ShapeDtypeStruct((out_rows, wide), f32) for wide in wides],
        in_specs=[hbm] * (1 + count + len(ins)),
        out_specs=[hbm] * 3 + [vmem] * count,
        scratch_shapes=scratch,
        compiler_params=pltpu.CompilerParams(
            collective_id=collective_id, has_side_effects=True, vmem_limit_bytes=60 << 20
        ),
    )(qkv_cot, *token_grads, *ins)


def on_device(
    tokens,
    out_grad,
    doc_ids,
    expert_picks,
    w_query,
    key_weight_matrix,
    value_weight_matrix,
    w_out,
    w_router,
    gain_attn,
    gain_moe,
    expert_in,
    expert_out,
):
    devices, parts = lax.axis_size("seq"), lax.axis_size("dp")
    me = lax.axis_index("seq")
    rows, width = tokens.shape[1:]
    length = rows * devices
    experts = w_router.shape[1]
    heads = QUERY_HEADS // devices
    group = QUERY_HEADS // KEY_VALUE_HEADS
    q_width = heads * HEAD_SIZE
    w_rows = w_query.shape[0]

    w_cols = HEADS_LANES + LANES
    in_low, out_low, mask, doc_rows, misc, gains = prepare(
        expert_in, expert_out, expert_picks[0], doc_ids, w_router, gain_attn, gain_moe
    )
    expert_in_full = lax.all_gather(in_low, "dp", axis=1, tiled=True)
    expert_out_full = lax.all_gather(out_low, "dp", axis=1, tiled=True)
    chips = devices // 2

    def shift(x, k):
        return lax.ppermute(x, "seq", [(i, (i + 2 * k) % devices) for i in range(devices)])

    tok_all, doc_all, mask_all, middle_cot, misc_full, gains_full, w_own_all, wo_full, w_all = first_exchange(
        0,
        tokens[0],
        out_grad[0],
        doc_rows,
        mask,
        misc,
        gains,
        w_query,
        key_weight_matrix,
        value_weight_matrix,
        w_out,
    )
    w_full = lax.all_gather(w_all, "dp", axis=1, tiled=True)
    held, tok_all = lax.optimization_barrier((out_grad[0], tok_all))
    cots = [held] + [
        middle_cot if k == chips // 2 else shift(held, k) for k in range(1, chips)
    ]
    w_own_all = w_own_all.reshape(width, w_cols)
    wo_full = wo_full.reshape(width, width)
    misc_full = misc_full.reshape(width, LANES)
    table = rope_table(devices, rows)

    normed_a, q_all, kv_all, attended_own, ot, lse = attend_forward(
        tok_all, w_own_all, gains_full, table, doc_all, heads
    )
    attended, mid, normed_m = attended_exchange(
        1, attended_own, tokens[0], wo_full, gains_full
    )
    (_, _, _, moe_sum, gate_cot, e_grads, *branches) = moe_exchange(
        2, normed_m, cots, mask_all, misc_full, expert_in_full, expert_out_full
    )
    e_grads = lax.psum_scatter(e_grads, "dp", scatter_dimension=1, tiled=True)
    heads_cot, router_pack, mid_cot, grad_wo = middle_exchange(
        4, moe_sum, gate_cot, normed_m, misc_full, mask, mid, out_grad[0], gains_full,
        wo_full, attended, q_width,
    )
    heads_cot, branches = lax.optimization_barrier((heads_cot, branches))
    branches = [
        branches[0],
        lax.ppermute(branches[1], "seq", [(i, i ^ 2) for i in range(devices)]),
    ] + [shift(branches[1 + k], 2 * k) for k in range(1, chips // 2)]
    qkv_cot = attend_backward(q_all, kv_all, heads_cot, ot, lse, table, doc_all, heads)
    qkv_cot, branches = lax.optimization_barrier((qkv_cot, branches))
    out_rows = w_rows // devices
    input_grad, output, grad_qkv, grad_wo, router_pack = final_exchange(
        5,
        qkv_cot,
        normed_a,
        [
            grad_wo.reshape(parts, devices, out_rows, width),
            router_pack.reshape(parts, devices, out_rows, LANES),
        ],
        w_full,
        tokens[0],
        mid_cot,
        gains_full,
        mid,
        branches,
    )

    (
        grad_e_in, grad_e_out, grad_wq, grad_wk, grad_wv, grad_wo, grad_router, grad_gain_m,
        grad_gain_a, input_grad, output,
    ) = finish(
        e_grads,
        grad_qkv,
        grad_wo,
        router_pack,
        input_grad,
        output,
        [w_query, key_weight_matrix, value_weight_matrix],
        gain_attn.reshape(devices, out_rows),
        heads,
        experts,
    )
    input_grad, output = input_grad[None], output[None]
    grad_gain_a = grad_gain_a.reshape(out_rows)
    grad_gain_m = grad_gain_m.reshape(out_rows)
    return (
        output,
        input_grad,
        grad_wq,
        grad_wk,
        grad_wv,
        grad_wo,
        grad_router,
        grad_gain_a,
        grad_gain_m,
        grad_e_in,
        grad_e_out,
    )


def solution(mesh):
    return jax.shard_map(
        on_device,
        mesh=mesh,
        in_specs=(
            P("dp", "seq", None),
            P("dp", "seq", None),
            P("dp", "seq"),
            P("dp", "seq", None),
            P("dp", None),
            P("dp", None),
            P("dp", None),
            P("dp", None),
            P("dp", None),
            P("dp"),
            P("dp"),
            P("seq", "dp", None),
            P("seq", "dp", None),
        ),
        out_specs=(
            P("dp", "seq", None),
            P("dp", "seq", None),
            P(("dp", "seq"), None),
            P(("dp", "seq"), None),
            P(("dp", "seq"), None),
            P(("dp", "seq"), None),
            P(("dp", "seq"), None),
            P(("dp", "seq")),
            P(("dp", "seq")),
            P("seq", "dp", None),
            P("seq", "dp", None),
        ),
        check_vma=False,
    )
```

```python
import functools

import jax
import jax.numpy as jnp
import numpy as np
from jax import lax
from jax.experimental import pallas as pl
from jax.experimental.pallas import tpu as pltpu
from jax.sharding import PartitionSpec as P

MESH = pl.DeviceIdType.MESH
PIECES = 2


def _block(ref, j, cut):
    if cut is None:
        return ref.at[j]
    return ref.at[:, pl.ds(pl.multiple_of(j * cut, cut), cut)]


def exchange(collective_id, ops, prepare=None, given=(), work=(), made=None, keep=None):
    axes = tuple(dict.fromkeys(axis for _, axis, _, _ in ops))
    size = {axis: lax.axis_size(axis) for axis in axes}
    out_shapes, out_specs, scratch, places = [], [], [], []
    for kind, axis, x, cut in ops:
        count = size[axis]
        out_spec = pl.BlockSpec(memory_space=pl.ANY)
        extra = []
        lead = (PIECES,) if kind == "gather" and axis == "seq" else ()
        if kind == "shift":
            shape, dtype, copies = x.shape, x.dtype, 1
        elif kind == "share":
            shape, dtype, copies = (count,) + x.shape, x.dtype, 2 * (count - 1)
        elif kind == "gather":
            shape, dtype = (count,) + x.shape, x.dtype
            copies = count - 1 if axis == "dp" else 3 + 4 * (count // 2 - 1)
        elif kind == "swap":
            copies, dtype = count - 1, x.dtype
            if cut is None:
                shape = x.shape
            elif cut[0] == "in":
                shape = (count, x.shape[0], cut[1])
            else:
                shape = (x.shape[1], count * cut[1])
        out_shapes.append(jax.ShapeDtypeStruct(shape, dtype))
        out_specs.append(out_spec)
        places.append((len(scratch), len(extra)))
        scratch += [
            pltpu.SemaphoreType.DMA(lead + (copies,)),
            pltpu.SemaphoreType.DMA(lead + (max(copies, count),)),
            pltpu.SemaphoreType.DMA,
        ] + extra

    early = [x for _, _, x, cut in ops if not isinstance(cut, int)]
    own_scratch = len(scratch)

    def kernel(*refs):
        ins, refs = list(refs[: len(early)]), refs[len(early) :]
        extra_in, refs = refs[: len(given)], refs[len(given) :]
        outs, refs = refs[: len(ops)], refs[len(ops) :]
        if keep is not None:
            kept, refs = refs[0], refs[1:]
        work, extra_work = refs[:own_scratch], refs[own_scratch:]
        ins += [None] * (len(ops) - len(early))
        me = {axis: lax.axis_index(axis) for axis in axes}
        barrier = pltpu.get_barrier_semaphore()
        for axis in axes:
            for k in range(1, size[axis]):
                pl.semaphore_signal(
                    barrier,
                    inc=1,
                    device_id={axis: lax.rem(me[axis] + k, size[axis])},
                    device_id_type=MESH,
                )
        pl.semaphore_wait(barrier, sum(size[axis] - 1 for axis in axes))

        def remote(axis, src, dst, send, recv, to):
            return pltpu.make_async_remote_copy(
                src_ref=src,
                dst_ref=dst,
                send_sem=send,
                recv_sem=recv,
                device_id={axis: to},
                device_id_type=MESH,
            )

        second, third = [], []
        for (kind, axis, _, cut), x, o, (at, extra) in zip(ops, ins, outs, places):
            if isinstance(cut, int):
                if x is None and cut == 0:
                    all_refs = list(extra_in) + list(extra_work[:-1])
                    prepare(all_refs)
                    late = made(all_refs)
                    leave = pltpu.make_async_copy(all_refs[keep[1]], kept, extra_work[-1])
                    leave.start()
                    third.append(leave.wait)
                x, cut = late[cut], None
            send, recv, local = work[at : at + 3]
            count, my = size[axis], me[axis]
            if kind == "swap":
                into = cut[1] if cut is not None and cut[0] == "out" else None
                outof = cut[1] if cut is not None and cut[0] == "in" else None
                own = pltpu.make_async_copy(_block(x, my, outof), _block(o, my, into), local)
                own.start()
                third.append(own.wait)
                for k in range(1, count):
                    to = lax.rem(my + k, count)
                    copy = remote(
                        axis,
                        _block(x, to, outof),
                        _block(o, my, into),
                        send.at[k - 1],
                        recv.at[k - 1],
                        to,
                    )
                    copy.start()
                    frm = lax.rem(my + count - k, count)
                    arrive = remote(
                        axis,
                        _block(x, to, outof),
                        _block(o, frm, into),
                        send.at[k - 1],
                        recv.at[k - 1],
                        to,
                    )
                    third.append(copy.wait_send)
                    third.append(arrive.wait_recv)
            elif kind == "gather" and axis == "dp":
                own = pltpu.make_async_copy(x, o.at[my], local)
                own.start()
                third.append(own.wait)
                for k in range(1, count):
                    to = lax.rem(my + k, count)
                    frm = lax.rem(my + count - k, count)
                    copy = remote(axis, x, o.at[my], send.at[k - 1], recv.at[k - 1], to)
                    copy.start()
                    third.append(copy.wait_send)
                    third.append(
                        remote(
                            axis, x, o.at[frm], send.at[k - 1], recv.at[k - 1], to
                        ).wait_recv
                    )
            elif kind == "shift":
                copy = remote(
                    axis, x, o, send.at[0], recv.at[0], lax.rem(my + 2 * (count // 4), count)
                )
                second.append((count // 4 + 0.9, copy.start))
                third.append(copy.wait)
            elif kind == "share":
                seq, half = me["seq"], x.shape[0] // 2
                core = lax.rem(seq, 2)
                sibling = seq + 1 - 2 * core
                own = pltpu.make_async_copy(x, o.at[my], local)
                own.start()
                third.append(own.wait)

                def side_of(ref, which, half=half):
                    return ref.at[pl.ds(which * half, half)]

                def relay(k, axis=axis, x=x, o=o, send=send, recv=recv, count=count, my=my, core=core, sibling=sibling, side_of=side_of):
                    to = lax.rem(my + k, count)
                    frm = lax.rem(my + count - k, count)
                    remote(
                        axis,
                        side_of(x, core),
                        side_of(o.at[frm], core),
                        send.at[k - 1],
                        recv.at[k - 1],
                        to,
                    ).wait_recv()
                    slot = count - 2 + k
                    spot = side_of(o.at[frm], core)
                    over = remote("seq", spot, spot, send.at[slot], recv.at[slot], sibling)
                    over.start()
                    third.append(over.wait_send)
                    third.append(
                        remote(
                            "seq",
                            spot,
                            side_of(o.at[frm], 1 - core),
                            send.at[slot],
                            recv.at[slot],
                            sibling,
                        ).wait_recv
                    )

                for k in range(1, count):
                    to = lax.rem(my + k, count)
                    copy = remote(
                        axis,
                        side_of(x, core),
                        side_of(o.at[my], core),
                        send.at[k - 1],
                        recv.at[k - 1],
                        to,
                    )
                    copy.start()
                    third.append(copy.wait_send)
                    second.append((k + 0.75, functools.partial(relay, k)))
            elif kind == "gather":
                chips = count // 2
                chip, core = my // 2, lax.rem(my, 2)
                sibling = my + 1 - 2 * core
                own = pltpu.make_async_copy(x, o.at[my], local)
                own.start()
                third.append(own.wait)

                cuts = PIECES if x.shape[0] % (16 * PIECES) == 0 else 1
                size_of = x.shape[0] // cuts

                def cut_of(ref, i, size_of=size_of):
                    return ref.at[pl.ds(i * size_of, size_of)]

                def line(src, b, i, slot, to, axis=axis, o=o, send=send, recv=recv, core=core, cut_of=cut_of):
                    return remote(
                        axis, src, cut_of(o.at[2 * b + core], i), send.at[i, slot], recv.at[i, b], to
                    )

                def across(src, b, i, slot, half, axis=axis, o=o, send=send, recv=recv, chips=chips, sibling=sibling, cut_of=cut_of):
                    return remote(
                        axis,
                        src,
                        cut_of(o.at[2 * b + half], i),
                        send.at[i, slot],
                        recv.at[i, chips + b],
                        sibling,
                    )

                def guarded(where, act):
                    pl.when(where)(act)

                for i in range(cuts):
                    for slot, where, to in ((0, chip > 0, my - 2), (1, chip < chips - 1, my + 2)):
                        copy = line(cut_of(x, i), chip, i, slot, to)
                        guarded(where, copy.start)
                        third.append(functools.partial(guarded, where, copy.wait_send))
                for i in range(cuts):
                    copy = across(cut_of(x, i), chip, i, 2, core)
                    copy.start()
                    third.append(copy.wait_send)
                    third.append(across(cut_of(x, i), chip, i, 2, 1 - core).wait_recv)

                def hop(k, side, i, chips=chips, chip=chip, core=core, my=my, x=x, o=o, line=line, across=across, cut_of=cut_of):
                    b = chip + side * k
                    there = (b >= 0) & (b < chips)
                    onward = there & ((chip - side >= 0) & (chip - side < chips))
                    slot = 3 + (k - 1) * 4 + (side + 1)
                    spot = cut_of(o.at[2 * b + core], i)
                    further = line(spot, b, i, slot, my - 2 * side)
                    over = across(spot, b, i, slot + 1, core)
                    arrived = line(cut_of(x, i), b, i, slot, my)
                    brought = across(cut_of(x, i), b, i, slot + 1, 1 - core)

                    @pl.when(there)
                    def _():
                        arrived.wait_recv()

                    guarded(onward, further.start)
                    guarded(there, over.start)
                    third.append(functools.partial(guarded, onward, further.wait_send))
                    third.append(functools.partial(guarded, there, over.wait_send))
                    third.append(functools.partial(guarded, there, brought.wait_recv))

                for k in range(1, chips):
                    for i in range(cuts):
                        for side in (-1, 1):
                            second.append((k + i / cuts, functools.partial(hop, k, side, i)))
        for _, run in sorted(second, key=lambda item: item[0]):
            run()
        for wait in third:
            wait()

    return pl.pallas_call(
        kernel,
        name=f"exchange{collective_id}",
        out_shape=out_shapes + ([] if keep is None else [keep[0]]),
        in_specs=[pl.BlockSpec(memory_space=pl.ANY)] * (len(early) + len(given)),
        out_specs=out_specs + ([] if keep is None else [pl.BlockSpec(memory_space=pl.ANY)]),
        scratch_shapes=scratch
        + list(work)
        + ([] if keep is None else [pltpu.SemaphoreType.DMA]),
        compiler_params=pltpu.CompilerParams(
            collective_id=collective_id, has_side_effects=True, vmem_limit_bytes=60 << 20
        ),
    )(*early, *given)

QUERY_HEADS = 16
KEY_VALUE_HEADS = 8
HEAD_SIZE = 64
FFE = 512
TOP = 8

att_mult = 0.015625
res_mult = 0.22
norm_eps = 1e-06
rope_theta = 10000.0
LANES = 128
bf16 = jnp.bfloat16
f32 = jnp.float32
HEADS_LANES = 128


def dot_nt(a, b):
    return lax.dot_general(a, b, (((1,), (1,)), ((), ())), preferred_element_type=f32)


def dot_nn(a, b):
    return lax.dot_general(a, b, (((1,), (0,)), ((), ())), preferred_element_type=f32)


def dot_tn(a, b):
    return lax.dot_general(a, b, (((0,), (0,)), ((), ())), preferred_element_type=f32)


def turn(x):
    half = HEAD_SIZE // 2
    lane = lax.broadcasted_iota(jnp.int32, x.shape, 1)
    width = x.shape[1]
    return jnp.where(
        lax.rem(lane, HEAD_SIZE) < half, pltpu.roll(x, width - half, 1), pltpu.roll(x, half, 1)
    )


def rope_table(blocks, rows):
    half = HEAD_SIZE // 2
    frequency = np.float32(rope_theta) ** (
        -np.arange(half, dtype=np.float32) * np.float32(2.0) / np.float32(HEAD_SIZE)
    )
    angles = (frequency[:, None] * np.arange(blocks * rows, dtype=np.float32)[None, :]).astype(
        np.float32
    )
    table = np.concatenate([np.cos(angles), np.sin(angles)], axis=0).astype(np.float32)
    return jnp.asarray(table.reshape(HEAD_SIZE, blocks, rows).transpose(1, 0, 2))


def spread_table(table):
    half = HEAD_SIZE // 2
    turned = table.T
    cos, sin = turned[:, :half], turned[:, half:]
    return (
        jnp.concatenate([cos, cos] * (LANES // HEAD_SIZE), axis=1),
        jnp.concatenate([-sin, sin] * (LANES // HEAD_SIZE), axis=1),
    )


def across_lanes(row, lanes):
    return jnp.broadcast_to(row, (lanes, row.shape[1])).T


def first_block(docs_ref, i):
    docs = docs_ref[:, 0, :].astype(f32)
    own = lax.broadcasted_iota(jnp.int32, docs.shape, 0) == i
    lane = lax.broadcasted_iota(jnp.int32, docs.shape, 1)
    start = jnp.sum(jnp.where(own & (lane == 0), docs, 0.0))
    ends = (lane == docs.shape[1] - 1) & (docs < start)
    return jnp.sum(jnp.where(ends, 1.0, 0.0)).astype(jnp.int32)


def stack_heads(x, heads):
    return jnp.concatenate(
        [x[:, h * HEAD_SIZE : (h + 1) * HEAD_SIZE] for h in range(heads)], axis=0
    )


def gain_row(ref, which):
    return jnp.concatenate(
        [ref[p, which : which + 1, :] for p in range(ref.shape[0])], axis=1
    ).astype(f32)


def attend_forward(tok_all, w_own, gain, table, docs, heads):
    blocks, rows, width = tok_all.shape
    length = blocks * rows
    cols = heads * rows
    out_width = heads * HEAD_SIZE

    def kernel(tok, w, gain_ref, table_ref, docs_ref, na_ref, q_ref, kv_ref, att_ref, ot_ref, lse_ref, k_scr, vt_scr, doc_scr):
        i = pl.program_id(0)
        x = tok[0].astype(f32)
        scale = lax.rsqrt(jnp.mean(x * x, axis=-1, keepdims=True) + norm_eps)
        na = (x * scale * gain_row(gain_ref, 0)).astype(bf16)
        na_ref[0] = na
        qkv = dot_nn(na, w[...])
        c, s = spread_table(table_ref[0])
        q, kv = qkv[:, :HEADS_LANES], qkv[:, HEADS_LANES:]
        q = (q * c + turn(q) * s).astype(bf16)
        lane = lax.broadcasted_iota(jnp.int32, kv.shape, 1)
        kv = jnp.where(lane < HEAD_SIZE, kv * c + turn(kv) * s, kv).astype(bf16)
        q_ref[0] = q
        kv_ref[0] = kv
        k_scr[i] = kv[:, :HEAD_SIZE]
        vt_scr[i] = kv.astype(f32).T[HEAD_SIZE:].astype(bf16)
        q2 = stack_heads(q, heads)
        doc_row = docs_ref[i, :1].astype(f32)
        doc_scr[i] = across_lanes(doc_row, LANES)
        doc_query = jnp.concatenate([doc_row] * heads, axis=1)
        query = i * rows + lax.rem(lax.broadcasted_iota(jnp.int32, (1, cols), 1), rows)
        key_iota = lax.broadcasted_iota(jnp.int32, (rows, cols), 0)

        def step(j, carry):
            top, total, ot = carry
            scores = dot_nt(k_scr[j], q2) * att_mult
            key = key_iota + j * rows
            same = jnp.concatenate([doc_scr[j]] * (cols // LANES), axis=1) == doc_query
            scores = jnp.where(same & (key <= query), scores, -1e30)
            new_top = jnp.maximum(top, jnp.max(scores, axis=0, keepdims=True))
            p = jnp.exp(scores - new_top)
            keep = jnp.exp(top - new_top)
            total = total * keep + jnp.sum(p, axis=0, keepdims=True)
            ot = ot * keep + dot_nn(vt_scr[j], p.astype(bf16))
            return new_top, total, ot

        top, total, ot = lax.fori_loop(
            first_block(docs_ref, i),
            i + 1,
            step,
            (
                jnp.full((1, cols), -1e30, f32),
                jnp.zeros((1, cols), f32),
                jnp.zeros((HEAD_SIZE, cols), f32),
            ),
        )
        ot = ot / total
        ot_ref[0] = ot
        lse_ref[0] = top + jnp.log(total)
        out = ot.T
        att_ref[0] = jnp.concatenate(
            [out[h * rows : (h + 1) * rows] for h in range(heads)], axis=1
        ).astype(bf16)

    def block(shape):
        return pl.BlockSpec((1,) + shape, lambda i: (i, 0, 0))

    def whole(shape):
        return pl.BlockSpec(shape, lambda i: (0,) * len(shape))

    grid_spec = pltpu.PrefetchScalarGridSpec(
        num_scalar_prefetch=0,
        grid=(blocks,),
        in_specs=[
            block((rows, width)),
            whole(w_own.shape),
            whole(gain.shape),
            block((HEAD_SIZE, rows)),
            whole(docs.shape),
        ],
        out_specs=[
            block((rows, width)),
            block((rows, HEADS_LANES)),
            block((rows, LANES)),
            block((rows, out_width)),
            block((HEAD_SIZE, cols)),
            block((1, cols)),
        ],
        scratch_shapes=[
            pltpu.VMEM((blocks, rows, HEAD_SIZE), bf16),
            pltpu.VMEM((blocks, HEAD_SIZE, rows), bf16),
            pltpu.VMEM((blocks, rows, LANES), f32),
        ],
    )
    return pl.pallas_call(
        kernel,
        name="attend_forward",
        grid_spec=grid_spec,
        out_shape=[
            jax.ShapeDtypeStruct((blocks, rows, width), bf16),
            jax.ShapeDtypeStruct((blocks, rows, HEADS_LANES), bf16),
            jax.ShapeDtypeStruct((blocks, rows, LANES), bf16),
            jax.ShapeDtypeStruct((blocks, rows, out_width), bf16),
            jax.ShapeDtypeStruct((blocks, HEAD_SIZE, cols), f32),
            jax.ShapeDtypeStruct((blocks, 1, cols), f32),
        ],
        cost_estimate=pl.CostEstimate(
            flops=2 * length * width * 256 + 2 * length * length * cols // rows * 128,
            bytes_accessed=2 * length * width * 4,
            transcendentals=length * length,
        ),
        compiler_params=pltpu.CompilerParams(
            dimension_semantics=("arbitrary",), vmem_limit_bytes=60 << 20
        ),
    )(
        tok_all,
        w_own,
        gain,
        table,
        docs,
    )


def attend_backward(q_all, kv_all, cot, ot, lse, table, docs, heads):
    blocks, rows, _ = q_all.shape
    length = blocks * rows
    cols = heads * rows

    def kernel(q_ref, kv_ref, do_ref, ot_ref, lse_ref, table_ref, docs_ref, out_ref, dk_scr, dv_scr, dq_scr, doc_scr):
        i = pl.program_id(0)

        @pl.when(i == 0)
        def _():
            dk_scr[...] = jnp.zeros_like(dk_scr)
            dv_scr[...] = jnp.zeros_like(dv_scr)

        q2 = stack_heads(q_ref[0], heads)
        do2 = stack_heads(do_ref[0], heads)
        delta = jnp.sum(do2.astype(f32).T * ot_ref[0], axis=0, keepdims=True)
        log_total = lse_ref[0]
        doc_row = docs_ref[i, :1].astype(f32)
        doc_scr[i] = across_lanes(doc_row, LANES)
        doc_query = jnp.concatenate([doc_row] * heads, axis=1)
        query = i * rows + lax.rem(lax.broadcasted_iota(jnp.int32, (1, cols), 1), rows)
        key_iota = lax.broadcasted_iota(jnp.int32, (rows, cols), 0)
        dq_scr[...] = jnp.zeros_like(dq_scr)

        @pl.loop(first_block(docs_ref, i), i + 1)
        def _(j):
            kv = kv_ref[j]
            k, v = kv[:, :HEAD_SIZE], kv[:, HEAD_SIZE:]
            scores = dot_nt(k, q2) * att_mult
            key = key_iota + j * rows
            same = jnp.concatenate([doc_scr[j]] * (cols // LANES), axis=1) == doc_query
            p = jnp.where(same & (key <= query), jnp.exp(scores - log_total), 0.0)
            ds = (p * (dot_nt(v, do2) - delta)).astype(bf16)
            dv_scr[j] += dot_nn(p.astype(bf16), do2)
            dk_scr[j] += dot_nn(ds, q2)
            dq_scr[...] += dot_tn(ds, k)

        def rope_back(x, c, s):
            return (x * c - turn(x) * s).astype(bf16)

        dq = dq_scr[...] * att_mult
        dq = [dq[h * rows : (h + 1) * rows] for h in range(heads)]
        if heads * HEAD_SIZE < HEADS_LANES:
            dq.append(jnp.zeros((rows, HEADS_LANES - heads * HEAD_SIZE), f32))
        dq = jnp.concatenate(dq, axis=1).astype(bf16).astype(f32)
        out_ref[i, :, :HEADS_LANES] = rope_back(dq, *spread_table(table_ref[i]))

        @pl.when(i == blocks - 1)
        def _():
            @pl.loop(0, blocks)
            def _(j):
                kv = jnp.concatenate([dk_scr[j] * att_mult, dv_scr[j]], axis=1)
                lane = lax.broadcasted_iota(jnp.int32, kv.shape, 1)
                c, s = spread_table(table_ref[j])
                kv = jnp.where(lane < HEAD_SIZE, kv * c - turn(kv) * s, kv).astype(bf16)
                out_ref[j, :, HEADS_LANES:] = kv

    def block(shape):
        return pl.BlockSpec((1,) + shape, lambda i: (i, 0, 0))

    def whole(shape):
        return pl.BlockSpec(shape, lambda i: (0,) * len(shape))

    grid_spec = pltpu.PrefetchScalarGridSpec(
        num_scalar_prefetch=0,
        grid=(blocks,),
        in_specs=[
            block((rows, HEADS_LANES)),
            whole((blocks, rows, LANES)),
            block((rows, heads * HEAD_SIZE)),
            block((HEAD_SIZE, cols)),
            block((1, cols)),
            whole((blocks, HEAD_SIZE, rows)),
            whole(docs.shape),
        ],
        out_specs=whole((blocks, rows, HEADS_LANES + LANES)),
        scratch_shapes=[
            pltpu.VMEM((blocks, rows, HEAD_SIZE), f32),
            pltpu.VMEM((blocks, rows, HEAD_SIZE), f32),
            pltpu.VMEM((cols, HEAD_SIZE), f32),
            pltpu.VMEM((blocks, rows, LANES), f32),
        ],
    )
    return pl.pallas_call(
        kernel,
        name="attend_backward",
        grid_spec=grid_spec,
        out_shape=jax.ShapeDtypeStruct((blocks, rows, HEADS_LANES + LANES), bf16),
        cost_estimate=pl.CostEstimate(
            flops=5 * length * length * cols // rows * 128,
            bytes_accessed=2 * length * 1024,
            transcendentals=length * length,
        ),
        compiler_params=pltpu.CompilerParams(
            dimension_semantics=("arbitrary",), vmem_limit_bytes=60 << 20
        ),
    )(
        q_all,
        kv_all,
        cot,
        ot,
        lse,
        table,
        docs,
    )


def moe_exchange(collective_id, normed, cots, mask, router, weights):
    devices = lax.axis_size("seq")
    chips = devices // 2
    rows, width = normed.shape
    own_experts = weights.shape[0]
    gate_rows = devices * own_experts

    def order(chip, k):
        left = chip < chips - 1 - chip
        longer = jnp.where(left, chips - 1 - chip, chip)
        near = jnp.where(left, chip + k, chip - k)
        return jnp.where(k <= longer, near, jnp.where(left, chips - 1 - k, k))

    def kernel(*refs):
        x_in, g_in = refs[0], refs[1 : 1 + chips]
        mask_ref, router_ref, w_given = refs[1 + chips : 4 + chips]
        (lin_out, slot_out, hid_out, n_sum, gate_out, g_out) = refs[4 + chips : 10 + chips]
        y_outs = refs[10 + chips : 11 + chips + chips // 2]
        (
            x_all, g_all, win, wout, y_acc, n_acc, gate_acc, gate_stage,
            n_mine, n_far, n_give, n_theirs, y_give, y_theirs, y_pre, y_in,
            lin_st, slot_st, hid_st, gin, gout, hid_ld,
            local, line_send, line_recv, sib_send, sib_recv, g_local, g_send, g_recv,
            n_send, n_recv, y_send, y_recv, far_send, far_recv, gate_send, gate_recv,
            st_sem, y_sem, ld_sem, w_sem, wg_sem, hand_send, hand_recv,
        ) = refs[11 + chips + chips // 2 :]
        me = lax.axis_index("seq")
        chip, core = me // 2, lax.rem(me, 2)
        sibling = me + 1 - 2 * core
        win_copy = pltpu.make_async_copy(
            w_given.at[:, :, pl.ds(0, 2 * FFE)], win, w_sem.at[0]
        )
        wout_copy = pltpu.make_async_copy(
            w_given.at[:, :, pl.ds(2 * FFE, FFE)], wout, w_sem.at[1]
        )
        win_copy.start()
        wout_copy.start()
        barrier = pltpu.get_barrier_semaphore()
        for k in range(1, devices):
            pl.semaphore_signal(
                barrier, inc=1, device_id={"seq": lax.rem(me + k, devices)}, device_id_type=MESH
            )
        pl.semaphore_wait(barrier, devices - 1)

        def remote(src, dst, send, recv, to):
            return pltpu.make_async_remote_copy(
                src_ref=src,
                dst_ref=dst,
                send_sem=send,
                recv_sem=recv,
                device_id={"seq": to},
                device_id_type=MESH,
            )

        half = rows // PIECES

        def piece(b, core_of, i):
            return x_all.at[2 * b + core_of, pl.ds(i * half, half)]

        def line(src, b, i, slot, to):
            return remote(
                src, piece(b, core, i), line_send.at[i, slot], line_recv.at[i, b], to
            )

        def across(src, b, core_of, i):
            return remote(
                src, piece(b, core_of, i), sib_send.at[i, b], sib_recv.at[i, b], sibling
            )

        def own_piece(i):
            return x_in.at[pl.ds(i * half, half)]

        def pass_on(b, i, to):
            return line(piece(b, core, i), b, i, 2 + b, to)

        def to_sibling(b, i):
            return across(piece(b, core, i), b, core, i)

        def own_sends(act):
            for i in range(PIECES):

                @pl.when(chip > 0)
                def _(i=i):
                    act(line(own_piece(i), chip, i, 0, me - 2))

                @pl.when(chip < chips - 1)
                def _(i=i):
                    act(line(own_piece(i), chip, i, 1, me + 2))

            for i in range(PIECES):
                act(across(own_piece(i), chip, core, i))

        def cot_to_sibling(k):
            b = lax.rem(chip + chips - k, chips)
            return remote(
                g_in[k], g_all.at[2 * b + core], g_send.at[k], g_recv.at[b], sibling
            )

        def cot_local(k):
            b = lax.rem(chip + chips - k, chips)
            return pltpu.make_async_copy(g_in[k], g_all.at[2 * b + core], g_local.at[k])

        own_sends(lambda copy: copy.start())
        own = pltpu.make_async_copy(x_in, x_all.at[me], local)
        own.start()
        for k in range(chips):
            cot_to_sibling(k).start()
            cot_local(k).start()
        own.wait()
        for k in range(chips):
            cot_local(k).wait()
        win_copy.wait()
        wout_copy.wait()

        def gate_copy(block):
            return remote(
                gate_stage.at[block],
                gate_out.at[me],
                gate_send.at[block],
                gate_recv.at[me],
                block,
            )

        def n_copy(p):
            return remote(n_give, n_theirs.at[p], n_send.at[p], n_recv.at[p], sibling)

        def y_copy(p):
            return remote(y_give, y_theirs.at[p], y_send.at[p], y_recv.at[p], sibling)

        pairs = chips // 2
        pair = chip // 2
        mate = chip + 1 - 2 * lax.rem(chip, 2)

        def y_leave(b, k):
            return pltpu.make_async_copy(y_pre.at[b], y_outs[k], y_sem.at[k])

        def y_hand(b):
            far = lax.rem(b // 2 + pairs - pair, pairs) - 1
            return remote(
                y_pre.at[b], y_in.at[far], hand_send.at[far], hand_recv.at[far], 2 * mate + core
            )

        def stage_copies(e, block):
            return [
                pltpu.make_async_copy(lin_st.at[e], lin_out.at[e, block], st_sem.at[0, e]),
                pltpu.make_async_copy(slot_st.at[e], slot_out.at[e, block], st_sem.at[1, e]),
                pltpu.make_async_copy(hid_st.at[e], hid_out.at[e, block], st_sem.at[2, e]),
            ]

        def far_copy(b):
            return remote(
                n_mine.at[b], n_far.at[chip], far_send.at[b], far_recv.at[chip], 2 * b + core
            )

        def fold(k):
            b, p = order(chip, k), lax.rem(k, 2)
            n_copy(p).wait_recv()
            both = n_acc[...].astype(bf16).astype(f32) + n_theirs[p].astype(f32)

            @pl.when(b == chip)
            def _():
                n_sum[...] = both

            @pl.when(b != chip)
            def _():
                n_mine[b] = both.astype(bf16)
                far_copy(b).start()

            y_copy(p).wait_recv()
            y_pre[b] = (y_acc[...] + y_theirs[p].astype(f32)).astype(bf16)

            @pl.when(b == chip)
            def _():
                y_leave(b, 0).start()

            @pl.when(b == mate)
            def _():
                y_leave(b, 1).start()

            @pl.when((b != mate) & (lax.rem(b + chip, 2) == 1))
            def _():
                y_hand(b).start()

        def compute(block, before):
            x = x_all[block]
            there = mask_ref[block] > 0
            logits = jnp.where(there, dot_nn(x, router_ref[...]), -1e30)
            gates = jnp.where(
                there, jnp.exp(logits - jnp.max(logits, axis=1, keepdims=True)), 0.0
            )
            gates = gates / jnp.sum(gates, axis=1, keepdims=True)
            lane = lax.broadcasted_iota(jnp.int32, gates.shape, 1)
            y_acc[...] = jnp.zeros_like(y_acc)
            n_acc[...] = jnp.zeros_like(n_acc)
            gate_acc[...] = jnp.zeros_like(gate_acc)

            @pl.loop(0, own_experts)
            def _(e):
                gate = jnp.sum(
                    jnp.where(lane == me * own_experts + e, gates, 0.0), axis=1, keepdims=True
                )
                lin = dot_nn(x_all[block], win[e])
                gate_lin, up_lin = lin[:, :FFE], lin[:, FFE:]
                sig = 0.5 + 0.5 * jnp.tanh(0.5 * gate_lin)
                silu = gate_lin * sig
                hidden = (silu * up_lin).astype(bf16)

                @pl.when(before)
                def _():
                    for copy in stage_copies(e, block):
                        copy.wait()

                hid_st[e] = hidden
                res = dot_nt(hidden, wout[e]).astype(bf16).astype(f32)
                y_acc[...] += gate * res
                cot = g_all[block].astype(f32) * res_mult
                gate_acc[...] += jnp.where(
                    lane == me * own_experts + e, jnp.sum(cot * res, axis=1, keepdims=True), 0.0
                )
                slot = (gate * cot).astype(bf16)
                slot_st[e] = slot
                hidden_cot = dot_nn(slot, wout[e])
                lin_cot = jnp.concatenate(
                    [
                        hidden_cot * up_lin * (sig * (1.0 + gate_lin * (1.0 - sig))),
                        hidden_cot * silu,
                    ],
                    axis=1,
                ).astype(bf16)
                lin_st[e] = lin_cot
                for copy in stage_copies(e, block):
                    copy.start()
                n_acc[...] += dot_nt(lin_cot, win[e]).astype(bf16).astype(f32)

            gate_stage[block] = gate_acc[...].T[:gate_rows]

            @pl.when(block != me)
            def _():
                gate_copy(block).start()

            @pl.when(block == me)
            def _():
                gate_out[block] = gate_stage[block]

        def hop(k, i):
            for side in (-1, 1):
                away = chip + side * k

                @pl.when((k > 0) & (k < chips) & (away >= 0) & (away < chips))
                def _(side=side, away=away):
                    pass_on(away, i, me).wait_recv()

                    @pl.when((chip - side >= 0) & (chip - side < chips))
                    def _():
                        pass_on(away, i, me - 2 * side).start()

                    to_sibling(away, i).start()

        @pl.loop(0, chips)
        def _(k):
            b = order(chip, k)
            hop(k, 1)
            for i in range(PIECES):
                across(own_piece(i), b, 1 - core, i).wait_recv()
            remote(
                x_in, g_all.at[2 * b + 1 - core], g_send.at[0], g_recv.at[b], sibling
            ).wait_recv()

            @pl.loop(0, 2)
            def _(h):
                @pl.when(h == 1)
                def _():
                    hop(k + 1, 0)

                compute(2 * b + lax.rem(core + 1 + h, 2), (k > 0) | (h > 0))

                @pl.when(h == 0)
                def _():
                    p = lax.rem(k, 2)

                    @pl.when(k > 0)
                    def _():
                        n_copy(1 - p).wait_send()
                        y_copy(1 - p).wait_send()

                    n_give[...] = n_acc[...].astype(bf16)
                    y_give[...] = y_acc[...].astype(bf16)
                    n_copy(p).start()
                    y_copy(p).start()

                @pl.when(h == 1)
                def _():
                    fold(k)

        for e in range(own_experts):
            for copy in stage_copies(e, 0):
                copy.wait()

        def loads(t, p):
            e, b = lax.rem(t, own_experts), t // own_experts
            pair = pl.ds(2 * b, 2)
            return [
                pltpu.make_async_copy(
                    lin_out.at[e, pair], g_all.at[pl.ds(4 * p, 2)], ld_sem.at[0, p]
                ),
                pltpu.make_async_copy(
                    slot_out.at[e, pair], g_all.at[pl.ds(4 * p + 2, 2)], ld_sem.at[1, p]
                ),
                pltpu.make_async_copy(hid_out.at[e, pair], hid_ld.at[p], ld_sem.at[2, p]),
            ]

        for copy in loads(jnp.int32(0), 0):
            copy.start()
        gin[...] = jnp.zeros_like(gin)
        gout[...] = jnp.zeros_like(gout)

        @pl.loop(0, chips * own_experts)
        def _(t):
            p = lax.rem(t, 2)
            for copy in loads(t, p):
                copy.wait()

            @pl.when(t + 1 < chips * own_experts)
            def _():
                for copy in loads(t + 1, 1 - p):
                    copy.start()

            e, b = lax.rem(t, own_experts), t // own_experts
            x = x_all[pl.ds(2 * b, 2)].reshape(2 * rows, width)
            lin_cot = g_all[pl.ds(4 * p, 2)].reshape(2 * rows, width)
            gin[e] += dot_tn(x, lin_cot)
            slot = g_all[pl.ds(4 * p + 2, 2)].reshape(2 * rows, width)
            gout[e] += dot_tn(slot, hid_ld[p].reshape(2 * rows, FFE))

        @pl.loop(1, chips)
        def _(k):
            for side in (-1, 1):
                away = chip + side * k

                for i in range(PIECES):

                    @pl.when((away >= 0) & (away < chips))
                    def _(side=side, away=away, i=i):
                        to_sibling(away, i).wait_send()

                        @pl.when((chip - side >= 0) & (chip - side < chips))
                        def _():
                            pass_on(away, i, me - 2 * side).wait_send()

        own_sends(lambda copy: copy.wait_send())

        def keep_of(j):
            return 2 * lax.rem(pair + 1 + j, pairs) + lax.rem(chip, 2)

        for j in range(pairs - 1):
            b = keep_of(j)
            y_hand(b).wait_recv()
            y_pre[b] = (y_pre[b].astype(f32) + y_in[j].astype(f32)).astype(bf16)
            y_leave(b, 2 + j).start()

        leaving = []
        for e in range(own_experts):
            for j in range(width // rows):
                i = e * (width // rows) + j
                x_all[i] = gin[e, j * rows : (j + 1) * rows].astype(bf16)
                g_all[i, :, :FFE] = gout[e, j * rows : (j + 1) * rows].astype(bf16)
                at = 2 * len(leaving)
                here = pl.ds(j * rows, rows)
                leaving.append(
                    (
                        pltpu.make_async_copy(
                            x_all.at[i], g_out.at[e, here, pl.ds(0, 2 * FFE)], wg_sem.at[at]
                        ),
                        pltpu.make_async_copy(
                            g_all.at[i, :, pl.ds(0, FFE)],
                            g_out.at[e, here, pl.ds(2 * FFE, FFE)],
                            wg_sem.at[at + 1],
                        ),
                    )
                )
                for copy in leaving[-1]:
                    copy.start()

        @pl.loop(1, chips)
        def _(k):
            b = order(chip, k)
            remote(
                n_mine.at[b], n_far.at[b], far_send.at[b], far_recv.at[b], 2 * b + core
            ).wait_recv()
            n_sum[...] += n_far[b].astype(f32)
            far_copy(b).wait_send()

        @pl.loop(1, devices)
        def _(k):
            block = lax.rem(me + k, devices)
            remote(
                gate_stage.at[block],
                gate_out.at[block],
                gate_send.at[block],
                gate_recv.at[block],
                block,
            ).wait_recv()
            gate_copy(block).wait_send()

        n_copy((chips - 1) % 2).wait_send()
        y_copy((chips - 1) % 2).wait_send()
        for both in leaving:
            for copy in both:
                copy.wait()
        y_leave(chip, 0).wait()
        y_leave(mate, 1).wait()
        for j in range(pairs - 1):
            y_leave(keep_of(j), 2 + j).wait()
            y_hand(keep_of(j) + mate - chip).wait_send()

        for k in range(chips):
            cot_to_sibling(k).wait_send()

    hbm = pl.BlockSpec(memory_space=pl.ANY)
    vmem = pl.BlockSpec(memory_space=pltpu.VMEM)
    block = (rows, width)
    dma = pltpu.SemaphoreType.DMA
    flops = 9 * own_experts * 2 * devices * rows * width * FFE // 1
    return pl.pallas_call(
        kernel,
        name="moe_exchange",
        out_shape=[
            jax.ShapeDtypeStruct((own_experts, devices, rows, 2 * FFE), bf16),
            jax.ShapeDtypeStruct((own_experts, devices) + block, bf16),
            jax.ShapeDtypeStruct((own_experts, devices, rows, FFE), bf16),
            jax.ShapeDtypeStruct(block, f32),
            jax.ShapeDtypeStruct((devices, gate_rows, rows), f32),
            jax.ShapeDtypeStruct((own_experts, width, 3 * FFE), bf16),
        ]
        + [jax.ShapeDtypeStruct(block, bf16)] * (1 + chips // 2),
        in_specs=[hbm] * (1 + chips) + [vmem] * 2 + [hbm],
        out_specs=[hbm] * 3 + [vmem] * 2 + [hbm] * (2 + chips // 2),
        scratch_shapes=[
            pltpu.VMEM((devices,) + block, bf16),
            pltpu.VMEM((devices,) + block, bf16),
            pltpu.VMEM((own_experts, width, 2 * FFE), bf16),
            pltpu.VMEM((own_experts, width, FFE), bf16),
            pltpu.VMEM(block, f32),
            pltpu.VMEM(block, f32),
            pltpu.VMEM((rows, LANES), f32),
            pltpu.VMEM((devices, gate_rows, rows), f32),
            pltpu.VMEM((chips,) + block, bf16),
            pltpu.VMEM((chips,) + block, bf16),
            pltpu.VMEM(block, bf16),
            pltpu.VMEM((2,) + block, bf16),
            pltpu.VMEM(block, bf16),
            pltpu.VMEM((2,) + block, bf16),
            pltpu.VMEM((chips,) + block, bf16),
            pltpu.VMEM((chips // 2 - 1,) + block, bf16),
            pltpu.VMEM((own_experts, rows, 2 * FFE), bf16),
            pltpu.VMEM((own_experts,) + block, bf16),
            pltpu.VMEM((own_experts, rows, FFE), bf16),
            pltpu.VMEM((own_experts, width, 2 * FFE), f32),
            pltpu.VMEM((own_experts, width, FFE), f32),
            pltpu.VMEM((2, 2, rows, FFE), bf16),
        ]
        + [dma]
        + [
            dma(count)
            for count in (
                (PIECES, chips + 2), (PIECES, chips), (PIECES, chips), (PIECES, chips),
                (chips,), (chips,), (chips,), (2,), (2,), (2,), (2,),
                (chips,), (chips,), (devices,), (devices,),
            )
        ]
        + [
            dma((3, own_experts)),
            dma((1 + chips // 2,)),
            dma((3, 2)),
            dma((2,)),
            dma((2 * own_experts * (width // rows),)),
            dma((chips // 2 - 1,)),
            dma((chips // 2 - 1,)),
        ],
        cost_estimate=pl.CostEstimate(
            flops=flops, bytes_accessed=40 << 20, transcendentals=devices * rows * FFE * 2
        ),
        compiler_params=pltpu.CompilerParams(
            collective_id=collective_id, has_side_effects=True, vmem_limit_bytes=63 << 20
        ),
    )(normed, *cots, mask, router, weights)


class Links:
    def __init__(self, axes):
        self.size = {axis: lax.axis_size(axis) for axis in axes}
        self.me = {axis: lax.axis_index(axis) for axis in axes}

    def barrier(self):
        sem = pltpu.get_barrier_semaphore()
        for axis, size in self.size.items():
            for k in range(1, size):
                pl.semaphore_signal(
                    sem,
                    inc=1,
                    device_id={axis: lax.rem(self.me[axis] + k, size)},
                    device_id_type=MESH,
                )
        pl.semaphore_wait(sem, sum(size - 1 for size in self.size.values()))

    def copy(self, axis, src, dst, send, recv, to):
        return pltpu.make_async_remote_copy(
            src_ref=src,
            dst_ref=dst,
            send_sem=send,
            recv_sem=recv,
            device_id={axis: to},
            device_id_type=MESH,
        )

    def swap_start(self, axis, src, dst, send, recv, local):
        me, size = self.me[axis], self.size[axis]
        pltpu.make_async_copy(src.at[me], dst.at[me], local).start()
        for k in range(1, size):
            to = lax.rem(me + k, size)
            self.copy(axis, src.at[to], dst.at[me], send.at[k - 1], recv.at[k - 1], to).start()

    def swap_wait(self, axis, src, dst, send, recv, local):
        me, size = self.me[axis], self.size[axis]
        pltpu.make_async_copy(src.at[me], dst.at[me], local).wait()
        for k in range(1, size):
            frm = lax.rem(me + size - k, size)
            self.copy(axis, src.at[frm], dst.at[frm], send.at[k - 1], recv.at[k - 1], frm).wait()


def loads(pairs, sems):
    copies = [
        pltpu.make_async_copy(src, dst, sems.at[i]) for i, (src, dst) in enumerate(pairs)
    ]
    for copy in copies:
        copy.start()
    return copies


def staged(arrays):
    return [pltpu.VMEM(x.shape, x.dtype) for x in arrays]


def swap_sems(size):
    dma = pltpu.SemaphoreType.DMA
    return [dma((size - 1,)), dma((size - 1,)), dma]


def attended_exchange(collective_id, attended_own, tokens, w_out, gain):
    devices, rows, cols = attended_own.shape
    width = tokens.shape[1]

    ins = [tokens, w_out, gain]
    outs = [
        jax.ShapeDtypeStruct((rows, width), bf16),
        jax.ShapeDtypeStruct((rows, width), f32),
        jax.ShapeDtypeStruct((rows, width), bf16),
    ]

    def kernel(att_in, *refs):
        given, results = refs[:3], refs[3:6]
        tok, w_all, gain_ref = refs[6:9]
        att_ref, mid_ref, norm_ref, got, in_sem, out_sem, *sems = refs[9:]
        links = Links(("seq",))
        arriving = loads(list(zip(given, (tok, w_all, gain_ref))), in_sem)
        links.barrier()
        links.swap_start("seq", att_in, got, *sems)
        for copy in arriving:
            copy.wait()
        links.swap_wait("seq", att_in, got, *sems)
        attended = jnp.concatenate([got[j] for j in range(devices)], axis=1)
        att_ref[...] = attended
        mid = tok[...].astype(f32) + res_mult * dot_nn(attended, w_all[...])
        mid_ref[...] = mid
        scale = lax.rsqrt(jnp.mean(mid * mid, axis=-1, keepdims=True) + norm_eps)
        norm_ref[...] = (mid * scale * gain_row(gain_ref, 1)).astype(bf16)
        for copy in loads(list(zip((att_ref, mid_ref, norm_ref), results)), out_sem):
            copy.wait()

    hbm = pl.BlockSpec(memory_space=pl.ANY)
    dma = pltpu.SemaphoreType.DMA
    return pl.pallas_call(
        kernel,
        name="attended_exchange",
        out_shape=outs,
        in_specs=[hbm] * 4,
        out_specs=[hbm] * 3,
        scratch_shapes=staged(ins)
        + staged(outs)
        + [pltpu.VMEM(attended_own.shape, bf16), dma((3,)), dma((3,))]
        + swap_sems(devices),
        compiler_params=pltpu.CompilerParams(
            collective_id=collective_id, has_side_effects=True, vmem_limit_bytes=60 << 20
        ),
    )(attended_own, *ins)


def middle_exchange(
    collective_id, moe_sum, gate_cot, normed, router, mask, mid, out_grad, gain, w_out, attended, cols
):
    devices, gate_rows, rows = gate_cot.shape
    width = normed.shape[1]
    experts = gate_rows

    ins = [moe_sum, gate_cot, normed, router, mask, mid, out_grad, gain, w_out, attended]
    outs = [
        jax.ShapeDtypeStruct((width, LANES), bf16),
        jax.ShapeDtypeStruct((rows, width), f32),
        jax.ShapeDtypeStruct((width, width), bf16),
    ]

    def kernel(*refs):
        given, heads_out, results, refs = refs[:10], refs[10], refs[11:14], refs[14:]
        (
            moe_ref, gate_ref, norm_ref, router_ref, mask_ref, mid_ref, cot_ref, gain_ref, w_all, att_ref,
            pack_out, mid_cot_out, wo_out, give, in_sem, out_sem, *sems,
        ) = refs
        links = Links(("seq",))
        arriving = loads(list(zip(given, refs[:10])), in_sem)
        links.barrier()
        for copy in arriving:
            copy.wait()
        there = mask_ref[...] > 0
        logits = jnp.where(there, dot_nn(norm_ref[...], router_ref[...]), -1e30)
        gates = jnp.where(
            there, jnp.exp(logits - jnp.max(logits, axis=1, keepdims=True)), 0.0
        )
        gates = gates / jnp.sum(gates, axis=1, keepdims=True)
        gate = gate_ref[0]
        for j in range(1, devices):
            gate = gate + gate_ref[j]
        gate = jnp.concatenate([gate, jnp.zeros((LANES - gate_rows, rows), f32)], axis=0).T
        pick_cot = gates * (gate - jnp.sum(gates * gate, axis=1, keepdims=True))
        logit_cot = pick_cot.astype(bf16)
        cot = moe_ref[...] + dot_nt(logit_cot, router_ref[...])
        mid = mid_ref[...]
        scale = lax.rsqrt(jnp.mean(mid * mid, axis=-1, keepdims=True) + norm_eps)
        gain_grad = jnp.sum(cot * mid * scale, axis=0, keepdims=True)
        weighted = cot * gain_row(gain_ref, 1)
        mid_cot = (
            cot_ref[...].astype(f32)
            + scale * weighted
            - mid * (scale * scale * scale) * jnp.mean(weighted * mid, axis=-1, keepdims=True)
        )
        mid_cot_out[...] = mid_cot
        branch_cot = (res_mult * mid_cot).astype(bf16)
        attended_cot = dot_nt(branch_cot, w_all[...]).astype(bf16)
        for j in range(devices):
            give[j] = attended_cot[:, j * cols : (j + 1) * cols]
        links.swap_start("seq", give, heads_out, *sems)
        wo_out[...] = dot_tn(att_ref[...], branch_cot).astype(bf16)
        pack = dot_tn(norm_ref[...], logit_cot)
        lane = lax.broadcasted_iota(jnp.int32, pack.shape, 1)
        pack_out[...] = jnp.where(
            lane == experts, jnp.broadcast_to(gain_grad, (LANES, width)).T, pack
        ).astype(bf16)
        for copy in loads(list(zip((pack_out, mid_cot_out, wo_out), results)), out_sem):
            copy.wait()
        links.swap_wait("seq", give, heads_out, *sems)

    hbm = pl.BlockSpec(memory_space=pl.ANY)
    dma = pltpu.SemaphoreType.DMA
    return pl.pallas_call(
        kernel,
        name="middle_exchange",
        out_shape=[jax.ShapeDtypeStruct((devices, rows, cols), bf16)] + outs,
        in_specs=[hbm] * 10,
        out_specs=[hbm] * 4,
        scratch_shapes=staged(ins)
        + staged(outs)
        + [pltpu.VMEM((devices, rows, cols), bf16), dma((10,)), dma((3,))]
        + swap_sems(devices),
        compiler_params=pltpu.CompilerParams(
            collective_id=collective_id, has_side_effects=True, vmem_limit_bytes=60 << 20
        ),
    )(*ins)


def finish(e_grads, grad_qkv, grad_wo, pack, input_grad, output, weights, gain, heads, experts):
    own_experts, e_rows, e_cols = e_grads.shape
    devices, out_rows, _ = grad_qkv.shape
    q_width = heads * HEAD_SIZE
    share = devices // KEY_VALUE_HEADS if devices > KEY_VALUE_HEADS else 1
    steps = 4
    chunk = e_rows // steps
    me = lax.axis_index("seq").astype(jnp.int32).reshape(1)

    def kernel(
        me_ref, e_ref, qkv_ref, wo_ref, pack_ref, in_ref, out_ref, wq, wk, wv, gain_ref,
        e_in, e_out, gq, gk, gv, gwo, grouter, ggain_m, ggain_a, in_grad, output_ref,
    ):
        e_in[...] = e_ref[:, :, : 2 * FFE].astype(f32)
        e_out[...] = e_ref[:, :, 2 * FFE :].astype(f32)

        @pl.when(pl.program_id(0) == 0)
        def _():
            blocks = [qkv_ref[j].astype(f32) for j in range(devices)]

            def per_head(first):
                heads_of = []
                for j in range(KEY_VALUE_HEADS):
                    part = blocks[j * share][:, first : first + HEAD_SIZE]
                    for i in range(1, share):
                        part = part + blocks[j * share + i][:, first : first + HEAD_SIZE]
                    heads_of.append(part)
                return jnp.concatenate(heads_of, axis=1)

            grad_q = jnp.concatenate([b[:, :q_width] for b in blocks], axis=1)
            grad_k = per_head(HEADS_LANES)
            grad_v = per_head(HEADS_LANES + HEAD_SIZE)
            gq[...], gk[...], gv[...] = grad_q, grad_k, grad_v

            def rounded(ref):
                return ref[...].astype(bf16).astype(f32)

            def row(column):
                return jnp.broadcast_to(column, (out_rows, LANES)).T[:1]

            gain_grad = (
                jnp.sum(rounded(wq) * grad_q, axis=1, keepdims=True)
                + jnp.sum(rounded(wk) * grad_k, axis=1, keepdims=True)
                + jnp.sum(rounded(wv) * grad_v, axis=1, keepdims=True)
            )
            own = lax.broadcasted_iota(jnp.int32, (devices, 1), 0) == me_ref[0]
            own_gain = jnp.sum(jnp.where(own, rounded(gain_ref), 0.0), axis=0, keepdims=True)
            ggain_a[...] = row(gain_grad) / own_gain
            gwo[...] = wo_ref[...]
            grouter[...] = pack_ref[...].T[:experts]
            ggain_m[...] = row(pack_ref[:, experts : experts + 1])
            in_grad[...] = in_ref[...]
            output_ref[...] = out_ref[...]

    def whole(x):
        return pl.BlockSpec(x.shape, lambda i, _: (0,) * len(x.shape))

    def own_rows(x):
        return pl.BlockSpec((out_rows, x.shape[1]), lambda i, me_ref: (me_ref[0], 0))

    def shape(*dims, dtype=f32):
        return jax.ShapeDtypeStruct(dims, dtype)

    rest = [grad_qkv, grad_wo, pack, input_grad, output]
    kv_width = KEY_VALUE_HEADS * HEAD_SIZE
    small = [
        shape(out_rows, devices * q_width),
        shape(out_rows, kv_width),
        shape(out_rows, kv_width),
        shape(*grad_wo.shape),
        shape(experts, out_rows),
        shape(1, out_rows),
        shape(1, out_rows),
        shape(*input_grad.shape, dtype=bf16),
        shape(*output.shape, dtype=bf16),
    ]
    return pl.pallas_call(
        kernel,
        name="finish",
        grid_spec=pltpu.PrefetchScalarGridSpec(
            num_scalar_prefetch=1,
            grid=(steps,),
            in_specs=[pl.BlockSpec((own_experts, chunk, e_cols), lambda i, _: (0, i, 0))]
            + [whole(x) for x in rest]
            + [own_rows(x) for x in weights]
            + [whole(gain)],
            out_specs=[
                pl.BlockSpec((own_experts, chunk, 2 * FFE), lambda i, _: (0, i, 0)),
                pl.BlockSpec((own_experts, chunk, FFE), lambda i, _: (0, i, 0)),
            ]
            + [whole(x) for x in small],
        ),
        out_shape=[
            shape(own_experts, e_rows, 2 * FFE),
            shape(own_experts, e_rows, FFE),
        ]
        + small,
        cost_estimate=pl.CostEstimate(flops=0, bytes_accessed=8 << 20, transcendentals=0),
        compiler_params=pltpu.CompilerParams(
            dimension_semantics=("arbitrary",), vmem_limit_bytes=60 << 20
        ),
    )(me, e_grads, *rest, *weights, gain)


def first_exchange(collective_id, tokens, out_grad, docs, mask, misc, gains, w_query, w_key, w_value, w_out):
    devices, parts = lax.axis_size("seq"), lax.axis_size("dp")
    w_rows, width = w_out.shape
    heads = QUERY_HEADS // devices
    q_width = heads * HEAD_SIZE
    group = QUERY_HEADS // KEY_VALUE_HEADS
    w_cols = HEADS_LANES + LANES
    weights = [w_query, w_key, w_value, w_out]

    def prepare(refs):
        given, (wq, wk, wv, wo, w_all, wo_low, sem) = refs[:4], refs[4:]
        for copy in loads(list(zip(given, (wq, wk, wv, wo))), sem):
            copy.wait()
        wo_low[...] = wo[...].astype(bf16)
        for s in range(devices):
            kv = s * heads // group * HEAD_SIZE
            pieces = [wq[:, s * q_width : (s + 1) * q_width]]
            if q_width < HEADS_LANES:
                pieces.append(jnp.zeros((w_rows, HEADS_LANES - q_width), f32))
            pieces += [wk[:, kv : kv + HEAD_SIZE], wv[:, kv : kv + HEAD_SIZE]]
            w_all[s] = jnp.concatenate(pieces, axis=1).astype(bf16)

    return exchange(
        collective_id,
        [
            ("gather", "seq", tokens, None),
            ("gather", "seq", docs, None),
            ("gather", "seq", mask, None),
            ("shift", "seq", out_grad, None),
            ("share", "dp", misc, None),
            ("gather", "dp", gains, None),
            ("gather", "dp", jax.ShapeDtypeStruct((w_rows, w_cols), bf16), 0),
            ("share", "dp", jax.ShapeDtypeStruct((w_rows, width), bf16), 1),
        ],
        prepare=prepare,
        given=weights,
        work=staged(weights)
        + [
            pltpu.VMEM((devices, w_rows, w_cols), bf16),
            pltpu.VMEM((w_rows, width), bf16),
            pltpu.SemaphoreType.DMA((4,)),
        ],
        made=lambda refs: (refs[8].at[lax.axis_index("seq")], refs[9]),
        keep=(jax.ShapeDtypeStruct((devices, w_rows, w_cols), bf16), 8),
    )


def prepare(expert_in, expert_out, picks, docs, w_router, gain_attn, gain_moe):
    own_experts, w_rows, _ = expert_in.shape
    rows, experts = picks.shape[1], w_router.shape[0]
    steps = 4
    chunk = w_rows // steps

    def kernel(
        e_in, e_out, picks_ref, docs_ref, router, gain_a, gain_m, low, mask, docs_out, misc, gains
    ):
        low[:, :, : 2 * FFE] = e_in[...].astype(bf16)
        low[:, :, 2 * FFE :] = e_out[...].astype(bf16)

        @pl.when(pl.program_id(0) == 0)
        def _():
            expert = lax.broadcasted_iota(jnp.int32, (LANES, rows), 0)
            chosen = picks_ref[:1] == expert
            for k in range(1, TOP):
                chosen = chosen | (picks_ref[k : k + 1] == expert)
            mask[...] = jnp.where(chosen, 1.0, 0.0).T.astype(bf16)
            docs_out[...] = jnp.broadcast_to(docs_ref[...], docs_out.shape)
            misc[...] = jnp.concatenate(
                [router[...], jnp.zeros((LANES - experts, w_rows), f32)], axis=0
            ).T.astype(bf16)
            upper = lax.broadcasted_iota(jnp.int32, (8, w_rows), 0) == 0
            gains[...] = jnp.where(upper, gain_a[...], gain_m[...]).astype(bf16)

    def whole(shape):
        return pl.BlockSpec(shape, lambda i: (0,) * len(shape))

    def part(x):
        return pl.BlockSpec((own_experts, chunk, x.shape[2]), lambda i: (0, i, 0))

    small = [picks, docs, w_router, gain_attn[None], gain_moe[None]]
    outs = [
        jax.ShapeDtypeStruct((rows, LANES), bf16),
        jax.ShapeDtypeStruct((8, rows), jnp.int32),
        jax.ShapeDtypeStruct((w_rows, LANES), bf16),
        jax.ShapeDtypeStruct((8, w_rows), bf16),
    ]
    return pl.pallas_call(
        kernel,
        name="prepare",
        grid=(steps,),
        out_shape=[jax.ShapeDtypeStruct((own_experts, w_rows, 3 * FFE), bf16)] + outs,
        in_specs=[part(expert_in), part(expert_out)] + [whole(x.shape) for x in small],
        out_specs=[pl.BlockSpec((own_experts, chunk, 3 * FFE), lambda i: (0, i, 0))]
        + [whole(x.shape) for x in outs],
        compiler_params=pltpu.CompilerParams(
            dimension_semantics=("arbitrary",), vmem_limit_bytes=60 << 20
        ),
    )(expert_in, expert_out, *small)


def final_exchange(
    collective_id, qkv_cot, normed, token_grads, w_full, tokens, mid_cot, gain, mid, branches
):
    devices, parts = lax.axis_size("seq"), lax.axis_size("dp")
    chips = devices // 2
    _, rows, cols = qkv_cot.shape
    width = tokens.shape[1]
    out_rows = token_grads[0].shape[2]
    gq_shape = (parts, devices, out_rows, cols)
    count = len(token_grads)
    wides = [x.shape[3] for x in token_grads]
    token_grads = [x.reshape(parts, chips, 2, out_rows, x.shape[3]) for x in token_grads]

    ins = [w_full, normed, qkv_cot, tokens, mid_cot, gain, mid, *branches]

    def kernel(*refs):
        qkv_in = refs[0]
        gt_in = refs[1 : 1 + count]
        given = refs[1 + count : 1 + count + len(ins)]
        refs = refs[1 + count + len(ins) :]
        in_grad_out, output_out, gq_out = refs[:3]
        gt_out = refs[3 : 3 + count]
        refs = refs[3 + count :]
        (
            qkv_tok, nac, gq_in, grad, gq_recv, gq_sum,
            q_send, q_recv, local, gq_send, gq_rsem, gqz_send, gqz_recv, gq_local,
        ) = refs[:14]
        work = [refs[14 + 11 * i : 25 + 11 * i] for i in range(count)]
        refs = refs[14 + 11 * count :]
        local_ins, (in_grad, output, in_sem, out_sem) = refs[: len(ins)], refs[len(ins) :]
        w_all, normed_all, qkv_all, tok_ref, mid_cot_ref, gain_ref, mid_ref, *y_refs = local_ins
        me, my = lax.axis_index("seq"), lax.axis_index("dp")
        chip, core = me // 2, lax.rem(me, 2)
        sibling = me + 1 - 2 * core
        arriving = loads(list(zip(given, local_ins)), in_sem)
        barrier = pltpu.get_barrier_semaphore()
        for axis, index, size in (("seq", me, devices), ("dp", my, parts)):
            for k in range(1, size):
                pl.semaphore_signal(
                    barrier,
                    inc=1,
                    device_id={axis: lax.rem(index + k, size)},
                    device_id_type=MESH,
                )
        pl.semaphore_wait(barrier, devices + parts - 2)

        def remote(axis, src, dst, send, recv, to):
            return pltpu.make_async_remote_copy(
                src_ref=src,
                dst_ref=dst,
                send_sem=send,
                recv_sem=recv,
                device_id={axis: to},
                device_id_type=MESH,
            )

        sent = []

        def columns(j):
            return qkv_tok.at[:, pl.ds(pl.multiple_of(j * cols, cols), cols)]

        for x, w in zip(gt_in, work):
            mine, theirs, far, near, last, sems, dp_send, dp_recv, z_send, z_recv, _ = w
            copy = remote(
                "seq", x.at[:, :, 1 - core], theirs, sems.at[0], sems.at[1], sibling
            )
            copy.start()
            sent.append(copy)
            pltpu.make_async_copy(x.at[:, :, core], mine, sems.at[2]).start()
        own = pltpu.make_async_copy(qkv_in.at[me], columns(me), local)
        own.start()
        for k in range(1, devices):
            to = lax.rem(me + k, devices)
            copy = remote(
                "seq", qkv_in.at[to], columns(me), q_send.at[k - 1], q_recv.at[k - 1], to
            )
            copy.start()
            sent.append(copy)

        for x, w in zip(gt_in, work):
            mine, theirs, far, near, last, sems, dp_send, dp_recv, z_send, z_recv, _ = w
            remote("seq", x.at[:, :, core], theirs, sems.at[0], sems.at[1], sibling).wait_recv()
            pltpu.make_async_copy(x.at[:, :, core], mine, sems.at[2]).wait()
            mine[...] = (mine[...].astype(f32) + theirs[...].astype(f32)).astype(bf16)
            for k in range(1, parts):
                to = lax.rem(my + k, parts)
                copy = remote(
                    "dp", mine.at[to], far.at[k - 1], dp_send.at[k - 1], dp_recv.at[k - 1], to
                )
                copy.start()
                sent.append(copy)

        for copy in arriving:
            copy.wait()
        grad[...] = jnp.zeros_like(grad)

        @pl.loop(0, devices)
        def _(j):
            grad[...] += dot_tn(normed_all[j], qkv_all[j])

        gq_in[...] = grad[...].astype(bf16).reshape(gq_shape)
        for k in range(1, parts):
            to = lax.rem(my + k, parts)
            copy = remote(
                "dp", gq_in.at[to], gq_recv.at[my], gq_send.at[k - 1], gq_rsem.at[k - 1], to
            )
            copy.start()
            sent.append(copy)
        own_q = pltpu.make_async_copy(gq_in.at[my], gq_recv.at[my], gq_local)
        own_q.start()
        total = y_refs[0][...].astype(f32)
        for k in range(1, len(branches)):
            total = total + y_refs[k][...].astype(f32)
        output[...] = (mid_ref[...] + res_mult * total).astype(bf16)
        leaving = [pltpu.make_async_copy(output, output_out, out_sem.at[0])]
        leaving[0].start()

        for k in range(devices):
            frm = lax.rem(me + devices - k, devices)
            if k == 0:
                own.wait()
            else:
                remote(
                    "seq", qkv_in.at[frm], columns(frm), q_send.at[k - 1], q_recv.at[k - 1], frm
                ).wait_recv()
            part = dot_nt(columns(frm)[...], w_all[frm])
            nac[...] = part if k == 0 else nac[...] + part

        resid = tok_ref[...].astype(f32)
        scale = lax.rsqrt(jnp.mean(resid * resid, axis=-1, keepdims=True) + norm_eps)
        weighted = nac[...] * gain_row(gain_ref, 0)
        in_grad[...] = (
            mid_cot_ref[...]
            + scale * weighted
            - resid
            * (scale * scale * scale)
            * jnp.mean(weighted * resid, axis=-1, keepdims=True)
        ).astype(bf16)

        leaving.append(pltpu.make_async_copy(in_grad, in_grad_out, out_sem.at[1]))
        leaving[1].start()
        own_q.wait()
        for k in range(1, parts):
            frm = lax.rem(my + parts - k, parts)
            remote(
                "dp", gq_in.at[frm], gq_recv.at[frm], gq_send.at[k - 1], gq_rsem.at[k - 1], frm
            ).wait_recv()
        summed = gq_recv[0].astype(f32)
        for p in range(1, parts):
            summed = summed + gq_recv[p].astype(f32)
        gq_sum[...] = summed.astype(bf16)
        own_z = pltpu.make_async_copy(gq_sum.at[me], gq_out.at[me], gq_local)
        own_z.start()
        for k in range(1, devices):
            to = lax.rem(me + k, devices)
            copy = remote(
                "seq", gq_sum.at[to], gq_out.at[me], gqz_send.at[k - 1], gqz_recv.at[k - 1], to
            )
            copy.start()
            sent.append(copy)
        for w in work:
            mine, theirs, far, near, last, sems, dp_send, dp_recv, z_send, z_recv, _ = w
            summed = mine[my].astype(f32)
            for k in range(1, parts):
                remote(
                    "dp", mine.at[0], far.at[k - 1], dp_send.at[k - 1], dp_recv.at[k - 1], my
                ).wait_recv()
                summed = summed + far[k - 1].astype(f32)
            near[...] = summed.astype(bf16)
            for k in range(1, chips):
                to = lax.rem(chip + k, chips)
                copy = remote(
                    "seq",
                    near.at[to],
                    last.at[k - 1],
                    z_send.at[k - 1],
                    z_recv.at[k - 1],
                    2 * to + core,
                )
                copy.start()
                sent.append(copy)

        for o, w in zip(gt_out, work):
            mine, theirs, far, near, last, sems, dp_send, dp_recv, z_send, z_recv, _ = w
            summed = near[chip].astype(f32)
            for k in range(1, chips):
                remote(
                    "seq", near.at[0], last.at[k - 1], z_send.at[k - 1], z_recv.at[k - 1], me
                ).wait_recv()
                summed = summed + last[k - 1].astype(f32)
            o[...] = summed
        own_z.wait()
        for k in range(1, devices):
            frm = lax.rem(me + devices - k, devices)
            remote(
                "seq", gq_sum.at[frm], gq_out.at[frm], gqz_send.at[k - 1], gqz_recv.at[k - 1], frm
            ).wait_recv()
        for copy in sent:
            copy.wait_send()
        for copy in leaving:
            copy.wait()

    hbm = pl.BlockSpec(memory_space=pl.ANY)
    vmem = pl.BlockSpec(memory_space=pltpu.VMEM)
    dma = pltpu.SemaphoreType.DMA
    scratch = [
        pltpu.VMEM((rows, devices * cols), bf16),
        pltpu.VMEM((rows, width), f32),
        pltpu.VMEM(gq_shape, bf16),
        pltpu.VMEM((width, cols), f32),
        pltpu.VMEM(gq_shape, bf16),
        pltpu.VMEM(gq_shape[1:], bf16),
        dma((devices - 1,)),
        dma((devices - 1,)),
        dma,
        dma((parts - 1,)),
        dma((parts - 1,)),
        dma((devices - 1,)),
        dma((devices - 1,)),
        dma,
    ]
    for wide in wides:
        piece = (out_rows, wide)
        scratch += [
            pltpu.VMEM((parts, chips) + piece, bf16),
            pltpu.VMEM((parts, chips) + piece, bf16),
            pltpu.VMEM((parts - 1, chips) + piece, bf16),
            pltpu.VMEM((chips,) + piece, bf16),
            pltpu.VMEM((chips - 1,) + piece, bf16),
            dma((3,)),
            dma((parts - 1,)),
            dma((parts - 1,)),
            dma((chips - 1,)),
            dma((chips - 1,)),
            dma,
        ]
    scratch += staged(ins) + [
        pltpu.VMEM((rows, width), bf16),
        pltpu.VMEM((rows, width), bf16),
        dma((len(ins),)),
        dma((2,)),
    ]
    return pl.pallas_call(
        kernel,
        name="final_exchange",
        out_shape=[
            jax.ShapeDtypeStruct((rows, width), bf16),
            jax.ShapeDtypeStruct((rows, width), bf16),
            jax.ShapeDtypeStruct(gq_shape[1:], bf16),
        ]
        + [jax.ShapeDtypeStruct((out_rows, wide), f32) for wide in wides],
        in_specs=[hbm] * (1 + count + len(ins)),
        out_specs=[hbm] * 3 + [vmem] * count,
        scratch_shapes=scratch,
        compiler_params=pltpu.CompilerParams(
            collective_id=collective_id, has_side_effects=True, vmem_limit_bytes=60 << 20
        ),
    )(qkv_cot, *token_grads, *ins)


def on_device(
    tokens,
    out_grad,
    doc_ids,
    expert_picks,
    w_query,
    key_weight_matrix,
    value_weight_matrix,
    w_out,
    w_router,
    gain_attn,
    gain_moe,
    expert_in,
    expert_out,
):
    devices, parts = lax.axis_size("seq"), lax.axis_size("dp")
    me = lax.axis_index("seq")
    rows, width = tokens.shape[1:]
    length = rows * devices
    experts = w_router.shape[1]
    heads = QUERY_HEADS // devices
    group = QUERY_HEADS // KEY_VALUE_HEADS
    q_width = heads * HEAD_SIZE
    w_rows = w_query.shape[0]

    w_cols = HEADS_LANES + LANES
    low, mask, doc_rows, misc, gains = prepare(
        expert_in, expert_out, expert_picks[0].T, doc_ids, w_router.T, gain_attn, gain_moe
    )
    expert_full = lax.all_gather(low, "dp", axis=1, tiled=True)
    chips = devices // 2

    def shift(x, k):
        return lax.ppermute(x, "seq", [(i, (i + 2 * k) % devices) for i in range(devices)])

    tok_all, doc_all, mask_all, middle_cot, misc_full, gains_full, w_own_all, wo_full, w_all = first_exchange(
        0,
        tokens[0],
        out_grad[0],
        doc_rows,
        mask,
        misc,
        gains,
        w_query,
        key_weight_matrix,
        value_weight_matrix,
        w_out,
    )
    w_full = lax.all_gather(w_all, "dp", axis=1, tiled=True)
    held, tok_all = lax.optimization_barrier((out_grad[0], tok_all))
    cots = [held] + [
        middle_cot if k == chips // 2 else shift(held, k) for k in range(1, chips)
    ]
    w_own_all = w_own_all.reshape(width, w_cols)
    wo_full = wo_full.reshape(width, width)
    misc_full = misc_full.reshape(width, LANES)
    table = rope_table(devices, rows)

    normed_a, q_all, kv_all, attended_own, ot, lse = attend_forward(
        tok_all, w_own_all, gains_full, table, doc_all, heads
    )
    attended, mid, normed_m = attended_exchange(
        1, attended_own, tokens[0], wo_full, gains_full
    )
    (_, _, _, moe_sum, gate_cot, e_grads, *branches) = moe_exchange(
        2, normed_m, cots, mask_all, misc_full, expert_full
    )
    e_grads = lax.psum_scatter(e_grads, "dp", scatter_dimension=1, tiled=True)
    heads_cot, router_pack, mid_cot, grad_wo = middle_exchange(
        4, moe_sum, gate_cot, normed_m, misc_full, mask, mid, out_grad[0], gains_full,
        wo_full, attended, q_width,
    )
    heads_cot, branches = lax.optimization_barrier((heads_cot, branches))
    branches = [
        branches[0],
        lax.ppermute(branches[1], "seq", [(i, i ^ 2) for i in range(devices)]),
    ] + [shift(branches[1 + k], 2 * k) for k in range(1, chips // 2)]
    qkv_cot = attend_backward(q_all, kv_all, heads_cot, ot, lse, table, doc_all, heads)
    qkv_cot, branches = lax.optimization_barrier((qkv_cot, branches))
    out_rows = w_rows // devices
    input_grad, output, grad_qkv, grad_wo, router_pack = final_exchange(
        5,
        qkv_cot,
        normed_a,
        [
            grad_wo.reshape(parts, devices, out_rows, width),
            router_pack.reshape(parts, devices, out_rows, LANES),
        ],
        w_full,
        tokens[0],
        mid_cot,
        gains_full,
        mid,
        branches,
    )

    (
        grad_e_in, grad_e_out, grad_wq, grad_wk, grad_wv, grad_wo, grad_router, grad_gain_m,
        grad_gain_a, input_grad, output,
    ) = finish(
        e_grads,
        grad_qkv,
        grad_wo,
        router_pack,
        input_grad,
        output,
        [w_query, key_weight_matrix, value_weight_matrix],
        gain_attn.reshape(devices, out_rows),
        heads,
        experts,
    )
    input_grad, output = input_grad[None], output[None]
    grad_router = grad_router.T
    grad_gain_a = grad_gain_a.reshape(out_rows)
    grad_gain_m = grad_gain_m.reshape(out_rows)
    return (
        output,
        input_grad,
        grad_wq,
        grad_wk,
        grad_wv,
        grad_wo,
        grad_router,
        grad_gain_a,
        grad_gain_m,
        grad_e_in,
        grad_e_out,
    )


def solution(mesh):
    return jax.shard_map(
        on_device,
        mesh=mesh,
        in_specs=(
            P("dp", "seq", None),
            P("dp", "seq", None),
            P("dp", "seq"),
            P("dp", "seq", None),
            P("dp", None),
            P("dp", None),
            P("dp", None),
            P("dp", None),
            P("dp", None),
            P("dp"),
            P("dp"),
            P("seq", "dp", None),
            P("seq", "dp", None),
        ),
        out_specs=(
            P("dp", "seq", None),
            P("dp", "seq", None),
            P(("dp", "seq"), None),
            P(("dp", "seq"), None),
            P(("dp", "seq"), None),
            P(("dp", "seq"), None),
            P(("dp", "seq"), None),
            P(("dp", "seq")),
            P(("dp", "seq")),
            P("seq", "dp", None),
            P("seq", "dp", None),
        ),
        check_vma=False,
    )
```

```python
import functools

import jax
import jax.numpy as jnp
import numpy as np
from jax import lax
from jax.experimental import pallas as pl
from jax.experimental.pallas import tpu as pltpu
from jax.sharding import PartitionSpec as P

MESH = pl.DeviceIdType.MESH
PIECES = 2


def _block(ref, j, cut):
    if cut is None:
        return ref.at[j]
    return ref.at[:, pl.ds(pl.multiple_of(j * cut, cut), cut)]


def exchange(collective_id, ops, prepare=None, given=(), work=(), made=None, keep=None):
    axes = tuple(dict.fromkeys(axis for _, axis, _, _ in ops))
    size = {axis: lax.axis_size(axis) for axis in axes}
    out_shapes, out_specs, scratch, places = [], [], [], []
    for kind, axis, x, cut in ops:
        count = size[axis]
        out_spec = pl.BlockSpec(memory_space=pl.ANY)
        extra = []
        lead = (PIECES,) if kind == "gather" and axis == "seq" else ()
        if kind == "shift":
            shape, dtype, copies = x.shape, x.dtype, 1
        elif kind == "share":
            shape, dtype, copies = (count,) + x.shape, x.dtype, 2 * (count - 1)
        elif kind == "gather":
            shape, dtype = (count,) + x.shape, x.dtype
            copies = count - 1 if axis == "dp" else 3 + 4 * (count // 2 - 1)
        elif kind == "swap":
            copies, dtype = count - 1, x.dtype
            if cut is None:
                shape = x.shape
            elif cut[0] == "in":
                shape = (count, x.shape[0], cut[1])
            else:
                shape = (x.shape[1], count * cut[1])
        out_shapes.append(jax.ShapeDtypeStruct(shape, dtype))
        out_specs.append(out_spec)
        places.append((len(scratch), len(extra)))
        scratch += [
            pltpu.SemaphoreType.DMA(lead + (copies,)),
            pltpu.SemaphoreType.DMA(lead + (max(copies, count),)),
            pltpu.SemaphoreType.DMA,
        ] + extra

    early = [x for _, _, x, cut in ops if not isinstance(cut, int)]
    own_scratch = len(scratch)

    def kernel(*refs):
        ins, refs = list(refs[: len(early)]), refs[len(early) :]
        extra_in, refs = refs[: len(given)], refs[len(given) :]
        outs, refs = refs[: len(ops)], refs[len(ops) :]
        if keep is not None:
            kept, refs = refs[0], refs[1:]
        work, extra_work = refs[:own_scratch], refs[own_scratch:]
        ins += [None] * (len(ops) - len(early))
        me = {axis: lax.axis_index(axis) for axis in axes}
        barrier = pltpu.get_barrier_semaphore()
        for axis in axes:
            for k in range(1, size[axis]):
                pl.semaphore_signal(
                    barrier,
                    inc=1,
                    device_id={axis: lax.rem(me[axis] + k, size[axis])},
                    device_id_type=MESH,
                )
        pl.semaphore_wait(barrier, sum(size[axis] - 1 for axis in axes))

        def remote(axis, src, dst, send, recv, to):
            return pltpu.make_async_remote_copy(
                src_ref=src,
                dst_ref=dst,
                send_sem=send,
                recv_sem=recv,
                device_id={axis: to},
                device_id_type=MESH,
            )

        second, third = [], []
        for (kind, axis, _, cut), x, o, (at, extra) in zip(ops, ins, outs, places):
            if isinstance(cut, int):
                if x is None and cut == 0:
                    all_refs = list(extra_in) + list(extra_work[:-1])
                    prepare(all_refs)
                    late = made(all_refs)
                    leave = pltpu.make_async_copy(all_refs[keep[1]], kept, extra_work[-1])
                    leave.start()
                    third.append(leave.wait)
                x, cut = late[cut], None
            send, recv, local = work[at : at + 3]
            count, my = size[axis], me[axis]
            if kind == "swap":
                into = cut[1] if cut is not None and cut[0] == "out" else None
                outof = cut[1] if cut is not None and cut[0] == "in" else None
                own = pltpu.make_async_copy(_block(x, my, outof), _block(o, my, into), local)
                own.start()
                third.append(own.wait)
                for k in range(1, count):
                    to = lax.rem(my + k, count)
                    copy = remote(
                        axis,
                        _block(x, to, outof),
                        _block(o, my, into),
                        send.at[k - 1],
                        recv.at[k - 1],
                        to,
                    )
                    copy.start()
                    frm = lax.rem(my + count - k, count)
                    arrive = remote(
                        axis,
                        _block(x, to, outof),
                        _block(o, frm, into),
                        send.at[k - 1],
                        recv.at[k - 1],
                        to,
                    )
                    third.append(copy.wait_send)
                    third.append(arrive.wait_recv)
            elif kind == "gather" and axis == "dp":
                own = pltpu.make_async_copy(x, o.at[my], local)
                own.start()
                third.append(own.wait)
                for k in range(1, count):
                    to = lax.rem(my + k, count)
                    frm = lax.rem(my + count - k, count)
                    copy = remote(axis, x, o.at[my], send.at[k - 1], recv.at[k - 1], to)
                    copy.start()
                    third.append(copy.wait_send)
                    third.append(
                        remote(
                            axis, x, o.at[frm], send.at[k - 1], recv.at[k - 1], to
                        ).wait_recv
                    )
            elif kind == "shift":
                copy = remote(
                    axis, x, o, send.at[0], recv.at[0], lax.rem(my + 2 * (count // 4), count)
                )
                second.append((count // 4 + 0.9, copy.start))
                third.append(copy.wait)
            elif kind == "share":
                seq, half = me["seq"], x.shape[0] // 2
                core = lax.rem(seq, 2)
                sibling = seq + 1 - 2 * core
                own = pltpu.make_async_copy(x, o.at[my], local)
                own.start()
                third.append(own.wait)

                def side_of(ref, which, half=half):
                    return ref.at[pl.ds(which * half, half)]

                def relay(k, axis=axis, x=x, o=o, send=send, recv=recv, count=count, my=my, core=core, sibling=sibling, side_of=side_of):
                    to = lax.rem(my + k, count)
                    frm = lax.rem(my + count - k, count)
                    remote(
                        axis,
                        side_of(x, core),
                        side_of(o.at[frm], core),
                        send.at[k - 1],
                        recv.at[k - 1],
                        to,
                    ).wait_recv()
                    slot = count - 2 + k
                    spot = side_of(o.at[frm], core)
                    over = remote("seq", spot, spot, send.at[slot], recv.at[slot], sibling)
                    over.start()
                    third.append(over.wait_send)
                    third.append(
                        remote(
                            "seq",
                            spot,
                            side_of(o.at[frm], 1 - core),
                            send.at[slot],
                            recv.at[slot],
                            sibling,
                        ).wait_recv
                    )

                for k in range(1, count):
                    to = lax.rem(my + k, count)
                    copy = remote(
                        axis,
                        side_of(x, core),
                        side_of(o.at[my], core),
                        send.at[k - 1],
                        recv.at[k - 1],
                        to,
                    )
                    copy.start()
                    third.append(copy.wait_send)
                    second.append((k + 0.75, functools.partial(relay, k)))
            elif kind == "gather":
                chips = count // 2
                chip, core = my // 2, lax.rem(my, 2)
                sibling = my + 1 - 2 * core
                own = pltpu.make_async_copy(x, o.at[my], local)
                own.start()
                third.append(own.wait)

                cuts = PIECES if x.shape[0] % (16 * PIECES) == 0 else 1
                size_of = x.shape[0] // cuts

                def cut_of(ref, i, size_of=size_of):
                    return ref.at[pl.ds(i * size_of, size_of)]

                def line(src, b, i, slot, to, axis=axis, o=o, send=send, recv=recv, core=core, cut_of=cut_of):
                    return remote(
                        axis, src, cut_of(o.at[2 * b + core], i), send.at[i, slot], recv.at[i, b], to
                    )

                def across(src, b, i, slot, half, axis=axis, o=o, send=send, recv=recv, chips=chips, sibling=sibling, cut_of=cut_of):
                    return remote(
                        axis,
                        src,
                        cut_of(o.at[2 * b + half], i),
                        send.at[i, slot],
                        recv.at[i, chips + b],
                        sibling,
                    )

                def guarded(where, act):
                    pl.when(where)(act)

                for i in range(cuts):
                    for slot, where, to in ((0, chip > 0, my - 2), (1, chip < chips - 1, my + 2)):
                        copy = line(cut_of(x, i), chip, i, slot, to)
                        guarded(where, copy.start)
                        third.append(functools.partial(guarded, where, copy.wait_send))
                for i in range(cuts):
                    copy = across(cut_of(x, i), chip, i, 2, core)
                    copy.start()
                    third.append(copy.wait_send)
                    third.append(across(cut_of(x, i), chip, i, 2, 1 - core).wait_recv)

                def hop(k, side, i, chips=chips, chip=chip, core=core, my=my, x=x, o=o, line=line, across=across, cut_of=cut_of):
                    b = chip + side * k
                    there = (b >= 0) & (b < chips)
                    onward = there & ((chip - side >= 0) & (chip - side < chips))
                    slot = 3 + (k - 1) * 4 + (side + 1)
                    spot = cut_of(o.at[2 * b + core], i)
                    further = line(spot, b, i, slot, my - 2 * side)
                    over = across(spot, b, i, slot + 1, core)
                    arrived = line(cut_of(x, i), b, i, slot, my)
                    brought = across(cut_of(x, i), b, i, slot + 1, 1 - core)

                    @pl.when(there)
                    def _():
                        arrived.wait_recv()

                    guarded(onward, further.start)
                    guarded(there, over.start)
                    third.append(functools.partial(guarded, onward, further.wait_send))
                    third.append(functools.partial(guarded, there, over.wait_send))
                    third.append(functools.partial(guarded, there, brought.wait_recv))

                for k in range(1, chips):
                    for i in range(cuts):
                        for side in (-1, 1):
                            second.append((k + i / cuts, functools.partial(hop, k, side, i)))
        for _, run in sorted(second, key=lambda item: item[0]):
            run()
        for wait in third:
            wait()

    return pl.pallas_call(
        kernel,
        name=f"exchange{collective_id}",
        out_shape=out_shapes + ([] if keep is None else [keep[0]]),
        in_specs=[pl.BlockSpec(memory_space=pl.ANY)] * (len(early) + len(given)),
        out_specs=out_specs + ([] if keep is None else [pl.BlockSpec(memory_space=pl.ANY)]),
        scratch_shapes=scratch
        + list(work)
        + ([] if keep is None else [pltpu.SemaphoreType.DMA]),
        compiler_params=pltpu.CompilerParams(
            collective_id=collective_id, has_side_effects=True, vmem_limit_bytes=60 << 20
        ),
    )(*early, *given)

QUERY_HEADS = 16
KEY_VALUE_HEADS = 8
HEAD_SIZE = 64
FFE = 512
TOP = 8

att_mult = 0.015625
res_mult = 0.22
norm_eps = 1e-06
rope_theta = 10000.0
LANES = 128
bf16 = jnp.bfloat16
f32 = jnp.float32
HEADS_LANES = 128


def dot_nt(a, b):
    return lax.dot_general(a, b, (((1,), (1,)), ((), ())), preferred_element_type=f32)


def dot_nn(a, b):
    return lax.dot_general(a, b, (((1,), (0,)), ((), ())), preferred_element_type=f32)


def dot_tn(a, b):
    return lax.dot_general(a, b, (((0,), (0,)), ((), ())), preferred_element_type=f32)


def turn(x):
    half = HEAD_SIZE // 2
    lane = lax.broadcasted_iota(jnp.int32, x.shape, 1)
    width = x.shape[1]
    return jnp.where(
        lax.rem(lane, HEAD_SIZE) < half, pltpu.roll(x, width - half, 1), pltpu.roll(x, half, 1)
    )


def rope_table(blocks, rows):
    half = HEAD_SIZE // 2
    frequency = np.float32(rope_theta) ** (
        -np.arange(half, dtype=np.float32) * np.float32(2.0) / np.float32(HEAD_SIZE)
    )
    angles = (frequency[:, None] * np.arange(blocks * rows, dtype=np.float32)[None, :]).astype(
        np.float32
    )
    table = np.concatenate([np.cos(angles), np.sin(angles)], axis=0).astype(np.float32)
    return jnp.asarray(table.reshape(HEAD_SIZE, blocks, rows).transpose(1, 0, 2))


def spread_table(table):
    half = HEAD_SIZE // 2
    turned = table.T
    cos, sin = turned[:, :half], turned[:, half:]
    return (
        jnp.concatenate([cos, cos] * (LANES // HEAD_SIZE), axis=1),
        jnp.concatenate([-sin, sin] * (LANES // HEAD_SIZE), axis=1),
    )


def across_lanes(row, lanes):
    return jnp.broadcast_to(row, (lanes, row.shape[1])).T


def first_block(docs_ref, i):
    docs = docs_ref[:, 0, :].astype(f32)
    own = lax.broadcasted_iota(jnp.int32, docs.shape, 0) == i
    lane = lax.broadcasted_iota(jnp.int32, docs.shape, 1)
    start = jnp.sum(jnp.where(own & (lane == 0), docs, 0.0))
    ends = (lane == docs.shape[1] - 1) & (docs < start)
    return jnp.sum(jnp.where(ends, 1.0, 0.0)).astype(jnp.int32)


def stack_heads(x, heads):
    return jnp.concatenate(
        [x[:, h * HEAD_SIZE : (h + 1) * HEAD_SIZE] for h in range(heads)], axis=0
    )


def gain_row(ref, which):
    return jnp.concatenate(
        [ref[p, which : which + 1, :] for p in range(ref.shape[0])], axis=1
    ).astype(f32)


def attend_forward(tok_all, w_own, gain, table, docs, heads):
    blocks, rows, width = tok_all.shape
    length = blocks * rows
    cols = heads * rows
    out_width = heads * HEAD_SIZE

    def kernel(tok, w, gain_ref, table_ref, docs_ref, na_ref, q_ref, kv_ref, att_ref, ot_ref, lse_ref, k_scr, vt_scr, doc_scr):
        i = pl.program_id(0)
        x = tok[0].astype(f32)
        scale = lax.rsqrt(jnp.mean(x * x, axis=-1, keepdims=True) + norm_eps)
        na = (x * scale * gain_row(gain_ref, 0)).astype(bf16)
        na_ref[0] = na
        qkv = dot_nn(na, w[...])
        c, s = spread_table(table_ref[0])
        q, kv = qkv[:, :HEADS_LANES], qkv[:, HEADS_LANES:]
        q = (q * c + turn(q) * s).astype(bf16)
        lane = lax.broadcasted_iota(jnp.int32, kv.shape, 1)
        kv = jnp.where(lane < HEAD_SIZE, kv * c + turn(kv) * s, kv).astype(bf16)
        q_ref[0] = q
        kv_ref[0] = kv
        k_scr[i] = kv[:, :HEAD_SIZE]
        vt_scr[i] = kv.astype(f32).T[HEAD_SIZE:].astype(bf16)
        q2 = stack_heads(q, heads)
        doc_row = docs_ref[i, :1].astype(f32)
        doc_scr[i] = across_lanes(doc_row, LANES)
        doc_query = jnp.concatenate([doc_row] * heads, axis=1)
        query = i * rows + lax.rem(lax.broadcasted_iota(jnp.int32, (1, cols), 1), rows)
        key_iota = lax.broadcasted_iota(jnp.int32, (rows, cols), 0)

        def step(j, carry):
            top, total, ot = carry
            scores = dot_nt(k_scr[j], q2) * att_mult
            key = key_iota + j * rows
            same = jnp.concatenate([doc_scr[j]] * (cols // LANES), axis=1) == doc_query
            scores = jnp.where(same & (key <= query), scores, -1e30)
            new_top = jnp.maximum(top, jnp.max(scores, axis=0, keepdims=True))
            p = jnp.exp(scores - new_top)
            keep = jnp.exp(top - new_top)
            total = total * keep + jnp.sum(p, axis=0, keepdims=True)
            ot = ot * keep + dot_nn(vt_scr[j], p.astype(bf16))
            return new_top, total, ot

        top, total, ot = lax.fori_loop(
            first_block(docs_ref, i),
            i + 1,
            step,
            (
                jnp.full((1, cols), -1e30, f32),
                jnp.zeros((1, cols), f32),
                jnp.zeros((HEAD_SIZE, cols), f32),
            ),
        )
        ot = ot / total
        ot_ref[0] = ot
        lse_ref[0] = top + jnp.log(total)
        out = ot.T
        att_ref[0] = jnp.concatenate(
            [out[h * rows : (h + 1) * rows] for h in range(heads)], axis=1
        ).astype(bf16)

    def block(shape):
        return pl.BlockSpec((1,) + shape, lambda i: (i, 0, 0))

    def whole(shape):
        return pl.BlockSpec(shape, lambda i: (0,) * len(shape))

    grid_spec = pltpu.PrefetchScalarGridSpec(
        num_scalar_prefetch=0,
        grid=(blocks,),
        in_specs=[
            block((rows, width)),
            whole(w_own.shape),
            whole(gain.shape),
            block((HEAD_SIZE, rows)),
            whole(docs.shape),
        ],
        out_specs=[
            block((rows, width)),
            block((rows, HEADS_LANES)),
            block((rows, LANES)),
            block((rows, out_width)),
            block((HEAD_SIZE, cols)),
            block((1, cols)),
        ],
        scratch_shapes=[
            pltpu.VMEM((blocks, rows, HEAD_SIZE), bf16),
            pltpu.VMEM((blocks, HEAD_SIZE, rows), bf16),
            pltpu.VMEM((blocks, rows, LANES), f32),
        ],
    )
    return pl.pallas_call(
        kernel,
        name="attend_forward",
        grid_spec=grid_spec,
        out_shape=[
            jax.ShapeDtypeStruct((blocks, rows, width), bf16),
            jax.ShapeDtypeStruct((blocks, rows, HEADS_LANES), bf16),
            jax.ShapeDtypeStruct((blocks, rows, LANES), bf16),
            jax.ShapeDtypeStruct((blocks, rows, out_width), bf16),
            jax.ShapeDtypeStruct((blocks, HEAD_SIZE, cols), f32),
            jax.ShapeDtypeStruct((blocks, 1, cols), f32),
        ],
        cost_estimate=pl.CostEstimate(
            flops=2 * length * width * 256 + 2 * length * length * cols // rows * 128,
            bytes_accessed=2 * length * width * 4,
            transcendentals=length * length,
        ),
        compiler_params=pltpu.CompilerParams(
            dimension_semantics=("arbitrary",), vmem_limit_bytes=60 << 20
        ),
    )(
        tok_all,
        w_own,
        gain,
        table,
        docs,
    )


def attend_backward(q_all, kv_all, cot, ot, lse, table, docs, heads):
    blocks, rows, _ = q_all.shape
    length = blocks * rows
    cols = heads * rows

    def kernel(q_ref, kv_ref, do_ref, ot_ref, lse_ref, table_ref, docs_ref, out_ref, dk_scr, dv_scr, dq_scr, doc_scr):
        i = pl.program_id(0)

        @pl.when(i == 0)
        def _():
            dk_scr[...] = jnp.zeros_like(dk_scr)
            dv_scr[...] = jnp.zeros_like(dv_scr)

        q2 = stack_heads(q_ref[0], heads)
        do2 = stack_heads(do_ref[0], heads)
        delta = jnp.sum(do2.astype(f32).T * ot_ref[0], axis=0, keepdims=True)
        log_total = lse_ref[0]
        doc_row = docs_ref[i, :1].astype(f32)
        doc_scr[i] = across_lanes(doc_row, LANES)
        doc_query = jnp.concatenate([doc_row] * heads, axis=1)
        query = i * rows + lax.rem(lax.broadcasted_iota(jnp.int32, (1, cols), 1), rows)
        key_iota = lax.broadcasted_iota(jnp.int32, (rows, cols), 0)
        dq_scr[...] = jnp.zeros_like(dq_scr)

        @pl.loop(first_block(docs_ref, i), i + 1)
        def _(j):
            kv = kv_ref[j]
            k, v = kv[:, :HEAD_SIZE], kv[:, HEAD_SIZE:]
            scores = dot_nt(k, q2) * att_mult
            key = key_iota + j * rows
            same = jnp.concatenate([doc_scr[j]] * (cols // LANES), axis=1) == doc_query
            p = jnp.where(same & (key <= query), jnp.exp(scores - log_total), 0.0)
            ds = (p * (dot_nt(v, do2) - delta)).astype(bf16)
            dv_scr[j] += dot_nn(p.astype(bf16), do2)
            dk_scr[j] += dot_nn(ds, q2)
            dq_scr[...] += dot_tn(ds, k)

        def rope_back(x, c, s):
            return (x * c - turn(x) * s).astype(bf16)

        dq = dq_scr[...] * att_mult
        dq = [dq[h * rows : (h + 1) * rows] for h in range(heads)]
        if heads * HEAD_SIZE < HEADS_LANES:
            dq.append(jnp.zeros((rows, HEADS_LANES - heads * HEAD_SIZE), f32))
        dq = jnp.concatenate(dq, axis=1).astype(bf16).astype(f32)
        out_ref[i, :, :HEADS_LANES] = rope_back(dq, *spread_table(table_ref[i]))

        @pl.when(i == blocks - 1)
        def _():
            @pl.loop(0, blocks)
            def _(j):
                kv = jnp.concatenate([dk_scr[j] * att_mult, dv_scr[j]], axis=1)
                lane = lax.broadcasted_iota(jnp.int32, kv.shape, 1)
                c, s = spread_table(table_ref[j])
                kv = jnp.where(lane < HEAD_SIZE, kv * c - turn(kv) * s, kv).astype(bf16)
                out_ref[j, :, HEADS_LANES:] = kv

    def block(shape):
        return pl.BlockSpec((1,) + shape, lambda i: (i, 0, 0))

    def whole(shape):
        return pl.BlockSpec(shape, lambda i: (0,) * len(shape))

    grid_spec = pltpu.PrefetchScalarGridSpec(
        num_scalar_prefetch=0,
        grid=(blocks,),
        in_specs=[
            block((rows, HEADS_LANES)),
            whole((blocks, rows, LANES)),
            block((rows, heads * HEAD_SIZE)),
            block((HEAD_SIZE, cols)),
            block((1, cols)),
            whole((blocks, HEAD_SIZE, rows)),
            whole(docs.shape),
        ],
        out_specs=whole((blocks, rows, HEADS_LANES + LANES)),
        scratch_shapes=[
            pltpu.VMEM((blocks, rows, HEAD_SIZE), f32),
            pltpu.VMEM((blocks, rows, HEAD_SIZE), f32),
            pltpu.VMEM((cols, HEAD_SIZE), f32),
            pltpu.VMEM((blocks, rows, LANES), f32),
        ],
    )
    return pl.pallas_call(
        kernel,
        name="attend_backward",
        grid_spec=grid_spec,
        out_shape=jax.ShapeDtypeStruct((blocks, rows, HEADS_LANES + LANES), bf16),
        cost_estimate=pl.CostEstimate(
            flops=5 * length * length * cols // rows * 128,
            bytes_accessed=2 * length * 1024,
            transcendentals=length * length,
        ),
        compiler_params=pltpu.CompilerParams(
            dimension_semantics=("arbitrary",), vmem_limit_bytes=60 << 20
        ),
    )(
        q_all,
        kv_all,
        cot,
        ot,
        lse,
        table,
        docs,
    )


def moe_exchange(collective_id, normed, cots, mask, router, weights):
    devices = lax.axis_size("seq")
    chips = devices // 2
    rows, width = normed.shape
    own_experts = weights.shape[0]
    gate_rows = devices * own_experts

    def order(chip, k):
        left = chip < chips - 1 - chip
        longer = jnp.where(left, chips - 1 - chip, chip)
        near = jnp.where(left, chip + k, chip - k)
        return jnp.where(k <= longer, near, jnp.where(left, chips - 1 - k, k))

    def kernel(*refs):
        x_in, g_in = refs[0], refs[1 : 1 + chips]
        mask_ref, router_ref, w_given = refs[1 + chips : 4 + chips]
        (lin_out, slot_out, hid_out, n_sum, gate_out, g_out) = refs[4 + chips : 10 + chips]
        y_outs = refs[10 + chips : 11 + chips + chips // 2]
        (
            x_all, g_all, win, wout, y_acc, n_acc, gate_acc, gate_stage,
            n_mine, n_far, n_give, n_theirs, y_give, y_theirs, y_pre, y_in,
            lin_st, slot_st, hid_st, gin, gout, hid_ld,
            local, line_send, line_recv, sib_send, sib_recv, g_local, g_send, g_recv,
            n_send, n_recv, y_send, y_recv, far_send, far_recv, gate_send, gate_recv,
            st_sem, y_sem, ld_sem, w_sem, wg_sem, hand_send, hand_recv,
        ) = refs[11 + chips + chips // 2 :]
        me = lax.axis_index("seq")
        chip, core = me // 2, lax.rem(me, 2)
        sibling = me + 1 - 2 * core
        win_copy = pltpu.make_async_copy(
            w_given.at[:, :, pl.ds(0, 2 * FFE)], win, w_sem.at[0]
        )
        wout_copy = pltpu.make_async_copy(
            w_given.at[:, :, pl.ds(2 * FFE, FFE)], wout, w_sem.at[1]
        )
        win_copy.start()
        wout_copy.start()
        barrier = pltpu.get_barrier_semaphore()
        for k in range(1, devices):
            pl.semaphore_signal(
                barrier, inc=1, device_id={"seq": lax.rem(me + k, devices)}, device_id_type=MESH
            )
        pl.semaphore_wait(barrier, devices - 1)

        def remote(src, dst, send, recv, to):
            return pltpu.make_async_remote_copy(
                src_ref=src,
                dst_ref=dst,
                send_sem=send,
                recv_sem=recv,
                device_id={"seq": to},
                device_id_type=MESH,
            )

        half = rows // PIECES

        def piece(b, core_of, i):
            return x_all.at[2 * b + core_of, pl.ds(i * half, half)]

        def line(src, b, i, slot, to):
            return remote(
                src, piece(b, core, i), line_send.at[i, slot], line_recv.at[i, b], to
            )

        def across(src, b, core_of, i):
            return remote(
                src, piece(b, core_of, i), sib_send.at[i, b], sib_recv.at[i, b], sibling
            )

        def own_piece(i):
            return x_in.at[pl.ds(i * half, half)]

        def pass_on(b, i, to):
            return line(piece(b, core, i), b, i, 2 + b, to)

        def to_sibling(b, i):
            return across(piece(b, core, i), b, core, i)

        def own_sends(act):
            for i in range(PIECES):

                @pl.when(chip > 0)
                def _(i=i):
                    act(line(own_piece(i), chip, i, 0, me - 2))

                @pl.when(chip < chips - 1)
                def _(i=i):
                    act(line(own_piece(i), chip, i, 1, me + 2))

            for i in range(PIECES):
                act(across(own_piece(i), chip, core, i))

        def cot_to_sibling(k):
            b = lax.rem(chip + chips - k, chips)
            return remote(
                g_in[k], g_all.at[2 * b + core], g_send.at[k], g_recv.at[b], sibling
            )

        def cot_local(k):
            b = lax.rem(chip + chips - k, chips)
            return pltpu.make_async_copy(g_in[k], g_all.at[2 * b + core], g_local.at[k])

        own_sends(lambda copy: copy.start())
        own = pltpu.make_async_copy(x_in, x_all.at[me], local)
        own.start()
        for k in range(chips):
            cot_to_sibling(k).start()
            cot_local(k).start()
        gin[...] = jnp.zeros_like(gin)
        gout[...] = jnp.zeros_like(gout)
        own.wait()
        for k in range(chips):
            cot_local(k).wait()
        win_copy.wait()
        wout_copy.wait()

        def gate_copy(block):
            return remote(
                gate_stage.at[block],
                gate_out.at[me],
                gate_send.at[block],
                gate_recv.at[me],
                block,
            )

        def n_copy(p):
            return remote(n_give, n_theirs.at[p], n_send.at[p], n_recv.at[p], sibling)

        def y_copy(p):
            return remote(y_give, y_theirs.at[p], y_send.at[p], y_recv.at[p], sibling)

        pairs = chips // 2
        pair = chip // 2
        mate = chip + 1 - 2 * lax.rem(chip, 2)

        def y_leave(b, k):
            return pltpu.make_async_copy(y_pre.at[b], y_outs[k], y_sem.at[k])

        def keep_of(j):
            return 2 * lax.rem(pair + 1 + j, pairs) + lax.rem(chip, 2)

        def y_hand(b):
            far = lax.rem(b // 2 + pairs - pair, pairs) - 1
            return remote(
                y_pre.at[b], y_in.at[far], hand_send.at[far], hand_recv.at[far], 2 * mate + core
            )

        def stage_copies(e, block):
            return [
                pltpu.make_async_copy(lin_st.at[e], lin_out.at[e, block], st_sem.at[0, e]),
                pltpu.make_async_copy(slot_st.at[e], slot_out.at[e, block], st_sem.at[1, e]),
                pltpu.make_async_copy(hid_st.at[e], hid_out.at[e, block], st_sem.at[2, e]),
            ]

        def far_copy(b):
            return remote(
                n_mine.at[b], n_far.at[chip], far_send.at[b], far_recv.at[chip], 2 * b + core
            )

        def fold(k):
            b, p = order(chip, k), lax.rem(k, 2)
            n_copy(p).wait_recv()
            both = n_acc[...].astype(bf16).astype(f32) + n_theirs[p].astype(f32)

            @pl.when(b == chip)
            def _():
                n_sum[...] = both

            @pl.when(b != chip)
            def _():
                n_mine[b] = both.astype(bf16)
                far_copy(b).start()

            y_copy(p).wait_recv()
            y_pre[b] = (y_acc[...] + y_theirs[p].astype(f32)).astype(bf16)

            @pl.when(b == chip)
            def _():
                y_leave(b, 0).start()

            @pl.when(b == mate)
            def _():
                y_leave(b, 1).start()

        def compute(block, before):
            x = x_all[block]
            there = mask_ref[block] > 0
            logits = jnp.where(there, dot_nn(x, router_ref[...]), -1e30)
            gates = jnp.where(
                there, jnp.exp(logits - jnp.max(logits, axis=1, keepdims=True)), 0.0
            )
            gates = gates / jnp.sum(gates, axis=1, keepdims=True)
            lane = lax.broadcasted_iota(jnp.int32, gates.shape, 1)
            y_acc[...] = jnp.zeros_like(y_acc)
            n_acc[...] = jnp.zeros_like(n_acc)
            gate_acc[...] = jnp.zeros_like(gate_acc)

            @pl.loop(0, own_experts)
            def _(e):
                gate = jnp.sum(
                    jnp.where(lane == me * own_experts + e, gates, 0.0), axis=1, keepdims=True
                )
                lin = dot_nn(x_all[block], win[e])
                gate_lin, up_lin = lin[:, :FFE], lin[:, FFE:]
                sig = 0.5 + 0.5 * jnp.tanh(0.5 * gate_lin)
                silu = gate_lin * sig
                hidden = (silu * up_lin).astype(bf16)

                @pl.when(before)
                def _():
                    for copy in stage_copies(e, block):
                        copy.wait()

                hid_st[e] = hidden
                res = dot_nt(hidden, wout[e]).astype(bf16).astype(f32)
                y_acc[...] += gate * res
                cot = g_all[block].astype(f32) * res_mult
                gate_acc[...] += jnp.where(
                    lane == me * own_experts + e, jnp.sum(cot * res, axis=1, keepdims=True), 0.0
                )
                slot = (gate * cot).astype(bf16)
                slot_st[e] = slot
                hidden_cot = dot_nn(slot, wout[e])
                lin_cot = jnp.concatenate(
                    [
                        hidden_cot * up_lin * (sig * (1.0 + gate_lin * (1.0 - sig))),
                        hidden_cot * silu,
                    ],
                    axis=1,
                ).astype(bf16)
                lin_st[e] = lin_cot
                for copy in stage_copies(e, block):
                    copy.start()
                n_acc[...] += dot_nt(lin_cot, win[e]).astype(bf16).astype(f32)

            gate_stage[block] = gate_acc[...].T[:gate_rows]

            @pl.when(block != me)
            def _():
                gate_copy(block).start()

            @pl.when(block == me)
            def _():
                gate_out[block] = gate_stage[block]

        def hop(k, i):
            for side in (-1, 1):
                away = chip + side * k

                @pl.when((k > 0) & (k < chips) & (away >= 0) & (away < chips))
                def _(side=side, away=away):
                    pass_on(away, i, me).wait_recv()

                    @pl.when((chip - side >= 0) & (chip - side < chips))
                    def _():
                        pass_on(away, i, me - 2 * side).start()

                    to_sibling(away, i).start()

        @pl.loop(0, chips)
        def _(k):
            b = order(chip, k)
            hop(k, 1)
            for i in range(PIECES):
                across(own_piece(i), b, 1 - core, i).wait_recv()
            remote(
                x_in, g_all.at[2 * b + 1 - core], g_send.at[0], g_recv.at[b], sibling
            ).wait_recv()

            @pl.loop(0, 2)
            def _(h):
                @pl.when(h == 1)
                def _():
                    hop(k + 1, 0)

                compute(2 * b + lax.rem(core + 1 + h, 2), (k > 0) | (h > 0))

                @pl.when(h == 0)
                def _():
                    p = lax.rem(k, 2)

                    @pl.when(k > 0)
                    def _():
                        n_copy(1 - p).wait_send()
                        y_copy(1 - p).wait_send()

                    n_give[...] = n_acc[...].astype(bf16)
                    y_give[...] = y_acc[...].astype(bf16)
                    n_copy(p).start()
                    y_copy(p).start()

                @pl.when(h == 1)
                def _():
                    fold(k)

        for j in range(pairs - 1):
            y_hand(keep_of(j) + mate - chip).start()

        for e in range(own_experts):
            for copy in stage_copies(e, 0):
                copy.wait()

        def loads(t, p):
            e, b = lax.rem(t, own_experts), t // own_experts
            pair = pl.ds(2 * b, 2)
            return [
                pltpu.make_async_copy(
                    lin_out.at[e, pair], g_all.at[pl.ds(4 * p, 2)], ld_sem.at[0, p]
                ),
                pltpu.make_async_copy(
                    slot_out.at[e, pair], g_all.at[pl.ds(4 * p + 2, 2)], ld_sem.at[1, p]
                ),
                pltpu.make_async_copy(hid_out.at[e, pair], hid_ld.at[p], ld_sem.at[2, p]),
            ]

        for copy in loads(jnp.int32(0), 0):
            copy.start()
        @pl.loop(0, chips * own_experts)
        def _(t):
            p = lax.rem(t, 2)
            for copy in loads(t, p):
                copy.wait()

            @pl.when(t + 1 < chips * own_experts)
            def _():
                for copy in loads(t + 1, 1 - p):
                    copy.start()

            e, b = lax.rem(t, own_experts), t // own_experts
            x = x_all[pl.ds(2 * b, 2)].reshape(2 * rows, width)
            lin_cot = g_all[pl.ds(4 * p, 2)].reshape(2 * rows, width)
            gin[e] += dot_tn(x, lin_cot)
            slot = g_all[pl.ds(4 * p + 2, 2)].reshape(2 * rows, width)
            gout[e] += dot_tn(slot, hid_ld[p].reshape(2 * rows, FFE))

        @pl.loop(1, chips)
        def _(k):
            for side in (-1, 1):
                away = chip + side * k

                for i in range(PIECES):

                    @pl.when((away >= 0) & (away < chips))
                    def _(side=side, away=away, i=i):
                        to_sibling(away, i).wait_send()

                        @pl.when((chip - side >= 0) & (chip - side < chips))
                        def _():
                            pass_on(away, i, me - 2 * side).wait_send()

        own_sends(lambda copy: copy.wait_send())

        for j in range(pairs - 1):
            b = keep_of(j)
            y_hand(b).wait_recv()
            y_pre[b] = (y_pre[b].astype(f32) + y_in[j].astype(f32)).astype(bf16)
            y_leave(b, 2 + j).start()

        leaving = []
        for e in range(own_experts):
            for j in range(width // rows):
                i = e * (width // rows) + j
                x_all[i] = gin[e, j * rows : (j + 1) * rows].astype(bf16)
                g_all[i, :, :FFE] = gout[e, j * rows : (j + 1) * rows].astype(bf16)
                at = 2 * len(leaving)
                here = pl.ds(j * rows, rows)
                leaving.append(
                    (
                        pltpu.make_async_copy(
                            x_all.at[i], g_out.at[e, here, pl.ds(0, 2 * FFE)], wg_sem.at[at]
                        ),
                        pltpu.make_async_copy(
                            g_all.at[i, :, pl.ds(0, FFE)],
                            g_out.at[e, here, pl.ds(2 * FFE, FFE)],
                            wg_sem.at[at + 1],
                        ),
                    )
                )
                for copy in leaving[-1]:
                    copy.start()

        @pl.loop(1, chips)
        def _(k):
            b = order(chip, k)
            remote(
                n_mine.at[b], n_far.at[b], far_send.at[b], far_recv.at[b], 2 * b + core
            ).wait_recv()
            n_sum[...] += n_far[b].astype(f32)
            far_copy(b).wait_send()

        @pl.loop(1, devices)
        def _(k):
            block = lax.rem(me + k, devices)
            remote(
                gate_stage.at[block],
                gate_out.at[block],
                gate_send.at[block],
                gate_recv.at[block],
                block,
            ).wait_recv()
            gate_copy(block).wait_send()

        n_copy((chips - 1) % 2).wait_send()
        y_copy((chips - 1) % 2).wait_send()
        for both in leaving:
            for copy in both:
                copy.wait()
        y_leave(chip, 0).wait()
        y_leave(mate, 1).wait()
        for j in range(pairs - 1):
            y_leave(keep_of(j), 2 + j).wait()
            y_hand(keep_of(j) + mate - chip).wait_send()

        for k in range(chips):
            cot_to_sibling(k).wait_send()

    hbm = pl.BlockSpec(memory_space=pl.ANY)
    vmem = pl.BlockSpec(memory_space=pltpu.VMEM)
    block = (rows, width)
    dma = pltpu.SemaphoreType.DMA
    flops = 9 * own_experts * 2 * devices * rows * width * FFE // 1
    return pl.pallas_call(
        kernel,
        name="moe_exchange",
        out_shape=[
            jax.ShapeDtypeStruct((own_experts, devices, rows, 2 * FFE), bf16),
            jax.ShapeDtypeStruct((own_experts, devices) + block, bf16),
            jax.ShapeDtypeStruct((own_experts, devices, rows, FFE), bf16),
            jax.ShapeDtypeStruct(block, f32),
            jax.ShapeDtypeStruct((devices, gate_rows, rows), f32),
            jax.ShapeDtypeStruct((own_experts, width, 3 * FFE), bf16),
        ]
        + [jax.ShapeDtypeStruct(block, bf16)] * (1 + chips // 2),
        in_specs=[hbm] * (1 + chips) + [vmem] * 2 + [hbm],
        out_specs=[hbm] * 3 + [vmem] * 2 + [hbm] * (2 + chips // 2),
        scratch_shapes=[
            pltpu.VMEM((devices,) + block, bf16),
            pltpu.VMEM((devices,) + block, bf16),
            pltpu.VMEM((own_experts, width, 2 * FFE), bf16),
            pltpu.VMEM((own_experts, width, FFE), bf16),
            pltpu.VMEM(block, f32),
            pltpu.VMEM(block, f32),
            pltpu.VMEM((rows, LANES), f32),
            pltpu.VMEM((devices, gate_rows, rows), f32),
            pltpu.VMEM((chips,) + block, bf16),
            pltpu.VMEM((chips,) + block, bf16),
            pltpu.VMEM(block, bf16),
            pltpu.VMEM((2,) + block, bf16),
            pltpu.VMEM(block, bf16),
            pltpu.VMEM((2,) + block, bf16),
            pltpu.VMEM((chips,) + block, bf16),
            pltpu.VMEM((chips // 2 - 1,) + block, bf16),
            pltpu.VMEM((own_experts, rows, 2 * FFE), bf16),
            pltpu.VMEM((own_experts,) + block, bf16),
            pltpu.VMEM((own_experts, rows, FFE), bf16),
            pltpu.VMEM((own_experts, width, 2 * FFE), f32),
            pltpu.VMEM((own_experts, width, FFE), f32),
            pltpu.VMEM((2, 2, rows, FFE), bf16),
        ]
        + [dma]
        + [
            dma(count)
            for count in (
                (PIECES, chips + 2), (PIECES, chips), (PIECES, chips), (PIECES, chips),
                (chips,), (chips,), (chips,), (2,), (2,), (2,), (2,),
                (chips,), (chips,), (devices,), (devices,),
            )
        ]
        + [
            dma((3, own_experts)),
            dma((1 + chips // 2,)),
            dma((3, 2)),
            dma((2,)),
            dma((2 * own_experts * (width // rows),)),
            dma((chips // 2 - 1,)),
            dma((chips // 2 - 1,)),
        ],
        cost_estimate=pl.CostEstimate(
            flops=flops, bytes_accessed=40 << 20, transcendentals=devices * rows * FFE * 2
        ),
        compiler_params=pltpu.CompilerParams(
            collective_id=collective_id, has_side_effects=True, vmem_limit_bytes=63 << 20
        ),
    )(normed, *cots, mask, router, weights)


class Links:
    def __init__(self, axes):
        self.size = {axis: lax.axis_size(axis) for axis in axes}
        self.me = {axis: lax.axis_index(axis) for axis in axes}

    def barrier(self):
        sem = pltpu.get_barrier_semaphore()
        for axis, size in self.size.items():
            for k in range(1, size):
                pl.semaphore_signal(
                    sem,
                    inc=1,
                    device_id={axis: lax.rem(self.me[axis] + k, size)},
                    device_id_type=MESH,
                )
        pl.semaphore_wait(sem, sum(size - 1 for size in self.size.values()))

    def copy(self, axis, src, dst, send, recv, to):
        return pltpu.make_async_remote_copy(
            src_ref=src,
            dst_ref=dst,
            send_sem=send,
            recv_sem=recv,
            device_id={axis: to},
            device_id_type=MESH,
        )

    def swap_start(self, axis, src, dst, send, recv, local):
        me, size = self.me[axis], self.size[axis]
        pltpu.make_async_copy(src.at[me], dst.at[me], local).start()
        for k in range(1, size):
            to = lax.rem(me + k, size)
            self.copy(axis, src.at[to], dst.at[me], send.at[k - 1], recv.at[k - 1], to).start()

    def swap_wait(self, axis, src, dst, send, recv, local):
        me, size = self.me[axis], self.size[axis]
        pltpu.make_async_copy(src.at[me], dst.at[me], local).wait()
        for k in range(1, size):
            frm = lax.rem(me + size - k, size)
            self.copy(axis, src.at[frm], dst.at[frm], send.at[k - 1], recv.at[k - 1], frm).wait()


def loads(pairs, sems):
    copies = [
        pltpu.make_async_copy(src, dst, sems.at[i]) for i, (src, dst) in enumerate(pairs)
    ]
    for copy in copies:
        copy.start()
    return copies


def staged(arrays):
    return [pltpu.VMEM(x.shape, x.dtype) for x in arrays]


def swap_sems(size):
    dma = pltpu.SemaphoreType.DMA
    return [dma((size - 1,)), dma((size - 1,)), dma]


def attended_exchange(collective_id, attended_own, tokens, w_out, gain):
    devices, rows, cols = attended_own.shape
    width = tokens.shape[1]

    ins = [tokens, w_out, gain]
    outs = [
        jax.ShapeDtypeStruct((rows, width), bf16),
        jax.ShapeDtypeStruct((rows, width), f32),
        jax.ShapeDtypeStruct((rows, width), bf16),
    ]

    def kernel(att_in, *refs):
        given, results = refs[:3], refs[3:6]
        tok, w_all, gain_ref = refs[6:9]
        att_ref, mid_ref, norm_ref, got, in_sem, out_sem, *sems = refs[9:]
        links = Links(("seq",))
        arriving = loads(list(zip(given, (tok, w_all, gain_ref))), in_sem)
        links.barrier()
        links.swap_start("seq", att_in, got, *sems)
        for copy in arriving:
            copy.wait()
        links.swap_wait("seq", att_in, got, *sems)
        attended = jnp.concatenate([got[j] for j in range(devices)], axis=1)
        att_ref[...] = attended
        mid = tok[...].astype(f32) + res_mult * dot_nn(attended, w_all[...])
        mid_ref[...] = mid
        scale = lax.rsqrt(jnp.mean(mid * mid, axis=-1, keepdims=True) + norm_eps)
        norm_ref[...] = (mid * scale * gain_row(gain_ref, 1)).astype(bf16)
        for copy in loads(list(zip((att_ref, mid_ref, norm_ref), results)), out_sem):
            copy.wait()

    hbm = pl.BlockSpec(memory_space=pl.ANY)
    dma = pltpu.SemaphoreType.DMA
    return pl.pallas_call(
        kernel,
        name="attended_exchange",
        out_shape=outs,
        in_specs=[hbm] * 4,
        out_specs=[hbm] * 3,
        scratch_shapes=staged(ins)
        + staged(outs)
        + [pltpu.VMEM(attended_own.shape, bf16), dma((3,)), dma((3,))]
        + swap_sems(devices),
        compiler_params=pltpu.CompilerParams(
            collective_id=collective_id, has_side_effects=True, vmem_limit_bytes=60 << 20
        ),
    )(attended_own, *ins)


def middle_exchange(
    collective_id, moe_sum, gate_cot, normed, router, mask, mid, out_grad, gain, w_out, attended, cols
):
    devices, gate_rows, rows = gate_cot.shape
    width = normed.shape[1]
    experts = gate_rows

    ins = [moe_sum, gate_cot, normed, router, mask, mid, out_grad, gain, w_out, attended]
    outs = [
        jax.ShapeDtypeStruct((width, LANES), bf16),
        jax.ShapeDtypeStruct((rows, width), f32),
        jax.ShapeDtypeStruct((width, width), bf16),
    ]

    def kernel(*refs):
        given, heads_out, results, refs = refs[:10], refs[10], refs[11:14], refs[14:]
        (
            moe_ref, gate_ref, norm_ref, router_ref, mask_ref, mid_ref, cot_ref, gain_ref, w_all, att_ref,
            pack_out, mid_cot_out, wo_out, give, in_sem, out_sem, *sems,
        ) = refs
        links = Links(("seq",))
        arriving = loads(list(zip(given, refs[:10])), in_sem)
        links.barrier()
        for copy in arriving:
            copy.wait()
        there = mask_ref[...] > 0
        logits = jnp.where(there, dot_nn(norm_ref[...], router_ref[...]), -1e30)
        gates = jnp.where(
            there, jnp.exp(logits - jnp.max(logits, axis=1, keepdims=True)), 0.0
        )
        gates = gates / jnp.sum(gates, axis=1, keepdims=True)
        gate = gate_ref[0]
        for j in range(1, devices):
            gate = gate + gate_ref[j]
        gate = jnp.concatenate([gate, jnp.zeros((LANES - gate_rows, rows), f32)], axis=0).T
        pick_cot = gates * (gate - jnp.sum(gates * gate, axis=1, keepdims=True))
        logit_cot = pick_cot.astype(bf16)
        cot = moe_ref[...] + dot_nt(logit_cot, router_ref[...])
        mid = mid_ref[...]
        scale = lax.rsqrt(jnp.mean(mid * mid, axis=-1, keepdims=True) + norm_eps)
        gain_grad = jnp.sum(cot * mid * scale, axis=0, keepdims=True)
        weighted = cot * gain_row(gain_ref, 1)
        mid_cot = (
            cot_ref[...].astype(f32)
            + scale * weighted
            - mid * (scale * scale * scale) * jnp.mean(weighted * mid, axis=-1, keepdims=True)
        )
        mid_cot_out[...] = mid_cot
        branch_cot = (res_mult * mid_cot).astype(bf16)
        attended_cot = dot_nt(branch_cot, w_all[...]).astype(bf16)
        for j in range(devices):
            give[j] = attended_cot[:, j * cols : (j + 1) * cols]
        links.swap_start("seq", give, heads_out, *sems)
        wo_out[...] = dot_tn(att_ref[...], branch_cot).astype(bf16)
        pack = dot_tn(norm_ref[...], logit_cot)
        lane = lax.broadcasted_iota(jnp.int32, pack.shape, 1)
        pack_out[...] = jnp.where(
            lane == experts, jnp.broadcast_to(gain_grad, (LANES, width)).T, pack
        ).astype(bf16)
        for copy in loads(list(zip((pack_out, mid_cot_out, wo_out), results)), out_sem):
            copy.wait()
        links.swap_wait("seq", give, heads_out, *sems)

    hbm = pl.BlockSpec(memory_space=pl.ANY)
    dma = pltpu.SemaphoreType.DMA
    return pl.pallas_call(
        kernel,
        name="middle_exchange",
        out_shape=[jax.ShapeDtypeStruct((devices, rows, cols), bf16)] + outs,
        in_specs=[hbm] * 10,
        out_specs=[hbm] * 4,
        scratch_shapes=staged(ins)
        + staged(outs)
        + [pltpu.VMEM((devices, rows, cols), bf16), dma((10,)), dma((3,))]
        + swap_sems(devices),
        compiler_params=pltpu.CompilerParams(
            collective_id=collective_id, has_side_effects=True, vmem_limit_bytes=60 << 20
        ),
    )(*ins)


def finish(e_grads, grad_qkv, grad_wo, pack, input_grad, output, weights, gain, heads, experts):
    own_experts, e_rows, e_cols = e_grads.shape
    devices, out_rows, _ = grad_qkv.shape
    q_width = heads * HEAD_SIZE
    share = devices // KEY_VALUE_HEADS if devices > KEY_VALUE_HEADS else 1
    steps = 4
    chunk = e_rows // steps
    me = lax.axis_index("seq").astype(jnp.int32).reshape(1)

    def kernel(
        me_ref, e_ref, qkv_ref, wo_ref, pack_ref, in_ref, out_ref, wq, wk, wv, gain_ref,
        e_in, e_out, gq, gk, gv, gwo, grouter, ggain_m, ggain_a, in_grad, output_ref,
    ):
        e_in[...] = e_ref[:, :, : 2 * FFE].astype(f32)
        e_out[...] = e_ref[:, :, 2 * FFE :].astype(f32)

        @pl.when(pl.program_id(0) == 0)
        def _():
            blocks = [qkv_ref[j].astype(f32) for j in range(devices)]

            def per_head(first):
                heads_of = []
                for j in range(KEY_VALUE_HEADS):
                    part = blocks[j * share][:, first : first + HEAD_SIZE]
                    for i in range(1, share):
                        part = part + blocks[j * share + i][:, first : first + HEAD_SIZE]
                    heads_of.append(part)
                return jnp.concatenate(heads_of, axis=1)

            grad_q = jnp.concatenate([b[:, :q_width] for b in blocks], axis=1)
            grad_k = per_head(HEADS_LANES)
            grad_v = per_head(HEADS_LANES + HEAD_SIZE)
            gq[...], gk[...], gv[...] = grad_q, grad_k, grad_v

            def rounded(ref):
                return ref[...].astype(bf16).astype(f32)

            def row(column):
                return jnp.broadcast_to(column, (out_rows, LANES)).T[:1]

            gain_grad = (
                jnp.sum(rounded(wq) * grad_q, axis=1, keepdims=True)
                + jnp.sum(rounded(wk) * grad_k, axis=1, keepdims=True)
                + jnp.sum(rounded(wv) * grad_v, axis=1, keepdims=True)
            )
            own = lax.broadcasted_iota(jnp.int32, (devices, 1), 0) == me_ref[0]
            own_gain = jnp.sum(jnp.where(own, rounded(gain_ref), 0.0), axis=0, keepdims=True)
            ggain_a[...] = row(gain_grad) / own_gain
            gwo[...] = wo_ref[...]
            grouter[...] = pack_ref[...].T[:experts]
            ggain_m[...] = row(pack_ref[:, experts : experts + 1])
            in_grad[...] = in_ref[...]
            output_ref[...] = out_ref[...]

    def whole(x):
        return pl.BlockSpec(x.shape, lambda i, _: (0,) * len(x.shape))

    def own_rows(x):
        return pl.BlockSpec((out_rows, x.shape[1]), lambda i, me_ref: (me_ref[0], 0))

    def shape(*dims, dtype=f32):
        return jax.ShapeDtypeStruct(dims, dtype)

    rest = [grad_qkv, grad_wo, pack, input_grad, output]
    kv_width = KEY_VALUE_HEADS * HEAD_SIZE
    small = [
        shape(out_rows, devices * q_width),
        shape(out_rows, kv_width),
        shape(out_rows, kv_width),
        shape(*grad_wo.shape),
        shape(experts, out_rows),
        shape(1, out_rows),
        shape(1, out_rows),
        shape(*input_grad.shape, dtype=bf16),
        shape(*output.shape, dtype=bf16),
    ]
    return pl.pallas_call(
        kernel,
        name="finish",
        grid_spec=pltpu.PrefetchScalarGridSpec(
            num_scalar_prefetch=1,
            grid=(steps,),
            in_specs=[pl.BlockSpec((own_experts, chunk, e_cols), lambda i, _: (0, i, 0))]
            + [whole(x) for x in rest]
            + [own_rows(x) for x in weights]
            + [whole(gain)],
            out_specs=[
                pl.BlockSpec((own_experts, chunk, 2 * FFE), lambda i, _: (0, i, 0)),
                pl.BlockSpec((own_experts, chunk, FFE), lambda i, _: (0, i, 0)),
            ]
            + [whole(x) for x in small],
        ),
        out_shape=[
            shape(own_experts, e_rows, 2 * FFE),
            shape(own_experts, e_rows, FFE),
        ]
        + small,
        cost_estimate=pl.CostEstimate(flops=0, bytes_accessed=8 << 20, transcendentals=0),
        compiler_params=pltpu.CompilerParams(
            dimension_semantics=("arbitrary",), vmem_limit_bytes=60 << 20
        ),
    )(me, e_grads, *rest, *weights, gain)


def first_exchange(collective_id, tokens, out_grad, docs, mask, misc, gains, w_query, w_key, w_value, w_out):
    devices, parts = lax.axis_size("seq"), lax.axis_size("dp")
    w_rows, width = w_out.shape
    heads = QUERY_HEADS // devices
    q_width = heads * HEAD_SIZE
    group = QUERY_HEADS // KEY_VALUE_HEADS
    w_cols = HEADS_LANES + LANES
    weights = [w_query, w_key, w_value, w_out]

    def prepare(refs):
        given, (wq, wk, wv, wo, w_all, wo_low, sem) = refs[:4], refs[4:]
        for copy in loads(list(zip(given, (wq, wk, wv, wo))), sem):
            copy.wait()
        wo_low[...] = wo[...].astype(bf16)
        for s in range(devices):
            kv = s * heads // group * HEAD_SIZE
            pieces = [wq[:, s * q_width : (s + 1) * q_width]]
            if q_width < HEADS_LANES:
                pieces.append(jnp.zeros((w_rows, HEADS_LANES - q_width), f32))
            pieces += [wk[:, kv : kv + HEAD_SIZE], wv[:, kv : kv + HEAD_SIZE]]
            w_all[s] = jnp.concatenate(pieces, axis=1).astype(bf16)

    return exchange(
        collective_id,
        [
            ("gather", "seq", tokens, None),
            ("gather", "seq", docs, None),
            ("gather", "seq", mask, None),
            ("shift", "seq", out_grad, None),
            ("share", "dp", misc, None),
            ("gather", "dp", gains, None),
            ("gather", "dp", jax.ShapeDtypeStruct((w_rows, w_cols), bf16), 0),
            ("share", "dp", jax.ShapeDtypeStruct((w_rows, width), bf16), 1),
        ],
        prepare=prepare,
        given=weights,
        work=staged(weights)
        + [
            pltpu.VMEM((devices, w_rows, w_cols), bf16),
            pltpu.VMEM((w_rows, width), bf16),
            pltpu.SemaphoreType.DMA((4,)),
        ],
        made=lambda refs: (refs[8].at[lax.axis_index("seq")], refs[9]),
        keep=(jax.ShapeDtypeStruct((devices, w_rows, w_cols), bf16), 8),
    )


def prepare(expert_in, expert_out, picks, docs, w_router, gain_attn, gain_moe):
    own_experts, w_rows, _ = expert_in.shape
    rows, experts = picks.shape[1], w_router.shape[0]
    steps = 4
    chunk = w_rows // steps

    def kernel(
        e_in, e_out, picks_ref, docs_ref, router, gain_a, gain_m, low, mask, docs_out, misc, gains
    ):
        low[:, :, : 2 * FFE] = e_in[...].astype(bf16)
        low[:, :, 2 * FFE :] = e_out[...].astype(bf16)

        @pl.when(pl.program_id(0) == 0)
        def _():
            expert = lax.broadcasted_iota(jnp.int32, (LANES, rows), 0)
            chosen = picks_ref[:1] == expert
            for k in range(1, TOP):
                chosen = chosen | (picks_ref[k : k + 1] == expert)
            mask[...] = jnp.where(chosen, 1.0, 0.0).T.astype(bf16)
            docs_out[...] = jnp.broadcast_to(docs_ref[...], docs_out.shape)
            misc[...] = jnp.concatenate(
                [router[...], jnp.zeros((LANES - experts, w_rows), f32)], axis=0
            ).T.astype(bf16)
            upper = lax.broadcasted_iota(jnp.int32, (8, w_rows), 0) == 0
            gains[...] = jnp.where(upper, gain_a[...], gain_m[...]).astype(bf16)

    def whole(shape):
        return pl.BlockSpec(shape, lambda i: (0,) * len(shape))

    def part(x):
        return pl.BlockSpec((own_experts, chunk, x.shape[2]), lambda i: (0, i, 0))

    small = [picks, docs, w_router, gain_attn[None], gain_moe[None]]
    outs = [
        jax.ShapeDtypeStruct((rows, LANES), bf16),
        jax.ShapeDtypeStruct((8, rows), jnp.int32),
        jax.ShapeDtypeStruct((w_rows, LANES), bf16),
        jax.ShapeDtypeStruct((8, w_rows), bf16),
    ]
    return pl.pallas_call(
        kernel,
        name="prepare",
        grid=(steps,),
        out_shape=[jax.ShapeDtypeStruct((own_experts, w_rows, 3 * FFE), bf16)] + outs,
        in_specs=[part(expert_in), part(expert_out)] + [whole(x.shape) for x in small],
        out_specs=[pl.BlockSpec((own_experts, chunk, 3 * FFE), lambda i: (0, i, 0))]
        + [whole(x.shape) for x in outs],
        compiler_params=pltpu.CompilerParams(
            dimension_semantics=("arbitrary",), vmem_limit_bytes=60 << 20
        ),
    )(expert_in, expert_out, *small)


def final_exchange(
    collective_id, qkv_cot, normed, token_grads, w_full, tokens, mid_cot, gain, mid, branches
):
    devices, parts = lax.axis_size("seq"), lax.axis_size("dp")
    chips = devices // 2
    _, rows, cols = qkv_cot.shape
    width = tokens.shape[1]
    out_rows = token_grads[0].shape[2]
    gq_shape = (parts, devices, out_rows, cols)
    count = len(token_grads)
    wides = [x.shape[3] for x in token_grads]
    token_grads = [x.reshape(parts, chips, 2, out_rows, x.shape[3]) for x in token_grads]

    ins = [w_full, normed, qkv_cot, tokens, mid_cot, gain, mid, *branches]

    def kernel(*refs):
        qkv_in = refs[0]
        gt_in = refs[1 : 1 + count]
        given = refs[1 + count : 1 + count + len(ins)]
        refs = refs[1 + count + len(ins) :]
        in_grad_out, output_out, gq_out = refs[:3]
        gt_out = refs[3 : 3 + count]
        refs = refs[3 + count :]
        (
            qkv_tok, nac, gq_in, grad, gq_recv, gq_sum,
            q_send, q_recv, local, gq_send, gq_rsem, gqz_send, gqz_recv, gq_local,
        ) = refs[:14]
        work = [refs[14 + 11 * i : 25 + 11 * i] for i in range(count)]
        refs = refs[14 + 11 * count :]
        local_ins, (in_grad, output, in_sem, out_sem) = refs[: len(ins)], refs[len(ins) :]
        w_all, normed_all, qkv_all, tok_ref, mid_cot_ref, gain_ref, mid_ref, *y_refs = local_ins
        me, my = lax.axis_index("seq"), lax.axis_index("dp")
        chip, core = me // 2, lax.rem(me, 2)
        sibling = me + 1 - 2 * core
        arriving = loads(list(zip(given, local_ins)), in_sem)
        barrier = pltpu.get_barrier_semaphore()
        for axis, index, size in (("seq", me, devices), ("dp", my, parts)):
            for k in range(1, size):
                pl.semaphore_signal(
                    barrier,
                    inc=1,
                    device_id={axis: lax.rem(index + k, size)},
                    device_id_type=MESH,
                )
        pl.semaphore_wait(barrier, devices + parts - 2)

        def remote(axis, src, dst, send, recv, to):
            return pltpu.make_async_remote_copy(
                src_ref=src,
                dst_ref=dst,
                send_sem=send,
                recv_sem=recv,
                device_id={axis: to},
                device_id_type=MESH,
            )

        sent = []

        def columns(j):
            return qkv_tok.at[:, pl.ds(pl.multiple_of(j * cols, cols), cols)]

        for x, w in zip(gt_in, work):
            mine, theirs, far, near, last, sems, dp_send, dp_recv, z_send, z_recv, _ = w
            copy = remote(
                "seq", x.at[:, :, 1 - core], theirs, sems.at[0], sems.at[1], sibling
            )
            copy.start()
            sent.append(copy)
            pltpu.make_async_copy(x.at[:, :, core], mine, sems.at[2]).start()
        own = pltpu.make_async_copy(qkv_in.at[me], columns(me), local)
        own.start()
        for k in range(1, devices):
            to = lax.rem(me + k, devices)
            copy = remote(
                "seq", qkv_in.at[to], columns(me), q_send.at[k - 1], q_recv.at[k - 1], to
            )
            copy.start()
            sent.append(copy)

        for x, w in zip(gt_in, work):
            mine, theirs, far, near, last, sems, dp_send, dp_recv, z_send, z_recv, _ = w
            remote("seq", x.at[:, :, core], theirs, sems.at[0], sems.at[1], sibling).wait_recv()
            pltpu.make_async_copy(x.at[:, :, core], mine, sems.at[2]).wait()
            mine[...] = (mine[...].astype(f32) + theirs[...].astype(f32)).astype(bf16)
            for k in range(1, parts):
                to = lax.rem(my + k, parts)
                copy = remote(
                    "dp", mine.at[to], far.at[k - 1], dp_send.at[k - 1], dp_recv.at[k - 1], to
                )
                copy.start()
                sent.append(copy)

        for copy in arriving:
            copy.wait()
        grad[...] = jnp.zeros_like(grad)

        @pl.loop(0, devices)
        def _(j):
            grad[...] += dot_tn(normed_all[j], qkv_all[j])

        gq_in[...] = grad[...].astype(bf16).reshape(gq_shape)
        for k in range(1, parts):
            to = lax.rem(my + k, parts)
            copy = remote(
                "dp", gq_in.at[to], gq_recv.at[my], gq_send.at[k - 1], gq_rsem.at[k - 1], to
            )
            copy.start()
            sent.append(copy)
        own_q = pltpu.make_async_copy(gq_in.at[my], gq_recv.at[my], gq_local)
        own_q.start()
        total = y_refs[0][...].astype(f32)
        for k in range(1, len(branches)):
            total = total + y_refs[k][...].astype(f32)
        output[...] = (mid_ref[...] + res_mult * total).astype(bf16)
        leaving = [pltpu.make_async_copy(output, output_out, out_sem.at[0])]
        leaving[0].start()

        for k in range(devices):
            frm = lax.rem(me + devices - k, devices)
            if k == 0:
                own.wait()
            else:
                remote(
                    "seq", qkv_in.at[frm], columns(frm), q_send.at[k - 1], q_recv.at[k - 1], frm
                ).wait_recv()
            part = dot_nt(columns(frm)[...], w_all[frm])
            nac[...] = part if k == 0 else nac[...] + part

        resid = tok_ref[...].astype(f32)
        scale = lax.rsqrt(jnp.mean(resid * resid, axis=-1, keepdims=True) + norm_eps)
        weighted = nac[...] * gain_row(gain_ref, 0)
        in_grad[...] = (
            mid_cot_ref[...]
            + scale * weighted
            - resid
            * (scale * scale * scale)
            * jnp.mean(weighted * resid, axis=-1, keepdims=True)
        ).astype(bf16)

        leaving.append(pltpu.make_async_copy(in_grad, in_grad_out, out_sem.at[1]))
        leaving[1].start()
        own_q.wait()
        for k in range(1, parts):
            frm = lax.rem(my + parts - k, parts)
            remote(
                "dp", gq_in.at[frm], gq_recv.at[frm], gq_send.at[k - 1], gq_rsem.at[k - 1], frm
            ).wait_recv()
        summed = gq_recv[0].astype(f32)
        for p in range(1, parts):
            summed = summed + gq_recv[p].astype(f32)
        gq_sum[...] = summed.astype(bf16)
        own_z = pltpu.make_async_copy(gq_sum.at[me], gq_out.at[me], gq_local)
        own_z.start()
        for k in range(1, devices):
            to = lax.rem(me + k, devices)
            copy = remote(
                "seq", gq_sum.at[to], gq_out.at[me], gqz_send.at[k - 1], gqz_recv.at[k - 1], to
            )
            copy.start()
            sent.append(copy)
        for w in work:
            mine, theirs, far, near, last, sems, dp_send, dp_recv, z_send, z_recv, _ = w
            summed = mine[my].astype(f32)
            for k in range(1, parts):
                remote(
                    "dp", mine.at[0], far.at[k - 1], dp_send.at[k - 1], dp_recv.at[k - 1], my
                ).wait_recv()
                summed = summed + far[k - 1].astype(f32)
            near[...] = summed.astype(bf16)
            for k in range(1, chips):
                to = lax.rem(chip + k, chips)
                copy = remote(
                    "seq",
                    near.at[to],
                    last.at[k - 1],
                    z_send.at[k - 1],
                    z_recv.at[k - 1],
                    2 * to + core,
                )
                copy.start()
                sent.append(copy)

        for o, w in zip(gt_out, work):
            mine, theirs, far, near, last, sems, dp_send, dp_recv, z_send, z_recv, _ = w
            summed = near[chip].astype(f32)
            for k in range(1, chips):
                remote(
                    "seq", near.at[0], last.at[k - 1], z_send.at[k - 1], z_recv.at[k - 1], me
                ).wait_recv()
                summed = summed + last[k - 1].astype(f32)
            o[...] = summed
        own_z.wait()
        for k in range(1, devices):
            frm = lax.rem(me + devices - k, devices)
            remote(
                "seq", gq_sum.at[frm], gq_out.at[frm], gqz_send.at[k - 1], gqz_recv.at[k - 1], frm
            ).wait_recv()
        for copy in sent:
            copy.wait_send()
        for copy in leaving:
            copy.wait()

    hbm = pl.BlockSpec(memory_space=pl.ANY)
    vmem = pl.BlockSpec(memory_space=pltpu.VMEM)
    dma = pltpu.SemaphoreType.DMA
    scratch = [
        pltpu.VMEM((rows, devices * cols), bf16),
        pltpu.VMEM((rows, width), f32),
        pltpu.VMEM(gq_shape, bf16),
        pltpu.VMEM((width, cols), f32),
        pltpu.VMEM(gq_shape, bf16),
        pltpu.VMEM(gq_shape[1:], bf16),
        dma((devices - 1,)),
        dma((devices - 1,)),
        dma,
        dma((parts - 1,)),
        dma((parts - 1,)),
        dma((devices - 1,)),
        dma((devices - 1,)),
        dma,
    ]
    for wide in wides:
        piece = (out_rows, wide)
        scratch += [
            pltpu.VMEM((parts, chips) + piece, bf16),
            pltpu.VMEM((parts, chips) + piece, bf16),
            pltpu.VMEM((parts - 1, chips) + piece, bf16),
            pltpu.VMEM((chips,) + piece, bf16),
            pltpu.VMEM((chips - 1,) + piece, bf16),
            dma((3,)),
            dma((parts - 1,)),
            dma((parts - 1,)),
            dma((chips - 1,)),
            dma((chips - 1,)),
            dma,
        ]
    scratch += staged(ins) + [
        pltpu.VMEM((rows, width), bf16),
        pltpu.VMEM((rows, width), bf16),
        dma((len(ins),)),
        dma((2,)),
    ]
    return pl.pallas_call(
        kernel,
        name="final_exchange",
        out_shape=[
            jax.ShapeDtypeStruct((rows, width), bf16),
            jax.ShapeDtypeStruct((rows, width), bf16),
            jax.ShapeDtypeStruct(gq_shape[1:], bf16),
        ]
        + [jax.ShapeDtypeStruct((out_rows, wide), f32) for wide in wides],
        in_specs=[hbm] * (1 + count + len(ins)),
        out_specs=[hbm] * 3 + [vmem] * count,
        scratch_shapes=scratch,
        compiler_params=pltpu.CompilerParams(
            collective_id=collective_id, has_side_effects=True, vmem_limit_bytes=60 << 20
        ),
    )(qkv_cot, *token_grads, *ins)


def on_device(
    tokens,
    out_grad,
    doc_ids,
    expert_picks,
    w_query,
    key_weight_matrix,
    value_weight_matrix,
    w_out,
    w_router,
    gain_attn,
    gain_moe,
    expert_in,
    expert_out,
):
    devices, parts = lax.axis_size("seq"), lax.axis_size("dp")
    me = lax.axis_index("seq")
    rows, width = tokens.shape[1:]
    length = rows * devices
    experts = w_router.shape[1]
    heads = QUERY_HEADS // devices
    group = QUERY_HEADS // KEY_VALUE_HEADS
    q_width = heads * HEAD_SIZE
    w_rows = w_query.shape[0]

    w_cols = HEADS_LANES + LANES
    low, mask, doc_rows, misc, gains = prepare(
        expert_in, expert_out, expert_picks[0].T, doc_ids, w_router.T, gain_attn, gain_moe
    )
    expert_full = lax.all_gather(low, "dp", axis=1, tiled=True)
    chips = devices // 2

    def shift(x, k):
        return lax.ppermute(x, "seq", [(i, (i + 2 * k) % devices) for i in range(devices)])

    tok_all, doc_all, mask_all, middle_cot, misc_full, gains_full, w_own_all, wo_full, w_all = first_exchange(
        0,
        tokens[0],
        out_grad[0],
        doc_rows,
        mask,
        misc,
        gains,
        w_query,
        key_weight_matrix,
        value_weight_matrix,
        w_out,
    )
    w_full = lax.all_gather(w_all, "dp", axis=1, tiled=True)
    held, tok_all = lax.optimization_barrier((out_grad[0], tok_all))
    cots = [held] + [
        middle_cot if k == chips // 2 else shift(held, k) for k in range(1, chips)
    ]
    w_own_all = w_own_all.reshape(width, w_cols)
    wo_full = wo_full.reshape(width, width)
    misc_full = misc_full.reshape(width, LANES)
    table = rope_table(devices, rows)

    normed_a, q_all, kv_all, attended_own, ot, lse = attend_forward(
        tok_all, w_own_all, gains_full, table, doc_all, heads
    )
    attended, mid, normed_m = attended_exchange(
        1, attended_own, tokens[0], wo_full, gains_full
    )
    (_, _, _, moe_sum, gate_cot, e_grads, *branches) = moe_exchange(
        2, normed_m, cots, mask_all, misc_full, expert_full
    )
    e_grads = lax.psum_scatter(e_grads, "dp", scatter_dimension=1, tiled=True)
    heads_cot, router_pack, mid_cot, grad_wo = middle_exchange(
        4, moe_sum, gate_cot, normed_m, misc_full, mask, mid, out_grad[0], gains_full,
        wo_full, attended, q_width,
    )
    heads_cot, branches = lax.optimization_barrier((heads_cot, branches))
    branches = [
        branches[0],
        lax.ppermute(branches[1], "seq", [(i, i ^ 2) for i in range(devices)]),
    ] + [shift(branches[1 + k], 2 * k) for k in range(1, chips // 2)]
    qkv_cot = attend_backward(q_all, kv_all, heads_cot, ot, lse, table, doc_all, heads)
    qkv_cot, branches = lax.optimization_barrier((qkv_cot, branches))
    out_rows = w_rows // devices
    input_grad, output, grad_qkv, grad_wo, router_pack = final_exchange(
        5,
        qkv_cot,
        normed_a,
        [
            grad_wo.reshape(parts, devices, out_rows, width),
            router_pack.reshape(parts, devices, out_rows, LANES),
        ],
        w_full,
        tokens[0],
        mid_cot,
        gains_full,
        mid,
        branches,
    )

    (
        grad_e_in, grad_e_out, grad_wq, grad_wk, grad_wv, grad_wo, grad_router, grad_gain_m,
        grad_gain_a, input_grad, output,
    ) = finish(
        e_grads,
        grad_qkv,
        grad_wo,
        router_pack,
        input_grad,
        output,
        [w_query, key_weight_matrix, value_weight_matrix],
        gain_attn.reshape(devices, out_rows),
        heads,
        experts,
    )
    input_grad, output = input_grad[None], output[None]
    grad_router = grad_router.T
    grad_gain_a = grad_gain_a.reshape(out_rows)
    grad_gain_m = grad_gain_m.reshape(out_rows)
    return (
        output,
        input_grad,
        grad_wq,
        grad_wk,
        grad_wv,
        grad_wo,
        grad_router,
        grad_gain_a,
        grad_gain_m,
        grad_e_in,
        grad_e_out,
    )


def solution(mesh):
    return jax.shard_map(
        on_device,
        mesh=mesh,
        in_specs=(
            P("dp", "seq", None),
            P("dp", "seq", None),
            P("dp", "seq"),
            P("dp", "seq", None),
            P("dp", None),
            P("dp", None),
            P("dp", None),
            P("dp", None),
            P("dp", None),
            P("dp"),
            P("dp"),
            P("seq", "dp", None),
            P("seq", "dp", None),
        ),
        out_specs=(
            P("dp", "seq", None),
            P("dp", "seq", None),
            P(("dp", "seq"), None),
            P(("dp", "seq"), None),
            P(("dp", "seq"), None),
            P(("dp", "seq"), None),
            P(("dp", "seq"), None),
            P(("dp", "seq")),
            P(("dp", "seq")),
            P("seq", "dp", None),
            P("seq", "dp", None),
        ),
        check_vma=False,
    )
```

```python
import functools

import jax
import jax.numpy as jnp
import numpy as np
from jax import lax
from jax.experimental import pallas as pl
from jax.experimental.pallas import tpu as pltpu
from jax.sharding import PartitionSpec as P

MESH = pl.DeviceIdType.MESH
PIECES = 2


def _block(ref, j, cut):
    if cut is None:
        return ref.at[j]
    return ref.at[:, pl.ds(pl.multiple_of(j * cut, cut), cut)]


def exchange(collective_id, ops, prepare=None, given=(), work=(), made=None, keep=None):
    axes = tuple(dict.fromkeys(axis for _, axis, _, _ in ops))
    size = {axis: lax.axis_size(axis) for axis in axes}
    out_shapes, out_specs, scratch, places = [], [], [], []
    for kind, axis, x, cut in ops:
        count = size[axis]
        out_spec = pl.BlockSpec(memory_space=pl.ANY)
        extra = []
        lead = (PIECES,) if kind == "gather" and axis == "seq" else ()
        if kind == "shift":
            shape, dtype, copies = x.shape, x.dtype, 1
        elif kind == "share":
            shape, dtype, copies = (count,) + x.shape, x.dtype, 2 * (count - 1)
        elif kind == "gather":
            shape, dtype = (count,) + x.shape, x.dtype
            copies = count - 1 if axis == "dp" else 3 + 4 * (count // 2 - 1)
        elif kind == "swap":
            copies, dtype = count - 1, x.dtype
            if cut is None:
                shape = x.shape
            elif cut[0] == "in":
                shape = (count, x.shape[0], cut[1])
            else:
                shape = (x.shape[1], count * cut[1])
        out_shapes.append(jax.ShapeDtypeStruct(shape, dtype))
        out_specs.append(out_spec)
        places.append((len(scratch), len(extra)))
        scratch += [
            pltpu.SemaphoreType.DMA(lead + (copies,)),
            pltpu.SemaphoreType.DMA(lead + (max(copies, count),)),
            pltpu.SemaphoreType.DMA,
        ] + extra

    early = [x for _, _, x, cut in ops if not isinstance(cut, int)]
    own_scratch = len(scratch)

    def kernel(*refs):
        ins, refs = list(refs[: len(early)]), refs[len(early) :]
        extra_in, refs = refs[: len(given)], refs[len(given) :]
        outs, refs = refs[: len(ops)], refs[len(ops) :]
        if keep is not None:
            kept, refs = refs[0], refs[1:]
        work, extra_work = refs[:own_scratch], refs[own_scratch:]
        ins += [None] * (len(ops) - len(early))
        me = {axis: lax.axis_index(axis) for axis in axes}
        barrier = pltpu.get_barrier_semaphore()
        for axis in axes:
            for k in range(1, size[axis]):
                pl.semaphore_signal(
                    barrier,
                    inc=1,
                    device_id={axis: lax.rem(me[axis] + k, size[axis])},
                    device_id_type=MESH,
                )
        pl.semaphore_wait(barrier, sum(size[axis] - 1 for axis in axes))

        def remote(axis, src, dst, send, recv, to):
            return pltpu.make_async_remote_copy(
                src_ref=src,
                dst_ref=dst,
                send_sem=send,
                recv_sem=recv,
                device_id={axis: to},
                device_id_type=MESH,
            )

        second, third = [], []
        for (kind, axis, _, cut), x, o, (at, extra) in zip(ops, ins, outs, places):
            if isinstance(cut, int):
                if x is None and cut == 0:
                    all_refs = list(extra_in) + list(extra_work[:-1])
                    prepare(all_refs)
                    late = made(all_refs)
                    leave = pltpu.make_async_copy(all_refs[keep[1]], kept, extra_work[-1])
                    leave.start()
                    third.append(leave.wait)
                x, cut = late[cut], None
            send, recv, local = work[at : at + 3]
            count, my = size[axis], me[axis]
            if kind == "swap":
                into = cut[1] if cut is not None and cut[0] == "out" else None
                outof = cut[1] if cut is not None and cut[0] == "in" else None
                own = pltpu.make_async_copy(_block(x, my, outof), _block(o, my, into), local)
                own.start()
                third.append(own.wait)
                for k in range(1, count):
                    to = lax.rem(my + k, count)
                    copy = remote(
                        axis,
                        _block(x, to, outof),
                        _block(o, my, into),
                        send.at[k - 1],
                        recv.at[k - 1],
                        to,
                    )
                    copy.start()
                    frm = lax.rem(my + count - k, count)
                    arrive = remote(
                        axis,
                        _block(x, to, outof),
                        _block(o, frm, into),
                        send.at[k - 1],
                        recv.at[k - 1],
                        to,
                    )
                    third.append(copy.wait_send)
                    third.append(arrive.wait_recv)
            elif kind == "gather" and axis == "dp":
                own = pltpu.make_async_copy(x, o.at[my], local)
                own.start()
                third.append(own.wait)
                for k in range(1, count):
                    to = lax.rem(my + k, count)
                    frm = lax.rem(my + count - k, count)
                    copy = remote(axis, x, o.at[my], send.at[k - 1], recv.at[k - 1], to)
                    copy.start()
                    third.append(copy.wait_send)
                    third.append(
                        remote(
                            axis, x, o.at[frm], send.at[k - 1], recv.at[k - 1], to
                        ).wait_recv
                    )
            elif kind == "shift":
                copy = remote(
                    axis, x, o, send.at[0], recv.at[0], lax.rem(my + 2 * (count // 4), count)
                )
                second.append((count // 4 + 0.9, copy.start))
                third.append(copy.wait)
            elif kind == "share":
                seq, half = me["seq"], x.shape[0] // 2
                core = lax.rem(seq, 2)
                sibling = seq + 1 - 2 * core
                own = pltpu.make_async_copy(x, o.at[my], local)
                own.start()
                third.append(own.wait)

                def side_of(ref, which, half=half):
                    return ref.at[pl.ds(which * half, half)]

                def relay(k, axis=axis, x=x, o=o, send=send, recv=recv, count=count, my=my, core=core, sibling=sibling, side_of=side_of):
                    to = lax.rem(my + k, count)
                    frm = lax.rem(my + count - k, count)
                    remote(
                        axis,
                        side_of(x, core),
                        side_of(o.at[frm], core),
                        send.at[k - 1],
                        recv.at[k - 1],
                        to,
                    ).wait_recv()
                    slot = count - 2 + k
                    spot = side_of(o.at[frm], core)
                    over = remote("seq", spot, spot, send.at[slot], recv.at[slot], sibling)
                    over.start()
                    third.append(over.wait_send)
                    third.append(
                        remote(
                            "seq",
                            spot,
                            side_of(o.at[frm], 1 - core),
                            send.at[slot],
                            recv.at[slot],
                            sibling,
                        ).wait_recv
                    )

                for k in range(1, count):
                    to = lax.rem(my + k, count)
                    copy = remote(
                        axis,
                        side_of(x, core),
                        side_of(o.at[my], core),
                        send.at[k - 1],
                        recv.at[k - 1],
                        to,
                    )
                    copy.start()
                    third.append(copy.wait_send)
                    second.append((k + 0.75, functools.partial(relay, k)))
            elif kind == "gather":
                chips = count // 2
                chip, core = my // 2, lax.rem(my, 2)
                sibling = my + 1 - 2 * core
                own = pltpu.make_async_copy(x, o.at[my], local)
                own.start()
                third.append(own.wait)

                cuts = PIECES if x.shape[0] % (16 * PIECES) == 0 else 1
                size_of = x.shape[0] // cuts

                def cut_of(ref, i, size_of=size_of):
                    return ref.at[pl.ds(i * size_of, size_of)]

                def line(src, b, i, slot, to, axis=axis, o=o, send=send, recv=recv, core=core, cut_of=cut_of):
                    return remote(
                        axis, src, cut_of(o.at[2 * b + core], i), send.at[i, slot], recv.at[i, b], to
                    )

                def across(src, b, i, slot, half, axis=axis, o=o, send=send, recv=recv, chips=chips, sibling=sibling, cut_of=cut_of):
                    return remote(
                        axis,
                        src,
                        cut_of(o.at[2 * b + half], i),
                        send.at[i, slot],
                        recv.at[i, chips + b],
                        sibling,
                    )

                def guarded(where, act):
                    pl.when(where)(act)

                for i in range(cuts):
                    for slot, where, to in ((0, chip > 0, my - 2), (1, chip < chips - 1, my + 2)):
                        copy = line(cut_of(x, i), chip, i, slot, to)
                        guarded(where, copy.start)
                        third.append(functools.partial(guarded, where, copy.wait_send))
                for i in range(cuts):
                    copy = across(cut_of(x, i), chip, i, 2, core)
                    copy.start()
                    third.append(copy.wait_send)
                    third.append(across(cut_of(x, i), chip, i, 2, 1 - core).wait_recv)

                def hop(k, side, i, chips=chips, chip=chip, core=core, my=my, x=x, o=o, line=line, across=across, cut_of=cut_of):
                    b = chip + side * k
                    there = (b >= 0) & (b < chips)
                    onward = there & ((chip - side >= 0) & (chip - side < chips))
                    slot = 3 + (k - 1) * 4 + (side + 1)
                    spot = cut_of(o.at[2 * b + core], i)
                    further = line(spot, b, i, slot, my - 2 * side)
                    over = across(spot, b, i, slot + 1, core)
                    arrived = line(cut_of(x, i), b, i, slot, my)
                    brought = across(cut_of(x, i), b, i, slot + 1, 1 - core)

                    @pl.when(there)
                    def _():
                        arrived.wait_recv()

                    guarded(onward, further.start)
                    guarded(there, over.start)
                    third.append(functools.partial(guarded, onward, further.wait_send))
                    third.append(functools.partial(guarded, there, over.wait_send))
                    third.append(functools.partial(guarded, there, brought.wait_recv))

                for k in range(1, chips):
                    for i in range(cuts):
                        for side in (-1, 1):
                            second.append((k + i / cuts, functools.partial(hop, k, side, i)))
        for _, run in sorted(second, key=lambda item: item[0]):
            run()
        for wait in third:
            wait()

    return pl.pallas_call(
        kernel,
        name=f"exchange{collective_id}",
        out_shape=out_shapes + ([] if keep is None else [keep[0]]),
        in_specs=[pl.BlockSpec(memory_space=pl.ANY)] * (len(early) + len(given)),
        out_specs=out_specs + ([] if keep is None else [pl.BlockSpec(memory_space=pl.ANY)]),
        scratch_shapes=scratch
        + list(work)
        + ([] if keep is None else [pltpu.SemaphoreType.DMA]),
        compiler_params=pltpu.CompilerParams(
            collective_id=collective_id, has_side_effects=True, vmem_limit_bytes=60 << 20
        ),
    )(*early, *given)

QUERY_HEADS = 16
KEY_VALUE_HEADS = 8
HEAD_SIZE = 64
FFE = 512
TOP = 8

att_mult = 0.015625
res_mult = 0.22
norm_eps = 1e-06
rope_theta = 10000.0
LANES = 128
bf16 = jnp.bfloat16
f32 = jnp.float32
HEADS_LANES = 128


def dot_nt(a, b):
    return lax.dot_general(a, b, (((1,), (1,)), ((), ())), preferred_element_type=f32)


def dot_nn(a, b):
    return lax.dot_general(a, b, (((1,), (0,)), ((), ())), preferred_element_type=f32)


def dot_tn(a, b):
    return lax.dot_general(a, b, (((0,), (0,)), ((), ())), preferred_element_type=f32)


def turn(x):
    half = HEAD_SIZE // 2
    lane = lax.broadcasted_iota(jnp.int32, x.shape, 1)
    width = x.shape[1]
    return jnp.where(
        lax.rem(lane, HEAD_SIZE) < half, pltpu.roll(x, width - half, 1), pltpu.roll(x, half, 1)
    )


def rope_table(blocks, rows):
    half = HEAD_SIZE // 2
    frequency = np.float32(rope_theta) ** (
        -np.arange(half, dtype=np.float32) * np.float32(2.0) / np.float32(HEAD_SIZE)
    )
    angles = (frequency[:, None] * np.arange(blocks * rows, dtype=np.float32)[None, :]).astype(
        np.float32
    )
    table = np.concatenate([np.cos(angles), np.sin(angles)], axis=0).astype(np.float32)
    return jnp.asarray(table.reshape(HEAD_SIZE, blocks, rows).transpose(1, 0, 2))


def spread_table(table):
    half = HEAD_SIZE // 2
    turned = table.T
    cos, sin = turned[:, :half], turned[:, half:]
    return (
        jnp.concatenate([cos, cos] * (LANES // HEAD_SIZE), axis=1),
        jnp.concatenate([-sin, sin] * (LANES // HEAD_SIZE), axis=1),
    )


def across_lanes(row, lanes):
    return jnp.broadcast_to(row, (lanes, row.shape[1])).T


def first_block(docs_ref, i):
    docs = docs_ref[:, 0, :].astype(f32)
    own = lax.broadcasted_iota(jnp.int32, docs.shape, 0) == i
    lane = lax.broadcasted_iota(jnp.int32, docs.shape, 1)
    start = jnp.sum(jnp.where(own & (lane == 0), docs, 0.0))
    ends = (lane == docs.shape[1] - 1) & (docs < start)
    return jnp.sum(jnp.where(ends, 1.0, 0.0)).astype(jnp.int32)


def stack_heads(x, heads):
    return jnp.concatenate(
        [x[:, h * HEAD_SIZE : (h + 1) * HEAD_SIZE] for h in range(heads)], axis=0
    )


def gain_row(ref, which):
    return jnp.concatenate(
        [ref[p, which : which + 1, :] for p in range(ref.shape[0])], axis=1
    ).astype(f32)


def attend_forward(tok_all, w_own, gain, table, docs, heads):
    blocks, rows, width = tok_all.shape
    length = blocks * rows
    cols = heads * rows
    out_width = heads * HEAD_SIZE

    def kernel(tok, w, gain_ref, table_ref, docs_ref, na_ref, q_ref, kv_ref, att_ref, ot_ref, lse_ref, k_scr, vt_scr, doc_scr):
        i = pl.program_id(0)
        x = tok[0].astype(f32)
        scale = lax.rsqrt(jnp.mean(x * x, axis=-1, keepdims=True) + norm_eps)
        na = (x * scale * gain_row(gain_ref, 0)).astype(bf16)
        na_ref[0] = na
        qkv = dot_nn(na, w[...])
        c, s = spread_table(table_ref[0])
        q, kv = qkv[:, :HEADS_LANES], qkv[:, HEADS_LANES:]
        q = (q * c + turn(q) * s).astype(bf16)
        lane = lax.broadcasted_iota(jnp.int32, kv.shape, 1)
        kv = jnp.where(lane < HEAD_SIZE, kv * c + turn(kv) * s, kv).astype(bf16)
        q_ref[0] = q
        kv_ref[0] = kv
        k_scr[i] = kv[:, :HEAD_SIZE]
        vt_scr[i] = kv.astype(f32).T[HEAD_SIZE:].astype(bf16)
        q2 = stack_heads(q, heads)
        doc_row = docs_ref[i, :1].astype(f32)
        doc_scr[i] = across_lanes(doc_row, LANES)
        doc_query = jnp.concatenate([doc_row] * heads, axis=1)
        query = i * rows + lax.rem(lax.broadcasted_iota(jnp.int32, (1, cols), 1), rows)
        key_iota = lax.broadcasted_iota(jnp.int32, (rows, cols), 0)

        def step(j, carry):
            top, total, ot = carry
            scores = dot_nt(k_scr[j], q2) * att_mult
            key = key_iota + j * rows
            same = jnp.concatenate([doc_scr[j]] * (cols // LANES), axis=1) == doc_query
            scores = jnp.where(same & (key <= query), scores, -1e30)
            new_top = jnp.maximum(top, jnp.max(scores, axis=0, keepdims=True))
            p = jnp.exp(scores - new_top)
            keep = jnp.exp(top - new_top)
            total = total * keep + jnp.sum(p, axis=0, keepdims=True)
            ot = ot * keep + dot_nn(vt_scr[j], p.astype(bf16))
            return new_top, total, ot

        top, total, ot = lax.fori_loop(
            first_block(docs_ref, i),
            i + 1,
            step,
            (
                jnp.full((1, cols), -1e30, f32),
                jnp.zeros((1, cols), f32),
                jnp.zeros((HEAD_SIZE, cols), f32),
            ),
        )
        ot = ot / total
        ot_ref[0] = ot
        lse_ref[0] = top + jnp.log(total)
        out = ot.T
        att_ref[0] = jnp.concatenate(
            [out[h * rows : (h + 1) * rows] for h in range(heads)], axis=1
        ).astype(bf16)

    def block(shape):
        return pl.BlockSpec((1,) + shape, lambda i: (i, 0, 0))

    def whole(shape):
        return pl.BlockSpec(shape, lambda i: (0,) * len(shape))

    grid_spec = pltpu.PrefetchScalarGridSpec(
        num_scalar_prefetch=0,
        grid=(blocks,),
        in_specs=[
            block((rows, width)),
            whole(w_own.shape),
            whole(gain.shape),
            block((HEAD_SIZE, rows)),
            whole(docs.shape),
        ],
        out_specs=[
            block((rows, width)),
            block((rows, HEADS_LANES)),
            block((rows, LANES)),
            block((rows, out_width)),
            block((HEAD_SIZE, cols)),
            block((1, cols)),
        ],
        scratch_shapes=[
            pltpu.VMEM((blocks, rows, HEAD_SIZE), bf16),
            pltpu.VMEM((blocks, HEAD_SIZE, rows), bf16),
            pltpu.VMEM((blocks, rows, LANES), f32),
        ],
    )
    return pl.pallas_call(
        kernel,
        name="attend_forward",
        grid_spec=grid_spec,
        out_shape=[
            jax.ShapeDtypeStruct((blocks, rows, width), bf16),
            jax.ShapeDtypeStruct((blocks, rows, HEADS_LANES), bf16),
            jax.ShapeDtypeStruct((blocks, rows, LANES), bf16),
            jax.ShapeDtypeStruct((blocks, rows, out_width), bf16),
            jax.ShapeDtypeStruct((blocks, HEAD_SIZE, cols), f32),
            jax.ShapeDtypeStruct((blocks, 1, cols), f32),
        ],
        cost_estimate=pl.CostEstimate(
            flops=2 * length * width * 256 + 2 * length * length * cols // rows * 128,
            bytes_accessed=2 * length * width * 4,
            transcendentals=length * length,
        ),
        compiler_params=pltpu.CompilerParams(
            dimension_semantics=("arbitrary",), vmem_limit_bytes=60 << 20
        ),
    )(
        tok_all,
        w_own,
        gain,
        table,
        docs,
    )


def attend_backward(q_all, kv_all, cot, ot, lse, table, docs, heads):
    blocks, rows, _ = q_all.shape
    length = blocks * rows
    cols = heads * rows

    def kernel(q_ref, kv_ref, do_ref, ot_ref, lse_ref, table_ref, docs_ref, out_ref, dk_scr, dv_scr, dq_scr, doc_scr):
        i = pl.program_id(0)

        @pl.when(i == 0)
        def _():
            dk_scr[...] = jnp.zeros_like(dk_scr)
            dv_scr[...] = jnp.zeros_like(dv_scr)

        q2 = stack_heads(q_ref[0], heads)
        do2 = stack_heads(do_ref[0], heads)
        delta = jnp.sum(do2.astype(f32).T * ot_ref[0], axis=0, keepdims=True)
        log_total = lse_ref[0]
        doc_row = docs_ref[i, :1].astype(f32)
        doc_scr[i] = across_lanes(doc_row, LANES)
        doc_query = jnp.concatenate([doc_row] * heads, axis=1)
        query = i * rows + lax.rem(lax.broadcasted_iota(jnp.int32, (1, cols), 1), rows)
        key_iota = lax.broadcasted_iota(jnp.int32, (rows, cols), 0)
        dq_scr[...] = jnp.zeros_like(dq_scr)

        @pl.loop(first_block(docs_ref, i), i + 1)
        def _(j):
            kv = kv_ref[j]
            k, v = kv[:, :HEAD_SIZE], kv[:, HEAD_SIZE:]
            scores = dot_nt(k, q2) * att_mult
            key = key_iota + j * rows
            same = jnp.concatenate([doc_scr[j]] * (cols // LANES), axis=1) == doc_query
            p = jnp.where(same & (key <= query), jnp.exp(scores - log_total), 0.0)
            ds = (p * (dot_nt(v, do2) - delta)).astype(bf16)
            dv_scr[j] += dot_nn(p.astype(bf16), do2)
            dk_scr[j] += dot_nn(ds, q2)
            dq_scr[...] += dot_tn(ds, k)

        def rope_back(x, c, s):
            return (x * c - turn(x) * s).astype(bf16)

        dq = dq_scr[...] * att_mult
        dq = [dq[h * rows : (h + 1) * rows] for h in range(heads)]
        if heads * HEAD_SIZE < HEADS_LANES:
            dq.append(jnp.zeros((rows, HEADS_LANES - heads * HEAD_SIZE), f32))
        dq = jnp.concatenate(dq, axis=1).astype(bf16).astype(f32)
        out_ref[i, :, :HEADS_LANES] = rope_back(dq, *spread_table(table_ref[i]))

        @pl.when(i == blocks - 1)
        def _():
            @pl.loop(0, blocks)
            def _(j):
                kv = jnp.concatenate([dk_scr[j] * att_mult, dv_scr[j]], axis=1)
                lane = lax.broadcasted_iota(jnp.int32, kv.shape, 1)
                c, s = spread_table(table_ref[j])
                kv = jnp.where(lane < HEAD_SIZE, kv * c - turn(kv) * s, kv).astype(bf16)
                out_ref[j, :, HEADS_LANES:] = kv

    def block(shape):
        return pl.BlockSpec((1,) + shape, lambda i: (i, 0, 0))

    def whole(shape):
        return pl.BlockSpec(shape, lambda i: (0,) * len(shape))

    grid_spec = pltpu.PrefetchScalarGridSpec(
        num_scalar_prefetch=0,
        grid=(blocks,),
        in_specs=[
            block((rows, HEADS_LANES)),
            whole((blocks, rows, LANES)),
            block((rows, heads * HEAD_SIZE)),
            block((HEAD_SIZE, cols)),
            block((1, cols)),
            whole((blocks, HEAD_SIZE, rows)),
            whole(docs.shape),
        ],
        out_specs=whole((blocks, rows, HEADS_LANES + LANES)),
        scratch_shapes=[
            pltpu.VMEM((blocks, rows, HEAD_SIZE), f32),
            pltpu.VMEM((blocks, rows, HEAD_SIZE), f32),
            pltpu.VMEM((cols, HEAD_SIZE), f32),
            pltpu.VMEM((blocks, rows, LANES), f32),
        ],
    )
    return pl.pallas_call(
        kernel,
        name="attend_backward",
        grid_spec=grid_spec,
        out_shape=jax.ShapeDtypeStruct((blocks, rows, HEADS_LANES + LANES), bf16),
        cost_estimate=pl.CostEstimate(
            flops=5 * length * length * cols // rows * 128,
            bytes_accessed=2 * length * 1024,
            transcendentals=length * length,
        ),
        compiler_params=pltpu.CompilerParams(
            dimension_semantics=("arbitrary",), vmem_limit_bytes=60 << 20
        ),
    )(
        q_all,
        kv_all,
        cot,
        ot,
        lse,
        table,
        docs,
    )


def moe_exchange(collective_id, normed, cots, mask, router, weights):
    devices = lax.axis_size("seq")
    chips = devices // 2
    rows, width = normed.shape
    own_experts = weights.shape[0]
    gate_rows = devices * own_experts

    def order(chip, k):
        left = chip < chips - 1 - chip
        longer = jnp.where(left, chips - 1 - chip, chip)
        near = jnp.where(left, chip + k, chip - k)
        return jnp.where(k <= longer, near, jnp.where(left, chips - 1 - k, k))

    def kernel(*refs):
        x_in, g_in = refs[0], refs[1 : 1 + chips]
        mask_ref, router_ref, w_given = refs[1 + chips : 4 + chips]
        (lin_out, slot_out, hid_out, n_sum, gate_out, g_out) = refs[4 + chips : 10 + chips]
        y_outs = refs[10 + chips : 11 + chips + chips // 2]
        (
            x_all, g_all, win, wout, y_acc, n_acc, gate_acc, gate_stage,
            n_mine, n_far, n_give, n_theirs, y_give, y_theirs, y_pre, y_in,
            lin_st, slot_st, hid_st, gin, gout, hid_ld,
            local, line_send, line_recv, sib_send, sib_recv, g_local, g_send, g_recv,
            n_send, n_recv, y_send, y_recv, far_send, far_recv, gate_send, gate_recv,
            st_sem, y_sem, ld_sem, w_sem, wg_sem, hand_send, hand_recv,
        ) = refs[11 + chips + chips // 2 :]
        me = lax.axis_index("seq")
        chip, core = me // 2, lax.rem(me, 2)
        sibling = me + 1 - 2 * core
        win_copy = pltpu.make_async_copy(
            w_given.at[:, :, pl.ds(0, 2 * FFE)], win, w_sem.at[0]
        )
        wout_copy = pltpu.make_async_copy(
            w_given.at[:, :, pl.ds(2 * FFE, FFE)], wout, w_sem.at[1]
        )
        win_copy.start()
        wout_copy.start()
        barrier = pltpu.get_barrier_semaphore()
        for k in range(1, devices):
            pl.semaphore_signal(
                barrier, inc=1, device_id={"seq": lax.rem(me + k, devices)}, device_id_type=MESH
            )
        pl.semaphore_wait(barrier, devices - 1)

        def remote(src, dst, send, recv, to):
            return pltpu.make_async_remote_copy(
                src_ref=src,
                dst_ref=dst,
                send_sem=send,
                recv_sem=recv,
                device_id={"seq": to},
                device_id_type=MESH,
            )

        half = rows // PIECES

        def piece(b, core_of, i):
            return x_all.at[2 * b + core_of, pl.ds(i * half, half)]

        def line(src, b, i, slot, to):
            return remote(
                src, piece(b, core, i), line_send.at[i, slot], line_recv.at[i, b], to
            )

        def across(src, b, core_of, i):
            return remote(
                src, piece(b, core_of, i), sib_send.at[i, b], sib_recv.at[i, b], sibling
            )

        def own_piece(i):
            return x_in.at[pl.ds(i * half, half)]

        def pass_on(b, i, to):
            return line(piece(b, core, i), b, i, 2 + b, to)

        def to_sibling(b, i):
            return across(piece(b, core, i), b, core, i)

        def own_sends(act):
            for i in range(PIECES):

                @pl.when(chip > 0)
                def _(i=i):
                    act(line(own_piece(i), chip, i, 0, me - 2))

                @pl.when(chip < chips - 1)
                def _(i=i):
                    act(line(own_piece(i), chip, i, 1, me + 2))

            for i in range(PIECES):
                act(across(own_piece(i), chip, core, i))

        def cot_to_sibling(k):
            b = lax.rem(chip + chips - k, chips)
            return remote(
                g_in[k], g_all.at[2 * b + core], g_send.at[k], g_recv.at[b], sibling
            )

        def cot_local(k):
            b = lax.rem(chip + chips - k, chips)
            return pltpu.make_async_copy(g_in[k], g_all.at[2 * b + core], g_local.at[k])

        own_sends(lambda copy: copy.start())
        own = pltpu.make_async_copy(x_in, x_all.at[me], local)
        own.start()
        for k in range(chips):
            cot_to_sibling(k).start()
            cot_local(k).start()
        gin[...] = jnp.zeros_like(gin)
        gout[...] = jnp.zeros_like(gout)
        own.wait()
        for k in range(chips):
            cot_local(k).wait()
        win_copy.wait()
        wout_copy.wait()

        def gate_copy(block):
            return remote(
                gate_stage.at[block],
                gate_out.at[me],
                gate_send.at[block],
                gate_recv.at[me],
                block,
            )

        def n_copy(p):
            return remote(n_give, n_theirs.at[p], n_send.at[p], n_recv.at[p], sibling)

        def y_copy(p):
            return remote(y_give, y_theirs.at[p], y_send.at[p], y_recv.at[p], sibling)

        pairs = chips // 2
        pair = chip // 2
        mate = chip + 1 - 2 * lax.rem(chip, 2)

        def y_leave(b, k):
            return pltpu.make_async_copy(y_pre.at[b], y_outs[k], y_sem.at[k])

        def y_hand(b):
            far = lax.rem(b // 2 + pairs - pair, pairs) - 1
            return remote(
                y_pre.at[b], y_in.at[far], hand_send.at[far], hand_recv.at[far], 2 * mate + core
            )

        def stage_copies(e, block):
            return [
                pltpu.make_async_copy(lin_st.at[e], lin_out.at[e, block], st_sem.at[0, e]),
                pltpu.make_async_copy(slot_st.at[e], slot_out.at[e, block], st_sem.at[1, e]),
                pltpu.make_async_copy(hid_st.at[e], hid_out.at[e, block], st_sem.at[2, e]),
            ]

        def far_copy(b):
            return remote(
                n_mine.at[b], n_far.at[chip], far_send.at[b], far_recv.at[chip], 2 * b + core
            )

        def fold(k):
            b, p = order(chip, k), lax.rem(k, 2)
            n_copy(p).wait_recv()
            both = n_acc[...].astype(bf16).astype(f32) + n_theirs[p].astype(f32)

            @pl.when(b == chip)
            def _():
                n_sum[...] = both

            @pl.when(b != chip)
            def _():
                n_mine[b] = both.astype(bf16)
                far_copy(b).start()

            y_copy(p).wait_recv()
            y_pre[b] = (y_acc[...] + y_theirs[p].astype(f32)).astype(bf16)

            @pl.when(b == chip)
            def _():
                y_leave(b, 0).start()

            @pl.when(b == mate)
            def _():
                y_leave(b, 1).start()

            @pl.when((b != chip) & (lax.rem(b + chip, 2) == 0))
            def _():
                y_hand(b).start()

        def compute(block, before):
            x = x_all[block]
            there = mask_ref[block] > 0
            logits = jnp.where(there, dot_nn(x, router_ref[...]), -1e30)
            gates = jnp.where(
                there, jnp.exp(logits - jnp.max(logits, axis=1, keepdims=True)), 0.0
            )
            gates = gates / jnp.sum(gates, axis=1, keepdims=True)
            lane = lax.broadcasted_iota(jnp.int32, gates.shape, 1)
            y_acc[...] = jnp.zeros_like(y_acc)
            n_acc[...] = jnp.zeros_like(n_acc)
            gate_acc[...] = jnp.zeros_like(gate_acc)

            @pl.loop(0, own_experts)
            def _(e):
                gate = jnp.sum(
                    jnp.where(lane == me * own_experts + e, gates, 0.0), axis=1, keepdims=True
                )
                lin = dot_nn(x_all[block], win[e])
                gate_lin, up_lin = lin[:, :FFE], lin[:, FFE:]
                sig = 0.5 + 0.5 * jnp.tanh(0.5 * gate_lin)
                silu = gate_lin * sig
                hidden = (silu * up_lin).astype(bf16)

                @pl.when(before)
                def _():
                    for copy in stage_copies(e, block):
                        copy.wait()

                hid_st[e] = hidden
                res = dot_nt(hidden, wout[e]).astype(bf16).astype(f32)
                y_acc[...] += gate * res
                cot = g_all[block].astype(f32) * res_mult
                gate_acc[...] += jnp.where(
                    lane == me * own_experts + e, jnp.sum(cot * res, axis=1, keepdims=True), 0.0
                )
                slot = (gate * cot).astype(bf16)
                slot_st[e] = slot
                hidden_cot = dot_nn(slot, wout[e])
                lin_cot = jnp.concatenate(
                    [
                        hidden_cot * up_lin * (sig * (1.0 + gate_lin * (1.0 - sig))),
                        hidden_cot * silu,
                    ],
                    axis=1,
                ).astype(bf16)
                lin_st[e] = lin_cot
                for copy in stage_copies(e, block):
                    copy.start()
                n_acc[...] += dot_nt(lin_cot, win[e]).astype(bf16).astype(f32)

            gate_stage[block] = gate_acc[...].T[:gate_rows]

            @pl.when(block != me)
            def _():
                gate_copy(block).start()

            @pl.when(block == me)
            def _():
                gate_out[block] = gate_stage[block]

        def hop(k, i):
            for side in (-1, 1):
                away = chip + side * k

                @pl.when((k > 0) & (k < chips) & (away >= 0) & (away < chips))
                def _(side=side, away=away):
                    pass_on(away, i, me).wait_recv()

                    @pl.when((chip - side >= 0) & (chip - side < chips))
                    def _():
                        pass_on(away, i, me - 2 * side).start()

                    to_sibling(away, i).start()

        @pl.loop(0, chips)
        def _(k):
            b = order(chip, k)
            hop(k, 1)
            for i in range(PIECES):
                across(own_piece(i), b, 1 - core, i).wait_recv()
            remote(
                x_in, g_all.at[2 * b + 1 - core], g_send.at[0], g_recv.at[b], sibling
            ).wait_recv()

            @pl.loop(0, 2)
            def _(h):
                @pl.when(h == 1)
                def _():
                    hop(k + 1, 0)

                compute(2 * b + lax.rem(core + 1 + h, 2), (k > 0) | (h > 0))

                @pl.when(h == 0)
                def _():
                    p = lax.rem(k, 2)

                    @pl.when(k > 0)
                    def _():
                        n_copy(1 - p).wait_send()
                        y_copy(1 - p).wait_send()

                    n_give[...] = n_acc[...].astype(bf16)
                    y_give[...] = y_acc[...].astype(bf16)
                    n_copy(p).start()
                    y_copy(p).start()

                @pl.when(h == 1)
                def _():
                    fold(k)

        for e in range(own_experts):
            for copy in stage_copies(e, 0):
                copy.wait()

        def loads(t, p):
            e, b = lax.rem(t, own_experts), t // own_experts
            pair = pl.ds(2 * b, 2)
            return [
                pltpu.make_async_copy(
                    lin_out.at[e, pair], g_all.at[pl.ds(4 * p, 2)], ld_sem.at[0, p]
                ),
                pltpu.make_async_copy(
                    slot_out.at[e, pair], g_all.at[pl.ds(4 * p + 2, 2)], ld_sem.at[1, p]
                ),
                pltpu.make_async_copy(hid_out.at[e, pair], hid_ld.at[p], ld_sem.at[2, p]),
            ]

        for copy in loads(jnp.int32(0), 0):
            copy.start()
        @pl.loop(0, chips * own_experts)
        def _(t):
            p = lax.rem(t, 2)
            for copy in loads(t, p):
                copy.wait()

            @pl.when(t + 1 < chips * own_experts)
            def _():
                for copy in loads(t + 1, 1 - p):
                    copy.start()

            e, b = lax.rem(t, own_experts), t // own_experts
            x = x_all[pl.ds(2 * b, 2)].reshape(2 * rows, width)
            lin_cot = g_all[pl.ds(4 * p, 2)].reshape(2 * rows, width)
            gin[e] += dot_tn(x, lin_cot)
            slot = g_all[pl.ds(4 * p + 2, 2)].reshape(2 * rows, width)
            gout[e] += dot_tn(slot, hid_ld[p].reshape(2 * rows, FFE))

        @pl.loop(1, chips)
        def _(k):
            for side in (-1, 1):
                away = chip + side * k

                for i in range(PIECES):

                    @pl.when((away >= 0) & (away < chips))
                    def _(side=side, away=away, i=i):
                        to_sibling(away, i).wait_send()

                        @pl.when((chip - side >= 0) & (chip - side < chips))
                        def _():
                            pass_on(away, i, me - 2 * side).wait_send()

        own_sends(lambda copy: copy.wait_send())

        def keep_of(j):
            return 2 * lax.rem(pair + 1 + j, pairs) + 1 - lax.rem(chip, 2)

        leaving = []
        for e in range(own_experts):
            for j in range(width // rows):
                i = e * (width // rows) + j
                x_all[i] = gin[e, j * rows : (j + 1) * rows].astype(bf16)
                g_all[i, :, :FFE] = gout[e, j * rows : (j + 1) * rows].astype(bf16)
                at = 2 * len(leaving)
                here = pl.ds(j * rows, rows)
                leaving.append(
                    (
                        pltpu.make_async_copy(
                            x_all.at[i], g_out.at[e, here, pl.ds(0, 2 * FFE)], wg_sem.at[at]
                        ),
                        pltpu.make_async_copy(
                            g_all.at[i, :, pl.ds(0, FFE)],
                            g_out.at[e, here, pl.ds(2 * FFE, FFE)],
                            wg_sem.at[at + 1],
                        ),
                    )
                )
                for copy in leaving[-1]:
                    copy.start()

        for j in range(pairs - 1):
            b = keep_of(j)
            y_hand(b).wait_recv()
            y_pre[b] = (y_pre[b].astype(f32) + y_in[j].astype(f32)).astype(bf16)
            y_leave(b, 2 + j).start()

        @pl.loop(1, chips)
        def _(k):
            b = order(chip, k)
            remote(
                n_mine.at[b], n_far.at[b], far_send.at[b], far_recv.at[b], 2 * b + core
            ).wait_recv()
            n_sum[...] += n_far[b].astype(f32)
            far_copy(b).wait_send()

        @pl.loop(1, devices)
        def _(k):
            block = lax.rem(me + k, devices)
            remote(
                gate_stage.at[block],
                gate_out.at[block],
                gate_send.at[block],
                gate_recv.at[block],
                block,
            ).wait_recv()
            gate_copy(block).wait_send()

        n_copy((chips - 1) % 2).wait_send()
        y_copy((chips - 1) % 2).wait_send()
        for both in leaving:
            for copy in both:
                copy.wait()
        y_leave(chip, 0).wait()
        y_leave(mate, 1).wait()
        for j in range(pairs - 1):
            y_leave(keep_of(j), 2 + j).wait()
            y_hand(keep_of(j) + chip - mate).wait_send()

        for k in range(chips):
            cot_to_sibling(k).wait_send()

    hbm = pl.BlockSpec(memory_space=pl.ANY)
    vmem = pl.BlockSpec(memory_space=pltpu.VMEM)
    block = (rows, width)
    dma = pltpu.SemaphoreType.DMA
    flops = 9 * own_experts * 2 * devices * rows * width * FFE // 1
    return pl.pallas_call(
        kernel,
        name="moe_exchange",
        out_shape=[
            jax.ShapeDtypeStruct((own_experts, devices, rows, 2 * FFE), bf16),
            jax.ShapeDtypeStruct((own_experts, devices) + block, bf16),
            jax.ShapeDtypeStruct((own_experts, devices, rows, FFE), bf16),
            jax.ShapeDtypeStruct(block, f32),
            jax.ShapeDtypeStruct((devices, gate_rows, rows), f32),
            jax.ShapeDtypeStruct((own_experts, width, 3 * FFE), bf16),
        ]
        + [jax.ShapeDtypeStruct(block, bf16)] * (1 + chips // 2),
        in_specs=[hbm] * (1 + chips) + [vmem] * 2 + [hbm],
        out_specs=[hbm] * 3 + [vmem] * 2 + [hbm] * (2 + chips // 2),
        scratch_shapes=[
            pltpu.VMEM((devices,) + block, bf16),
            pltpu.VMEM((devices,) + block, bf16),
            pltpu.VMEM((own_experts, width, 2 * FFE), bf16),
            pltpu.VMEM((own_experts, width, FFE), bf16),
            pltpu.VMEM(block, f32),
            pltpu.VMEM(block, f32),
            pltpu.VMEM((rows, LANES), f32),
            pltpu.VMEM((devices, gate_rows, rows), f32),
            pltpu.VMEM((chips,) + block, bf16),
            pltpu.VMEM((chips,) + block, bf16),
            pltpu.VMEM(block, bf16),
            pltpu.VMEM((2,) + block, bf16),
            pltpu.VMEM(block, bf16),
            pltpu.VMEM((2,) + block, bf16),
            pltpu.VMEM((chips,) + block, bf16),
            pltpu.VMEM((chips // 2 - 1,) + block, bf16),
            pltpu.VMEM((own_experts, rows, 2 * FFE), bf16),
            pltpu.VMEM((own_experts,) + block, bf16),
            pltpu.VMEM((own_experts, rows, FFE), bf16),
            pltpu.VMEM((own_experts, width, 2 * FFE), f32),
            pltpu.VMEM((own_experts, width, FFE), f32),
            pltpu.VMEM((2, 2, rows, FFE), bf16),
        ]
        + [dma]
        + [
            dma(count)
            for count in (
                (PIECES, chips + 2), (PIECES, chips), (PIECES, chips), (PIECES, chips),
                (chips,), (chips,), (chips,), (2,), (2,), (2,), (2,),
                (chips,), (chips,), (devices,), (devices,),
            )
        ]
        + [
            dma((3, own_experts)),
            dma((1 + chips // 2,)),
            dma((3, 2)),
            dma((2,)),
            dma((2 * own_experts * (width // rows),)),
            dma((chips // 2 - 1,)),
            dma((chips // 2 - 1,)),
        ],
        cost_estimate=pl.CostEstimate(
            flops=flops, bytes_accessed=40 << 20, transcendentals=devices * rows * FFE * 2
        ),
        compiler_params=pltpu.CompilerParams(
            collective_id=collective_id, has_side_effects=True, vmem_limit_bytes=63 << 20
        ),
    )(normed, *cots, mask, router, weights)


class Links:
    def __init__(self, axes):
        self.size = {axis: lax.axis_size(axis) for axis in axes}
        self.me = {axis: lax.axis_index(axis) for axis in axes}

    def barrier(self):
        sem = pltpu.get_barrier_semaphore()
        for axis, size in self.size.items():
            for k in range(1, size):
                pl.semaphore_signal(
                    sem,
                    inc=1,
                    device_id={axis: lax.rem(self.me[axis] + k, size)},
                    device_id_type=MESH,
                )
        pl.semaphore_wait(sem, sum(size - 1 for size in self.size.values()))

    def copy(self, axis, src, dst, send, recv, to):
        return pltpu.make_async_remote_copy(
            src_ref=src,
            dst_ref=dst,
            send_sem=send,
            recv_sem=recv,
            device_id={axis: to},
            device_id_type=MESH,
        )

    def swap_start(self, axis, src, dst, send, recv, local):
        me, size = self.me[axis], self.size[axis]
        pltpu.make_async_copy(src.at[me], dst.at[me], local).start()
        for k in range(1, size):
            to = lax.rem(me + k, size)
            self.copy(axis, src.at[to], dst.at[me], send.at[k - 1], recv.at[k - 1], to).start()

    def swap_wait(self, axis, src, dst, send, recv, local):
        me, size = self.me[axis], self.size[axis]
        pltpu.make_async_copy(src.at[me], dst.at[me], local).wait()
        for k in range(1, size):
            frm = lax.rem(me + size - k, size)
            self.copy(axis, src.at[frm], dst.at[frm], send.at[k - 1], recv.at[k - 1], frm).wait()


def loads(pairs, sems):
    copies = [
        pltpu.make_async_copy(src, dst, sems.at[i]) for i, (src, dst) in enumerate(pairs)
    ]
    for copy in copies:
        copy.start()
    return copies


def staged(arrays):
    return [pltpu.VMEM(x.shape, x.dtype) for x in arrays]


def swap_sems(size):
    dma = pltpu.SemaphoreType.DMA
    return [dma((size - 1,)), dma((size - 1,)), dma]


def attended_exchange(collective_id, attended_own, tokens, w_out, gain):
    devices, rows, cols = attended_own.shape
    width = tokens.shape[1]

    ins = [tokens, w_out, gain]
    outs = [
        jax.ShapeDtypeStruct((rows, width), bf16),
        jax.ShapeDtypeStruct((rows, width), f32),
        jax.ShapeDtypeStruct((rows, width), bf16),
    ]

    def kernel(att_in, *refs):
        given, results = refs[:3], refs[3:6]
        tok, w_all, gain_ref = refs[6:9]
        att_ref, mid_ref, norm_ref, got, in_sem, out_sem, *sems = refs[9:]
        links = Links(("seq",))
        arriving = loads(list(zip(given, (tok, w_all, gain_ref))), in_sem)
        links.barrier()
        links.swap_start("seq", att_in, got, *sems)
        for copy in arriving:
            copy.wait()
        links.swap_wait("seq", att_in, got, *sems)
        attended = jnp.concatenate([got[j] for j in range(devices)], axis=1)
        att_ref[...] = attended
        mid = tok[...].astype(f32) + res_mult * dot_nn(attended, w_all[...])
        mid_ref[...] = mid
        scale = lax.rsqrt(jnp.mean(mid * mid, axis=-1, keepdims=True) + norm_eps)
        norm_ref[...] = (mid * scale * gain_row(gain_ref, 1)).astype(bf16)
        for copy in loads(list(zip((att_ref, mid_ref, norm_ref), results)), out_sem):
            copy.wait()

    hbm = pl.BlockSpec(memory_space=pl.ANY)
    dma = pltpu.SemaphoreType.DMA
    return pl.pallas_call(
        kernel,
        name="attended_exchange",
        out_shape=outs,
        in_specs=[hbm] * 4,
        out_specs=[hbm] * 3,
        scratch_shapes=staged(ins)
        + staged(outs)
        + [pltpu.VMEM(attended_own.shape, bf16), dma((3,)), dma((3,))]
        + swap_sems(devices),
        compiler_params=pltpu.CompilerParams(
            collective_id=collective_id, has_side_effects=True, vmem_limit_bytes=60 << 20
        ),
    )(attended_own, *ins)


def middle_exchange(
    collective_id, moe_sum, gate_cot, normed, router, mask, mid, out_grad, gain, w_out, attended, cols
):
    devices, gate_rows, rows = gate_cot.shape
    width = normed.shape[1]
    experts = gate_rows

    ins = [moe_sum, gate_cot, normed, router, mask, mid, out_grad, gain, w_out, attended]
    outs = [
        jax.ShapeDtypeStruct((width, LANES), bf16),
        jax.ShapeDtypeStruct((rows, width), f32),
        jax.ShapeDtypeStruct((width, width), bf16),
    ]

    def kernel(*refs):
        given, heads_out, results, refs = refs[:10], refs[10], refs[11:14], refs[14:]
        (
            moe_ref, gate_ref, norm_ref, router_ref, mask_ref, mid_ref, cot_ref, gain_ref, w_all, att_ref,
            pack_out, mid_cot_out, wo_out, give, in_sem, out_sem, *sems,
        ) = refs
        links = Links(("seq",))
        arriving = loads(list(zip(given, refs[:10])), in_sem)
        links.barrier()
        for copy in arriving:
            copy.wait()
        there = mask_ref[...] > 0
        logits = jnp.where(there, dot_nn(norm_ref[...], router_ref[...]), -1e30)
        gates = jnp.where(
            there, jnp.exp(logits - jnp.max(logits, axis=1, keepdims=True)), 0.0
        )
        gates = gates / jnp.sum(gates, axis=1, keepdims=True)
        gate = gate_ref[0]
        for j in range(1, devices):
            gate = gate + gate_ref[j]
        gate = jnp.concatenate([gate, jnp.zeros((LANES - gate_rows, rows), f32)], axis=0).T
        pick_cot = gates * (gate - jnp.sum(gates * gate, axis=1, keepdims=True))
        logit_cot = pick_cot.astype(bf16)
        cot = moe_ref[...] + dot_nt(logit_cot, router_ref[...])
        mid = mid_ref[...]
        scale = lax.rsqrt(jnp.mean(mid * mid, axis=-1, keepdims=True) + norm_eps)
        gain_grad = jnp.sum(cot * mid * scale, axis=0, keepdims=True)
        weighted = cot * gain_row(gain_ref, 1)
        mid_cot = (
            cot_ref[...].astype(f32)
            + scale * weighted
            - mid * (scale * scale * scale) * jnp.mean(weighted * mid, axis=-1, keepdims=True)
        )
        mid_cot_out[...] = mid_cot
        branch_cot = (res_mult * mid_cot).astype(bf16)
        attended_cot = dot_nt(branch_cot, w_all[...]).astype(bf16)
        for j in range(devices):
            give[j] = attended_cot[:, j * cols : (j + 1) * cols]
        links.swap_start("seq", give, heads_out, *sems)
        wo_out[...] = dot_tn(att_ref[...], branch_cot).astype(bf16)
        pack = dot_tn(norm_ref[...], logit_cot)
        lane = lax.broadcasted_iota(jnp.int32, pack.shape, 1)
        pack_out[...] = jnp.where(
            lane == experts, jnp.broadcast_to(gain_grad, (LANES, width)).T, pack
        ).astype(bf16)
        for copy in loads(list(zip((pack_out, mid_cot_out, wo_out), results)), out_sem):
            copy.wait()
        links.swap_wait("seq", give, heads_out, *sems)

    hbm = pl.BlockSpec(memory_space=pl.ANY)
    dma = pltpu.SemaphoreType.DMA
    return pl.pallas_call(
        kernel,
        name="middle_exchange",
        out_shape=[jax.ShapeDtypeStruct((devices, rows, cols), bf16)] + outs,
        in_specs=[hbm] * 10,
        out_specs=[hbm] * 4,
        scratch_shapes=staged(ins)
        + staged(outs)
        + [pltpu.VMEM((devices, rows, cols), bf16), dma((10,)), dma((3,))]
        + swap_sems(devices),
        compiler_params=pltpu.CompilerParams(
            collective_id=collective_id, has_side_effects=True, vmem_limit_bytes=60 << 20
        ),
    )(*ins)


def finish(e_grads, grad_qkv, grad_wo, pack, input_grad, output, weights, gain, heads, experts):
    own_experts, e_rows, e_cols = e_grads.shape
    devices, out_rows, _ = grad_qkv.shape
    q_width = heads * HEAD_SIZE
    share = devices // KEY_VALUE_HEADS if devices > KEY_VALUE_HEADS else 1
    steps = 4
    chunk = e_rows // steps
    me = lax.axis_index("seq").astype(jnp.int32).reshape(1)

    def kernel(
        me_ref, e_ref, qkv_ref, wo_ref, pack_ref, in_ref, out_ref, wq, wk, wv, gain_ref,
        e_in, e_out, gq, gk, gv, gwo, grouter, ggain_m, ggain_a, in_grad, output_ref,
    ):
        e_in[...] = e_ref[:, :, : 2 * FFE].astype(f32)
        e_out[...] = e_ref[:, :, 2 * FFE :].astype(f32)

        @pl.when(pl.program_id(0) == 0)
        def _():
            blocks = [qkv_ref[j].astype(f32) for j in range(devices)]

            def per_head(first):
                heads_of = []
                for j in range(KEY_VALUE_HEADS):
                    part = blocks[j * share][:, first : first + HEAD_SIZE]
                    for i in range(1, share):
                        part = part + blocks[j * share + i][:, first : first + HEAD_SIZE]
                    heads_of.append(part)
                return jnp.concatenate(heads_of, axis=1)

            grad_q = jnp.concatenate([b[:, :q_width] for b in blocks], axis=1)
            grad_k = per_head(HEADS_LANES)
            grad_v = per_head(HEADS_LANES + HEAD_SIZE)
            gq[...], gk[...], gv[...] = grad_q, grad_k, grad_v

            def rounded(ref):
                return ref[...].astype(bf16).astype(f32)

            def row(column):
                return jnp.broadcast_to(column, (out_rows, LANES)).T[:1]

            gain_grad = (
                jnp.sum(rounded(wq) * grad_q, axis=1, keepdims=True)
                + jnp.sum(rounded(wk) * grad_k, axis=1, keepdims=True)
                + jnp.sum(rounded(wv) * grad_v, axis=1, keepdims=True)
            )
            own = lax.broadcasted_iota(jnp.int32, (devices, 1), 0) == me_ref[0]
            own_gain = jnp.sum(jnp.where(own, rounded(gain_ref), 0.0), axis=0, keepdims=True)
            ggain_a[...] = row(gain_grad) / own_gain
            gwo[...] = wo_ref[...]
            grouter[...] = pack_ref[...].T[:experts]
            ggain_m[...] = row(pack_ref[:, experts : experts + 1])
            in_grad[...] = in_ref[...]
            output_ref[...] = out_ref[...]

    def whole(x):
        return pl.BlockSpec(x.shape, lambda i, _: (0,) * len(x.shape))

    def own_rows(x):
        return pl.BlockSpec((out_rows, x.shape[1]), lambda i, me_ref: (me_ref[0], 0))

    def shape(*dims, dtype=f32):
        return jax.ShapeDtypeStruct(dims, dtype)

    rest = [grad_qkv, grad_wo, pack, input_grad, output]
    kv_width = KEY_VALUE_HEADS * HEAD_SIZE
    small = [
        shape(out_rows, devices * q_width),
        shape(out_rows, kv_width),
        shape(out_rows, kv_width),
        shape(*grad_wo.shape),
        shape(experts, out_rows),
        shape(1, out_rows),
        shape(1, out_rows),
        shape(*input_grad.shape, dtype=bf16),
        shape(*output.shape, dtype=bf16),
    ]
    return pl.pallas_call(
        kernel,
        name="finish",
        grid_spec=pltpu.PrefetchScalarGridSpec(
            num_scalar_prefetch=1,
            grid=(steps,),
            in_specs=[pl.BlockSpec((own_experts, chunk, e_cols), lambda i, _: (0, i, 0))]
            + [whole(x) for x in rest]
            + [own_rows(x) for x in weights]
            + [whole(gain)],
            out_specs=[
                pl.BlockSpec((own_experts, chunk, 2 * FFE), lambda i, _: (0, i, 0)),
                pl.BlockSpec((own_experts, chunk, FFE), lambda i, _: (0, i, 0)),
            ]
            + [whole(x) for x in small],
        ),
        out_shape=[
            shape(own_experts, e_rows, 2 * FFE),
            shape(own_experts, e_rows, FFE),
        ]
        + small,
        cost_estimate=pl.CostEstimate(flops=0, bytes_accessed=8 << 20, transcendentals=0),
        compiler_params=pltpu.CompilerParams(
            dimension_semantics=("arbitrary",), vmem_limit_bytes=60 << 20
        ),
    )(me, e_grads, *rest, *weights, gain)


def first_exchange(collective_id, tokens, out_grad, docs, mask, misc, gains, w_query, w_key, w_value, w_out):
    devices, parts = lax.axis_size("seq"), lax.axis_size("dp")
    w_rows, width = w_out.shape
    heads = QUERY_HEADS // devices
    q_width = heads * HEAD_SIZE
    group = QUERY_HEADS // KEY_VALUE_HEADS
    w_cols = HEADS_LANES + LANES
    weights = [w_query, w_key, w_value, w_out]

    def prepare(refs):
        given, (wq, wk, wv, wo, w_all, wo_low, sem) = refs[:4], refs[4:]
        for copy in loads(list(zip(given, (wq, wk, wv, wo))), sem):
            copy.wait()
        wo_low[...] = wo[...].astype(bf16)
        for s in range(devices):
            kv = s * heads // group * HEAD_SIZE
            pieces = [wq[:, s * q_width : (s + 1) * q_width]]
            if q_width < HEADS_LANES:
                pieces.append(jnp.zeros((w_rows, HEADS_LANES - q_width), f32))
            pieces += [wk[:, kv : kv + HEAD_SIZE], wv[:, kv : kv + HEAD_SIZE]]
            w_all[s] = jnp.concatenate(pieces, axis=1).astype(bf16)

    return exchange(
        collective_id,
        [
            ("gather", "seq", tokens, None),
            ("gather", "seq", docs, None),
            ("gather", "seq", mask, None),
            ("shift", "seq", out_grad, None),
            ("share", "dp", misc, None),
            ("gather", "dp", gains, None),
            ("gather", "dp", jax.ShapeDtypeStruct((w_rows, w_cols), bf16), 0),
            ("share", "dp", jax.ShapeDtypeStruct((w_rows, width), bf16), 1),
        ],
        prepare=prepare,
        given=weights,
        work=staged(weights)
        + [
            pltpu.VMEM((devices, w_rows, w_cols), bf16),
            pltpu.VMEM((w_rows, width), bf16),
            pltpu.SemaphoreType.DMA((4,)),
        ],
        made=lambda refs: (refs[8].at[lax.axis_index("seq")], refs[9]),
        keep=(jax.ShapeDtypeStruct((devices, w_rows, w_cols), bf16), 8),
    )


def prepare(expert_in, expert_out, picks, docs, w_router, gain_attn, gain_moe):
    own_experts, w_rows, _ = expert_in.shape
    rows, experts = picks.shape[1], w_router.shape[0]
    steps = 4
    chunk = w_rows // steps

    def kernel(
        e_in, e_out, picks_ref, docs_ref, router, gain_a, gain_m, low, mask, docs_out, misc, gains
    ):
        low[:, :, : 2 * FFE] = e_in[...].astype(bf16)
        low[:, :, 2 * FFE :] = e_out[...].astype(bf16)

        @pl.when(pl.program_id(0) == 0)
        def _():
            expert = lax.broadcasted_iota(jnp.int32, (LANES, rows), 0)
            chosen = picks_ref[:1] == expert
            for k in range(1, TOP):
                chosen = chosen | (picks_ref[k : k + 1] == expert)
            mask[...] = jnp.where(chosen, 1.0, 0.0).T.astype(bf16)
            docs_out[...] = jnp.broadcast_to(docs_ref[...], docs_out.shape)
            misc[...] = jnp.concatenate(
                [router[...], jnp.zeros((LANES - experts, w_rows), f32)], axis=0
            ).T.astype(bf16)
            upper = lax.broadcasted_iota(jnp.int32, (8, w_rows), 0) == 0
            gains[...] = jnp.where(upper, gain_a[...], gain_m[...]).astype(bf16)

    def whole(shape):
        return pl.BlockSpec(shape, lambda i: (0,) * len(shape))

    def part(x):
        return pl.BlockSpec((own_experts, chunk, x.shape[2]), lambda i: (0, i, 0))

    small = [picks, docs, w_router, gain_attn[None], gain_moe[None]]
    outs = [
        jax.ShapeDtypeStruct((rows, LANES), bf16),
        jax.ShapeDtypeStruct((8, rows), jnp.int32),
        jax.ShapeDtypeStruct((w_rows, LANES), bf16),
        jax.ShapeDtypeStruct((8, w_rows), bf16),
    ]
    return pl.pallas_call(
        kernel,
        name="prepare",
        grid=(steps,),
        out_shape=[jax.ShapeDtypeStruct((own_experts, w_rows, 3 * FFE), bf16)] + outs,
        in_specs=[part(expert_in), part(expert_out)] + [whole(x.shape) for x in small],
        out_specs=[pl.BlockSpec((own_experts, chunk, 3 * FFE), lambda i: (0, i, 0))]
        + [whole(x.shape) for x in outs],
        compiler_params=pltpu.CompilerParams(
            dimension_semantics=("arbitrary",), vmem_limit_bytes=60 << 20
        ),
    )(expert_in, expert_out, *small)


def final_exchange(
    collective_id, qkv_cot, normed, token_grads, w_full, tokens, mid_cot, gain, mid, branches
):
    devices, parts = lax.axis_size("seq"), lax.axis_size("dp")
    chips = devices // 2
    _, rows, cols = qkv_cot.shape
    width = tokens.shape[1]
    out_rows = token_grads[0].shape[2]
    gq_shape = (parts, devices, out_rows, cols)
    count = len(token_grads)
    wides = [x.shape[3] for x in token_grads]
    token_grads = [x.reshape(parts, chips, 2, out_rows, x.shape[3]) for x in token_grads]

    ins = [w_full, normed, qkv_cot, tokens, mid_cot, gain, mid, *branches]

    def kernel(*refs):
        qkv_in = refs[0]
        gt_in = refs[1 : 1 + count]
        given = refs[1 + count : 1 + count + len(ins)]
        refs = refs[1 + count + len(ins) :]
        in_grad_out, output_out, gq_out = refs[:3]
        gt_out = refs[3 : 3 + count]
        refs = refs[3 + count :]
        (
            qkv_tok, nac, gq_in, grad, gq_recv, gq_sum,
            q_send, q_recv, local, gq_send, gq_rsem, gqz_send, gqz_recv, gq_local,
        ) = refs[:14]
        work = [refs[14 + 11 * i : 25 + 11 * i] for i in range(count)]
        refs = refs[14 + 11 * count :]
        local_ins, (in_grad, output, in_sem, out_sem) = refs[: len(ins)], refs[len(ins) :]
        w_all, normed_all, qkv_all, tok_ref, mid_cot_ref, gain_ref, mid_ref, *y_refs = local_ins
        me, my = lax.axis_index("seq"), lax.axis_index("dp")
        chip, core = me // 2, lax.rem(me, 2)
        sibling = me + 1 - 2 * core
        arriving = loads(list(zip(given, local_ins)), in_sem)
        barrier = pltpu.get_barrier_semaphore()
        for axis, index, size in (("seq", me, devices), ("dp", my, parts)):
            for k in range(1, size):
                pl.semaphore_signal(
                    barrier,
                    inc=1,
                    device_id={axis: lax.rem(index + k, size)},
                    device_id_type=MESH,
                )
        pl.semaphore_wait(barrier, devices + parts - 2)

        def remote(axis, src, dst, send, recv, to):
            return pltpu.make_async_remote_copy(
                src_ref=src,
                dst_ref=dst,
                send_sem=send,
                recv_sem=recv,
                device_id={axis: to},
                device_id_type=MESH,
            )

        sent = []

        def columns(j):
            return qkv_tok.at[:, pl.ds(pl.multiple_of(j * cols, cols), cols)]

        for x, w in zip(gt_in, work):
            mine, theirs, far, near, last, sems, dp_send, dp_recv, z_send, z_recv, _ = w
            copy = remote(
                "seq", x.at[:, :, 1 - core], theirs, sems.at[0], sems.at[1], sibling
            )
            copy.start()
            sent.append(copy)
            pltpu.make_async_copy(x.at[:, :, core], mine, sems.at[2]).start()
        own = pltpu.make_async_copy(qkv_in.at[me], columns(me), local)
        own.start()
        for k in range(1, devices):
            to = lax.rem(me + k, devices)
            copy = remote(
                "seq", qkv_in.at[to], columns(me), q_send.at[k - 1], q_recv.at[k - 1], to
            )
            copy.start()
            sent.append(copy)

        for x, w in zip(gt_in, work):
            mine, theirs, far, near, last, sems, dp_send, dp_recv, z_send, z_recv, _ = w
            remote("seq", x.at[:, :, core], theirs, sems.at[0], sems.at[1], sibling).wait_recv()
            pltpu.make_async_copy(x.at[:, :, core], mine, sems.at[2]).wait()
            mine[...] = (mine[...].astype(f32) + theirs[...].astype(f32)).astype(bf16)
            for k in range(1, parts):
                to = lax.rem(my + k, parts)
                copy = remote(
                    "dp", mine.at[to], far.at[k - 1], dp_send.at[k - 1], dp_recv.at[k - 1], to
                )
                copy.start()
                sent.append(copy)

        for copy in arriving:
            copy.wait()
        grad[...] = jnp.zeros_like(grad)

        @pl.loop(0, devices)
        def _(j):
            grad[...] += dot_tn(normed_all[j], qkv_all[j])

        gq_in[...] = grad[...].astype(bf16).reshape(gq_shape)
        for k in range(1, parts):
            to = lax.rem(my + k, parts)
            copy = remote(
                "dp", gq_in.at[to], gq_recv.at[my], gq_send.at[k - 1], gq_rsem.at[k - 1], to
            )
            copy.start()
            sent.append(copy)
        own_q = pltpu.make_async_copy(gq_in.at[my], gq_recv.at[my], gq_local)
        own_q.start()
        total = y_refs[0][...].astype(f32)
        for k in range(1, len(branches)):
            total = total + y_refs[k][...].astype(f32)
        output[...] = (mid_ref[...] + res_mult * total).astype(bf16)
        leaving = [pltpu.make_async_copy(output, output_out, out_sem.at[0])]
        leaving[0].start()

        for k in range(devices):
            frm = lax.rem(me + devices - k, devices)
            if k == 0:
                own.wait()
            else:
                remote(
                    "seq", qkv_in.at[frm], columns(frm), q_send.at[k - 1], q_recv.at[k - 1], frm
                ).wait_recv()
            part = dot_nt(columns(frm)[...], w_all[frm])
            nac[...] = part if k == 0 else nac[...] + part

        resid = tok_ref[...].astype(f32)
        scale = lax.rsqrt(jnp.mean(resid * resid, axis=-1, keepdims=True) + norm_eps)
        weighted = nac[...] * gain_row(gain_ref, 0)
        in_grad[...] = (
            mid_cot_ref[...]
            + scale * weighted
            - resid
            * (scale * scale * scale)
            * jnp.mean(weighted * resid, axis=-1, keepdims=True)
        ).astype(bf16)

        leaving.append(pltpu.make_async_copy(in_grad, in_grad_out, out_sem.at[1]))
        leaving[1].start()
        own_q.wait()
        for k in range(1, parts):
            frm = lax.rem(my + parts - k, parts)
            remote(
                "dp", gq_in.at[frm], gq_recv.at[frm], gq_send.at[k - 1], gq_rsem.at[k - 1], frm
            ).wait_recv()
        summed = gq_recv[0].astype(f32)
        for p in range(1, parts):
            summed = summed + gq_recv[p].astype(f32)
        gq_sum[...] = summed.astype(bf16)
        own_z = pltpu.make_async_copy(gq_sum.at[me], gq_out.at[me], gq_local)
        own_z.start()
        for k in range(1, devices):
            to = lax.rem(me + k, devices)
            copy = remote(
                "seq", gq_sum.at[to], gq_out.at[me], gqz_send.at[k - 1], gqz_recv.at[k - 1], to
            )
            copy.start()
            sent.append(copy)
        for w in work:
            mine, theirs, far, near, last, sems, dp_send, dp_recv, z_send, z_recv, _ = w
            summed = mine[my].astype(f32)
            for k in range(1, parts):
                remote(
                    "dp", mine.at[0], far.at[k - 1], dp_send.at[k - 1], dp_recv.at[k - 1], my
                ).wait_recv()
                summed = summed + far[k - 1].astype(f32)
            near[...] = summed.astype(bf16)
            for k in range(1, chips):
                to = lax.rem(chip + k, chips)
                copy = remote(
                    "seq",
                    near.at[to],
                    last.at[k - 1],
                    z_send.at[k - 1],
                    z_recv.at[k - 1],
                    2 * to + core,
                )
                copy.start()
                sent.append(copy)

        for o, w in zip(gt_out, work):
            mine, theirs, far, near, last, sems, dp_send, dp_recv, z_send, z_recv, _ = w
            summed = near[chip].astype(f32)
            for k in range(1, chips):
                remote(
                    "seq", near.at[0], last.at[k - 1], z_send.at[k - 1], z_recv.at[k - 1], me
                ).wait_recv()
                summed = summed + last[k - 1].astype(f32)
            o[...] = summed
        own_z.wait()
        for k in range(1, devices):
            frm = lax.rem(me + devices - k, devices)
            remote(
                "seq", gq_sum.at[frm], gq_out.at[frm], gqz_send.at[k - 1], gqz_recv.at[k - 1], frm
            ).wait_recv()
        for copy in sent:
            copy.wait_send()
        for copy in leaving:
            copy.wait()

    hbm = pl.BlockSpec(memory_space=pl.ANY)
    vmem = pl.BlockSpec(memory_space=pltpu.VMEM)
    dma = pltpu.SemaphoreType.DMA
    scratch = [
        pltpu.VMEM((rows, devices * cols), bf16),
        pltpu.VMEM((rows, width), f32),
        pltpu.VMEM(gq_shape, bf16),
        pltpu.VMEM((width, cols), f32),
        pltpu.VMEM(gq_shape, bf16),
        pltpu.VMEM(gq_shape[1:], bf16),
        dma((devices - 1,)),
        dma((devices - 1,)),
        dma,
        dma((parts - 1,)),
        dma((parts - 1,)),
        dma((devices - 1,)),
        dma((devices - 1,)),
        dma,
    ]
    for wide in wides:
        piece = (out_rows, wide)
        scratch += [
            pltpu.VMEM((parts, chips) + piece, bf16),
            pltpu.VMEM((parts, chips) + piece, bf16),
            pltpu.VMEM((parts - 1, chips) + piece, bf16),
            pltpu.VMEM((chips,) + piece, bf16),
            pltpu.VMEM((chips - 1,) + piece, bf16),
            dma((3,)),
            dma((parts - 1,)),
            dma((parts - 1,)),
            dma((chips - 1,)),
            dma((chips - 1,)),
            dma,
        ]
    scratch += staged(ins) + [
        pltpu.VMEM((rows, width), bf16),
        pltpu.VMEM((rows, width), bf16),
        dma((len(ins),)),
        dma((2,)),
    ]
    return pl.pallas_call(
        kernel,
        name="final_exchange",
        out_shape=[
            jax.ShapeDtypeStruct((rows, width), bf16),
            jax.ShapeDtypeStruct((rows, width), bf16),
            jax.ShapeDtypeStruct(gq_shape[1:], bf16),
        ]
        + [jax.ShapeDtypeStruct((out_rows, wide), f32) for wide in wides],
        in_specs=[hbm] * (1 + count + len(ins)),
        out_specs=[hbm] * 3 + [vmem] * count,
        scratch_shapes=scratch,
        compiler_params=pltpu.CompilerParams(
            collective_id=collective_id, has_side_effects=True, vmem_limit_bytes=60 << 20
        ),
    )(qkv_cot, *token_grads, *ins)


def on_device(
    tokens,
    out_grad,
    doc_ids,
    expert_picks,
    w_query,
    key_weight_matrix,
    value_weight_matrix,
    w_out,
    w_router,
    gain_attn,
    gain_moe,
    expert_in,
    expert_out,
):
    devices, parts = lax.axis_size("seq"), lax.axis_size("dp")
    me = lax.axis_index("seq")
    rows, width = tokens.shape[1:]
    length = rows * devices
    experts = w_router.shape[1]
    heads = QUERY_HEADS // devices
    group = QUERY_HEADS // KEY_VALUE_HEADS
    q_width = heads * HEAD_SIZE
    w_rows = w_query.shape[0]

    w_cols = HEADS_LANES + LANES
    low, mask, doc_rows, misc, gains = prepare(
        expert_in, expert_out, expert_picks[0].T, doc_ids, w_router.T, gain_attn, gain_moe
    )
    expert_full = lax.all_gather(low, "dp", axis=1, tiled=True)
    chips = devices // 2

    def shift(x, k):
        return lax.ppermute(x, "seq", [(i, (i + 2 * k) % devices) for i in range(devices)])

    tok_all, doc_all, mask_all, middle_cot, misc_full, gains_full, w_own_all, wo_full, w_all = first_exchange(
        0,
        tokens[0],
        out_grad[0],
        doc_rows,
        mask,
        misc,
        gains,
        w_query,
        key_weight_matrix,
        value_weight_matrix,
        w_out,
    )
    w_full = lax.all_gather(w_all, "dp", axis=1, tiled=True)
    held, tok_all = lax.optimization_barrier((out_grad[0], tok_all))
    cots = [held] + [
        middle_cot if k == chips // 2 else shift(held, k) for k in range(1, chips)
    ]
    w_own_all = w_own_all.reshape(width, w_cols)
    wo_full = wo_full.reshape(width, width)
    misc_full = misc_full.reshape(width, LANES)
    table = rope_table(devices, rows)

    normed_a, q_all, kv_all, attended_own, ot, lse = attend_forward(
        tok_all, w_own_all, gains_full, table, doc_all, heads
    )
    attended, mid, normed_m = attended_exchange(
        1, attended_own, tokens[0], wo_full, gains_full
    )
    (_, _, _, moe_sum, gate_cot, e_grads, *branches) = moe_exchange(
        2, normed_m, cots, mask_all, misc_full, expert_full
    )
    e_grads = lax.psum_scatter(e_grads, "dp", scatter_dimension=1, tiled=True)
    heads_cot, router_pack, mid_cot, grad_wo = middle_exchange(
        4, moe_sum, gate_cot, normed_m, misc_full, mask, mid, out_grad[0], gains_full,
        wo_full, attended, q_width,
    )
    def across_pairs(x, k):
        def there(i):
            chip = i // 2
            return 2 * (2 * ((chip // 2 + k) % (chips // 2)) + 1 - chip % 2) + i % 2

        return lax.ppermute(x, "seq", [(i, there(i)) for i in range(devices)])

    heads_cot, branches = lax.optimization_barrier((heads_cot, branches))
    branches = [
        branches[0],
        lax.ppermute(branches[1], "seq", [(i, i ^ 2) for i in range(devices)]),
    ] + [across_pairs(branches[1 + k], k) for k in range(1, chips // 2)]
    qkv_cot = attend_backward(q_all, kv_all, heads_cot, ot, lse, table, doc_all, heads)
    qkv_cot, branches = lax.optimization_barrier((qkv_cot, branches))
    out_rows = w_rows // devices
    input_grad, output, grad_qkv, grad_wo, router_pack = final_exchange(
        5,
        qkv_cot,
        normed_a,
        [
            grad_wo.reshape(parts, devices, out_rows, width),
            router_pack.reshape(parts, devices, out_rows, LANES),
        ],
        w_full,
        tokens[0],
        mid_cot,
        gains_full,
        mid,
        branches,
    )

    (
        grad_e_in, grad_e_out, grad_wq, grad_wk, grad_wv, grad_wo, grad_router, grad_gain_m,
        grad_gain_a, input_grad, output,
    ) = finish(
        e_grads,
        grad_qkv,
        grad_wo,
        router_pack,
        input_grad,
        output,
        [w_query, key_weight_matrix, value_weight_matrix],
        gain_attn.reshape(devices, out_rows),
        heads,
        experts,
    )
    input_grad, output = input_grad[None], output[None]
    grad_router = grad_router.T
    grad_gain_a = grad_gain_a.reshape(out_rows)
    grad_gain_m = grad_gain_m.reshape(out_rows)
    return (
        output,
        input_grad,
        grad_wq,
        grad_wk,
        grad_wv,
        grad_wo,
        grad_router,
        grad_gain_a,
        grad_gain_m,
        grad_e_in,
        grad_e_out,
    )


def solution(mesh):
    return jax.shard_map(
        on_device,
        mesh=mesh,
        in_specs=(
            P("dp", "seq", None),
            P("dp", "seq", None),
            P("dp", "seq"),
            P("dp", "seq", None),
            P("dp", None),
            P("dp", None),
            P("dp", None),
            P("dp", None),
            P("dp", None),
            P("dp"),
            P("dp"),
            P("seq", "dp", None),
            P("seq", "dp", None),
        ),
        out_specs=(
            P("dp", "seq", None),
            P("dp", "seq", None),
            P(("dp", "seq"), None),
            P(("dp", "seq"), None),
            P(("dp", "seq"), None),
            P(("dp", "seq"), None),
            P(("dp", "seq"), None),
            P(("dp", "seq")),
            P(("dp", "seq")),
            P("seq", "dp", None),
            P("seq", "dp", None),
        ),
        check_vma=False,
    )
```

```python
import functools

import jax
import jax.numpy as jnp
import numpy as np
from jax import lax
from jax.experimental import pallas as pl
from jax.experimental.pallas import tpu as pltpu
from jax.sharding import PartitionSpec as P

MESH = pl.DeviceIdType.MESH
PIECES = 2


def _block(ref, j, cut):
    if cut is None:
        return ref.at[j]
    return ref.at[:, pl.ds(pl.multiple_of(j * cut, cut), cut)]


def exchange(collective_id, ops, prepare=None, given=(), work=(), made=None, keep=None):
    axes = tuple(dict.fromkeys(axis for _, axis, _, _ in ops))
    size = {axis: lax.axis_size(axis) for axis in axes}
    out_shapes, out_specs, scratch, places = [], [], [], []
    for kind, axis, x, cut in ops:
        count = size[axis]
        out_spec = pl.BlockSpec(memory_space=pl.ANY)
        extra = []
        lead = (PIECES,) if kind == "gather" and axis == "seq" else ()
        if kind == "shift":
            shape, dtype, copies = x.shape, x.dtype, 1
        elif kind == "share":
            shape, dtype, copies = (count,) + x.shape, x.dtype, 2 * (count - 1)
        elif kind == "gather":
            shape, dtype = (count,) + x.shape, x.dtype
            copies = count - 1 if axis == "dp" else 3 + 4 * (count // 2 - 1)
        elif kind == "swap":
            copies, dtype = count - 1, x.dtype
            if cut is None:
                shape = x.shape
            elif cut[0] == "in":
                shape = (count, x.shape[0], cut[1])
            else:
                shape = (x.shape[1], count * cut[1])
        out_shapes.append(jax.ShapeDtypeStruct(shape, dtype))
        out_specs.append(out_spec)
        places.append((len(scratch), len(extra)))
        scratch += [
            pltpu.SemaphoreType.DMA(lead + (copies,)),
            pltpu.SemaphoreType.DMA(lead + (max(copies, count),)),
            pltpu.SemaphoreType.DMA,
        ] + extra

    early = [x for _, _, x, cut in ops if not isinstance(cut, int)]
    own_scratch = len(scratch)

    def kernel(*refs):
        ins, refs = list(refs[: len(early)]), refs[len(early) :]
        extra_in, refs = refs[: len(given)], refs[len(given) :]
        outs, refs = refs[: len(ops)], refs[len(ops) :]
        if keep is not None:
            kept, refs = refs[0], refs[1:]
        work, extra_work = refs[:own_scratch], refs[own_scratch:]
        ins += [None] * (len(ops) - len(early))
        me = {axis: lax.axis_index(axis) for axis in axes}
        barrier = pltpu.get_barrier_semaphore()
        for axis in axes:
            for k in range(1, size[axis]):
                pl.semaphore_signal(
                    barrier,
                    inc=1,
                    device_id={axis: lax.rem(me[axis] + k, size[axis])},
                    device_id_type=MESH,
                )
        pl.semaphore_wait(barrier, sum(size[axis] - 1 for axis in axes))

        def remote(axis, src, dst, send, recv, to):
            return pltpu.make_async_remote_copy(
                src_ref=src,
                dst_ref=dst,
                send_sem=send,
                recv_sem=recv,
                device_id={axis: to},
                device_id_type=MESH,
            )

        second, third = [], []
        for (kind, axis, _, cut), x, o, (at, extra) in zip(ops, ins, outs, places):
            if isinstance(cut, int):
                if x is None and cut == 0:
                    all_refs = list(extra_in) + list(extra_work[:-1])
                    prepare(all_refs)
                    late = made(all_refs)
                    leave = pltpu.make_async_copy(all_refs[keep[1]], kept, extra_work[-1])
                    leave.start()
                    third.append(leave.wait)
                x, cut = late[cut], None
            send, recv, local = work[at : at + 3]
            count, my = size[axis], me[axis]
            if kind == "swap":
                into = cut[1] if cut is not None and cut[0] == "out" else None
                outof = cut[1] if cut is not None and cut[0] == "in" else None
                own = pltpu.make_async_copy(_block(x, my, outof), _block(o, my, into), local)
                own.start()
                third.append(own.wait)
                for k in range(1, count):
                    to = lax.rem(my + k, count)
                    copy = remote(
                        axis,
                        _block(x, to, outof),
                        _block(o, my, into),
                        send.at[k - 1],
                        recv.at[k - 1],
                        to,
                    )
                    copy.start()
                    frm = lax.rem(my + count - k, count)
                    arrive = remote(
                        axis,
                        _block(x, to, outof),
                        _block(o, frm, into),
                        send.at[k - 1],
                        recv.at[k - 1],
                        to,
                    )
                    third.append(copy.wait_send)
                    third.append(arrive.wait_recv)
            elif kind == "gather" and axis == "dp":
                own = pltpu.make_async_copy(x, o.at[my], local)
                own.start()
                third.append(own.wait)
                for k in range(1, count):
                    to = lax.rem(my + k, count)
                    frm = lax.rem(my + count - k, count)
                    copy = remote(axis, x, o.at[my], send.at[k - 1], recv.at[k - 1], to)
                    copy.start()
                    third.append(copy.wait_send)
                    third.append(
                        remote(
                            axis, x, o.at[frm], send.at[k - 1], recv.at[k - 1], to
                        ).wait_recv
                    )
            elif kind == "shift":
                copy = remote(
                    axis, x, o, send.at[0], recv.at[0], lax.rem(my + 2 * (count // 4), count)
                )
                second.append((count // 4 + 0.9, copy.start))
                third.append(copy.wait)
            elif kind == "share":
                seq, half = me["seq"], x.shape[0] // 2
                core = lax.rem(seq, 2)
                sibling = seq + 1 - 2 * core
                own = pltpu.make_async_copy(x, o.at[my], local)
                own.start()
                third.append(own.wait)

                def side_of(ref, which, half=half):
                    return ref.at[pl.ds(which * half, half)]

                def relay(k, axis=axis, x=x, o=o, send=send, recv=recv, count=count, my=my, core=core, sibling=sibling, side_of=side_of):
                    to = lax.rem(my + k, count)
                    frm = lax.rem(my + count - k, count)
                    remote(
                        axis,
                        side_of(x, core),
                        side_of(o.at[frm], core),
                        send.at[k - 1],
                        recv.at[k - 1],
                        to,
                    ).wait_recv()
                    slot = count - 2 + k
                    spot = side_of(o.at[frm], core)
                    over = remote("seq", spot, spot, send.at[slot], recv.at[slot], sibling)
                    over.start()
                    third.append(over.wait_send)
                    third.append(
                        remote(
                            "seq",
                            spot,
                            side_of(o.at[frm], 1 - core),
                            send.at[slot],
                            recv.at[slot],
                            sibling,
                        ).wait_recv
                    )

                for k in range(1, count):
                    to = lax.rem(my + k, count)
                    copy = remote(
                        axis,
                        side_of(x, core),
                        side_of(o.at[my], core),
                        send.at[k - 1],
                        recv.at[k - 1],
                        to,
                    )
                    copy.start()
                    third.append(copy.wait_send)
                    second.append((k + 0.75, functools.partial(relay, k)))
            elif kind == "gather":
                chips = count // 2
                chip, core = my // 2, lax.rem(my, 2)
                sibling = my + 1 - 2 * core
                own = pltpu.make_async_copy(x, o.at[my], local)
                own.start()
                third.append(own.wait)

                cuts = PIECES if x.shape[0] % (16 * PIECES) == 0 else 1
                size_of = x.shape[0] // cuts

                def cut_of(ref, i, size_of=size_of):
                    return ref.at[pl.ds(i * size_of, size_of)]

                def line(src, b, i, slot, to, axis=axis, o=o, send=send, recv=recv, core=core, cut_of=cut_of):
                    return remote(
                        axis, src, cut_of(o.at[2 * b + core], i), send.at[i, slot], recv.at[i, b], to
                    )

                def across(src, b, i, slot, half, axis=axis, o=o, send=send, recv=recv, chips=chips, sibling=sibling, cut_of=cut_of):
                    return remote(
                        axis,
                        src,
                        cut_of(o.at[2 * b + half], i),
                        send.at[i, slot],
                        recv.at[i, chips + b],
                        sibling,
                    )

                def guarded(where, act):
                    pl.when(where)(act)

                for i in range(cuts):
                    for slot, where, to in ((0, chip > 0, my - 2), (1, chip < chips - 1, my + 2)):
                        copy = line(cut_of(x, i), chip, i, slot, to)
                        guarded(where, copy.start)
                        third.append(functools.partial(guarded, where, copy.wait_send))
                for i in range(cuts):
                    copy = across(cut_of(x, i), chip, i, 2, core)
                    copy.start()
                    third.append(copy.wait_send)
                    third.append(across(cut_of(x, i), chip, i, 2, 1 - core).wait_recv)

                def hop(k, side, i, chips=chips, chip=chip, core=core, my=my, x=x, o=o, line=line, across=across, cut_of=cut_of):
                    b = chip + side * k
                    there = (b >= 0) & (b < chips)
                    onward = there & ((chip - side >= 0) & (chip - side < chips))
                    slot = 3 + (k - 1) * 4 + (side + 1)
                    spot = cut_of(o.at[2 * b + core], i)
                    further = line(spot, b, i, slot, my - 2 * side)
                    over = across(spot, b, i, slot + 1, core)
                    arrived = line(cut_of(x, i), b, i, slot, my)
                    brought = across(cut_of(x, i), b, i, slot + 1, 1 - core)

                    @pl.when(there)
                    def _():
                        arrived.wait_recv()

                    guarded(onward, further.start)
                    guarded(there, over.start)
                    third.append(functools.partial(guarded, onward, further.wait_send))
                    third.append(functools.partial(guarded, there, over.wait_send))
                    third.append(functools.partial(guarded, there, brought.wait_recv))

                for k in range(1, chips):
                    for i in range(cuts):
                        for side in (-1, 1):
                            second.append((k + i / cuts, functools.partial(hop, k, side, i)))
        for _, run in sorted(second, key=lambda item: item[0]):
            run()
        for wait in third:
            wait()

    return pl.pallas_call(
        kernel,
        name=f"exchange{collective_id}",
        out_shape=out_shapes + ([] if keep is None else [keep[0]]),
        in_specs=[pl.BlockSpec(memory_space=pl.ANY)] * (len(early) + len(given)),
        out_specs=out_specs + ([] if keep is None else [pl.BlockSpec(memory_space=pl.ANY)]),
        scratch_shapes=scratch
        + list(work)
        + ([] if keep is None else [pltpu.SemaphoreType.DMA]),
        compiler_params=pltpu.CompilerParams(
            collective_id=collective_id, has_side_effects=True, vmem_limit_bytes=60 << 20
        ),
    )(*early, *given)

QUERY_HEADS = 16
KEY_VALUE_HEADS = 8
HEAD_SIZE = 64
FFE = 512
TOP = 8

att_mult = 0.015625
res_mult = 0.22
norm_eps = 1e-06
rope_theta = 10000.0
LANES = 128
bf16 = jnp.bfloat16
f32 = jnp.float32
HEADS_LANES = 128


def dot_nt(a, b):
    return lax.dot_general(a, b, (((1,), (1,)), ((), ())), preferred_element_type=f32)


def dot_nn(a, b):
    return lax.dot_general(a, b, (((1,), (0,)), ((), ())), preferred_element_type=f32)


def dot_tn(a, b):
    return lax.dot_general(a, b, (((0,), (0,)), ((), ())), preferred_element_type=f32)


def turn(x):
    half = HEAD_SIZE // 2
    lane = lax.broadcasted_iota(jnp.int32, x.shape, 1)
    width = x.shape[1]
    return jnp.where(
        lax.rem(lane, HEAD_SIZE) < half, pltpu.roll(x, width - half, 1), pltpu.roll(x, half, 1)
    )


def rope_table(blocks, rows):
    half = HEAD_SIZE // 2
    frequency = np.float32(rope_theta) ** (
        -np.arange(half, dtype=np.float32) * np.float32(2.0) / np.float32(HEAD_SIZE)
    )
    angles = (frequency[:, None] * np.arange(blocks * rows, dtype=np.float32)[None, :]).astype(
        np.float32
    )
    table = np.concatenate([np.cos(angles), np.sin(angles)], axis=0).astype(np.float32)
    return jnp.asarray(table.reshape(HEAD_SIZE, blocks, rows).transpose(1, 0, 2))


def spread_table(table):
    half = HEAD_SIZE // 2
    turned = table.T
    cos, sin = turned[:, :half], turned[:, half:]
    return (
        jnp.concatenate([cos, cos] * (LANES // HEAD_SIZE), axis=1),
        jnp.concatenate([-sin, sin] * (LANES // HEAD_SIZE), axis=1),
    )


def across_lanes(row, lanes):
    return jnp.broadcast_to(row, (lanes, row.shape[1])).T


def first_block(docs_ref, i):
    docs = docs_ref[:, 0, :].astype(f32)
    own = lax.broadcasted_iota(jnp.int32, docs.shape, 0) == i
    lane = lax.broadcasted_iota(jnp.int32, docs.shape, 1)
    start = jnp.sum(jnp.where(own & (lane == 0), docs, 0.0))
    ends = (lane == docs.shape[1] - 1) & (docs < start)
    return jnp.sum(jnp.where(ends, 1.0, 0.0)).astype(jnp.int32)


def stack_heads(x, heads):
    return jnp.concatenate(
        [x[:, h * HEAD_SIZE : (h + 1) * HEAD_SIZE] for h in range(heads)], axis=0
    )


def gain_row(ref, which):
    return jnp.concatenate(
        [ref[p, which : which + 1, :] for p in range(ref.shape[0])], axis=1
    ).astype(f32)


def attend_forward(tok_all, w_own, gain, table, docs, heads):
    blocks, rows, width = tok_all.shape
    length = blocks * rows
    cols = heads * rows
    out_width = heads * HEAD_SIZE

    def kernel(tok, w, gain_ref, table_ref, docs_ref, na_ref, q_ref, kv_ref, att_ref, ot_ref, lse_ref, k_scr, vt_scr, doc_scr):
        i = pl.program_id(0)
        x = tok[0].astype(f32)
        scale = lax.rsqrt(jnp.mean(x * x, axis=-1, keepdims=True) + norm_eps)
        na = (x * scale * gain_row(gain_ref, 0)).astype(bf16)
        na_ref[0] = na
        qkv = dot_nn(na, w[...])
        c, s = spread_table(table_ref[0])
        q, kv = qkv[:, :HEADS_LANES], qkv[:, HEADS_LANES:]
        q = (q * c + turn(q) * s).astype(bf16)
        lane = lax.broadcasted_iota(jnp.int32, kv.shape, 1)
        kv = jnp.where(lane < HEAD_SIZE, kv * c + turn(kv) * s, kv).astype(bf16)
        q_ref[0] = q
        kv_ref[0] = kv
        k_scr[i] = kv[:, :HEAD_SIZE]
        vt_scr[i] = kv.astype(f32).T[HEAD_SIZE:].astype(bf16)
        q2 = stack_heads(q, heads)
        doc_row = docs_ref[i, :1].astype(f32)
        doc_scr[i] = across_lanes(doc_row, LANES)
        doc_query = jnp.concatenate([doc_row] * heads, axis=1)
        query = i * rows + lax.rem(lax.broadcasted_iota(jnp.int32, (1, cols), 1), rows)
        key_iota = lax.broadcasted_iota(jnp.int32, (rows, cols), 0)

        def step(j, carry):
            top, total, ot = carry
            scores = dot_nt(k_scr[j], q2) * att_mult
            key = key_iota + j * rows
            same = jnp.concatenate([doc_scr[j]] * (cols // LANES), axis=1) == doc_query
            scores = jnp.where(same & (key <= query), scores, -1e30)
            new_top = jnp.maximum(top, jnp.max(scores, axis=0, keepdims=True))
            p = jnp.exp(scores - new_top)
            keep = jnp.exp(top - new_top)
            total = total * keep + jnp.sum(p, axis=0, keepdims=True)
            ot = ot * keep + dot_nn(vt_scr[j], p.astype(bf16))
            return new_top, total, ot

        top, total, ot = lax.fori_loop(
            first_block(docs_ref, i),
            i + 1,
            step,
            (
                jnp.full((1, cols), -1e30, f32),
                jnp.zeros((1, cols), f32),
                jnp.zeros((HEAD_SIZE, cols), f32),
            ),
        )
        ot = ot / total
        ot_ref[0] = ot
        lse_ref[0] = top + jnp.log(total)
        out = ot.T
        att_ref[0] = jnp.concatenate(
            [out[h * rows : (h + 1) * rows] for h in range(heads)], axis=1
        ).astype(bf16)

    def block(shape):
        return pl.BlockSpec((1,) + shape, lambda i: (i, 0, 0))

    def whole(shape):
        return pl.BlockSpec(shape, lambda i: (0,) * len(shape))

    grid_spec = pltpu.PrefetchScalarGridSpec(
        num_scalar_prefetch=0,
        grid=(blocks,),
        in_specs=[
            block((rows, width)),
            whole(w_own.shape),
            whole(gain.shape),
            block((HEAD_SIZE, rows)),
            whole(docs.shape),
        ],
        out_specs=[
            block((rows, width)),
            block((rows, HEADS_LANES)),
            block((rows, LANES)),
            block((rows, out_width)),
            block((HEAD_SIZE, cols)),
            block((1, cols)),
        ],
        scratch_shapes=[
            pltpu.VMEM((blocks, rows, HEAD_SIZE), bf16),
            pltpu.VMEM((blocks, HEAD_SIZE, rows), bf16),
            pltpu.VMEM((blocks, rows, LANES), f32),
        ],
    )
    return pl.pallas_call(
        kernel,
        name="attend_forward",
        grid_spec=grid_spec,
        out_shape=[
            jax.ShapeDtypeStruct((blocks, rows, width), bf16),
            jax.ShapeDtypeStruct((blocks, rows, HEADS_LANES), bf16),
            jax.ShapeDtypeStruct((blocks, rows, LANES), bf16),
            jax.ShapeDtypeStruct((blocks, rows, out_width), bf16),
            jax.ShapeDtypeStruct((blocks, HEAD_SIZE, cols), f32),
            jax.ShapeDtypeStruct((blocks, 1, cols), f32),
        ],
        cost_estimate=pl.CostEstimate(
            flops=2 * length * width * 256 + 2 * length * length * cols // rows * 128,
            bytes_accessed=2 * length * width * 4,
            transcendentals=length * length,
        ),
        compiler_params=pltpu.CompilerParams(
            dimension_semantics=("arbitrary",), vmem_limit_bytes=60 << 20
        ),
    )(
        tok_all,
        w_own,
        gain,
        table,
        docs,
    )


def attend_backward(q_all, kv_all, cot, ot, lse, table, docs, heads):
    blocks, rows, _ = q_all.shape
    length = blocks * rows
    cols = heads * rows

    def kernel(q_ref, kv_ref, do_ref, ot_ref, lse_ref, table_ref, docs_ref, out_ref, dk_scr, dv_scr, dq_scr, doc_scr):
        i = pl.program_id(0)

        @pl.when(i == 0)
        def _():
            dk_scr[...] = jnp.zeros_like(dk_scr)
            dv_scr[...] = jnp.zeros_like(dv_scr)

        q2 = stack_heads(q_ref[0], heads)
        do2 = stack_heads(do_ref[0], heads)
        delta = jnp.sum(do2.astype(f32).T * ot_ref[0], axis=0, keepdims=True)
        log_total = lse_ref[0]
        doc_row = docs_ref[i, :1].astype(f32)
        doc_scr[i] = across_lanes(doc_row, LANES)
        doc_query = jnp.concatenate([doc_row] * heads, axis=1)
        query = i * rows + lax.rem(lax.broadcasted_iota(jnp.int32, (1, cols), 1), rows)
        key_iota = lax.broadcasted_iota(jnp.int32, (rows, cols), 0)
        dq_scr[...] = jnp.zeros_like(dq_scr)

        @pl.loop(first_block(docs_ref, i), i + 1)
        def _(j):
            kv = kv_ref[j]
            k, v = kv[:, :HEAD_SIZE], kv[:, HEAD_SIZE:]
            scores = dot_nt(k, q2) * att_mult
            key = key_iota + j * rows
            same = jnp.concatenate([doc_scr[j]] * (cols // LANES), axis=1) == doc_query
            p = jnp.where(same & (key <= query), jnp.exp(scores - log_total), 0.0)
            ds = (p * (dot_nt(v, do2) - delta)).astype(bf16)
            dv_scr[j] += dot_nn(p.astype(bf16), do2)
            dk_scr[j] += dot_nn(ds, q2)
            dq_scr[...] += dot_tn(ds, k)

        def rope_back(x, c, s):
            return (x * c - turn(x) * s).astype(bf16)

        dq = dq_scr[...] * att_mult
        dq = [dq[h * rows : (h + 1) * rows] for h in range(heads)]
        if heads * HEAD_SIZE < HEADS_LANES:
            dq.append(jnp.zeros((rows, HEADS_LANES - heads * HEAD_SIZE), f32))
        dq = jnp.concatenate(dq, axis=1).astype(bf16).astype(f32)
        out_ref[i, :, :HEADS_LANES] = rope_back(dq, *spread_table(table_ref[i]))

        @pl.when(i == blocks - 1)
        def _():
            @pl.loop(0, blocks)
            def _(j):
                kv = jnp.concatenate([dk_scr[j] * att_mult, dv_scr[j]], axis=1)
                lane = lax.broadcasted_iota(jnp.int32, kv.shape, 1)
                c, s = spread_table(table_ref[j])
                kv = jnp.where(lane < HEAD_SIZE, kv * c - turn(kv) * s, kv).astype(bf16)
                out_ref[j, :, HEADS_LANES:] = kv

    def block(shape):
        return pl.BlockSpec((1,) + shape, lambda i: (i, 0, 0))

    def whole(shape):
        return pl.BlockSpec(shape, lambda i: (0,) * len(shape))

    grid_spec = pltpu.PrefetchScalarGridSpec(
        num_scalar_prefetch=0,
        grid=(blocks,),
        in_specs=[
            block((rows, HEADS_LANES)),
            whole((blocks, rows, LANES)),
            block((rows, heads * HEAD_SIZE)),
            block((HEAD_SIZE, cols)),
            block((1, cols)),
            whole((blocks, HEAD_SIZE, rows)),
            whole(docs.shape),
        ],
        out_specs=whole((blocks, rows, HEADS_LANES + LANES)),
        scratch_shapes=[
            pltpu.VMEM((blocks, rows, HEAD_SIZE), f32),
            pltpu.VMEM((blocks, rows, HEAD_SIZE), f32),
            pltpu.VMEM((cols, HEAD_SIZE), f32),
            pltpu.VMEM((blocks, rows, LANES), f32),
        ],
    )
    return pl.pallas_call(
        kernel,
        name="attend_backward",
        grid_spec=grid_spec,
        out_shape=jax.ShapeDtypeStruct((blocks, rows, HEADS_LANES + LANES), bf16),
        cost_estimate=pl.CostEstimate(
            flops=5 * length * length * cols // rows * 128,
            bytes_accessed=2 * length * 1024,
            transcendentals=length * length,
        ),
        compiler_params=pltpu.CompilerParams(
            dimension_semantics=("arbitrary",), vmem_limit_bytes=60 << 20
        ),
    )(
        q_all,
        kv_all,
        cot,
        ot,
        lse,
        table,
        docs,
    )


def moe_exchange(collective_id, normed, cots, mask, router, weights, parts):
    devices = lax.axis_size("seq")
    chips = devices // 2
    rows, width = normed.shape
    own_experts = weights.shape[0]
    gate_rows = devices * own_experts

    def order(chip, k):
        left = chip < chips - 1 - chip
        longer = jnp.where(left, chips - 1 - chip, chip)
        near = jnp.where(left, chip + k, chip - k)
        return jnp.where(k <= longer, near, jnp.where(left, chips - 1 - k, k))

    def kernel(*refs):
        x_in, g_in = refs[0], refs[1 : 1 + chips]
        mask_ref, router_ref, w_given = refs[1 + chips : 4 + chips]
        (lin_out, slot_out, hid_out, n_sum, gate_out, g_out) = refs[4 + chips : 10 + chips]
        y_outs = refs[10 + chips : 11 + chips + chips // 2]
        (
            x_all, g_all, win, wout, y_acc, n_acc, gate_acc, gate_stage,
            n_mine, n_far, n_give, n_theirs, y_give, y_theirs, y_pre, y_in,
            lin_st, slot_st, hid_st, gin, gout, hid_ld,
            local, line_send, line_recv, sib_send, sib_recv, g_local, g_send, g_recv,
            n_send, n_recv, y_send, y_recv, far_send, far_recv, gate_send, gate_recv,
            st_sem, y_sem, ld_sem, w_sem, wg_sem, hand_send, hand_recv,
        ) = refs[11 + chips + chips // 2 :]
        me = lax.axis_index("seq")
        chip, core = me // 2, lax.rem(me, 2)
        sibling = me + 1 - 2 * core
        win_copy = pltpu.make_async_copy(
            w_given.at[:, :, pl.ds(0, 2 * FFE)], win, w_sem.at[0]
        )
        wout_copy = pltpu.make_async_copy(
            w_given.at[:, :, pl.ds(2 * FFE, FFE)], wout, w_sem.at[1]
        )
        win_copy.start()
        wout_copy.start()
        barrier = pltpu.get_barrier_semaphore()
        for k in range(1, devices):
            pl.semaphore_signal(
                barrier, inc=1, device_id={"seq": lax.rem(me + k, devices)}, device_id_type=MESH
            )
        pl.semaphore_wait(barrier, devices - 1)

        def remote(src, dst, send, recv, to):
            return pltpu.make_async_remote_copy(
                src_ref=src,
                dst_ref=dst,
                send_sem=send,
                recv_sem=recv,
                device_id={"seq": to},
                device_id_type=MESH,
            )

        half = rows // PIECES

        def piece(b, core_of, i):
            return x_all.at[2 * b + core_of, pl.ds(i * half, half)]

        def line(src, b, i, slot, to):
            return remote(
                src, piece(b, core, i), line_send.at[i, slot], line_recv.at[i, b], to
            )

        def across(src, b, core_of, i):
            return remote(
                src, piece(b, core_of, i), sib_send.at[i, b], sib_recv.at[i, b], sibling
            )

        def own_piece(i):
            return x_in.at[pl.ds(i * half, half)]

        def pass_on(b, i, to):
            return line(piece(b, core, i), b, i, 2 + b, to)

        def to_sibling(b, i):
            return across(piece(b, core, i), b, core, i)

        def own_sends(act):
            for i in range(PIECES):

                @pl.when(chip > 0)
                def _(i=i):
                    act(line(own_piece(i), chip, i, 0, me - 2))

                @pl.when(chip < chips - 1)
                def _(i=i):
                    act(line(own_piece(i), chip, i, 1, me + 2))

            for i in range(PIECES):
                act(across(own_piece(i), chip, core, i))

        def cot_to_sibling(k):
            b = lax.rem(chip + chips - k, chips)
            return remote(
                g_in[k], g_all.at[2 * b + core], g_send.at[k], g_recv.at[b], sibling
            )

        def cot_local(k):
            b = lax.rem(chip + chips - k, chips)
            return pltpu.make_async_copy(g_in[k], g_all.at[2 * b + core], g_local.at[k])

        own_sends(lambda copy: copy.start())
        own = pltpu.make_async_copy(x_in, x_all.at[me], local)
        own.start()
        for k in range(chips):
            cot_to_sibling(k).start()
            cot_local(k).start()
        own.wait()
        for k in range(chips):
            cot_local(k).wait()
        win_copy.wait()
        wout_copy.wait()

        def gate_copy(block):
            return remote(
                gate_stage.at[block],
                gate_out.at[me],
                gate_send.at[block],
                gate_recv.at[me],
                block,
            )

        def n_copy(p):
            return remote(n_give, n_theirs.at[p], n_send.at[p], n_recv.at[p], sibling)

        def y_copy(p):
            return remote(y_give, y_theirs.at[p], y_send.at[p], y_recv.at[p], sibling)

        pairs = chips // 2
        pair = chip // 2
        mate = chip + 1 - 2 * lax.rem(chip, 2)

        def y_leave(b, k):
            return pltpu.make_async_copy(y_pre.at[b], y_outs[k], y_sem.at[k])

        def y_hand(b):
            far = lax.rem(b // 2 + pairs - pair, pairs) - 1
            return remote(
                y_pre.at[b], y_in.at[far], hand_send.at[far], hand_recv.at[far], 2 * mate + core
            )

        def stage_copies(e, block):
            return [
                pltpu.make_async_copy(lin_st.at[e], lin_out.at[e, block], st_sem.at[0, e]),
                pltpu.make_async_copy(slot_st.at[e], slot_out.at[e, block], st_sem.at[1, e]),
                pltpu.make_async_copy(hid_st.at[e], hid_out.at[e, block], st_sem.at[2, e]),
            ]

        def far_copy(b):
            return remote(
                n_mine.at[b], n_far.at[chip], far_send.at[b], far_recv.at[chip], 2 * b + core
            )

        def fold(k):
            b, p = order(chip, k), lax.rem(k, 2)
            n_copy(p).wait_recv()
            both = n_acc[...].astype(bf16).astype(f32) + n_theirs[p].astype(f32)

            @pl.when(b == chip)
            def _():
                n_sum[...] = both

            @pl.when(b != chip)
            def _():
                n_mine[b] = both.astype(bf16)
                far_copy(b).start()

            y_copy(p).wait_recv()
            y_pre[b] = (y_acc[...] + y_theirs[p].astype(f32)).astype(bf16)

            @pl.when(b == chip)
            def _():
                y_leave(b, 0).start()

            @pl.when(b == mate)
            def _():
                y_leave(b, 1).start()

            @pl.when((b != mate) & (lax.rem(b + chip, 2) == 1))
            def _():
                y_hand(b).start()

        def compute(block, before):
            x = x_all[block]
            there = mask_ref[block] > 0
            logits = jnp.where(there, dot_nn(x, router_ref[...]), -1e30)
            gates = jnp.where(
                there, jnp.exp(logits - jnp.max(logits, axis=1, keepdims=True)), 0.0
            )
            gates = gates / jnp.sum(gates, axis=1, keepdims=True)
            lane = lax.broadcasted_iota(jnp.int32, gates.shape, 1)
            y_acc[...] = jnp.zeros_like(y_acc)
            n_acc[...] = jnp.zeros_like(n_acc)
            gate_acc[...] = jnp.zeros_like(gate_acc)

            @pl.loop(0, own_experts)
            def _(e):
                gate = jnp.sum(
                    jnp.where(lane == me * own_experts + e, gates, 0.0), axis=1, keepdims=True
                )
                lin = dot_nn(x_all[block], win[e])
                gate_lin, up_lin = lin[:, :FFE], lin[:, FFE:]
                sig = 0.5 + 0.5 * jnp.tanh(0.5 * gate_lin)
                silu = gate_lin * sig
                hidden = (silu * up_lin).astype(bf16)

                @pl.when(before)
                def _():
                    for copy in stage_copies(e, block):
                        copy.wait()

                hid_st[e] = hidden
                res = dot_nt(hidden, wout[e]).astype(bf16).astype(f32)
                y_acc[...] += gate * res
                cot = g_all[block].astype(f32) * res_mult
                gate_acc[...] += jnp.where(
                    lane == me * own_experts + e, jnp.sum(cot * res, axis=1, keepdims=True), 0.0
                )
                slot = (gate * cot).astype(bf16)
                slot_st[e] = slot
                hidden_cot = dot_nn(slot, wout[e])
                lin_cot = jnp.concatenate(
                    [
                        hidden_cot * up_lin * (sig * (1.0 + gate_lin * (1.0 - sig))),
                        hidden_cot * silu,
                    ],
                    axis=1,
                ).astype(bf16)
                lin_st[e] = lin_cot
                for copy in stage_copies(e, block):
                    copy.start()
                n_acc[...] += dot_nt(lin_cot, win[e]).astype(bf16).astype(f32)

            gate_stage[block] = gate_acc[...].T[:gate_rows]

            @pl.when(block != me)
            def _():
                gate_copy(block).start()

            @pl.when(block == me)
            def _():
                gate_out[block] = gate_stage[block]

        def hop(k, i):
            for side in (-1, 1):
                away = chip + side * k

                @pl.when((k > 0) & (k < chips) & (away >= 0) & (away < chips))
                def _(side=side, away=away):
                    pass_on(away, i, me).wait_recv()

                    @pl.when((chip - side >= 0) & (chip - side < chips))
                    def _():
                        pass_on(away, i, me - 2 * side).start()

                    to_sibling(away, i).start()

        @pl.loop(0, chips)
        def _(k):
            b = order(chip, k)
            hop(k, 1)
            for i in range(PIECES):
                across(own_piece(i), b, 1 - core, i).wait_recv()
            remote(
                x_in, g_all.at[2 * b + 1 - core], g_send.at[0], g_recv.at[b], sibling
            ).wait_recv()

            @pl.loop(0, 2)
            def _(h):
                @pl.when(h == 1)
                def _():
                    hop(k + 1, 0)

                compute(2 * b + lax.rem(core + 1 + h, 2), (k > 0) | (h > 0))

                @pl.when(h == 0)
                def _():
                    p = lax.rem(k, 2)

                    @pl.when(k > 0)
                    def _():
                        n_copy(1 - p).wait_send()
                        y_copy(1 - p).wait_send()

                    n_give[...] = n_acc[...].astype(bf16)
                    y_give[...] = y_acc[...].astype(bf16)
                    n_copy(p).start()
                    y_copy(p).start()

                @pl.when(h == 1)
                def _():
                    fold(k)

        for e in range(own_experts):
            for copy in stage_copies(e, 0):
                copy.wait()

        def loads(t, p):
            e, b = lax.rem(t, own_experts), t // own_experts
            pair = pl.ds(2 * b, 2)
            return [
                pltpu.make_async_copy(
                    lin_out.at[e, pair], g_all.at[pl.ds(4 * p, 2)], ld_sem.at[0, p]
                ),
                pltpu.make_async_copy(
                    slot_out.at[e, pair], g_all.at[pl.ds(4 * p + 2, 2)], ld_sem.at[1, p]
                ),
                pltpu.make_async_copy(hid_out.at[e, pair], hid_ld.at[p], ld_sem.at[2, p]),
            ]

        for copy in loads(jnp.int32(0), 0):
            copy.start()
        gin[...] = jnp.zeros_like(gin)
        gout[...] = jnp.zeros_like(gout)

        @pl.loop(0, chips * own_experts)
        def _(t):
            p = lax.rem(t, 2)
            for copy in loads(t, p):
                copy.wait()

            @pl.when(t + 1 < chips * own_experts)
            def _():
                for copy in loads(t + 1, 1 - p):
                    copy.start()

            e, b = lax.rem(t, own_experts), t // own_experts
            x = x_all[pl.ds(2 * b, 2)].reshape(2 * rows, width)
            lin_cot = g_all[pl.ds(4 * p, 2)].reshape(2 * rows, width)
            gin[e] += dot_tn(x, lin_cot)
            slot = g_all[pl.ds(4 * p + 2, 2)].reshape(2 * rows, width)
            gout[e] += dot_tn(slot, hid_ld[p].reshape(2 * rows, FFE))

        @pl.loop(1, chips)
        def _(k):
            for side in (-1, 1):
                away = chip + side * k

                for i in range(PIECES):

                    @pl.when((away >= 0) & (away < chips))
                    def _(side=side, away=away, i=i):
                        to_sibling(away, i).wait_send()

                        @pl.when((chip - side >= 0) & (chip - side < chips))
                        def _():
                            pass_on(away, i, me - 2 * side).wait_send()

        own_sends(lambda copy: copy.wait_send())

        def keep_of(j):
            return 2 * lax.rem(pair + 1 + j, pairs) + lax.rem(chip, 2)

        for j in range(pairs - 1):
            b = keep_of(j)
            y_hand(b).wait_recv()
            y_pre[b] = (y_pre[b].astype(f32) + y_in[j].astype(f32)).astype(bf16)
            y_leave(b, 2 + j).start()

        part_rows = width // parts
        leaving = []
        for e in range(own_experts):
            for j in range(width // rows):
                i = e * (width // rows) + j
                x_all[i] = gin[e, j * rows : (j + 1) * rows].astype(bf16)
                g_all[i, :, :FFE] = gout[e, j * rows : (j + 1) * rows].astype(bf16)
                copies = []
                for q in range(rows // part_rows):
                    here = pl.ds(q * part_rows, part_rows)
                    part = (j * rows) // part_rows + q
                    copies += [
                        pltpu.make_async_copy(
                            x_all.at[i, here],
                            g_out.at[part, e, :, pl.ds(0, 2 * FFE)],
                            wg_sem.at[i, 2 * q],
                        ),
                        pltpu.make_async_copy(
                            g_all.at[i, here, pl.ds(0, FFE)],
                            g_out.at[part, e, :, pl.ds(2 * FFE, FFE)],
                            wg_sem.at[i, 2 * q + 1],
                        ),
                    ]
                leaving.append(copies)
                for copy in leaving[-1]:
                    copy.start()

        @pl.loop(1, chips)
        def _(k):
            b = order(chip, k)
            remote(
                n_mine.at[b], n_far.at[b], far_send.at[b], far_recv.at[b], 2 * b + core
            ).wait_recv()
            n_sum[...] += n_far[b].astype(f32)
            far_copy(b).wait_send()

        @pl.loop(1, devices)
        def _(k):
            block = lax.rem(me + k, devices)
            remote(
                gate_stage.at[block],
                gate_out.at[block],
                gate_send.at[block],
                gate_recv.at[block],
                block,
            ).wait_recv()
            gate_copy(block).wait_send()

        n_copy((chips - 1) % 2).wait_send()
        y_copy((chips - 1) % 2).wait_send()
        for both in leaving:
            for copy in both:
                copy.wait()
        y_leave(chip, 0).wait()
        y_leave(mate, 1).wait()
        for j in range(pairs - 1):
            y_leave(keep_of(j), 2 + j).wait()
            y_hand(keep_of(j) + mate - chip).wait_send()

        for k in range(chips):
            cot_to_sibling(k).wait_send()

    hbm = pl.BlockSpec(memory_space=pl.ANY)
    vmem = pl.BlockSpec(memory_space=pltpu.VMEM)
    block = (rows, width)
    dma = pltpu.SemaphoreType.DMA
    flops = 9 * own_experts * 2 * devices * rows * width * FFE // 1
    return pl.pallas_call(
        kernel,
        name="moe_exchange",
        out_shape=[
            jax.ShapeDtypeStruct((own_experts, devices, rows, 2 * FFE), bf16),
            jax.ShapeDtypeStruct((own_experts, devices) + block, bf16),
            jax.ShapeDtypeStruct((own_experts, devices, rows, FFE), bf16),
            jax.ShapeDtypeStruct(block, f32),
            jax.ShapeDtypeStruct((devices, gate_rows, rows), f32),
            jax.ShapeDtypeStruct((parts, own_experts, width // parts, 3 * FFE), bf16),
        ]
        + [jax.ShapeDtypeStruct(block, bf16)] * (1 + chips // 2),
        in_specs=[hbm] * (1 + chips) + [vmem] * 2 + [hbm],
        out_specs=[hbm] * 3 + [vmem] * 2 + [hbm] * (2 + chips // 2),
        scratch_shapes=[
            pltpu.VMEM((devices,) + block, bf16),
            pltpu.VMEM((devices,) + block, bf16),
            pltpu.VMEM((own_experts, width, 2 * FFE), bf16),
            pltpu.VMEM((own_experts, width, FFE), bf16),
            pltpu.VMEM(block, f32),
            pltpu.VMEM(block, f32),
            pltpu.VMEM((rows, LANES), f32),
            pltpu.VMEM((devices, gate_rows, rows), f32),
            pltpu.VMEM((chips,) + block, bf16),
            pltpu.VMEM((chips,) + block, bf16),
            pltpu.VMEM(block, bf16),
            pltpu.VMEM((2,) + block, bf16),
            pltpu.VMEM(block, bf16),
            pltpu.VMEM((2,) + block, bf16),
            pltpu.VMEM((chips,) + block, bf16),
            pltpu.VMEM((chips // 2 - 1,) + block, bf16),
            pltpu.VMEM((own_experts, rows, 2 * FFE), bf16),
            pltpu.VMEM((own_experts,) + block, bf16),
            pltpu.VMEM((own_experts, rows, FFE), bf16),
            pltpu.VMEM((own_experts, width, 2 * FFE), f32),
            pltpu.VMEM((own_experts, width, FFE), f32),
            pltpu.VMEM((2, 2, rows, FFE), bf16),
        ]
        + [dma]
        + [
            dma(count)
            for count in (
                (PIECES, chips + 2), (PIECES, chips), (PIECES, chips), (PIECES, chips),
                (chips,), (chips,), (chips,), (2,), (2,), (2,), (2,),
                (chips,), (chips,), (devices,), (devices,),
            )
        ]
        + [
            dma((3, own_experts)),
            dma((1 + chips // 2,)),
            dma((3, 2)),
            dma((2,)),
            dma((own_experts * (width // rows), 2 * rows * parts // width)),
            dma((chips // 2 - 1,)),
            dma((chips // 2 - 1,)),
        ],
        cost_estimate=pl.CostEstimate(
            flops=flops, bytes_accessed=40 << 20, transcendentals=devices * rows * FFE * 2
        ),
        compiler_params=pltpu.CompilerParams(
            collective_id=collective_id, has_side_effects=True, vmem_limit_bytes=63 << 20
        ),
    )(normed, *cots, mask, router, weights)


class Links:
    def __init__(self, axes):
        self.size = {axis: lax.axis_size(axis) for axis in axes}
        self.me = {axis: lax.axis_index(axis) for axis in axes}

    def barrier(self):
        sem = pltpu.get_barrier_semaphore()
        for axis, size in self.size.items():
            for k in range(1, size):
                pl.semaphore_signal(
                    sem,
                    inc=1,
                    device_id={axis: lax.rem(self.me[axis] + k, size)},
                    device_id_type=MESH,
                )
        pl.semaphore_wait(sem, sum(size - 1 for size in self.size.values()))

    def copy(self, axis, src, dst, send, recv, to):
        return pltpu.make_async_remote_copy(
            src_ref=src,
            dst_ref=dst,
            send_sem=send,
            recv_sem=recv,
            device_id={axis: to},
            device_id_type=MESH,
        )

    def swap_start(self, axis, src, dst, send, recv, local):
        me, size = self.me[axis], self.size[axis]
        pltpu.make_async_copy(src.at[me], dst.at[me], local).start()
        for k in range(1, size):
            to = lax.rem(me + k, size)
            self.copy(axis, src.at[to], dst.at[me], send.at[k - 1], recv.at[k - 1], to).start()

    def swap_wait(self, axis, src, dst, send, recv, local):
        me, size = self.me[axis], self.size[axis]
        pltpu.make_async_copy(src.at[me], dst.at[me], local).wait()
        for k in range(1, size):
            frm = lax.rem(me + size - k, size)
            self.copy(axis, src.at[frm], dst.at[frm], send.at[k - 1], recv.at[k - 1], frm).wait()


def loads(pairs, sems):
    copies = [
        pltpu.make_async_copy(src, dst, sems.at[i]) for i, (src, dst) in enumerate(pairs)
    ]
    for copy in copies:
        copy.start()
    return copies


def staged(arrays):
    return [pltpu.VMEM(x.shape, x.dtype) for x in arrays]


def swap_sems(size):
    dma = pltpu.SemaphoreType.DMA
    return [dma((size - 1,)), dma((size - 1,)), dma]


def attended_exchange(collective_id, attended_own, tokens, w_out, gain):
    devices, rows, cols = attended_own.shape
    width = tokens.shape[1]

    ins = [tokens, w_out, gain]
    outs = [
        jax.ShapeDtypeStruct((rows, width), bf16),
        jax.ShapeDtypeStruct((rows, width), f32),
        jax.ShapeDtypeStruct((rows, width), bf16),
    ]

    def kernel(att_in, *refs):
        given, results = refs[:3], refs[3:6]
        tok, w_all, gain_ref = refs[6:9]
        att_ref, mid_ref, norm_ref, got, in_sem, out_sem, *sems = refs[9:]
        links = Links(("seq",))
        arriving = loads(list(zip(given, (tok, w_all, gain_ref))), in_sem)
        links.barrier()
        links.swap_start("seq", att_in, got, *sems)
        for copy in arriving:
            copy.wait()
        links.swap_wait("seq", att_in, got, *sems)
        attended = jnp.concatenate([got[j] for j in range(devices)], axis=1)
        att_ref[...] = attended
        mid = tok[...].astype(f32) + res_mult * dot_nn(attended, w_all[...])
        mid_ref[...] = mid
        scale = lax.rsqrt(jnp.mean(mid * mid, axis=-1, keepdims=True) + norm_eps)
        norm_ref[...] = (mid * scale * gain_row(gain_ref, 1)).astype(bf16)
        for copy in loads(list(zip((att_ref, mid_ref, norm_ref), results)), out_sem):
            copy.wait()

    hbm = pl.BlockSpec(memory_space=pl.ANY)
    dma = pltpu.SemaphoreType.DMA
    return pl.pallas_call(
        kernel,
        name="attended_exchange",
        out_shape=outs,
        in_specs=[hbm] * 4,
        out_specs=[hbm] * 3,
        scratch_shapes=staged(ins)
        + staged(outs)
        + [pltpu.VMEM(attended_own.shape, bf16), dma((3,)), dma((3,))]
        + swap_sems(devices),
        compiler_params=pltpu.CompilerParams(
            collective_id=collective_id, has_side_effects=True, vmem_limit_bytes=60 << 20
        ),
    )(attended_own, *ins)


def middle_exchange(
    collective_id, moe_sum, gate_cot, normed, router, mask, mid, out_grad, gain, w_out, attended, cols
):
    devices, gate_rows, rows = gate_cot.shape
    width = normed.shape[1]
    experts = gate_rows

    ins = [moe_sum, gate_cot, normed, router, mask, mid, out_grad, gain, w_out, attended]
    outs = [
        jax.ShapeDtypeStruct((width, LANES), bf16),
        jax.ShapeDtypeStruct((rows, width), f32),
        jax.ShapeDtypeStruct((width, width), bf16),
    ]

    def kernel(*refs):
        given, heads_out, results, refs = refs[:10], refs[10], refs[11:14], refs[14:]
        (
            moe_ref, gate_ref, norm_ref, router_ref, mask_ref, mid_ref, cot_ref, gain_ref, w_all, att_ref,
            pack_out, mid_cot_out, wo_out, give, in_sem, out_sem, *sems,
        ) = refs
        links = Links(("seq",))
        arriving = loads(list(zip(given, refs[:10])), in_sem)
        links.barrier()
        for copy in arriving:
            copy.wait()
        there = mask_ref[...] > 0
        logits = jnp.where(there, dot_nn(norm_ref[...], router_ref[...]), -1e30)
        gates = jnp.where(
            there, jnp.exp(logits - jnp.max(logits, axis=1, keepdims=True)), 0.0
        )
        gates = gates / jnp.sum(gates, axis=1, keepdims=True)
        gate = gate_ref[0]
        for j in range(1, devices):
            gate = gate + gate_ref[j]
        gate = jnp.concatenate([gate, jnp.zeros((LANES - gate_rows, rows), f32)], axis=0).T
        pick_cot = gates * (gate - jnp.sum(gates * gate, axis=1, keepdims=True))
        logit_cot = pick_cot.astype(bf16)
        cot = moe_ref[...] + dot_nt(logit_cot, router_ref[...])
        mid = mid_ref[...]
        scale = lax.rsqrt(jnp.mean(mid * mid, axis=-1, keepdims=True) + norm_eps)
        gain_grad = jnp.sum(cot * mid * scale, axis=0, keepdims=True)
        weighted = cot * gain_row(gain_ref, 1)
        mid_cot = (
            cot_ref[...].astype(f32)
            + scale * weighted
            - mid * (scale * scale * scale) * jnp.mean(weighted * mid, axis=-1, keepdims=True)
        )
        mid_cot_out[...] = mid_cot
        branch_cot = (res_mult * mid_cot).astype(bf16)
        attended_cot = dot_nt(branch_cot, w_all[...]).astype(bf16)
        for j in range(devices):
            give[j] = attended_cot[:, j * cols : (j + 1) * cols]
        links.swap_start("seq", give, heads_out, *sems)
        wo_out[...] = dot_tn(att_ref[...], branch_cot).astype(bf16)
        pack = dot_tn(norm_ref[...], logit_cot)
        lane = lax.broadcasted_iota(jnp.int32, pack.shape, 1)
        pack_out[...] = jnp.where(
            lane == experts, jnp.broadcast_to(gain_grad, (LANES, width)).T, pack
        ).astype(bf16)
        for copy in loads(list(zip((pack_out, mid_cot_out, wo_out), results)), out_sem):
            copy.wait()
        links.swap_wait("seq", give, heads_out, *sems)

    hbm = pl.BlockSpec(memory_space=pl.ANY)
    dma = pltpu.SemaphoreType.DMA
    return pl.pallas_call(
        kernel,
        name="middle_exchange",
        out_shape=[jax.ShapeDtypeStruct((devices, rows, cols), bf16)] + outs,
        in_specs=[hbm] * 10,
        out_specs=[hbm] * 4,
        scratch_shapes=staged(ins)
        + staged(outs)
        + [pltpu.VMEM((devices, rows, cols), bf16), dma((10,)), dma((3,))]
        + swap_sems(devices),
        compiler_params=pltpu.CompilerParams(
            collective_id=collective_id, has_side_effects=True, vmem_limit_bytes=60 << 20
        ),
    )(*ins)


def finish(e_grads, grad_qkv, grad_wo, pack, input_grad, output, weights, gain, heads, experts):
    parts, own_experts, e_rows, e_cols = e_grads.shape
    devices, out_rows, _ = grad_qkv.shape
    q_width = heads * HEAD_SIZE
    share = devices // KEY_VALUE_HEADS if devices > KEY_VALUE_HEADS else 1
    steps = 4
    chunk = e_rows // steps
    me = lax.axis_index("seq").astype(jnp.int32).reshape(1)

    def kernel(
        me_ref, e_ref, qkv_ref, wo_ref, pack_ref, in_ref, out_ref, wq, wk, wv, gain_ref,
        e_in, e_out, gq, gk, gv, gwo, grouter, ggain_m, ggain_a, in_grad, output_ref,
    ):
        total = e_ref[0].astype(f32)
        for p in range(1, parts):
            total = total + e_ref[p].astype(f32)
        e_in[...] = total[:, :, : 2 * FFE]
        e_out[...] = total[:, :, 2 * FFE :]

        @pl.when(pl.program_id(0) == 0)
        def _():
            blocks = [qkv_ref[j].astype(f32) for j in range(devices)]

            def per_head(first):
                heads_of = []
                for j in range(KEY_VALUE_HEADS):
                    part = blocks[j * share][:, first : first + HEAD_SIZE]
                    for i in range(1, share):
                        part = part + blocks[j * share + i][:, first : first + HEAD_SIZE]
                    heads_of.append(part)
                return jnp.concatenate(heads_of, axis=1)

            grad_q = jnp.concatenate([b[:, :q_width] for b in blocks], axis=1)
            grad_k = per_head(HEADS_LANES)
            grad_v = per_head(HEADS_LANES + HEAD_SIZE)
            gq[...], gk[...], gv[...] = grad_q, grad_k, grad_v

            def rounded(ref):
                return ref[...].astype(bf16).astype(f32)

            def row(column):
                return jnp.broadcast_to(column, (out_rows, LANES)).T[:1]

            gain_grad = (
                jnp.sum(rounded(wq) * grad_q, axis=1, keepdims=True)
                + jnp.sum(rounded(wk) * grad_k, axis=1, keepdims=True)
                + jnp.sum(rounded(wv) * grad_v, axis=1, keepdims=True)
            )
            own = lax.broadcasted_iota(jnp.int32, (devices, 1), 0) == me_ref[0]
            own_gain = jnp.sum(jnp.where(own, rounded(gain_ref), 0.0), axis=0, keepdims=True)
            ggain_a[...] = row(gain_grad) / own_gain
            gwo[...] = wo_ref[...]
            grouter[...] = pack_ref[...].T[:experts]
            ggain_m[...] = row(pack_ref[:, experts : experts + 1])
            in_grad[...] = in_ref[...]
            output_ref[...] = out_ref[...]

    def whole(x):
        return pl.BlockSpec(x.shape, lambda i, _: (0,) * len(x.shape))

    def own_rows(x):
        return pl.BlockSpec((out_rows, x.shape[1]), lambda i, me_ref: (me_ref[0], 0))

    def shape(*dims, dtype=f32):
        return jax.ShapeDtypeStruct(dims, dtype)

    rest = [grad_qkv, grad_wo, pack, input_grad, output]
    kv_width = KEY_VALUE_HEADS * HEAD_SIZE
    small = [
        shape(out_rows, devices * q_width),
        shape(out_rows, kv_width),
        shape(out_rows, kv_width),
        shape(*grad_wo.shape),
        shape(experts, out_rows),
        shape(1, out_rows),
        shape(1, out_rows),
        shape(*input_grad.shape, dtype=bf16),
        shape(*output.shape, dtype=bf16),
    ]
    return pl.pallas_call(
        kernel,
        name="finish",
        grid_spec=pltpu.PrefetchScalarGridSpec(
            num_scalar_prefetch=1,
            grid=(steps,),
            in_specs=[pl.BlockSpec((parts, own_experts, chunk, e_cols), lambda i, _: (0, 0, i, 0))]
            + [whole(x) for x in rest]
            + [own_rows(x) for x in weights]
            + [whole(gain)],
            out_specs=[
                pl.BlockSpec((own_experts, chunk, 2 * FFE), lambda i, _: (0, i, 0)),
                pl.BlockSpec((own_experts, chunk, FFE), lambda i, _: (0, i, 0)),
            ]
            + [whole(x) for x in small],
        ),
        out_shape=[
            shape(own_experts, e_rows, 2 * FFE),
            shape(own_experts, e_rows, FFE),
        ]
        + small,
        cost_estimate=pl.CostEstimate(flops=0, bytes_accessed=8 << 20, transcendentals=0),
        compiler_params=pltpu.CompilerParams(
            dimension_semantics=("arbitrary",), vmem_limit_bytes=60 << 20
        ),
    )(me, e_grads, *rest, *weights, gain)


def first_exchange(collective_id, tokens, out_grad, docs, mask, misc, gains, w_query, w_key, w_value, w_out):
    devices, parts = lax.axis_size("seq"), lax.axis_size("dp")
    w_rows, width = w_out.shape
    heads = QUERY_HEADS // devices
    q_width = heads * HEAD_SIZE
    group = QUERY_HEADS // KEY_VALUE_HEADS
    w_cols = HEADS_LANES + LANES
    weights = [w_query, w_key, w_value, w_out]

    def prepare(refs):
        given, (wq, wk, wv, wo, w_all, wo_low, sem) = refs[:4], refs[4:]
        for copy in loads(list(zip(given, (wq, wk, wv, wo))), sem):
            copy.wait()
        wo_low[...] = wo[...].astype(bf16)
        for s in range(devices):
            kv = s * heads // group * HEAD_SIZE
            pieces = [wq[:, s * q_width : (s + 1) * q_width]]
            if q_width < HEADS_LANES:
                pieces.append(jnp.zeros((w_rows, HEADS_LANES - q_width), f32))
            pieces += [wk[:, kv : kv + HEAD_SIZE], wv[:, kv : kv + HEAD_SIZE]]
            w_all[s] = jnp.concatenate(pieces, axis=1).astype(bf16)

    return exchange(
        collective_id,
        [
            ("gather", "seq", tokens, None),
            ("gather", "seq", docs, None),
            ("gather", "seq", mask, None),
            ("shift", "seq", out_grad, None),
            ("share", "dp", misc, None),
            ("gather", "dp", gains, None),
            ("gather", "dp", jax.ShapeDtypeStruct((w_rows, w_cols), bf16), 0),
            ("share", "dp", jax.ShapeDtypeStruct((w_rows, width), bf16), 1),
        ],
        prepare=prepare,
        given=weights,
        work=staged(weights)
        + [
            pltpu.VMEM((devices, w_rows, w_cols), bf16),
            pltpu.VMEM((w_rows, width), bf16),
            pltpu.SemaphoreType.DMA((4,)),
        ],
        made=lambda refs: (refs[8].at[lax.axis_index("seq")], refs[9]),
        keep=(jax.ShapeDtypeStruct((devices, w_rows, w_cols), bf16), 8),
    )


def prepare(expert_in, expert_out, picks, docs, w_router, gain_attn, gain_moe):
    own_experts, w_rows, _ = expert_in.shape
    rows, experts = picks.shape[1], w_router.shape[0]
    steps = 4
    chunk = w_rows // steps

    def kernel(
        e_in, e_out, picks_ref, docs_ref, router, gain_a, gain_m, low, mask, docs_out, misc, gains
    ):
        low[:, :, : 2 * FFE] = e_in[...].astype(bf16)
        low[:, :, 2 * FFE :] = e_out[...].astype(bf16)

        @pl.when(pl.program_id(0) == 0)
        def _():
            expert = lax.broadcasted_iota(jnp.int32, (LANES, rows), 0)
            chosen = picks_ref[:1] == expert
            for k in range(1, TOP):
                chosen = chosen | (picks_ref[k : k + 1] == expert)
            mask[...] = jnp.where(chosen, 1.0, 0.0).T.astype(bf16)
            docs_out[...] = jnp.broadcast_to(docs_ref[...], docs_out.shape)
            misc[...] = jnp.concatenate(
                [router[...], jnp.zeros((LANES - experts, w_rows), f32)], axis=0
            ).T.astype(bf16)
            upper = lax.broadcasted_iota(jnp.int32, (8, w_rows), 0) == 0
            gains[...] = jnp.where(upper, gain_a[...], gain_m[...]).astype(bf16)

    def whole(shape):
        return pl.BlockSpec(shape, lambda i: (0,) * len(shape))

    def part(x):
        return pl.BlockSpec((own_experts, chunk, x.shape[2]), lambda i: (0, i, 0))

    small = [picks, docs, w_router, gain_attn[None], gain_moe[None]]
    outs = [
        jax.ShapeDtypeStruct((rows, LANES), bf16),
        jax.ShapeDtypeStruct((8, rows), jnp.int32),
        jax.ShapeDtypeStruct((w_rows, LANES), bf16),
        jax.ShapeDtypeStruct((8, w_rows), bf16),
    ]
    return pl.pallas_call(
        kernel,
        name="prepare",
        grid=(steps,),
        out_shape=[jax.ShapeDtypeStruct((own_experts, w_rows, 3 * FFE), bf16)] + outs,
        in_specs=[part(expert_in), part(expert_out)] + [whole(x.shape) for x in small],
        out_specs=[pl.BlockSpec((own_experts, chunk, 3 * FFE), lambda i: (0, i, 0))]
        + [whole(x.shape) for x in outs],
        compiler_params=pltpu.CompilerParams(
            dimension_semantics=("arbitrary",), vmem_limit_bytes=60 << 20
        ),
    )(expert_in, expert_out, *small)


def final_exchange(
    collective_id, qkv_cot, normed, token_grads, w_full, tokens, mid_cot, gain, mid, branches
):
    devices, parts = lax.axis_size("seq"), lax.axis_size("dp")
    chips = devices // 2
    _, rows, cols = qkv_cot.shape
    width = tokens.shape[1]
    out_rows = token_grads[0].shape[2]
    gq_shape = (parts, devices, out_rows, cols)
    count = len(token_grads)
    wides = [x.shape[3] for x in token_grads]
    token_grads = [x.reshape(parts, chips, 2, out_rows, x.shape[3]) for x in token_grads]

    ins = [w_full, normed, qkv_cot, tokens, mid_cot, gain, mid, *branches]

    def kernel(*refs):
        qkv_in = refs[0]
        gt_in = refs[1 : 1 + count]
        given = refs[1 + count : 1 + count + len(ins)]
        refs = refs[1 + count + len(ins) :]
        in_grad_out, output_out, gq_out = refs[:3]
        gt_out = refs[3 : 3 + count]
        refs = refs[3 + count :]
        (
            qkv_tok, nac, gq_in, grad, gq_recv, gq_sum,
            q_send, q_recv, local, gq_send, gq_rsem, gqz_send, gqz_recv, gq_local,
        ) = refs[:14]
        work = [refs[14 + 11 * i : 25 + 11 * i] for i in range(count)]
        refs = refs[14 + 11 * count :]
        local_ins, (in_grad, output, in_sem, out_sem) = refs[: len(ins)], refs[len(ins) :]
        w_all, normed_all, qkv_all, tok_ref, mid_cot_ref, gain_ref, mid_ref, *y_refs = local_ins
        me, my = lax.axis_index("seq"), lax.axis_index("dp")
        chip, core = me // 2, lax.rem(me, 2)
        sibling = me + 1 - 2 * core
        arriving = loads(list(zip(given, local_ins)), in_sem)
        barrier = pltpu.get_barrier_semaphore()
        for axis, index, size in (("seq", me, devices), ("dp", my, parts)):
            for k in range(1, size):
                pl.semaphore_signal(
                    barrier,
                    inc=1,
                    device_id={axis: lax.rem(index + k, size)},
                    device_id_type=MESH,
                )
        pl.semaphore_wait(barrier, devices + parts - 2)

        def remote(axis, src, dst, send, recv, to):
            return pltpu.make_async_remote_copy(
                src_ref=src,
                dst_ref=dst,
                send_sem=send,
                recv_sem=recv,
                device_id={axis: to},
                device_id_type=MESH,
            )

        sent = []

        def columns(j):
            return qkv_tok.at[:, pl.ds(pl.multiple_of(j * cols, cols), cols)]

        for x, w in zip(gt_in, work):
            mine, theirs, far, near, last, sems, dp_send, dp_recv, z_send, z_recv, _ = w
            copy = remote(
                "seq", x.at[:, :, 1 - core], theirs, sems.at[0], sems.at[1], sibling
            )
            copy.start()
            sent.append(copy)
            pltpu.make_async_copy(x.at[:, :, core], mine, sems.at[2]).start()
        own = pltpu.make_async_copy(qkv_in.at[me], columns(me), local)
        own.start()
        for k in range(1, devices):
            to = lax.rem(me + k, devices)
            copy = remote(
                "seq", qkv_in.at[to], columns(me), q_send.at[k - 1], q_recv.at[k - 1], to
            )
            copy.start()
            sent.append(copy)

        for x, w in zip(gt_in, work):
            mine, theirs, far, near, last, sems, dp_send, dp_recv, z_send, z_recv, _ = w
            remote("seq", x.at[:, :, core], theirs, sems.at[0], sems.at[1], sibling).wait_recv()
            pltpu.make_async_copy(x.at[:, :, core], mine, sems.at[2]).wait()
            mine[...] = (mine[...].astype(f32) + theirs[...].astype(f32)).astype(bf16)
            for k in range(1, parts):
                to = lax.rem(my + k, parts)
                copy = remote(
                    "dp", mine.at[to], far.at[k - 1], dp_send.at[k - 1], dp_recv.at[k - 1], to
                )
                copy.start()
                sent.append(copy)

        for copy in arriving:
            copy.wait()
        grad[...] = jnp.zeros_like(grad)

        @pl.loop(0, devices)
        def _(j):
            grad[...] += dot_tn(normed_all[j], qkv_all[j])

        gq_in[...] = grad[...].astype(bf16).reshape(gq_shape)
        for k in range(1, parts):
            to = lax.rem(my + k, parts)
            copy = remote(
                "dp", gq_in.at[to], gq_recv.at[my], gq_send.at[k - 1], gq_rsem.at[k - 1], to
            )
            copy.start()
            sent.append(copy)
        own_q = pltpu.make_async_copy(gq_in.at[my], gq_recv.at[my], gq_local)
        own_q.start()
        total = y_refs[0][...].astype(f32)
        for k in range(1, len(branches)):
            total = total + y_refs[k][...].astype(f32)
        output[...] = (mid_ref[...] + res_mult * total).astype(bf16)
        leaving = [pltpu.make_async_copy(output, output_out, out_sem.at[0])]
        leaving[0].start()

        for k in range(devices):
            frm = lax.rem(me + devices - k, devices)
            if k == 0:
                own.wait()
            else:
                remote(
                    "seq", qkv_in.at[frm], columns(frm), q_send.at[k - 1], q_recv.at[k - 1], frm
                ).wait_recv()
            part = dot_nt(columns(frm)[...], w_all[frm])
            nac[...] = part if k == 0 else nac[...] + part

        resid = tok_ref[...].astype(f32)
        scale = lax.rsqrt(jnp.mean(resid * resid, axis=-1, keepdims=True) + norm_eps)
        weighted = nac[...] * gain_row(gain_ref, 0)
        in_grad[...] = (
            mid_cot_ref[...]
            + scale * weighted
            - resid
            * (scale * scale * scale)
            * jnp.mean(weighted * resid, axis=-1, keepdims=True)
        ).astype(bf16)

        leaving.append(pltpu.make_async_copy(in_grad, in_grad_out, out_sem.at[1]))
        leaving[1].start()
        own_q.wait()
        for k in range(1, parts):
            frm = lax.rem(my + parts - k, parts)
            remote(
                "dp", gq_in.at[frm], gq_recv.at[frm], gq_send.at[k - 1], gq_rsem.at[k - 1], frm
            ).wait_recv()
        summed = gq_recv[0].astype(f32)
        for p in range(1, parts):
            summed = summed + gq_recv[p].astype(f32)
        gq_sum[...] = summed.astype(bf16)
        own_z = pltpu.make_async_copy(gq_sum.at[me], gq_out.at[me], gq_local)
        own_z.start()
        for k in range(1, devices):
            to = lax.rem(me + k, devices)
            copy = remote(
                "seq", gq_sum.at[to], gq_out.at[me], gqz_send.at[k - 1], gqz_recv.at[k - 1], to
            )
            copy.start()
            sent.append(copy)
        for w in work:
            mine, theirs, far, near, last, sems, dp_send, dp_recv, z_send, z_recv, _ = w
            summed = mine[my].astype(f32)
            for k in range(1, parts):
                remote(
                    "dp", mine.at[0], far.at[k - 1], dp_send.at[k - 1], dp_recv.at[k - 1], my
                ).wait_recv()
                summed = summed + far[k - 1].astype(f32)
            near[...] = summed.astype(bf16)
            for k in range(1, chips):
                to = lax.rem(chip + k, chips)
                copy = remote(
                    "seq",
                    near.at[to],
                    last.at[k - 1],
                    z_send.at[k - 1],
                    z_recv.at[k - 1],
                    2 * to + core,
                )
                copy.start()
                sent.append(copy)

        for o, w in zip(gt_out, work):
            mine, theirs, far, near, last, sems, dp_send, dp_recv, z_send, z_recv, _ = w
            summed = near[chip].astype(f32)
            for k in range(1, chips):
                remote(
                    "seq", near.at[0], last.at[k - 1], z_send.at[k - 1], z_recv.at[k - 1], me
                ).wait_recv()
                summed = summed + last[k - 1].astype(f32)
            o[...] = summed
        own_z.wait()
        for k in range(1, devices):
            frm = lax.rem(me + devices - k, devices)
            remote(
                "seq", gq_sum.at[frm], gq_out.at[frm], gqz_send.at[k - 1], gqz_recv.at[k - 1], frm
            ).wait_recv()
        for copy in sent:
            copy.wait_send()
        for copy in leaving:
            copy.wait()

    hbm = pl.BlockSpec(memory_space=pl.ANY)
    vmem = pl.BlockSpec(memory_space=pltpu.VMEM)
    dma = pltpu.SemaphoreType.DMA
    scratch = [
        pltpu.VMEM((rows, devices * cols), bf16),
        pltpu.VMEM((rows, width), f32),
        pltpu.VMEM(gq_shape, bf16),
        pltpu.VMEM((width, cols), f32),
        pltpu.VMEM(gq_shape, bf16),
        pltpu.VMEM(gq_shape[1:], bf16),
        dma((devices - 1,)),
        dma((devices - 1,)),
        dma,
        dma((parts - 1,)),
        dma((parts - 1,)),
        dma((devices - 1,)),
        dma((devices - 1,)),
        dma,
    ]
    for wide in wides:
        piece = (out_rows, wide)
        scratch += [
            pltpu.VMEM((parts, chips) + piece, bf16),
            pltpu.VMEM((parts, chips) + piece, bf16),
            pltpu.VMEM((parts - 1, chips) + piece, bf16),
            pltpu.VMEM((chips,) + piece, bf16),
            pltpu.VMEM((chips - 1,) + piece, bf16),
            dma((3,)),
            dma((parts - 1,)),
            dma((parts - 1,)),
            dma((chips - 1,)),
            dma((chips - 1,)),
            dma,
        ]
    scratch += staged(ins) + [
        pltpu.VMEM((rows, width), bf16),
        pltpu.VMEM((rows, width), bf16),
        dma((len(ins),)),
        dma((2,)),
    ]
    return pl.pallas_call(
        kernel,
        name="final_exchange",
        out_shape=[
            jax.ShapeDtypeStruct((rows, width), bf16),
            jax.ShapeDtypeStruct((rows, width), bf16),
            jax.ShapeDtypeStruct(gq_shape[1:], bf16),
        ]
        + [jax.ShapeDtypeStruct((out_rows, wide), f32) for wide in wides],
        in_specs=[hbm] * (1 + count + len(ins)),
        out_specs=[hbm] * 3 + [vmem] * count,
        scratch_shapes=scratch,
        compiler_params=pltpu.CompilerParams(
            collective_id=collective_id, has_side_effects=True, vmem_limit_bytes=60 << 20
        ),
    )(qkv_cot, *token_grads, *ins)


def on_device(
    tokens,
    out_grad,
    doc_ids,
    expert_picks,
    w_query,
    key_weight_matrix,
    value_weight_matrix,
    w_out,
    w_router,
    gain_attn,
    gain_moe,
    expert_in,
    expert_out,
):
    devices, parts = lax.axis_size("seq"), lax.axis_size("dp")
    me = lax.axis_index("seq")
    rows, width = tokens.shape[1:]
    length = rows * devices
    experts = w_router.shape[1]
    heads = QUERY_HEADS // devices
    group = QUERY_HEADS // KEY_VALUE_HEADS
    q_width = heads * HEAD_SIZE
    w_rows = w_query.shape[0]

    w_cols = HEADS_LANES + LANES
    low, mask, doc_rows, misc, gains = prepare(
        expert_in, expert_out, expert_picks[0].T, doc_ids, w_router.T, gain_attn, gain_moe
    )
    expert_full = lax.all_gather(low, "dp", axis=1, tiled=True)
    chips = devices // 2

    def shift(x, k):
        return lax.ppermute(x, "seq", [(i, (i + 2 * k) % devices) for i in range(devices)])

    tok_all, doc_all, mask_all, middle_cot, misc_full, gains_full, w_own_all, wo_full, w_all = first_exchange(
        0,
        tokens[0],
        out_grad[0],
        doc_rows,
        mask,
        misc,
        gains,
        w_query,
        key_weight_matrix,
        value_weight_matrix,
        w_out,
    )
    w_full = lax.all_gather(w_all, "dp", axis=1, tiled=True)
    held, tok_all = lax.optimization_barrier((out_grad[0], tok_all))
    cots = [held] + [
        middle_cot if k == chips // 2 else shift(held, k) for k in range(1, chips)
    ]
    w_own_all = w_own_all.reshape(width, w_cols)
    wo_full = wo_full.reshape(width, width)
    misc_full = misc_full.reshape(width, LANES)
    table = rope_table(devices, rows)

    normed_a, q_all, kv_all, attended_own, ot, lse = attend_forward(
        tok_all, w_own_all, gains_full, table, doc_all, heads
    )
    attended, mid, normed_m = attended_exchange(
        1, attended_own, tokens[0], wo_full, gains_full
    )
    (_, _, _, moe_sum, gate_cot, e_grads, *branches) = moe_exchange(
        2, normed_m, cots, mask_all, misc_full, expert_full, parts
    )
    e_grads = lax.all_to_all(e_grads, "dp", split_axis=0, concat_axis=0)
    heads_cot, router_pack, mid_cot, grad_wo = middle_exchange(
        4, moe_sum, gate_cot, normed_m, misc_full, mask, mid, out_grad[0], gains_full,
        wo_full, attended, q_width,
    )
    heads_cot, branches = lax.optimization_barrier((heads_cot, branches))
    branches = [
        branches[0],
        lax.ppermute(branches[1], "seq", [(i, i ^ 2) for i in range(devices)]),
    ] + [shift(branches[1 + k], 2 * k) for k in range(1, chips // 2)]
    qkv_cot = attend_backward(q_all, kv_all, heads_cot, ot, lse, table, doc_all, heads)
    qkv_cot, branches = lax.optimization_barrier((qkv_cot, branches))
    out_rows = w_rows // devices
    input_grad, output, grad_qkv, grad_wo, router_pack = final_exchange(
        5,
        qkv_cot,
        normed_a,
        [
            grad_wo.reshape(parts, devices, out_rows, width),
            router_pack.reshape(parts, devices, out_rows, LANES),
        ],
        w_full,
        tokens[0],
        mid_cot,
        gains_full,
        mid,
        branches,
    )

    (
        grad_e_in, grad_e_out, grad_wq, grad_wk, grad_wv, grad_wo, grad_router, grad_gain_m,
        grad_gain_a, input_grad, output,
    ) = finish(
        e_grads,
        grad_qkv,
        grad_wo,
        router_pack,
        input_grad,
        output,
        [w_query, key_weight_matrix, value_weight_matrix],
        gain_attn.reshape(devices, out_rows),
        heads,
        experts,
    )
    input_grad, output = input_grad[None], output[None]
    grad_router = grad_router.T
    grad_gain_a = grad_gain_a.reshape(out_rows)
    grad_gain_m = grad_gain_m.reshape(out_rows)
    return (
        output,
        input_grad,
        grad_wq,
        grad_wk,
        grad_wv,
        grad_wo,
        grad_router,
        grad_gain_a,
        grad_gain_m,
        grad_e_in,
        grad_e_out,
    )


def solution(mesh):
    return jax.shard_map(
        on_device,
        mesh=mesh,
        in_specs=(
            P("dp", "seq", None),
            P("dp", "seq", None),
            P("dp", "seq"),
            P("dp", "seq", None),
            P("dp", None),
            P("dp", None),
            P("dp", None),
            P("dp", None),
            P("dp", None),
            P("dp"),
            P("dp"),
            P("seq", "dp", None),
            P("seq", "dp", None),
        ),
        out_specs=(
            P("dp", "seq", None),
            P("dp", "seq", None),
            P(("dp", "seq"), None),
            P(("dp", "seq"), None),
            P(("dp", "seq"), None),
            P(("dp", "seq"), None),
            P(("dp", "seq"), None),
            P(("dp", "seq")),
            P(("dp", "seq")),
            P("seq", "dp", None),
            P("seq", "dp", None),
        ),
        check_vma=False,
    )
```

```python
import functools

import jax
import jax.numpy as jnp
import numpy as np
from jax import lax
from jax.experimental import pallas as pl
from jax.experimental.pallas import tpu as pltpu
from jax.sharding import PartitionSpec as P

MESH = pl.DeviceIdType.MESH
PIECES = 2


def _block(ref, j, cut):
    if cut is None:
        return ref.at[j]
    return ref.at[:, pl.ds(pl.multiple_of(j * cut, cut), cut)]


def exchange(collective_id, ops, prepare=None, given=(), work=(), made=None, keep=None):
    axes = tuple(dict.fromkeys(axis for _, axis, _, _ in ops))
    size = {axis: lax.axis_size(axis) for axis in axes}
    out_shapes, out_specs, scratch, places = [], [], [], []
    for kind, axis, x, cut in ops:
        count = size[axis]
        out_spec = pl.BlockSpec(memory_space=pl.ANY)
        extra = []
        lead = (PIECES,) if kind == "gather" and axis == "seq" else ()
        if kind == "shift":
            shape, dtype, copies = x.shape, x.dtype, 1
        elif kind == "share":
            shape, dtype, copies = (count,) + x.shape, x.dtype, 2 * (count - 1)
        elif kind == "gather":
            shape, dtype = (count,) + x.shape, x.dtype
            copies = count - 1 if axis == "dp" else 3 + 4 * (count // 2 - 1)
        elif kind == "swap":
            copies, dtype = count - 1, x.dtype
            if cut is None:
                shape = x.shape
            elif cut[0] == "in":
                shape = (count, x.shape[0], cut[1])
            else:
                shape = (x.shape[1], count * cut[1])
        out_shapes.append(jax.ShapeDtypeStruct(shape, dtype))
        out_specs.append(out_spec)
        places.append((len(scratch), len(extra)))
        scratch += [
            pltpu.SemaphoreType.DMA(lead + (copies,)),
            pltpu.SemaphoreType.DMA(lead + (max(copies, count),)),
            pltpu.SemaphoreType.DMA,
        ] + extra

    early = [x for _, _, x, cut in ops if not isinstance(cut, int)]
    own_scratch = len(scratch)

    def kernel(*refs):
        ins, refs = list(refs[: len(early)]), refs[len(early) :]
        extra_in, refs = refs[: len(given)], refs[len(given) :]
        outs, refs = refs[: len(ops)], refs[len(ops) :]
        if keep is not None:
            kept, refs = refs[0], refs[1:]
        work, extra_work = refs[:own_scratch], refs[own_scratch:]
        ins += [None] * (len(ops) - len(early))
        me = {axis: lax.axis_index(axis) for axis in axes}
        barrier = pltpu.get_barrier_semaphore()
        for axis in axes:
            for k in range(1, size[axis]):
                pl.semaphore_signal(
                    barrier,
                    inc=1,
                    device_id={axis: lax.rem(me[axis] + k, size[axis])},
                    device_id_type=MESH,
                )
        pl.semaphore_wait(barrier, sum(size[axis] - 1 for axis in axes))

        def remote(axis, src, dst, send, recv, to):
            return pltpu.make_async_remote_copy(
                src_ref=src,
                dst_ref=dst,
                send_sem=send,
                recv_sem=recv,
                device_id={axis: to},
                device_id_type=MESH,
            )

        second, third = [], []
        for (kind, axis, _, cut), x, o, (at, extra) in zip(ops, ins, outs, places):
            if isinstance(cut, int):
                if x is None and cut == 0:
                    all_refs = list(extra_in) + list(extra_work[:-1])
                    prepare(all_refs)
                    late = made(all_refs)
                    leave = pltpu.make_async_copy(all_refs[keep[1]], kept, extra_work[-1])
                    leave.start()
                    third.append(leave.wait)
                x, cut = late[cut], None
            send, recv, local = work[at : at + 3]
            count, my = size[axis], me[axis]
            if kind == "swap":
                into = cut[1] if cut is not None and cut[0] == "out" else None
                outof = cut[1] if cut is not None and cut[0] == "in" else None
                own = pltpu.make_async_copy(_block(x, my, outof), _block(o, my, into), local)
                own.start()
                third.append(own.wait)
                for k in range(1, count):
                    to = lax.rem(my + k, count)
                    copy = remote(
                        axis,
                        _block(x, to, outof),
                        _block(o, my, into),
                        send.at[k - 1],
                        recv.at[k - 1],
                        to,
                    )
                    copy.start()
                    frm = lax.rem(my + count - k, count)
                    arrive = remote(
                        axis,
                        _block(x, to, outof),
                        _block(o, frm, into),
                        send.at[k - 1],
                        recv.at[k - 1],
                        to,
                    )
                    third.append(copy.wait_send)
                    third.append(arrive.wait_recv)
            elif kind == "gather" and axis == "dp":
                own = pltpu.make_async_copy(x, o.at[my], local)
                own.start()
                third.append(own.wait)
                for k in range(1, count):
                    to = lax.rem(my + k, count)
                    frm = lax.rem(my + count - k, count)
                    copy = remote(axis, x, o.at[my], send.at[k - 1], recv.at[k - 1], to)
                    copy.start()
                    third.append(copy.wait_send)
                    third.append(
                        remote(
                            axis, x, o.at[frm], send.at[k - 1], recv.at[k - 1], to
                        ).wait_recv
                    )
            elif kind == "shift":
                copy = remote(
                    axis, x, o, send.at[0], recv.at[0], lax.rem(my + 2 * (count // 4), count)
                )
                second.append((count // 4 + 0.9, copy.start))
                third.append(copy.wait)
            elif kind == "share":
                seq, half = me["seq"], x.shape[0] // 2
                core = lax.rem(seq, 2)
                sibling = seq + 1 - 2 * core
                own = pltpu.make_async_copy(x, o.at[my], local)
                own.start()
                third.append(own.wait)

                def side_of(ref, which, half=half):
                    return ref.at[pl.ds(which * half, half)]

                def relay(k, axis=axis, x=x, o=o, send=send, recv=recv, count=count, my=my, core=core, sibling=sibling, side_of=side_of):
                    to = lax.rem(my + k, count)
                    frm = lax.rem(my + count - k, count)
                    remote(
                        axis,
                        side_of(x, core),
                        side_of(o.at[frm], core),
                        send.at[k - 1],
                        recv.at[k - 1],
                        to,
                    ).wait_recv()
                    slot = count - 2 + k
                    spot = side_of(o.at[frm], core)
                    over = remote("seq", spot, spot, send.at[slot], recv.at[slot], sibling)
                    over.start()
                    third.append(over.wait_send)
                    third.append(
                        remote(
                            "seq",
                            spot,
                            side_of(o.at[frm], 1 - core),
                            send.at[slot],
                            recv.at[slot],
                            sibling,
                        ).wait_recv
                    )

                for k in range(1, count):
                    to = lax.rem(my + k, count)
                    copy = remote(
                        axis,
                        side_of(x, core),
                        side_of(o.at[my], core),
                        send.at[k - 1],
                        recv.at[k - 1],
                        to,
                    )
                    copy.start()
                    third.append(copy.wait_send)
                    second.append((k + 0.75, functools.partial(relay, k)))
            elif kind == "gather":
                chips = count // 2
                chip, core = my // 2, lax.rem(my, 2)
                sibling = my + 1 - 2 * core
                own = pltpu.make_async_copy(x, o.at[my], local)
                own.start()
                third.append(own.wait)

                cuts = PIECES if x.shape[0] % (16 * PIECES) == 0 else 1
                size_of = x.shape[0] // cuts

                def cut_of(ref, i, size_of=size_of):
                    return ref.at[pl.ds(i * size_of, size_of)]

                def line(src, b, i, slot, to, axis=axis, o=o, send=send, recv=recv, core=core, cut_of=cut_of):
                    return remote(
                        axis, src, cut_of(o.at[2 * b + core], i), send.at[i, slot], recv.at[i, b], to
                    )

                def across(src, b, i, slot, half, axis=axis, o=o, send=send, recv=recv, chips=chips, sibling=sibling, cut_of=cut_of):
                    return remote(
                        axis,
                        src,
                        cut_of(o.at[2 * b + half], i),
                        send.at[i, slot],
                        recv.at[i, chips + b],
                        sibling,
                    )

                def guarded(where, act):
                    pl.when(where)(act)

                for i in range(cuts):
                    for slot, where, to in ((0, chip > 0, my - 2), (1, chip < chips - 1, my + 2)):
                        copy = line(cut_of(x, i), chip, i, slot, to)
                        guarded(where, copy.start)
                        third.append(functools.partial(guarded, where, copy.wait_send))
                for i in range(cuts):
                    copy = across(cut_of(x, i), chip, i, 2, core)
                    copy.start()
                    third.append(copy.wait_send)
                    third.append(across(cut_of(x, i), chip, i, 2, 1 - core).wait_recv)

                def hop(k, side, i, chips=chips, chip=chip, core=core, my=my, x=x, o=o, line=line, across=across, cut_of=cut_of):
                    b = chip + side * k
                    there = (b >= 0) & (b < chips)
                    onward = there & ((chip - side >= 0) & (chip - side < chips))
                    slot = 3 + (k - 1) * 4 + (side + 1)
                    spot = cut_of(o.at[2 * b + core], i)
                    further = line(spot, b, i, slot, my - 2 * side)
                    over = across(spot, b, i, slot + 1, core)
                    arrived = line(cut_of(x, i), b, i, slot, my)
                    brought = across(cut_of(x, i), b, i, slot + 1, 1 - core)

                    @pl.when(there)
                    def _():
                        arrived.wait_recv()

                    guarded(onward, further.start)
                    guarded(there, over.start)
                    third.append(functools.partial(guarded, onward, further.wait_send))
                    third.append(functools.partial(guarded, there, over.wait_send))
                    third.append(functools.partial(guarded, there, brought.wait_recv))

                for k in range(1, chips):
                    for i in range(cuts):
                        for side in (-1, 1):
                            second.append((k + i / cuts, functools.partial(hop, k, side, i)))
        for _, run in sorted(second, key=lambda item: item[0]):
            run()
        for wait in third:
            wait()

    return pl.pallas_call(
        kernel,
        name=f"exchange{collective_id}",
        out_shape=out_shapes + ([] if keep is None else [keep[0]]),
        in_specs=[pl.BlockSpec(memory_space=pl.ANY)] * (len(early) + len(given)),
        out_specs=out_specs + ([] if keep is None else [pl.BlockSpec(memory_space=pl.ANY)]),
        scratch_shapes=scratch
        + list(work)
        + ([] if keep is None else [pltpu.SemaphoreType.DMA]),
        compiler_params=pltpu.CompilerParams(
            collective_id=collective_id, has_side_effects=True, vmem_limit_bytes=60 << 20
        ),
    )(*early, *given)

QUERY_HEADS = 16
KEY_VALUE_HEADS = 8
HEAD_SIZE = 64
FFE = 512
TOP = 8

att_mult = 0.015625
res_mult = 0.22
norm_eps = 1e-06
rope_theta = 10000.0
LANES = 128
bf16 = jnp.bfloat16
f32 = jnp.float32
HEADS_LANES = 128


def dot_nt(a, b):
    return lax.dot_general(a, b, (((1,), (1,)), ((), ())), preferred_element_type=f32)


def dot_nn(a, b):
    return lax.dot_general(a, b, (((1,), (0,)), ((), ())), preferred_element_type=f32)


def dot_tn(a, b):
    return lax.dot_general(a, b, (((0,), (0,)), ((), ())), preferred_element_type=f32)


def turn(x):
    half = HEAD_SIZE // 2
    lane = lax.broadcasted_iota(jnp.int32, x.shape, 1)
    width = x.shape[1]
    return jnp.where(
        lax.rem(lane, HEAD_SIZE) < half, pltpu.roll(x, width - half, 1), pltpu.roll(x, half, 1)
    )


def rope_table(blocks, rows):
    half = HEAD_SIZE // 2
    frequency = np.float32(rope_theta) ** (
        -np.arange(half, dtype=np.float32) * np.float32(2.0) / np.float32(HEAD_SIZE)
    )
    angles = (frequency[:, None] * np.arange(blocks * rows, dtype=np.float32)[None, :]).astype(
        np.float32
    )
    table = np.concatenate([np.cos(angles), np.sin(angles)], axis=0).astype(np.float32)
    return jnp.asarray(table.reshape(HEAD_SIZE, blocks, rows).transpose(1, 0, 2))


def spread_table(table):
    half = HEAD_SIZE // 2
    turned = table.T
    cos, sin = turned[:, :half], turned[:, half:]
    return (
        jnp.concatenate([cos, cos] * (LANES // HEAD_SIZE), axis=1),
        jnp.concatenate([-sin, sin] * (LANES // HEAD_SIZE), axis=1),
    )


def across_lanes(row, lanes):
    return jnp.broadcast_to(row, (lanes, row.shape[1])).T


def first_block(docs_ref, i):
    docs = docs_ref[:, 0, :].astype(f32)
    own = lax.broadcasted_iota(jnp.int32, docs.shape, 0) == i
    lane = lax.broadcasted_iota(jnp.int32, docs.shape, 1)
    start = jnp.sum(jnp.where(own & (lane == 0), docs, 0.0))
    ends = (lane == docs.shape[1] - 1) & (docs < start)
    return jnp.sum(jnp.where(ends, 1.0, 0.0)).astype(jnp.int32)


def stack_heads(x, heads):
    return jnp.concatenate(
        [x[:, h * HEAD_SIZE : (h + 1) * HEAD_SIZE] for h in range(heads)], axis=0
    )


def gain_row(ref, which):
    return jnp.concatenate(
        [ref[p, which : which + 1, :] for p in range(ref.shape[0])], axis=1
    ).astype(f32)


def attend_forward(tok_all, w_own, gain, table, docs, heads):
    blocks, rows, width = tok_all.shape
    length = blocks * rows
    cols = heads * rows
    out_width = heads * HEAD_SIZE

    def kernel(tok, w, gain_ref, table_ref, docs_ref, na_ref, q_ref, kv_ref, att_ref, ot_ref, lse_ref, k_scr, vt_scr, doc_scr):
        i = pl.program_id(0)
        x = tok[0].astype(f32)
        scale = lax.rsqrt(jnp.mean(x * x, axis=-1, keepdims=True) + norm_eps)
        na = (x * scale * gain_row(gain_ref, 0)).astype(bf16)
        na_ref[0] = na
        qkv = dot_nn(na, w[...])
        c, s = spread_table(table_ref[0])
        q, kv = qkv[:, :HEADS_LANES], qkv[:, HEADS_LANES:]
        q = (q * c + turn(q) * s).astype(bf16)
        lane = lax.broadcasted_iota(jnp.int32, kv.shape, 1)
        kv = jnp.where(lane < HEAD_SIZE, kv * c + turn(kv) * s, kv).astype(bf16)
        q_ref[0] = q
        kv_ref[0] = kv
        k_scr[i] = kv[:, :HEAD_SIZE]
        vt_scr[i] = kv.astype(f32).T[HEAD_SIZE:].astype(bf16)
        q2 = stack_heads(q * jnp.bfloat16(att_mult), heads)
        doc_row = docs_ref[i, :1].astype(f32)
        doc_scr[i] = across_lanes(doc_row, LANES)
        doc_query = jnp.concatenate([doc_row] * heads, axis=1)
        query = i * rows + lax.rem(lax.broadcasted_iota(jnp.int32, (1, cols), 1), rows)
        key_iota = lax.broadcasted_iota(jnp.int32, (rows, cols), 0)

        def step(j, carry, diagonal):
            top, total, ot = carry
            scores = dot_nt(k_scr[j], q2)
            seen = jnp.concatenate([doc_scr[j]] * (cols // LANES), axis=1) == doc_query
            if diagonal:
                seen = seen & (key_iota + j * rows <= query)
            scores = jnp.where(seen, scores, -1e30)
            new_top = jnp.maximum(top, jnp.max(scores, axis=0, keepdims=True))
            p = jnp.exp(scores - new_top)
            keep = jnp.exp(top - new_top)
            total = total * keep + jnp.sum(p, axis=0, keepdims=True)
            ot = ot * keep + dot_nn(vt_scr[j], p.astype(bf16))
            return new_top, total, ot

        top, total, ot = lax.fori_loop(
            first_block(docs_ref, i),
            i,
            functools.partial(step, diagonal=False),
            (
                jnp.full((1, cols), -1e30, f32),
                jnp.zeros((1, cols), f32),
                jnp.zeros((HEAD_SIZE, cols), f32),
            ),
        )
        top, total, ot = step(i, (top, total, ot), diagonal=True)
        ot = ot / total
        ot_ref[0] = ot
        lse_ref[0] = top + jnp.log(total)
        out = ot.T
        att_ref[0] = jnp.concatenate(
            [out[h * rows : (h + 1) * rows] for h in range(heads)], axis=1
        ).astype(bf16)

    def block(shape):
        return pl.BlockSpec((1,) + shape, lambda i: (i, 0, 0))

    def whole(shape):
        return pl.BlockSpec(shape, lambda i: (0,) * len(shape))

    grid_spec = pltpu.PrefetchScalarGridSpec(
        num_scalar_prefetch=0,
        grid=(blocks,),
        in_specs=[
            block((rows, width)),
            whole(w_own.shape),
            whole(gain.shape),
            block((HEAD_SIZE, rows)),
            whole(docs.shape),
        ],
        out_specs=[
            block((rows, width)),
            block((rows, HEADS_LANES)),
            block((rows, LANES)),
            block((rows, out_width)),
            block((HEAD_SIZE, cols)),
            block((1, cols)),
        ],
        scratch_shapes=[
            pltpu.VMEM((blocks, rows, HEAD_SIZE), bf16),
            pltpu.VMEM((blocks, HEAD_SIZE, rows), bf16),
            pltpu.VMEM((blocks, rows, LANES), f32),
        ],
    )
    return pl.pallas_call(
        kernel,
        name="attend_forward",
        grid_spec=grid_spec,
        out_shape=[
            jax.ShapeDtypeStruct((blocks, rows, width), bf16),
            jax.ShapeDtypeStruct((blocks, rows, HEADS_LANES), bf16),
            jax.ShapeDtypeStruct((blocks, rows, LANES), bf16),
            jax.ShapeDtypeStruct((blocks, rows, out_width), bf16),
            jax.ShapeDtypeStruct((blocks, HEAD_SIZE, cols), f32),
            jax.ShapeDtypeStruct((blocks, 1, cols), f32),
        ],
        cost_estimate=pl.CostEstimate(
            flops=2 * length * width * 256 + 2 * length * length * cols // rows * 128,
            bytes_accessed=2 * length * width * 4,
            transcendentals=length * length,
        ),
        compiler_params=pltpu.CompilerParams(
            dimension_semantics=("arbitrary",), vmem_limit_bytes=60 << 20
        ),
    )(
        tok_all,
        w_own,
        gain,
        table,
        docs,
    )


def attend_backward(q_all, kv_all, cot, ot, lse, table, docs, heads):
    blocks, rows, _ = q_all.shape
    length = blocks * rows
    cols = heads * rows

    def kernel(q_ref, kv_ref, do_ref, ot_ref, lse_ref, table_ref, docs_ref, out_ref, dk_scr, dv_scr, dq_scr, doc_scr):
        i = pl.program_id(0)

        @pl.when(i == 0)
        def _():
            dk_scr[...] = jnp.zeros_like(dk_scr)
            dv_scr[...] = jnp.zeros_like(dv_scr)

        q2 = stack_heads(q_ref[0], heads)
        do2 = stack_heads(do_ref[0], heads)
        delta = jnp.sum(do2.astype(f32).T * ot_ref[0], axis=0, keepdims=True)
        log_total = lse_ref[0]
        doc_row = docs_ref[i, :1].astype(f32)
        doc_scr[i] = across_lanes(doc_row, LANES)
        doc_query = jnp.concatenate([doc_row] * heads, axis=1)
        query = i * rows + lax.rem(lax.broadcasted_iota(jnp.int32, (1, cols), 1), rows)
        key_iota = lax.broadcasted_iota(jnp.int32, (rows, cols), 0)
        dq_scr[...] = jnp.zeros_like(dq_scr)

        @pl.loop(first_block(docs_ref, i), i + 1)
        def _(j):
            kv = kv_ref[j]
            k, v = kv[:, :HEAD_SIZE], kv[:, HEAD_SIZE:]
            scores = dot_nt(k, q2) * att_mult
            key = key_iota + j * rows
            same = jnp.concatenate([doc_scr[j]] * (cols // LANES), axis=1) == doc_query
            p = jnp.where(same & (key <= query), jnp.exp(scores - log_total), 0.0)
            ds = (p * (dot_nt(v, do2) - delta)).astype(bf16)
            dv_scr[j] += dot_nn(p.astype(bf16), do2)
            dk_scr[j] += dot_nn(ds, q2)
            dq_scr[...] += dot_tn(ds, k)

        def rope_back(x, c, s):
            return (x * c - turn(x) * s).astype(bf16)

        dq = dq_scr[...] * att_mult
        dq = [dq[h * rows : (h + 1) * rows] for h in range(heads)]
        if heads * HEAD_SIZE < HEADS_LANES:
            dq.append(jnp.zeros((rows, HEADS_LANES - heads * HEAD_SIZE), f32))
        dq = jnp.concatenate(dq, axis=1).astype(bf16).astype(f32)
        out_ref[i, :, :HEADS_LANES] = rope_back(dq, *spread_table(table_ref[i]))

        @pl.when(i == blocks - 1)
        def _():
            @pl.loop(0, blocks)
            def _(j):
                kv = jnp.concatenate([dk_scr[j] * att_mult, dv_scr[j]], axis=1)
                lane = lax.broadcasted_iota(jnp.int32, kv.shape, 1)
                c, s = spread_table(table_ref[j])
                kv = jnp.where(lane < HEAD_SIZE, kv * c - turn(kv) * s, kv).astype(bf16)
                out_ref[j, :, HEADS_LANES:] = kv

    def block(shape):
        return pl.BlockSpec((1,) + shape, lambda i: (i, 0, 0))

    def whole(shape):
        return pl.BlockSpec(shape, lambda i: (0,) * len(shape))

    grid_spec = pltpu.PrefetchScalarGridSpec(
        num_scalar_prefetch=0,
        grid=(blocks,),
        in_specs=[
            block((rows, HEADS_LANES)),
            whole((blocks, rows, LANES)),
            block((rows, heads * HEAD_SIZE)),
            block((HEAD_SIZE, cols)),
            block((1, cols)),
            whole((blocks, HEAD_SIZE, rows)),
            whole(docs.shape),
        ],
        out_specs=whole((blocks, rows, HEADS_LANES + LANES)),
        scratch_shapes=[
            pltpu.VMEM((blocks, rows, HEAD_SIZE), f32),
            pltpu.VMEM((blocks, rows, HEAD_SIZE), f32),
            pltpu.VMEM((cols, HEAD_SIZE), f32),
            pltpu.VMEM((blocks, rows, LANES), f32),
        ],
    )
    return pl.pallas_call(
        kernel,
        name="attend_backward",
        grid_spec=grid_spec,
        out_shape=jax.ShapeDtypeStruct((blocks, rows, HEADS_LANES + LANES), bf16),
        cost_estimate=pl.CostEstimate(
            flops=5 * length * length * cols // rows * 128,
            bytes_accessed=2 * length * 1024,
            transcendentals=length * length,
        ),
        compiler_params=pltpu.CompilerParams(
            dimension_semantics=("arbitrary",), vmem_limit_bytes=60 << 20
        ),
    )(
        q_all,
        kv_all,
        cot,
        ot,
        lse,
        table,
        docs,
    )


def moe_exchange(collective_id, normed, cots, mask, router, weights):
    devices = lax.axis_size("seq")
    chips = devices // 2
    rows, width = normed.shape
    own_experts = weights.shape[0]
    gate_rows = devices * own_experts

    def order(chip, k):
        left = chip < chips - 1 - chip
        longer = jnp.where(left, chips - 1 - chip, chip)
        near = jnp.where(left, chip + k, chip - k)
        return jnp.where(k <= longer, near, jnp.where(left, chips - 1 - k, k))

    def kernel(*refs):
        x_in, g_in = refs[0], refs[1 : 1 + chips]
        mask_ref, router_ref, w_given = refs[1 + chips : 4 + chips]
        (lin_out, slot_out, hid_out, n_sum, gate_out, g_out) = refs[4 + chips : 10 + chips]
        y_outs = refs[10 + chips : 11 + chips + chips // 2]
        (
            x_all, g_all, win, wout, y_acc, n_acc, gate_acc, gate_stage,
            n_mine, n_far, n_give, n_theirs, y_give, y_theirs, y_pre, y_in,
            lin_st, slot_st, hid_st, gin, gout, hid_ld,
            local, line_send, line_recv, sib_send, sib_recv, g_local, g_send, g_recv,
            n_send, n_recv, y_send, y_recv, far_send, far_recv, gate_send, gate_recv,
            st_sem, y_sem, ld_sem, w_sem, wg_sem, hand_send, hand_recv,
        ) = refs[11 + chips + chips // 2 :]
        me = lax.axis_index("seq")
        chip, core = me // 2, lax.rem(me, 2)
        sibling = me + 1 - 2 * core
        win_copy = pltpu.make_async_copy(
            w_given.at[:, :, pl.ds(0, 2 * FFE)], win, w_sem.at[0]
        )
        wout_copy = pltpu.make_async_copy(
            w_given.at[:, :, pl.ds(2 * FFE, FFE)], wout, w_sem.at[1]
        )
        win_copy.start()
        wout_copy.start()
        barrier = pltpu.get_barrier_semaphore()
        for k in range(1, devices):
            pl.semaphore_signal(
                barrier, inc=1, device_id={"seq": lax.rem(me + k, devices)}, device_id_type=MESH
            )
        pl.semaphore_wait(barrier, devices - 1)

        def remote(src, dst, send, recv, to):
            return pltpu.make_async_remote_copy(
                src_ref=src,
                dst_ref=dst,
                send_sem=send,
                recv_sem=recv,
                device_id={"seq": to},
                device_id_type=MESH,
            )

        half = rows // PIECES

        def piece(b, core_of, i):
            return x_all.at[2 * b + core_of, pl.ds(i * half, half)]

        def line(src, b, i, slot, to):
            return remote(
                src, piece(b, core, i), line_send.at[i, slot], line_recv.at[i, b], to
            )

        def across(src, b, core_of, i):
            return remote(
                src, piece(b, core_of, i), sib_send.at[i, b], sib_recv.at[i, b], sibling
            )

        def own_piece(i):
            return x_in.at[pl.ds(i * half, half)]

        def pass_on(b, i, to):
            return line(piece(b, core, i), b, i, 2 + b, to)

        def to_sibling(b, i):
            return across(piece(b, core, i), b, core, i)

        def own_sends(act):
            for i in range(PIECES):

                @pl.when(chip > 0)
                def _(i=i):
                    act(line(own_piece(i), chip, i, 0, me - 2))

                @pl.when(chip < chips - 1)
                def _(i=i):
                    act(line(own_piece(i), chip, i, 1, me + 2))

            for i in range(PIECES):
                act(across(own_piece(i), chip, core, i))

        def cot_to_sibling(k):
            b = lax.rem(chip + chips - k, chips)
            return remote(
                g_in[k], g_all.at[2 * b + core], g_send.at[k], g_recv.at[b], sibling
            )

        def cot_local(k):
            b = lax.rem(chip + chips - k, chips)
            return pltpu.make_async_copy(g_in[k], g_all.at[2 * b + core], g_local.at[k])

        own_sends(lambda copy: copy.start())
        own = pltpu.make_async_copy(x_in, x_all.at[me], local)
        own.start()
        for k in range(chips):
            cot_to_sibling(k).start()
            cot_local(k).start()
        own.wait()
        for k in range(chips):
            cot_local(k).wait()
        win_copy.wait()
        wout_copy.wait()

        def gate_copy(block):
            return remote(
                gate_stage.at[block],
                gate_out.at[me],
                gate_send.at[block],
                gate_recv.at[me],
                block,
            )

        def n_copy(p):
            return remote(n_give, n_theirs.at[p], n_send.at[p], n_recv.at[p], sibling)

        def y_copy(p):
            return remote(y_give, y_theirs.at[p], y_send.at[p], y_recv.at[p], sibling)

        pairs = chips // 2
        pair = chip // 2
        mate = chip + 1 - 2 * lax.rem(chip, 2)

        def y_leave(b, k):
            return pltpu.make_async_copy(y_pre.at[b], y_outs[k], y_sem.at[k])

        def y_hand(b):
            far = lax.rem(b // 2 + pairs - pair, pairs) - 1
            return remote(
                y_pre.at[b], y_in.at[far], hand_send.at[far], hand_recv.at[far], 2 * mate + core
            )

        def stage_copies(e, block):
            return [
                pltpu.make_async_copy(lin_st.at[e], lin_out.at[e, block], st_sem.at[0, e]),
                pltpu.make_async_copy(slot_st.at[e], slot_out.at[e, block], st_sem.at[1, e]),
                pltpu.make_async_copy(hid_st.at[e], hid_out.at[e, block], st_sem.at[2, e]),
            ]

        def far_copy(b):
            return remote(
                n_mine.at[b], n_far.at[chip], far_send.at[b], far_recv.at[chip], 2 * b + core
            )

        def fold(k):
            b, p = order(chip, k), lax.rem(k, 2)
            n_copy(p).wait_recv()
            both = n_acc[...].astype(bf16).astype(f32) + n_theirs[p].astype(f32)

            @pl.when(b == chip)
            def _():
                n_sum[...] = both

            @pl.when(b != chip)
            def _():
                n_mine[b] = both.astype(bf16)
                far_copy(b).start()

            y_copy(p).wait_recv()
            y_pre[b] = (y_acc[...] + y_theirs[p].astype(f32)).astype(bf16)

            @pl.when(b == chip)
            def _():
                y_leave(b, 0).start()

            @pl.when(b == mate)
            def _():
                y_leave(b, 1).start()

            @pl.when((b != mate) & (lax.rem(b + chip, 2) == 1))
            def _():
                y_hand(b).start()

        def compute(block, before):
            x = x_all[block]
            there = mask_ref[block] > 0
            logits = jnp.where(there, dot_nn(x, router_ref[...]), -1e30)
            gates = jnp.where(
                there, jnp.exp(logits - jnp.max(logits, axis=1, keepdims=True)), 0.0
            )
            gates = gates / jnp.sum(gates, axis=1, keepdims=True)
            lane = lax.broadcasted_iota(jnp.int32, gates.shape, 1)
            y_acc[...] = jnp.zeros_like(y_acc)
            n_acc[...] = jnp.zeros_like(n_acc)
            gate_acc[...] = jnp.zeros_like(gate_acc)

            @pl.loop(0, own_experts)
            def _(e):
                gate = jnp.sum(
                    jnp.where(lane == me * own_experts + e, gates, 0.0), axis=1, keepdims=True
                )
                lin = dot_nn(x_all[block], win[e])
                gate_lin, up_lin = lin[:, :FFE], lin[:, FFE:]
                sig = 0.5 + 0.5 * jnp.tanh(0.5 * gate_lin)
                silu = gate_lin * sig
                hidden = (silu * up_lin).astype(bf16)

                @pl.when(before)
                def _():
                    for copy in stage_copies(e, block):
                        copy.wait()

                hid_st[e] = hidden
                res = dot_nt(hidden, wout[e]).astype(bf16).astype(f32)
                y_acc[...] += gate * res
                cot = g_all[block].astype(f32) * res_mult
                gate_acc[...] += jnp.where(
                    lane == me * own_experts + e, jnp.sum(cot * res, axis=1, keepdims=True), 0.0
                )
                slot = (gate * cot).astype(bf16)
                slot_st[e] = slot
                hidden_cot = dot_nn(slot, wout[e])
                lin_cot = jnp.concatenate(
                    [
                        hidden_cot * up_lin * (sig * (1.0 + gate_lin * (1.0 - sig))),
                        hidden_cot * silu,
                    ],
                    axis=1,
                ).astype(bf16)
                lin_st[e] = lin_cot
                for copy in stage_copies(e, block):
                    copy.start()
                n_acc[...] += dot_nt(lin_cot, win[e]).astype(bf16).astype(f32)

            gate_stage[block] = gate_acc[...].T[:gate_rows]

            @pl.when(block != me)
            def _():
                gate_copy(block).start()

            @pl.when(block == me)
            def _():
                gate_out[block] = gate_stage[block]

        def hop(k, i):
            for side in (-1, 1):
                away = chip + side * k

                @pl.when((k > 0) & (k < chips) & (away >= 0) & (away < chips))
                def _(side=side, away=away):
                    pass_on(away, i, me).wait_recv()

                    @pl.when((chip - side >= 0) & (chip - side < chips))
                    def _():
                        pass_on(away, i, me - 2 * side).start()

                    to_sibling(away, i).start()

        @pl.loop(0, chips)
        def _(k):
            b = order(chip, k)
            hop(k, 1)
            for i in range(PIECES):
                across(own_piece(i), b, 1 - core, i).wait_recv()
            remote(
                x_in, g_all.at[2 * b + 1 - core], g_send.at[0], g_recv.at[b], sibling
            ).wait_recv()

            @pl.loop(0, 2)
            def _(h):
                @pl.when(h == 1)
                def _():
                    hop(k + 1, 0)

                compute(2 * b + lax.rem(core + 1 + h, 2), (k > 0) | (h > 0))

                @pl.when(h == 0)
                def _():
                    p = lax.rem(k, 2)

                    @pl.when(k > 0)
                    def _():
                        n_copy(1 - p).wait_send()
                        y_copy(1 - p).wait_send()

                    n_give[...] = n_acc[...].astype(bf16)
                    y_give[...] = y_acc[...].astype(bf16)
                    n_copy(p).start()
                    y_copy(p).start()

                @pl.when(h == 1)
                def _():
                    fold(k)

        for e in range(own_experts):
            for copy in stage_copies(e, 0):
                copy.wait()

        def loads(t, p):
            e, b = lax.rem(t, own_experts), t // own_experts
            pair = pl.ds(2 * b, 2)
            return [
                pltpu.make_async_copy(
                    lin_out.at[e, pair], g_all.at[pl.ds(4 * p, 2)], ld_sem.at[0, p]
                ),
                pltpu.make_async_copy(
                    slot_out.at[e, pair], g_all.at[pl.ds(4 * p + 2, 2)], ld_sem.at[1, p]
                ),
                pltpu.make_async_copy(hid_out.at[e, pair], hid_ld.at[p], ld_sem.at[2, p]),
            ]

        for copy in loads(jnp.int32(0), 0):
            copy.start()
        gin[...] = jnp.zeros_like(gin)
        gout[...] = jnp.zeros_like(gout)

        @pl.loop(0, chips * own_experts)
        def _(t):
            p = lax.rem(t, 2)
            for copy in loads(t, p):
                copy.wait()

            @pl.when(t + 1 < chips * own_experts)
            def _():
                for copy in loads(t + 1, 1 - p):
                    copy.start()

            e, b = lax.rem(t, own_experts), t // own_experts
            x = x_all[pl.ds(2 * b, 2)].reshape(2 * rows, width)
            lin_cot = g_all[pl.ds(4 * p, 2)].reshape(2 * rows, width)
            gin[e] += dot_tn(x, lin_cot)
            slot = g_all[pl.ds(4 * p + 2, 2)].reshape(2 * rows, width)
            gout[e] += dot_tn(slot, hid_ld[p].reshape(2 * rows, FFE))

        @pl.loop(1, chips)
        def _(k):
            for side in (-1, 1):
                away = chip + side * k

                for i in range(PIECES):

                    @pl.when((away >= 0) & (away < chips))
                    def _(side=side, away=away, i=i):
                        to_sibling(away, i).wait_send()

                        @pl.when((chip - side >= 0) & (chip - side < chips))
                        def _():
                            pass_on(away, i, me - 2 * side).wait_send()

        own_sends(lambda copy: copy.wait_send())

        def keep_of(j):
            return 2 * lax.rem(pair + 1 + j, pairs) + lax.rem(chip, 2)

        for j in range(pairs - 1):
            b = keep_of(j)
            y_hand(b).wait_recv()
            y_pre[b] = (y_pre[b].astype(f32) + y_in[j].astype(f32)).astype(bf16)
            y_leave(b, 2 + j).start()

        leaving = []
        for e in range(own_experts):
            for j in range(width // rows):
                i = e * (width // rows) + j
                x_all[i] = gin[e, j * rows : (j + 1) * rows].astype(bf16)
                g_all[i, :, :FFE] = gout[e, j * rows : (j + 1) * rows].astype(bf16)
                at = 2 * len(leaving)
                here = pl.ds(j * rows, rows)
                leaving.append(
                    (
                        pltpu.make_async_copy(
                            x_all.at[i], g_out.at[e, here, pl.ds(0, 2 * FFE)], wg_sem.at[at]
                        ),
                        pltpu.make_async_copy(
                            g_all.at[i, :, pl.ds(0, FFE)],
                            g_out.at[e, here, pl.ds(2 * FFE, FFE)],
                            wg_sem.at[at + 1],
                        ),
                    )
                )
                for copy in leaving[-1]:
                    copy.start()

        @pl.loop(1, chips)
        def _(k):
            b = order(chip, k)
            remote(
                n_mine.at[b], n_far.at[b], far_send.at[b], far_recv.at[b], 2 * b + core
            ).wait_recv()
            n_sum[...] += n_far[b].astype(f32)
            far_copy(b).wait_send()

        @pl.loop(1, devices)
        def _(k):
            block = lax.rem(me + k, devices)
            remote(
                gate_stage.at[block],
                gate_out.at[block],
                gate_send.at[block],
                gate_recv.at[block],
                block,
            ).wait_recv()
            gate_copy(block).wait_send()

        n_copy((chips - 1) % 2).wait_send()
        y_copy((chips - 1) % 2).wait_send()
        for both in leaving:
            for copy in both:
                copy.wait()
        y_leave(chip, 0).wait()
        y_leave(mate, 1).wait()
        for j in range(pairs - 1):
            y_leave(keep_of(j), 2 + j).wait()
            y_hand(keep_of(j) + mate - chip).wait_send()

        for k in range(chips):
            cot_to_sibling(k).wait_send()

    hbm = pl.BlockSpec(memory_space=pl.ANY)
    vmem = pl.BlockSpec(memory_space=pltpu.VMEM)
    block = (rows, width)
    dma = pltpu.SemaphoreType.DMA
    flops = 9 * own_experts * 2 * devices * rows * width * FFE // 1
    return pl.pallas_call(
        kernel,
        name="moe_exchange",
        out_shape=[
            jax.ShapeDtypeStruct((own_experts, devices, rows, 2 * FFE), bf16),
            jax.ShapeDtypeStruct((own_experts, devices) + block, bf16),
            jax.ShapeDtypeStruct((own_experts, devices, rows, FFE), bf16),
            jax.ShapeDtypeStruct(block, f32),
            jax.ShapeDtypeStruct((devices, gate_rows, rows), f32),
            jax.ShapeDtypeStruct((own_experts, width, 3 * FFE), bf16),
        ]
        + [jax.ShapeDtypeStruct(block, bf16)] * (1 + chips // 2),
        in_specs=[hbm] * (1 + chips) + [vmem] * 2 + [hbm],
        out_specs=[hbm] * 3 + [vmem] * 2 + [hbm] * (2 + chips // 2),
        scratch_shapes=[
            pltpu.VMEM((devices,) + block, bf16),
            pltpu.VMEM((devices,) + block, bf16),
            pltpu.VMEM((own_experts, width, 2 * FFE), bf16),
            pltpu.VMEM((own_experts, width, FFE), bf16),
            pltpu.VMEM(block, f32),
            pltpu.VMEM(block, f32),
            pltpu.VMEM((rows, LANES), f32),
            pltpu.VMEM((devices, gate_rows, rows), f32),
            pltpu.VMEM((chips,) + block, bf16),
            pltpu.VMEM((chips,) + block, bf16),
            pltpu.VMEM(block, bf16),
            pltpu.VMEM((2,) + block, bf16),
            pltpu.VMEM(block, bf16),
            pltpu.VMEM((2,) + block, bf16),
            pltpu.VMEM((chips,) + block, bf16),
            pltpu.VMEM((chips // 2 - 1,) + block, bf16),
            pltpu.VMEM((own_experts, rows, 2 * FFE), bf16),
            pltpu.VMEM((own_experts,) + block, bf16),
            pltpu.VMEM((own_experts, rows, FFE), bf16),
            pltpu.VMEM((own_experts, width, 2 * FFE), f32),
            pltpu.VMEM((own_experts, width, FFE), f32),
            pltpu.VMEM((2, 2, rows, FFE), bf16),
        ]
        + [dma]
        + [
            dma(count)
            for count in (
                (PIECES, chips + 2), (PIECES, chips), (PIECES, chips), (PIECES, chips),
                (chips,), (chips,), (chips,), (2,), (2,), (2,), (2,),
                (chips,), (chips,), (devices,), (devices,),
            )
        ]
        + [
            dma((3, own_experts)),
            dma((1 + chips // 2,)),
            dma((3, 2)),
            dma((2,)),
            dma((2 * own_experts * (width // rows),)),
            dma((chips // 2 - 1,)),
            dma((chips // 2 - 1,)),
        ],
        cost_estimate=pl.CostEstimate(
            flops=flops, bytes_accessed=40 << 20, transcendentals=devices * rows * FFE * 2
        ),
        compiler_params=pltpu.CompilerParams(
            collective_id=collective_id, has_side_effects=True, vmem_limit_bytes=63 << 20
        ),
    )(normed, *cots, mask, router, weights)


class Links:
    def __init__(self, axes):
        self.size = {axis: lax.axis_size(axis) for axis in axes}
        self.me = {axis: lax.axis_index(axis) for axis in axes}

    def barrier(self):
        sem = pltpu.get_barrier_semaphore()
        for axis, size in self.size.items():
            for k in range(1, size):
                pl.semaphore_signal(
                    sem,
                    inc=1,
                    device_id={axis: lax.rem(self.me[axis] + k, size)},
                    device_id_type=MESH,
                )
        pl.semaphore_wait(sem, sum(size - 1 for size in self.size.values()))

    def copy(self, axis, src, dst, send, recv, to):
        return pltpu.make_async_remote_copy(
            src_ref=src,
            dst_ref=dst,
            send_sem=send,
            recv_sem=recv,
            device_id={axis: to},
            device_id_type=MESH,
        )

    def swap_start(self, axis, src, dst, send, recv, local):
        me, size = self.me[axis], self.size[axis]
        pltpu.make_async_copy(src.at[me], dst.at[me], local).start()
        for k in range(1, size):
            to = lax.rem(me + k, size)
            self.copy(axis, src.at[to], dst.at[me], send.at[k - 1], recv.at[k - 1], to).start()

    def swap_wait(self, axis, src, dst, send, recv, local):
        me, size = self.me[axis], self.size[axis]
        pltpu.make_async_copy(src.at[me], dst.at[me], local).wait()
        for k in range(1, size):
            frm = lax.rem(me + size - k, size)
            self.copy(axis, src.at[frm], dst.at[frm], send.at[k - 1], recv.at[k - 1], frm).wait()


def loads(pairs, sems):
    copies = [
        pltpu.make_async_copy(src, dst, sems.at[i]) for i, (src, dst) in enumerate(pairs)
    ]
    for copy in copies:
        copy.start()
    return copies


def staged(arrays):
    return [pltpu.VMEM(x.shape, x.dtype) for x in arrays]


def swap_sems(size):
    dma = pltpu.SemaphoreType.DMA
    return [dma((size - 1,)), dma((size - 1,)), dma]


def attended_exchange(collective_id, attended_own, tokens, w_out, gain):
    devices, rows, cols = attended_own.shape
    width = tokens.shape[1]

    ins = [tokens, w_out, gain]
    outs = [
        jax.ShapeDtypeStruct((rows, width), bf16),
        jax.ShapeDtypeStruct((rows, width), f32),
        jax.ShapeDtypeStruct((rows, width), bf16),
    ]

    def kernel(att_in, *refs):
        given, results = refs[:3], refs[3:6]
        tok, w_all, gain_ref = refs[6:9]
        att_ref, mid_ref, norm_ref, got, in_sem, out_sem, *sems = refs[9:]
        links = Links(("seq",))
        arriving = loads(list(zip(given, (tok, w_all, gain_ref))), in_sem)
        links.barrier()
        links.swap_start("seq", att_in, got, *sems)
        for copy in arriving:
            copy.wait()
        links.swap_wait("seq", att_in, got, *sems)
        attended = jnp.concatenate([got[j] for j in range(devices)], axis=1)
        att_ref[...] = attended
        mid = tok[...].astype(f32) + res_mult * dot_nn(attended, w_all[...])
        mid_ref[...] = mid
        scale = lax.rsqrt(jnp.mean(mid * mid, axis=-1, keepdims=True) + norm_eps)
        norm_ref[...] = (mid * scale * gain_row(gain_ref, 1)).astype(bf16)
        for copy in loads(list(zip((att_ref, mid_ref, norm_ref), results)), out_sem):
            copy.wait()

    hbm = pl.BlockSpec(memory_space=pl.ANY)
    dma = pltpu.SemaphoreType.DMA
    return pl.pallas_call(
        kernel,
        name="attended_exchange",
        out_shape=outs,
        in_specs=[hbm] * 4,
        out_specs=[hbm] * 3,
        scratch_shapes=staged(ins)
        + staged(outs)
        + [pltpu.VMEM(attended_own.shape, bf16), dma((3,)), dma((3,))]
        + swap_sems(devices),
        compiler_params=pltpu.CompilerParams(
            collective_id=collective_id, has_side_effects=True, vmem_limit_bytes=60 << 20
        ),
    )(attended_own, *ins)


def middle_exchange(
    collective_id, moe_sum, gate_cot, normed, router, mask, mid, out_grad, gain, w_out, attended, cols
):
    devices, gate_rows, rows = gate_cot.shape
    width = normed.shape[1]
    experts = gate_rows

    ins = [moe_sum, gate_cot, normed, router, mask, mid, out_grad, gain, w_out, attended]
    outs = [
        jax.ShapeDtypeStruct((width, LANES), bf16),
        jax.ShapeDtypeStruct((rows, width), f32),
        jax.ShapeDtypeStruct((width, width), bf16),
    ]

    def kernel(*refs):
        given, heads_out, results, refs = refs[:10], refs[10], refs[11:14], refs[14:]
        (
            moe_ref, gate_ref, norm_ref, router_ref, mask_ref, mid_ref, cot_ref, gain_ref, w_all, att_ref,
            pack_out, mid_cot_out, wo_out, give, in_sem, out_sem, *sems,
        ) = refs
        links = Links(("seq",))
        arriving = loads(list(zip(given, refs[:10])), in_sem)
        links.barrier()
        for copy in arriving:
            copy.wait()
        there = mask_ref[...] > 0
        logits = jnp.where(there, dot_nn(norm_ref[...], router_ref[...]), -1e30)
        gates = jnp.where(
            there, jnp.exp(logits - jnp.max(logits, axis=1, keepdims=True)), 0.0
        )
        gates = gates / jnp.sum(gates, axis=1, keepdims=True)
        gate = gate_ref[0]
        for j in range(1, devices):
            gate = gate + gate_ref[j]
        gate = jnp.concatenate([gate, jnp.zeros((LANES - gate_rows, rows), f32)], axis=0).T
        pick_cot = gates * (gate - jnp.sum(gates * gate, axis=1, keepdims=True))
        logit_cot = pick_cot.astype(bf16)
        cot = moe_ref[...] + dot_nt(logit_cot, router_ref[...])
        mid = mid_ref[...]
        scale = lax.rsqrt(jnp.mean(mid * mid, axis=-1, keepdims=True) + norm_eps)
        gain_grad = jnp.sum(cot * mid * scale, axis=0, keepdims=True)
        weighted = cot * gain_row(gain_ref, 1)
        mid_cot = (
            cot_ref[...].astype(f32)
            + scale * weighted
            - mid * (scale * scale * scale) * jnp.mean(weighted * mid, axis=-1, keepdims=True)
        )
        mid_cot_out[...] = mid_cot
        branch_cot = (res_mult * mid_cot).astype(bf16)
        attended_cot = dot_nt(branch_cot, w_all[...]).astype(bf16)
        for j in range(devices):
            give[j] = attended_cot[:, j * cols : (j + 1) * cols]
        links.swap_start("seq", give, heads_out, *sems)
        wo_out[...] = dot_tn(att_ref[...], branch_cot).astype(bf16)
        pack = dot_tn(norm_ref[...], logit_cot)
        lane = lax.broadcasted_iota(jnp.int32, pack.shape, 1)
        pack_out[...] = jnp.where(
            lane == experts, jnp.broadcast_to(gain_grad, (LANES, width)).T, pack
        ).astype(bf16)
        for copy in loads(list(zip((pack_out, mid_cot_out, wo_out), results)), out_sem):
            copy.wait()
        links.swap_wait("seq", give, heads_out, *sems)

    hbm = pl.BlockSpec(memory_space=pl.ANY)
    dma = pltpu.SemaphoreType.DMA
    return pl.pallas_call(
        kernel,
        name="middle_exchange",
        out_shape=[jax.ShapeDtypeStruct((devices, rows, cols), bf16)] + outs,
        in_specs=[hbm] * 10,
        out_specs=[hbm] * 4,
        scratch_shapes=staged(ins)
        + staged(outs)
        + [pltpu.VMEM((devices, rows, cols), bf16), dma((10,)), dma((3,))]
        + swap_sems(devices),
        compiler_params=pltpu.CompilerParams(
            collective_id=collective_id, has_side_effects=True, vmem_limit_bytes=60 << 20
        ),
    )(*ins)


def finish(e_grads, grad_qkv, grad_wo, pack, input_grad, output, weights, gain, heads, experts):
    own_experts, e_rows, e_cols = e_grads.shape
    devices, out_rows, _ = grad_qkv.shape
    q_width = heads * HEAD_SIZE
    share = devices // KEY_VALUE_HEADS if devices > KEY_VALUE_HEADS else 1
    steps = 4
    chunk = e_rows // steps
    me = lax.axis_index("seq").astype(jnp.int32).reshape(1)

    def kernel(
        me_ref, e_ref, qkv_ref, wo_ref, pack_ref, in_ref, out_ref, wq, wk, wv, gain_ref,
        e_in, e_out, gq, gk, gv, gwo, grouter, ggain_m, ggain_a, in_grad, output_ref,
    ):
        e_in[...] = e_ref[:, :, : 2 * FFE].astype(f32)
        e_out[...] = e_ref[:, :, 2 * FFE :].astype(f32)

        @pl.when(pl.program_id(0) == 0)
        def _():
            blocks = [qkv_ref[j].astype(f32) for j in range(devices)]

            def per_head(first):
                heads_of = []
                for j in range(KEY_VALUE_HEADS):
                    part = blocks[j * share][:, first : first + HEAD_SIZE]
                    for i in range(1, share):
                        part = part + blocks[j * share + i][:, first : first + HEAD_SIZE]
                    heads_of.append(part)
                return jnp.concatenate(heads_of, axis=1)

            grad_q = jnp.concatenate([b[:, :q_width] for b in blocks], axis=1)
            grad_k = per_head(HEADS_LANES)
            grad_v = per_head(HEADS_LANES + HEAD_SIZE)
            gq[...], gk[...], gv[...] = grad_q, grad_k, grad_v

            def rounded(ref):
                return ref[...].astype(bf16).astype(f32)

            def row(column):
                return jnp.broadcast_to(column, (out_rows, LANES)).T[:1]

            gain_grad = (
                jnp.sum(rounded(wq) * grad_q, axis=1, keepdims=True)
                + jnp.sum(rounded(wk) * grad_k, axis=1, keepdims=True)
                + jnp.sum(rounded(wv) * grad_v, axis=1, keepdims=True)
            )
            own = lax.broadcasted_iota(jnp.int32, (devices, 1), 0) == me_ref[0]
            own_gain = jnp.sum(jnp.where(own, rounded(gain_ref), 0.0), axis=0, keepdims=True)
            ggain_a[...] = row(gain_grad) / own_gain
            gwo[...] = wo_ref[...]
            grouter[...] = pack_ref[...].T[:experts]
            ggain_m[...] = row(pack_ref[:, experts : experts + 1])
            in_grad[...] = in_ref[...]
            output_ref[...] = out_ref[...]

    def whole(x):
        return pl.BlockSpec(x.shape, lambda i, _: (0,) * len(x.shape))

    def own_rows(x):
        return pl.BlockSpec((out_rows, x.shape[1]), lambda i, me_ref: (me_ref[0], 0))

    def shape(*dims, dtype=f32):
        return jax.ShapeDtypeStruct(dims, dtype)

    rest = [grad_qkv, grad_wo, pack, input_grad, output]
    kv_width = KEY_VALUE_HEADS * HEAD_SIZE
    small = [
        shape(out_rows, devices * q_width),
        shape(out_rows, kv_width),
        shape(out_rows, kv_width),
        shape(*grad_wo.shape),
        shape(experts, out_rows),
        shape(1, out_rows),
        shape(1, out_rows),
        shape(*input_grad.shape, dtype=bf16),
        shape(*output.shape, dtype=bf16),
    ]
    return pl.pallas_call(
        kernel,
        name="finish",
        grid_spec=pltpu.PrefetchScalarGridSpec(
            num_scalar_prefetch=1,
            grid=(steps,),
            in_specs=[pl.BlockSpec((own_experts, chunk, e_cols), lambda i, _: (0, i, 0))]
            + [whole(x) for x in rest]
            + [own_rows(x) for x in weights]
            + [whole(gain)],
            out_specs=[
                pl.BlockSpec((own_experts, chunk, 2 * FFE), lambda i, _: (0, i, 0)),
                pl.BlockSpec((own_experts, chunk, FFE), lambda i, _: (0, i, 0)),
            ]
            + [whole(x) for x in small],
        ),
        out_shape=[
            shape(own_experts, e_rows, 2 * FFE),
            shape(own_experts, e_rows, FFE),
        ]
        + small,
        cost_estimate=pl.CostEstimate(flops=0, bytes_accessed=8 << 20, transcendentals=0),
        compiler_params=pltpu.CompilerParams(
            dimension_semantics=("arbitrary",), vmem_limit_bytes=60 << 20
        ),
    )(me, e_grads, *rest, *weights, gain)


def first_exchange(collective_id, tokens, out_grad, docs, mask, misc, gains, w_query, w_key, w_value, w_out):
    devices, parts = lax.axis_size("seq"), lax.axis_size("dp")
    w_rows, width = w_out.shape
    heads = QUERY_HEADS // devices
    q_width = heads * HEAD_SIZE
    group = QUERY_HEADS // KEY_VALUE_HEADS
    w_cols = HEADS_LANES + LANES
    weights = [w_query, w_key, w_value, w_out]

    def prepare(refs):
        given, (wq, wk, wv, wo, w_all, wo_low, sem) = refs[:4], refs[4:]
        for copy in loads(list(zip(given, (wq, wk, wv, wo))), sem):
            copy.wait()
        wo_low[...] = wo[...].astype(bf16)
        for s in range(devices):
            kv = s * heads // group * HEAD_SIZE
            pieces = [wq[:, s * q_width : (s + 1) * q_width]]
            if q_width < HEADS_LANES:
                pieces.append(jnp.zeros((w_rows, HEADS_LANES - q_width), f32))
            pieces += [wk[:, kv : kv + HEAD_SIZE], wv[:, kv : kv + HEAD_SIZE]]
            w_all[s] = jnp.concatenate(pieces, axis=1).astype(bf16)

    return exchange(
        collective_id,
        [
            ("gather", "seq", tokens, None),
            ("gather", "seq", docs, None),
            ("gather", "seq", mask, None),
            ("shift", "seq", out_grad, None),
            ("share", "dp", misc, None),
            ("gather", "dp", gains, None),
            ("gather", "dp", jax.ShapeDtypeStruct((w_rows, w_cols), bf16), 0),
            ("share", "dp", jax.ShapeDtypeStruct((w_rows, width), bf16), 1),
        ],
        prepare=prepare,
        given=weights,
        work=staged(weights)
        + [
            pltpu.VMEM((devices, w_rows, w_cols), bf16),
            pltpu.VMEM((w_rows, width), bf16),
            pltpu.SemaphoreType.DMA((4,)),
        ],
        made=lambda refs: (refs[8].at[lax.axis_index("seq")], refs[9]),
        keep=(jax.ShapeDtypeStruct((devices, w_rows, w_cols), bf16), 8),
    )


def prepare(expert_in, expert_out, picks, docs, w_router, gain_attn, gain_moe):
    own_experts, w_rows, _ = expert_in.shape
    rows, experts = picks.shape[1], w_router.shape[0]
    steps = 4
    chunk = w_rows // steps

    def kernel(
        e_in, e_out, picks_ref, docs_ref, router, gain_a, gain_m, low, mask, docs_out, misc, gains
    ):
        low[:, :, : 2 * FFE] = e_in[...].astype(bf16)
        low[:, :, 2 * FFE :] = e_out[...].astype(bf16)

        @pl.when(pl.program_id(0) == 0)
        def _():
            expert = lax.broadcasted_iota(jnp.int32, (LANES, rows), 0)
            chosen = picks_ref[:1] == expert
            for k in range(1, TOP):
                chosen = chosen | (picks_ref[k : k + 1] == expert)
            mask[...] = jnp.where(chosen, 1.0, 0.0).T.astype(bf16)
            docs_out[...] = jnp.broadcast_to(docs_ref[...], docs_out.shape)
            misc[...] = jnp.concatenate(
                [router[...], jnp.zeros((LANES - experts, w_rows), f32)], axis=0
            ).T.astype(bf16)
            upper = lax.broadcasted_iota(jnp.int32, (8, w_rows), 0) == 0
            gains[...] = jnp.where(upper, gain_a[...], gain_m[...]).astype(bf16)

    def whole(shape):
        return pl.BlockSpec(shape, lambda i: (0,) * len(shape))

    def part(x):
        return pl.BlockSpec((own_experts, chunk, x.shape[2]), lambda i: (0, i, 0))

    small = [picks, docs, w_router, gain_attn[None], gain_moe[None]]
    outs = [
        jax.ShapeDtypeStruct((rows, LANES), bf16),
        jax.ShapeDtypeStruct((8, rows), jnp.int32),
        jax.ShapeDtypeStruct((w_rows, LANES), bf16),
        jax.ShapeDtypeStruct((8, w_rows), bf16),
    ]
    return pl.pallas_call(
        kernel,
        name="prepare",
        grid=(steps,),
        out_shape=[jax.ShapeDtypeStruct((own_experts, w_rows, 3 * FFE), bf16)] + outs,
        in_specs=[part(expert_in), part(expert_out)] + [whole(x.shape) for x in small],
        out_specs=[pl.BlockSpec((own_experts, chunk, 3 * FFE), lambda i: (0, i, 0))]
        + [whole(x.shape) for x in outs],
        compiler_params=pltpu.CompilerParams(
            dimension_semantics=("arbitrary",), vmem_limit_bytes=60 << 20
        ),
    )(expert_in, expert_out, *small)


def final_exchange(
    collective_id, qkv_cot, normed, token_grads, w_full, tokens, mid_cot, gain, mid, branches
):
    devices, parts = lax.axis_size("seq"), lax.axis_size("dp")
    chips = devices // 2
    _, rows, cols = qkv_cot.shape
    width = tokens.shape[1]
    out_rows = token_grads[0].shape[2]
    gq_shape = (parts, devices, out_rows, cols)
    count = len(token_grads)
    wides = [x.shape[3] for x in token_grads]
    token_grads = [x.reshape(parts, chips, 2, out_rows, x.shape[3]) for x in token_grads]

    ins = [w_full, normed, qkv_cot, tokens, mid_cot, gain, mid, *branches]

    def kernel(*refs):
        qkv_in = refs[0]
        gt_in = refs[1 : 1 + count]
        given = refs[1 + count : 1 + count + len(ins)]
        refs = refs[1 + count + len(ins) :]
        in_grad_out, output_out, gq_out = refs[:3]
        gt_out = refs[3 : 3 + count]
        refs = refs[3 + count :]
        (
            qkv_tok, nac, gq_in, grad, gq_recv, gq_sum,
            q_send, q_recv, local, gq_send, gq_rsem, gqz_send, gqz_recv, gq_local,
        ) = refs[:14]
        work = [refs[14 + 11 * i : 25 + 11 * i] for i in range(count)]
        refs = refs[14 + 11 * count :]
        local_ins, (in_grad, output, in_sem, out_sem) = refs[: len(ins)], refs[len(ins) :]
        w_all, normed_all, qkv_all, tok_ref, mid_cot_ref, gain_ref, mid_ref, *y_refs = local_ins
        me, my = lax.axis_index("seq"), lax.axis_index("dp")
        chip, core = me // 2, lax.rem(me, 2)
        sibling = me + 1 - 2 * core
        arriving = loads(list(zip(given, local_ins)), in_sem)
        barrier = pltpu.get_barrier_semaphore()
        for axis, index, size in (("seq", me, devices), ("dp", my, parts)):
            for k in range(1, size):
                pl.semaphore_signal(
                    barrier,
                    inc=1,
                    device_id={axis: lax.rem(index + k, size)},
                    device_id_type=MESH,
                )
        pl.semaphore_wait(barrier, devices + parts - 2)

        def remote(axis, src, dst, send, recv, to):
            return pltpu.make_async_remote_copy(
                src_ref=src,
                dst_ref=dst,
                send_sem=send,
                recv_sem=recv,
                device_id={axis: to},
                device_id_type=MESH,
            )

        sent = []

        def columns(j):
            return qkv_tok.at[:, pl.ds(pl.multiple_of(j * cols, cols), cols)]

        for x, w in zip(gt_in, work):
            mine, theirs, far, near, last, sems, dp_send, dp_recv, z_send, z_recv, _ = w
            copy = remote(
                "seq", x.at[:, :, 1 - core], theirs, sems.at[0], sems.at[1], sibling
            )
            copy.start()
            sent.append(copy)
            pltpu.make_async_copy(x.at[:, :, core], mine, sems.at[2]).start()
        own = pltpu.make_async_copy(qkv_in.at[me], columns(me), local)
        own.start()
        for k in range(1, devices):
            to = lax.rem(me + k, devices)
            copy = remote(
                "seq", qkv_in.at[to], columns(me), q_send.at[k - 1], q_recv.at[k - 1], to
            )
            copy.start()
            sent.append(copy)

        for x, w in zip(gt_in, work):
            mine, theirs, far, near, last, sems, dp_send, dp_recv, z_send, z_recv, _ = w
            remote("seq", x.at[:, :, core], theirs, sems.at[0], sems.at[1], sibling).wait_recv()
            pltpu.make_async_copy(x.at[:, :, core], mine, sems.at[2]).wait()
            mine[...] = (mine[...].astype(f32) + theirs[...].astype(f32)).astype(bf16)
            for k in range(1, parts):
                to = lax.rem(my + k, parts)
                copy = remote(
                    "dp", mine.at[to], far.at[k - 1], dp_send.at[k - 1], dp_recv.at[k - 1], to
                )
                copy.start()
                sent.append(copy)

        for copy in arriving:
            copy.wait()
        grad[...] = jnp.zeros_like(grad)

        @pl.loop(0, devices)
        def _(j):
            grad[...] += dot_tn(normed_all[j], qkv_all[j])

        gq_in[...] = grad[...].astype(bf16).reshape(gq_shape)
        for k in range(1, parts):
            to = lax.rem(my + k, parts)
            copy = remote(
                "dp", gq_in.at[to], gq_recv.at[my], gq_send.at[k - 1], gq_rsem.at[k - 1], to
            )
            copy.start()
            sent.append(copy)
        own_q = pltpu.make_async_copy(gq_in.at[my], gq_recv.at[my], gq_local)
        own_q.start()
        total = y_refs[0][...].astype(f32)
        for k in range(1, len(branches)):
            total = total + y_refs[k][...].astype(f32)
        output[...] = (mid_ref[...] + res_mult * total).astype(bf16)
        leaving = [pltpu.make_async_copy(output, output_out, out_sem.at[0])]
        leaving[0].start()

        for k in range(devices):
            frm = lax.rem(me + devices - k, devices)
            if k == 0:
                own.wait()
            else:
                remote(
                    "seq", qkv_in.at[frm], columns(frm), q_send.at[k - 1], q_recv.at[k - 1], frm
                ).wait_recv()
            part = dot_nt(columns(frm)[...], w_all[frm])
            nac[...] = part if k == 0 else nac[...] + part

        resid = tok_ref[...].astype(f32)
        scale = lax.rsqrt(jnp.mean(resid * resid, axis=-1, keepdims=True) + norm_eps)
        weighted = nac[...] * gain_row(gain_ref, 0)
        in_grad[...] = (
            mid_cot_ref[...]
            + scale * weighted
            - resid
            * (scale * scale * scale)
            * jnp.mean(weighted * resid, axis=-1, keepdims=True)
        ).astype(bf16)

        leaving.append(pltpu.make_async_copy(in_grad, in_grad_out, out_sem.at[1]))
        leaving[1].start()
        own_q.wait()
        for k in range(1, parts):
            frm = lax.rem(my + parts - k, parts)
            remote(
                "dp", gq_in.at[frm], gq_recv.at[frm], gq_send.at[k - 1], gq_rsem.at[k - 1], frm
            ).wait_recv()
        summed = gq_recv[0].astype(f32)
        for p in range(1, parts):
            summed = summed + gq_recv[p].astype(f32)
        gq_sum[...] = summed.astype(bf16)
        own_z = pltpu.make_async_copy(gq_sum.at[me], gq_out.at[me], gq_local)
        own_z.start()
        for k in range(1, devices):
            to = lax.rem(me + k, devices)
            copy = remote(
                "seq", gq_sum.at[to], gq_out.at[me], gqz_send.at[k - 1], gqz_recv.at[k - 1], to
            )
            copy.start()
            sent.append(copy)
        for w in work:
            mine, theirs, far, near, last, sems, dp_send, dp_recv, z_send, z_recv, _ = w
            summed = mine[my].astype(f32)
            for k in range(1, parts):
                remote(
                    "dp", mine.at[0], far.at[k - 1], dp_send.at[k - 1], dp_recv.at[k - 1], my
                ).wait_recv()
                summed = summed + far[k - 1].astype(f32)
            near[...] = summed.astype(bf16)
            for k in range(1, chips):
                to = lax.rem(chip + k, chips)
                copy = remote(
                    "seq",
                    near.at[to],
                    last.at[k - 1],
                    z_send.at[k - 1],
                    z_recv.at[k - 1],
                    2 * to + core,
                )
                copy.start()
                sent.append(copy)

        for o, w in zip(gt_out, work):
            mine, theirs, far, near, last, sems, dp_send, dp_recv, z_send, z_recv, _ = w
            summed = near[chip].astype(f32)
            for k in range(1, chips):
                remote(
                    "seq", near.at[0], last.at[k - 1], z_send.at[k - 1], z_recv.at[k - 1], me
                ).wait_recv()
                summed = summed + last[k - 1].astype(f32)
            o[...] = summed
        own_z.wait()
        for k in range(1, devices):
            frm = lax.rem(me + devices - k, devices)
            remote(
                "seq", gq_sum.at[frm], gq_out.at[frm], gqz_send.at[k - 1], gqz_recv.at[k - 1], frm
            ).wait_recv()
        for copy in sent:
            copy.wait_send()
        for copy in leaving:
            copy.wait()

    hbm = pl.BlockSpec(memory_space=pl.ANY)
    vmem = pl.BlockSpec(memory_space=pltpu.VMEM)
    dma = pltpu.SemaphoreType.DMA
    scratch = [
        pltpu.VMEM((rows, devices * cols), bf16),
        pltpu.VMEM((rows, width), f32),
        pltpu.VMEM(gq_shape, bf16),
        pltpu.VMEM((width, cols), f32),
        pltpu.VMEM(gq_shape, bf16),
        pltpu.VMEM(gq_shape[1:], bf16),
        dma((devices - 1,)),
        dma((devices - 1,)),
        dma,
        dma((parts - 1,)),
        dma((parts - 1,)),
        dma((devices - 1,)),
        dma((devices - 1,)),
        dma,
    ]
    for wide in wides:
        piece = (out_rows, wide)
        scratch += [
            pltpu.VMEM((parts, chips) + piece, bf16),
            pltpu.VMEM((parts, chips) + piece, bf16),
            pltpu.VMEM((parts - 1, chips) + piece, bf16),
            pltpu.VMEM((chips,) + piece, bf16),
            pltpu.VMEM((chips - 1,) + piece, bf16),
            dma((3,)),
            dma((parts - 1,)),
            dma((parts - 1,)),
            dma((chips - 1,)),
            dma((chips - 1,)),
            dma,
        ]
    scratch += staged(ins) + [
        pltpu.VMEM((rows, width), bf16),
        pltpu.VMEM((rows, width), bf16),
        dma((len(ins),)),
        dma((2,)),
    ]
    return pl.pallas_call(
        kernel,
        name="final_exchange",
        out_shape=[
            jax.ShapeDtypeStruct((rows, width), bf16),
            jax.ShapeDtypeStruct((rows, width), bf16),
            jax.ShapeDtypeStruct(gq_shape[1:], bf16),
        ]
        + [jax.ShapeDtypeStruct((out_rows, wide), f32) for wide in wides],
        in_specs=[hbm] * (1 + count + len(ins)),
        out_specs=[hbm] * 3 + [vmem] * count,
        scratch_shapes=scratch,
        compiler_params=pltpu.CompilerParams(
            collective_id=collective_id, has_side_effects=True, vmem_limit_bytes=60 << 20
        ),
    )(qkv_cot, *token_grads, *ins)


def on_device(
    tokens,
    out_grad,
    doc_ids,
    expert_picks,
    w_query,
    key_weight_matrix,
    value_weight_matrix,
    w_out,
    w_router,
    gain_attn,
    gain_moe,
    expert_in,
    expert_out,
):
    devices, parts = lax.axis_size("seq"), lax.axis_size("dp")
    me = lax.axis_index("seq")
    rows, width = tokens.shape[1:]
    length = rows * devices
    experts = w_router.shape[1]
    heads = QUERY_HEADS // devices
    group = QUERY_HEADS // KEY_VALUE_HEADS
    q_width = heads * HEAD_SIZE
    w_rows = w_query.shape[0]

    w_cols = HEADS_LANES + LANES
    low, mask, doc_rows, misc, gains = prepare(
        expert_in, expert_out, expert_picks[0].T, doc_ids, w_router.T, gain_attn, gain_moe
    )
    expert_full = lax.all_gather(low, "dp", axis=1, tiled=True)
    chips = devices // 2

    def shift(x, k):
        return lax.ppermute(x, "seq", [(i, (i + 2 * k) % devices) for i in range(devices)])

    tok_all, doc_all, mask_all, middle_cot, misc_full, gains_full, w_own_all, wo_full, w_all = first_exchange(
        0,
        tokens[0],
        out_grad[0],
        doc_rows,
        mask,
        misc,
        gains,
        w_query,
        key_weight_matrix,
        value_weight_matrix,
        w_out,
    )
    w_full = lax.all_gather(w_all, "dp", axis=1, tiled=True)
    held, tok_all = lax.optimization_barrier((out_grad[0], tok_all))
    cots = [held] + [
        middle_cot if k == chips // 2 else shift(held, k) for k in range(1, chips)
    ]
    w_own_all = w_own_all.reshape(width, w_cols)
    wo_full = wo_full.reshape(width, width)
    misc_full = misc_full.reshape(width, LANES)
    table = rope_table(devices, rows)

    normed_a, q_all, kv_all, attended_own, ot, lse = attend_forward(
        tok_all, w_own_all, gains_full, table, doc_all, heads
    )
    attended, mid, normed_m = attended_exchange(
        1, attended_own, tokens[0], wo_full, gains_full
    )
    (_, _, _, moe_sum, gate_cot, e_grads, *branches) = moe_exchange(
        2, normed_m, cots, mask_all, misc_full, expert_full
    )
    e_grads = lax.psum_scatter(e_grads, "dp", scatter_dimension=1, tiled=True)
    heads_cot, router_pack, mid_cot, grad_wo = middle_exchange(
        4, moe_sum, gate_cot, normed_m, misc_full, mask, mid, out_grad[0], gains_full,
        wo_full, attended, q_width,
    )
    heads_cot, branches = lax.optimization_barrier((heads_cot, branches))
    branches = [
        branches[0],
        lax.ppermute(branches[1], "seq", [(i, i ^ 2) for i in range(devices)]),
    ] + [shift(branches[1 + k], 2 * k) for k in range(1, chips // 2)]
    qkv_cot = attend_backward(q_all, kv_all, heads_cot, ot, lse, table, doc_all, heads)
    qkv_cot, branches = lax.optimization_barrier((qkv_cot, branches))
    out_rows = w_rows // devices
    input_grad, output, grad_qkv, grad_wo, router_pack = final_exchange(
        5,
        qkv_cot,
        normed_a,
        [
            grad_wo.reshape(parts, devices, out_rows, width),
            router_pack.reshape(parts, devices, out_rows, LANES),
        ],
        w_full,
        tokens[0],
        mid_cot,
        gains_full,
        mid,
        branches,
    )

    (
        grad_e_in, grad_e_out, grad_wq, grad_wk, grad_wv, grad_wo, grad_router, grad_gain_m,
        grad_gain_a, input_grad, output,
    ) = finish(
        e_grads,
        grad_qkv,
        grad_wo,
        router_pack,
        input_grad,
        output,
        [w_query, key_weight_matrix, value_weight_matrix],
        gain_attn.reshape(devices, out_rows),
        heads,
        experts,
    )
    input_grad, output = input_grad[None], output[None]
    grad_router = grad_router.T
    grad_gain_a = grad_gain_a.reshape(out_rows)
    grad_gain_m = grad_gain_m.reshape(out_rows)
    return (
        output,
        input_grad,
        grad_wq,
        grad_wk,
        grad_wv,
        grad_wo,
        grad_router,
        grad_gain_a,
        grad_gain_m,
        grad_e_in,
        grad_e_out,
    )


def solution(mesh):
    return jax.shard_map(
        on_device,
        mesh=mesh,
        in_specs=(
            P("dp", "seq", None),
            P("dp", "seq", None),
            P("dp", "seq"),
            P("dp", "seq", None),
            P("dp", None),
            P("dp", None),
            P("dp", None),
            P("dp", None),
            P("dp", None),
            P("dp"),
            P("dp"),
            P("seq", "dp", None),
            P("seq", "dp", None),
        ),
        out_specs=(
            P("dp", "seq", None),
            P("dp", "seq", None),
            P(("dp", "seq"), None),
            P(("dp", "seq"), None),
            P(("dp", "seq"), None),
            P(("dp", "seq"), None),
            P(("dp", "seq"), None),
            P(("dp", "seq")),
            P(("dp", "seq")),
            P("seq", "dp", None),
            P("seq", "dp", None),
        ),
        check_vma=False,
    )
```

```python
import functools

import jax
import jax.numpy as jnp
import numpy as np
from jax import lax
from jax.experimental import pallas as pl
from jax.experimental.pallas import tpu as pltpu
from jax.sharding import PartitionSpec as P

MESH = pl.DeviceIdType.MESH
PIECES = 2


def _block(ref, j, cut):
    if cut is None:
        return ref.at[j]
    return ref.at[:, pl.ds(pl.multiple_of(j * cut, cut), cut)]


def exchange(collective_id, ops, prepare=None, given=(), work=(), made=None, keep=None):
    axes = tuple(dict.fromkeys(axis for _, axis, _, _ in ops))
    size = {axis: lax.axis_size(axis) for axis in axes}
    out_shapes, out_specs, scratch, places = [], [], [], []
    for kind, axis, x, cut in ops:
        count = size[axis]
        out_spec = pl.BlockSpec(memory_space=pl.ANY)
        extra = []
        lead = (PIECES,) if kind == "gather" and axis == "seq" else ()
        if kind == "shift":
            shape, dtype, copies = x.shape, x.dtype, 1
        elif kind == "share":
            shape, dtype, copies = (count,) + x.shape, x.dtype, 2 * (count - 1)
        elif kind == "gather":
            shape, dtype = (count,) + x.shape, x.dtype
            copies = count - 1 if axis == "dp" else 3 + 4 * (count // 2 - 1)
        elif kind == "swap":
            copies, dtype = count - 1, x.dtype
            if cut is None:
                shape = x.shape
            elif cut[0] == "in":
                shape = (count, x.shape[0], cut[1])
            else:
                shape = (x.shape[1], count * cut[1])
        out_shapes.append(jax.ShapeDtypeStruct(shape, dtype))
        out_specs.append(out_spec)
        places.append((len(scratch), len(extra)))
        scratch += [
            pltpu.SemaphoreType.DMA(lead + (copies,)),
            pltpu.SemaphoreType.DMA(lead + (max(copies, count),)),
            pltpu.SemaphoreType.DMA,
        ] + extra

    early = [x for _, _, x, cut in ops if not isinstance(cut, int)]
    own_scratch = len(scratch)

    def kernel(*refs):
        ins, refs = list(refs[: len(early)]), refs[len(early) :]
        extra_in, refs = refs[: len(given)], refs[len(given) :]
        outs, refs = refs[: len(ops)], refs[len(ops) :]
        if keep is not None:
            kept, refs = refs[0], refs[1:]
        work, extra_work = refs[:own_scratch], refs[own_scratch:]
        ins += [None] * (len(ops) - len(early))
        me = {axis: lax.axis_index(axis) for axis in axes}
        barrier = pltpu.get_barrier_semaphore()
        for axis in axes:
            for k in range(1, size[axis]):
                pl.semaphore_signal(
                    barrier,
                    inc=1,
                    device_id={axis: lax.rem(me[axis] + k, size[axis])},
                    device_id_type=MESH,
                )
        pl.semaphore_wait(barrier, sum(size[axis] - 1 for axis in axes))

        def remote(axis, src, dst, send, recv, to):
            return pltpu.make_async_remote_copy(
                src_ref=src,
                dst_ref=dst,
                send_sem=send,
                recv_sem=recv,
                device_id={axis: to},
                device_id_type=MESH,
            )

        second, third = [], []
        for (kind, axis, _, cut), x, o, (at, extra) in zip(ops, ins, outs, places):
            if isinstance(cut, int):
                if x is None and cut == 0:
                    all_refs = list(extra_in) + list(extra_work[:-1])
                    prepare(all_refs)
                    late = made(all_refs)
                    leave = pltpu.make_async_copy(all_refs[keep[1]], kept, extra_work[-1])
                    leave.start()
                    third.append(leave.wait)
                x, cut = late[cut], None
            send, recv, local = work[at : at + 3]
            count, my = size[axis], me[axis]
            if kind == "swap":
                into = cut[1] if cut is not None and cut[0] == "out" else None
                outof = cut[1] if cut is not None and cut[0] == "in" else None
                own = pltpu.make_async_copy(_block(x, my, outof), _block(o, my, into), local)
                own.start()
                third.append(own.wait)
                for k in range(1, count):
                    to = lax.rem(my + k, count)
                    copy = remote(
                        axis,
                        _block(x, to, outof),
                        _block(o, my, into),
                        send.at[k - 1],
                        recv.at[k - 1],
                        to,
                    )
                    copy.start()
                    frm = lax.rem(my + count - k, count)
                    arrive = remote(
                        axis,
                        _block(x, to, outof),
                        _block(o, frm, into),
                        send.at[k - 1],
                        recv.at[k - 1],
                        to,
                    )
                    third.append(copy.wait_send)
                    third.append(arrive.wait_recv)
            elif kind == "gather" and axis == "dp":
                own = pltpu.make_async_copy(x, o.at[my], local)
                own.start()
                third.append(own.wait)
                for k in range(1, count):
                    to = lax.rem(my + k, count)
                    frm = lax.rem(my + count - k, count)
                    copy = remote(axis, x, o.at[my], send.at[k - 1], recv.at[k - 1], to)
                    copy.start()
                    third.append(copy.wait_send)
                    third.append(
                        remote(
                            axis, x, o.at[frm], send.at[k - 1], recv.at[k - 1], to
                        ).wait_recv
                    )
            elif kind == "shift":
                copy = remote(
                    axis, x, o, send.at[0], recv.at[0], lax.rem(my + 2 * (count // 4), count)
                )
                second.append((count // 4 + 0.9, copy.start))
                third.append(copy.wait)
            elif kind == "share":
                seq, half = me["seq"], x.shape[0] // 2
                core = lax.rem(seq, 2)
                sibling = seq + 1 - 2 * core
                own = pltpu.make_async_copy(x, o.at[my], local)
                own.start()
                third.append(own.wait)

                def side_of(ref, which, half=half):
                    return ref.at[pl.ds(which * half, half)]

                def relay(k, axis=axis, x=x, o=o, send=send, recv=recv, count=count, my=my, core=core, sibling=sibling, side_of=side_of):
                    to = lax.rem(my + k, count)
                    frm = lax.rem(my + count - k, count)
                    remote(
                        axis,
                        side_of(x, core),
                        side_of(o.at[frm], core),
                        send.at[k - 1],
                        recv.at[k - 1],
                        to,
                    ).wait_recv()
                    slot = count - 2 + k
                    spot = side_of(o.at[frm], core)
                    over = remote("seq", spot, spot, send.at[slot], recv.at[slot], sibling)
                    over.start()
                    third.append(over.wait_send)
                    third.append(
                        remote(
                            "seq",
                            spot,
                            side_of(o.at[frm], 1 - core),
                            send.at[slot],
                            recv.at[slot],
                            sibling,
                        ).wait_recv
                    )

                for k in range(1, count):
                    to = lax.rem(my + k, count)
                    copy = remote(
                        axis,
                        side_of(x, core),
                        side_of(o.at[my], core),
                        send.at[k - 1],
                        recv.at[k - 1],
                        to,
                    )
                    copy.start()
                    third.append(copy.wait_send)
                    second.append((k + 0.75, functools.partial(relay, k)))
            elif kind == "gather":
                chips = count // 2
                chip, core = my // 2, lax.rem(my, 2)
                sibling = my + 1 - 2 * core
                own = pltpu.make_async_copy(x, o.at[my], local)
                own.start()
                third.append(own.wait)

                cuts = PIECES if x.shape[0] % (16 * PIECES) == 0 else 1
                size_of = x.shape[0] // cuts

                def cut_of(ref, i, size_of=size_of):
                    return ref.at[pl.ds(i * size_of, size_of)]

                def line(src, b, i, slot, to, axis=axis, o=o, send=send, recv=recv, core=core, cut_of=cut_of):
                    return remote(
                        axis, src, cut_of(o.at[2 * b + core], i), send.at[i, slot], recv.at[i, b], to
                    )

                def across(src, b, i, slot, half, axis=axis, o=o, send=send, recv=recv, chips=chips, sibling=sibling, cut_of=cut_of):
                    return remote(
                        axis,
                        src,
                        cut_of(o.at[2 * b + half], i),
                        send.at[i, slot],
                        recv.at[i, chips + b],
                        sibling,
                    )

                def guarded(where, act):
                    pl.when(where)(act)

                for i in range(cuts):
                    for slot, where, to in ((0, chip > 0, my - 2), (1, chip < chips - 1, my + 2)):
                        copy = line(cut_of(x, i), chip, i, slot, to)
                        guarded(where, copy.start)
                        third.append(functools.partial(guarded, where, copy.wait_send))
                for i in range(cuts):
                    copy = across(cut_of(x, i), chip, i, 2, core)
                    copy.start()
                    third.append(copy.wait_send)
                    third.append(across(cut_of(x, i), chip, i, 2, 1 - core).wait_recv)

                def hop(k, side, i, chips=chips, chip=chip, core=core, my=my, x=x, o=o, line=line, across=across, cut_of=cut_of):
                    b = chip + side * k
                    there = (b >= 0) & (b < chips)
                    onward = there & ((chip - side >= 0) & (chip - side < chips))
                    slot = 3 + (k - 1) * 4 + (side + 1)
                    spot = cut_of(o.at[2 * b + core], i)
                    further = line(spot, b, i, slot, my - 2 * side)
                    over = across(spot, b, i, slot + 1, core)
                    arrived = line(cut_of(x, i), b, i, slot, my)
                    brought = across(cut_of(x, i), b, i, slot + 1, 1 - core)

                    @pl.when(there)
                    def _():
                        arrived.wait_recv()

                    guarded(onward, further.start)
                    guarded(there, over.start)
                    third.append(functools.partial(guarded, onward, further.wait_send))
                    third.append(functools.partial(guarded, there, over.wait_send))
                    third.append(functools.partial(guarded, there, brought.wait_recv))

                for k in range(1, chips):
                    for i in range(cuts):
                        for side in (-1, 1):
                            second.append((k + i / cuts, functools.partial(hop, k, side, i)))
        for _, run in sorted(second, key=lambda item: item[0]):
            run()
        for wait in third:
            wait()

    return pl.pallas_call(
        kernel,
        name=f"exchange{collective_id}",
        out_shape=out_shapes + ([] if keep is None else [keep[0]]),
        in_specs=[pl.BlockSpec(memory_space=pl.ANY)] * (len(early) + len(given)),
        out_specs=out_specs + ([] if keep is None else [pl.BlockSpec(memory_space=pl.ANY)]),
        scratch_shapes=scratch
        + list(work)
        + ([] if keep is None else [pltpu.SemaphoreType.DMA]),
        compiler_params=pltpu.CompilerParams(
            collective_id=collective_id, has_side_effects=True, vmem_limit_bytes=60 << 20
        ),
    )(*early, *given)

QUERY_HEADS = 16
KEY_VALUE_HEADS = 8
HEAD_SIZE = 64
FFE = 512
TOP = 8

att_mult = 0.015625
res_mult = 0.22
norm_eps = 1e-06
rope_theta = 10000.0
LANES = 128
bf16 = jnp.bfloat16
f32 = jnp.float32
HEADS_LANES = 128


def dot_nt(a, b):
    return lax.dot_general(a, b, (((1,), (1,)), ((), ())), preferred_element_type=f32)


def dot_nn(a, b):
    return lax.dot_general(a, b, (((1,), (0,)), ((), ())), preferred_element_type=f32)


def dot_tn(a, b):
    return lax.dot_general(a, b, (((0,), (0,)), ((), ())), preferred_element_type=f32)


def turn(x):
    half = HEAD_SIZE // 2
    lane = lax.broadcasted_iota(jnp.int32, x.shape, 1)
    width = x.shape[1]
    return jnp.where(
        lax.rem(lane, HEAD_SIZE) < half, pltpu.roll(x, width - half, 1), pltpu.roll(x, half, 1)
    )


def rope_table(blocks, rows):
    half = HEAD_SIZE // 2
    frequency = np.float32(rope_theta) ** (
        -np.arange(half, dtype=np.float32) * np.float32(2.0) / np.float32(HEAD_SIZE)
    )
    angles = (frequency[:, None] * np.arange(blocks * rows, dtype=np.float32)[None, :]).astype(
        np.float32
    )
    table = np.concatenate([np.cos(angles), np.sin(angles)], axis=0).astype(np.float32)
    return jnp.asarray(table.reshape(HEAD_SIZE, blocks, rows).transpose(1, 0, 2))


def spread_table(table):
    half = HEAD_SIZE // 2
    turned = table.T
    cos, sin = turned[:, :half], turned[:, half:]
    return (
        jnp.concatenate([cos, cos] * (LANES // HEAD_SIZE), axis=1),
        jnp.concatenate([-sin, sin] * (LANES // HEAD_SIZE), axis=1),
    )


def across_lanes(row, lanes):
    return jnp.broadcast_to(row, (lanes, row.shape[1])).T


def first_block(docs_ref, i):
    docs = docs_ref[:, 0, :].astype(f32)
    own = lax.broadcasted_iota(jnp.int32, docs.shape, 0) == i
    lane = lax.broadcasted_iota(jnp.int32, docs.shape, 1)
    start = jnp.sum(jnp.where(own & (lane == 0), docs, 0.0))
    ends = (lane == docs.shape[1] - 1) & (docs < start)
    return jnp.sum(jnp.where(ends, 1.0, 0.0)).astype(jnp.int32)


def stack_heads(x, heads):
    return jnp.concatenate(
        [x[:, h * HEAD_SIZE : (h + 1) * HEAD_SIZE] for h in range(heads)], axis=0
    )


def gain_row(ref, which):
    return jnp.concatenate(
        [ref[p, which : which + 1, :] for p in range(ref.shape[0])], axis=1
    ).astype(f32)


def attend_forward(tok_all, w_own, gain, table, docs, heads):
    blocks, rows, width = tok_all.shape
    length = blocks * rows
    cols = heads * rows
    out_width = heads * HEAD_SIZE

    def kernel(tok, w, gain_ref, table_ref, docs_ref, na_ref, q_ref, kv_ref, att_ref, ot_ref, lse_ref, k_scr, vt_scr, doc_scr):
        i = pl.program_id(0)
        x = tok[0].astype(f32)
        scale = lax.rsqrt(jnp.mean(x * x, axis=-1, keepdims=True) + norm_eps)
        na = (x * scale * gain_row(gain_ref, 0)).astype(bf16)
        na_ref[0] = na
        qkv = dot_nn(na, w[...])
        c, s = spread_table(table_ref[0])
        q, kv = qkv[:, :HEADS_LANES], qkv[:, HEADS_LANES:]
        q = (q * c + turn(q) * s).astype(bf16)
        lane = lax.broadcasted_iota(jnp.int32, kv.shape, 1)
        kv = jnp.where(lane < HEAD_SIZE, kv * c + turn(kv) * s, kv).astype(bf16)
        q_ref[0] = q
        kv_ref[0] = kv
        k_scr[i] = kv[:, :HEAD_SIZE]
        vt_scr[i] = kv.astype(f32).T[HEAD_SIZE:].astype(bf16)
        q2 = stack_heads(q * jnp.bfloat16(att_mult), heads)
        doc_row = docs_ref[i, :1].astype(f32)
        doc_scr[i] = across_lanes(doc_row, LANES)
        doc_query = jnp.concatenate([doc_row] * heads, axis=1)
        query = i * rows + lax.rem(lax.broadcasted_iota(jnp.int32, (1, cols), 1), rows)
        key_iota = lax.broadcasted_iota(jnp.int32, (rows, cols), 0)

        def step(j, carry, diagonal):
            top, total, ot = carry
            scores = dot_nt(k_scr[j], q2)
            seen = jnp.concatenate([doc_scr[j]] * (cols // LANES), axis=1) == doc_query
            if diagonal:
                seen = seen & (key_iota + j * rows <= query)
            scores = jnp.where(seen, scores, -1e30)
            new_top = jnp.maximum(top, jnp.max(scores, axis=0, keepdims=True))
            p = jnp.exp(scores - new_top)
            keep = jnp.exp(top - new_top)
            total = total * keep + jnp.sum(p, axis=0, keepdims=True)
            ot = ot * keep + dot_nn(vt_scr[j], p.astype(bf16))
            return new_top, total, ot

        top, total, ot = lax.fori_loop(
            first_block(docs_ref, i),
            i,
            functools.partial(step, diagonal=False),
            (
                jnp.full((1, cols), -1e30, f32),
                jnp.zeros((1, cols), f32),
                jnp.zeros((HEAD_SIZE, cols), f32),
            ),
        )
        top, total, ot = step(i, (top, total, ot), diagonal=True)
        ot = ot / total
        ot_ref[0] = ot
        lse_ref[0] = top + jnp.log(total)
        out = ot.T
        att_ref[0] = jnp.concatenate(
            [out[h * rows : (h + 1) * rows] for h in range(heads)], axis=1
        ).astype(bf16)

    def block(shape):
        return pl.BlockSpec((1,) + shape, lambda i: (i, 0, 0))

    def whole(shape):
        return pl.BlockSpec(shape, lambda i: (0,) * len(shape))

    grid_spec = pltpu.PrefetchScalarGridSpec(
        num_scalar_prefetch=0,
        grid=(blocks,),
        in_specs=[
            block((rows, width)),
            whole(w_own.shape),
            whole(gain.shape),
            block((HEAD_SIZE, rows)),
            whole(docs.shape),
        ],
        out_specs=[
            block((rows, width)),
            block((rows, HEADS_LANES)),
            block((rows, LANES)),
            block((rows, out_width)),
            block((HEAD_SIZE, cols)),
            block((1, cols)),
        ],
        scratch_shapes=[
            pltpu.VMEM((blocks, rows, HEAD_SIZE), bf16),
            pltpu.VMEM((blocks, HEAD_SIZE, rows), bf16),
            pltpu.VMEM((blocks, rows, LANES), f32),
        ],
    )
    return pl.pallas_call(
        kernel,
        name="attend_forward",
        grid_spec=grid_spec,
        out_shape=[
            jax.ShapeDtypeStruct((blocks, rows, width), bf16),
            jax.ShapeDtypeStruct((blocks, rows, HEADS_LANES), bf16),
            jax.ShapeDtypeStruct((blocks, rows, LANES), bf16),
            jax.ShapeDtypeStruct((blocks, rows, out_width), bf16),
            jax.ShapeDtypeStruct((blocks, HEAD_SIZE, cols), f32),
            jax.ShapeDtypeStruct((blocks, 1, cols), f32),
        ],
        cost_estimate=pl.CostEstimate(
            flops=2 * length * width * 256 + 2 * length * length * cols // rows * 128,
            bytes_accessed=2 * length * width * 4,
            transcendentals=length * length,
        ),
        compiler_params=pltpu.CompilerParams(
            dimension_semantics=("arbitrary",), vmem_limit_bytes=60 << 20
        ),
    )(
        tok_all,
        w_own,
        gain,
        table,
        docs,
    )


def attend_backward(q_all, kv_all, cot, ot, lse, table, docs, heads):
    blocks, rows, _ = q_all.shape
    length = blocks * rows
    cols = heads * rows

    def kernel(q_ref, kv_ref, do_ref, ot_ref, lse_ref, table_ref, docs_ref, out_ref, dk_scr, dv_scr, dq_scr, doc_scr):
        i = pl.program_id(0)

        @pl.when(i == 0)
        def _():
            dk_scr[...] = jnp.zeros_like(dk_scr)
            dv_scr[...] = jnp.zeros_like(dv_scr)

        q2 = stack_heads(q_ref[0] * jnp.bfloat16(att_mult), heads)
        do2 = stack_heads(do_ref[0], heads)
        delta = jnp.sum(do2.astype(f32).T * ot_ref[0], axis=0, keepdims=True)
        log_total = lse_ref[0]
        doc_row = docs_ref[i, :1].astype(f32)
        doc_scr[i] = across_lanes(doc_row, LANES)
        doc_query = jnp.concatenate([doc_row] * heads, axis=1)
        query = i * rows + lax.rem(lax.broadcasted_iota(jnp.int32, (1, cols), 1), rows)
        key_iota = lax.broadcasted_iota(jnp.int32, (rows, cols), 0)
        dq_scr[...] = jnp.zeros_like(dq_scr)

        @pl.loop(first_block(docs_ref, i), i + 1)
        def _(j):
            kv = kv_ref[j]
            k, v = kv[:, :HEAD_SIZE], kv[:, HEAD_SIZE:]
            scores = dot_nt(k, q2)
            key = key_iota + j * rows
            same = jnp.concatenate([doc_scr[j]] * (cols // LANES), axis=1) == doc_query
            p = jnp.where(same & (key <= query), jnp.exp(scores - log_total), 0.0)
            ds = (p * (dot_nt(v, do2) - delta)).astype(bf16)
            dv_scr[j] += dot_nn(p.astype(bf16), do2)
            dk_scr[j] += dot_nn(ds, q2)
            dq_scr[...] += dot_tn(ds, k)

        def rope_back(x, c, s):
            return (x * c - turn(x) * s).astype(bf16)

        dq = dq_scr[...] * att_mult
        dq = [dq[h * rows : (h + 1) * rows] for h in range(heads)]
        if heads * HEAD_SIZE < HEADS_LANES:
            dq.append(jnp.zeros((rows, HEADS_LANES - heads * HEAD_SIZE), f32))
        dq = jnp.concatenate(dq, axis=1).astype(bf16).astype(f32)
        out_ref[i, :, :HEADS_LANES] = rope_back(dq, *spread_table(table_ref[i]))

        @pl.when(i == blocks - 1)
        def _():
            @pl.loop(0, blocks)
            def _(j):
                kv = jnp.concatenate([dk_scr[j], dv_scr[j]], axis=1)
                lane = lax.broadcasted_iota(jnp.int32, kv.shape, 1)
                c, s = spread_table(table_ref[j])
                kv = jnp.where(lane < HEAD_SIZE, kv * c - turn(kv) * s, kv).astype(bf16)
                out_ref[j, :, HEADS_LANES:] = kv

    def block(shape):
        return pl.BlockSpec((1,) + shape, lambda i: (i, 0, 0))

    def whole(shape):
        return pl.BlockSpec(shape, lambda i: (0,) * len(shape))

    grid_spec = pltpu.PrefetchScalarGridSpec(
        num_scalar_prefetch=0,
        grid=(blocks,),
        in_specs=[
            block((rows, HEADS_LANES)),
            whole((blocks, rows, LANES)),
            block((rows, heads * HEAD_SIZE)),
            block((HEAD_SIZE, cols)),
            block((1, cols)),
            whole((blocks, HEAD_SIZE, rows)),
            whole(docs.shape),
        ],
        out_specs=whole((blocks, rows, HEADS_LANES + LANES)),
        scratch_shapes=[
            pltpu.VMEM((blocks, rows, HEAD_SIZE), f32),
            pltpu.VMEM((blocks, rows, HEAD_SIZE), f32),
            pltpu.VMEM((cols, HEAD_SIZE), f32),
            pltpu.VMEM((blocks, rows, LANES), f32),
        ],
    )
    return pl.pallas_call(
        kernel,
        name="attend_backward",
        grid_spec=grid_spec,
        out_shape=jax.ShapeDtypeStruct((blocks, rows, HEADS_LANES + LANES), bf16),
        cost_estimate=pl.CostEstimate(
            flops=5 * length * length * cols // rows * 128,
            bytes_accessed=2 * length * 1024,
            transcendentals=length * length,
        ),
        compiler_params=pltpu.CompilerParams(
            dimension_semantics=("arbitrary",), vmem_limit_bytes=60 << 20
        ),
    )(
        q_all,
        kv_all,
        cot,
        ot,
        lse,
        table,
        docs,
    )


def moe_exchange(collective_id, normed, cots, mask, router, weights):
    devices = lax.axis_size("seq")
    chips = devices // 2
    rows, width = normed.shape
    own_experts = weights.shape[0]
    gate_rows = devices * own_experts

    def order(chip, k):
        left = chip < chips - 1 - chip
        longer = jnp.where(left, chips - 1 - chip, chip)
        near = jnp.where(left, chip + k, chip - k)
        return jnp.where(k <= longer, near, jnp.where(left, chips - 1 - k, k))

    def kernel(*refs):
        x_in, g_in = refs[0], refs[1 : 1 + chips]
        mask_ref, router_ref, w_given = refs[1 + chips : 4 + chips]
        (lin_out, slot_out, hid_out, n_sum, gate_out, g_out) = refs[4 + chips : 10 + chips]
        y_outs = refs[10 + chips : 11 + chips + chips // 2]
        (
            x_all, g_all, win, wout, y_acc, n_acc, gate_acc, gate_stage,
            n_mine, n_far, n_give, n_theirs, y_give, y_theirs, y_pre, y_in,
            lin_st, slot_st, hid_st, gin, gout, hid_ld,
            local, line_send, line_recv, sib_send, sib_recv, g_local, g_send, g_recv,
            n_send, n_recv, y_send, y_recv, far_send, far_recv, gate_send, gate_recv,
            st_sem, y_sem, ld_sem, w_sem, wg_sem, hand_send, hand_recv,
        ) = refs[11 + chips + chips // 2 :]
        me = lax.axis_index("seq")
        chip, core = me // 2, lax.rem(me, 2)
        sibling = me + 1 - 2 * core
        win_copy = pltpu.make_async_copy(
            w_given.at[:, :, pl.ds(0, 2 * FFE)], win, w_sem.at[0]
        )
        wout_copy = pltpu.make_async_copy(
            w_given.at[:, :, pl.ds(2 * FFE, FFE)], wout, w_sem.at[1]
        )
        win_copy.start()
        wout_copy.start()
        barrier = pltpu.get_barrier_semaphore()
        for k in range(1, devices):
            pl.semaphore_signal(
                barrier, inc=1, device_id={"seq": lax.rem(me + k, devices)}, device_id_type=MESH
            )
        pl.semaphore_wait(barrier, devices - 1)

        def remote(src, dst, send, recv, to):
            return pltpu.make_async_remote_copy(
                src_ref=src,
                dst_ref=dst,
                send_sem=send,
                recv_sem=recv,
                device_id={"seq": to},
                device_id_type=MESH,
            )

        half = rows // PIECES

        def piece(b, core_of, i):
            return x_all.at[2 * b + core_of, pl.ds(i * half, half)]

        def line(src, b, i, slot, to):
            return remote(
                src, piece(b, core, i), line_send.at[i, slot], line_recv.at[i, b], to
            )

        def across(src, b, core_of, i):
            return remote(
                src, piece(b, core_of, i), sib_send.at[i, b], sib_recv.at[i, b], sibling
            )

        def own_piece(i):
            return x_in.at[pl.ds(i * half, half)]

        def pass_on(b, i, to):
            return line(piece(b, core, i), b, i, 2 + b, to)

        def to_sibling(b, i):
            return across(piece(b, core, i), b, core, i)

        def own_sends(act):
            for i in range(PIECES):

                @pl.when(chip > 0)
                def _(i=i):
                    act(line(own_piece(i), chip, i, 0, me - 2))

                @pl.when(chip < chips - 1)
                def _(i=i):
                    act(line(own_piece(i), chip, i, 1, me + 2))

            for i in range(PIECES):
                act(across(own_piece(i), chip, core, i))

        def cot_to_sibling(k):
            b = lax.rem(chip + chips - k, chips)
            return remote(
                g_in[k], g_all.at[2 * b + core], g_send.at[k], g_recv.at[b], sibling
            )

        def cot_local(k):
            b = lax.rem(chip + chips - k, chips)
            return pltpu.make_async_copy(g_in[k], g_all.at[2 * b + core], g_local.at[k])

        own_sends(lambda copy: copy.start())
        own = pltpu.make_async_copy(x_in, x_all.at[me], local)
        own.start()
        for k in range(chips):
            cot_to_sibling(k).start()
            cot_local(k).start()
        own.wait()
        for k in range(chips):
            cot_local(k).wait()
        win_copy.wait()
        wout_copy.wait()

        def gate_copy(block):
            return remote(
                gate_stage.at[block],
                gate_out.at[me],
                gate_send.at[block],
                gate_recv.at[me],
                block,
            )

        def n_copy(p):
            return remote(n_give, n_theirs.at[p], n_send.at[p], n_recv.at[p], sibling)

        def y_copy(p):
            return remote(y_give, y_theirs.at[p], y_send.at[p], y_recv.at[p], sibling)

        pairs = chips // 2
        pair = chip // 2
        mate = chip + 1 - 2 * lax.rem(chip, 2)

        def y_leave(b, k):
            return pltpu.make_async_copy(y_pre.at[b], y_outs[k], y_sem.at[k])

        def y_hand(b):
            far = lax.rem(b // 2 + pairs - pair, pairs) - 1
            return remote(
                y_pre.at[b], y_in.at[far], hand_send.at[far], hand_recv.at[far], 2 * mate + core
            )

        def stage_copies(e, block):
            return [
                pltpu.make_async_copy(lin_st.at[e], lin_out.at[e, block], st_sem.at[0, e]),
                pltpu.make_async_copy(slot_st.at[e], slot_out.at[e, block], st_sem.at[1, e]),
                pltpu.make_async_copy(hid_st.at[e], hid_out.at[e, block], st_sem.at[2, e]),
            ]

        def far_copy(b):
            return remote(
                n_mine.at[b], n_far.at[chip], far_send.at[b], far_recv.at[chip], 2 * b + core
            )

        def fold(k):
            b, p = order(chip, k), lax.rem(k, 2)
            n_copy(p).wait_recv()
            both = n_acc[...].astype(bf16).astype(f32) + n_theirs[p].astype(f32)

            @pl.when(b == chip)
            def _():
                n_sum[...] = both

            @pl.when(b != chip)
            def _():
                n_mine[b] = both.astype(bf16)
                far_copy(b).start()

            y_copy(p).wait_recv()
            y_pre[b] = (y_acc[...] + y_theirs[p].astype(f32)).astype(bf16)

            @pl.when(b == chip)
            def _():
                y_leave(b, 0).start()

            @pl.when(b == mate)
            def _():
                y_leave(b, 1).start()

            @pl.when((b != mate) & (lax.rem(b + chip, 2) == 1))
            def _():
                y_hand(b).start()

        def compute(block, before):
            x = x_all[block]
            there = mask_ref[block] > 0
            logits = jnp.where(there, dot_nn(x, router_ref[...]), -1e30)
            gates = jnp.where(
                there, jnp.exp(logits - jnp.max(logits, axis=1, keepdims=True)), 0.0
            )
            gates = gates / jnp.sum(gates, axis=1, keepdims=True)
            lane = lax.broadcasted_iota(jnp.int32, gates.shape, 1)
            y_acc[...] = jnp.zeros_like(y_acc)
            n_acc[...] = jnp.zeros_like(n_acc)
            gate_acc[...] = jnp.zeros_like(gate_acc)

            @pl.loop(0, own_experts)
            def _(e):
                gate = jnp.sum(
                    jnp.where(lane == me * own_experts + e, gates, 0.0), axis=1, keepdims=True
                )
                lin = dot_nn(x_all[block], win[e])
                gate_lin, up_lin = lin[:, :FFE], lin[:, FFE:]
                sig = 0.5 + 0.5 * jnp.tanh(0.5 * gate_lin)
                silu = gate_lin * sig
                hidden = (silu * up_lin).astype(bf16)

                @pl.when(before)
                def _():
                    for copy in stage_copies(e, block):
                        copy.wait()

                hid_st[e] = hidden
                res = dot_nt(hidden, wout[e]).astype(bf16).astype(f32)
                y_acc[...] += gate * res
                cot = g_all[block].astype(f32) * res_mult
                gate_acc[...] += jnp.where(
                    lane == me * own_experts + e, jnp.sum(cot * res, axis=1, keepdims=True), 0.0
                )
                slot = (gate * cot).astype(bf16)
                slot_st[e] = slot
                hidden_cot = dot_nn(slot, wout[e])
                lin_cot = jnp.concatenate(
                    [
                        hidden_cot * up_lin * (sig * (1.0 + gate_lin * (1.0 - sig))),
                        hidden_cot * silu,
                    ],
                    axis=1,
                ).astype(bf16)
                lin_st[e] = lin_cot
                for copy in stage_copies(e, block):
                    copy.start()
                n_acc[...] += dot_nt(lin_cot, win[e]).astype(bf16).astype(f32)

            gate_stage[block] = gate_acc[...].T[:gate_rows]

            @pl.when(block != me)
            def _():
                gate_copy(block).start()

            @pl.when(block == me)
            def _():
                gate_out[block] = gate_stage[block]

        def hop(k, i):
            for side in (-1, 1):
                away = chip + side * k

                @pl.when((k > 0) & (k < chips) & (away >= 0) & (away < chips))
                def _(side=side, away=away):
                    pass_on(away, i, me).wait_recv()

                    @pl.when((chip - side >= 0) & (chip - side < chips))
                    def _():
                        pass_on(away, i, me - 2 * side).start()

                    to_sibling(away, i).start()

        @pl.loop(0, chips)
        def _(k):
            b = order(chip, k)
            hop(k, 1)
            for i in range(PIECES):
                across(own_piece(i), b, 1 - core, i).wait_recv()
            remote(
                x_in, g_all.at[2 * b + 1 - core], g_send.at[0], g_recv.at[b], sibling
            ).wait_recv()

            @pl.loop(0, 2)
            def _(h):
                @pl.when(h == 1)
                def _():
                    hop(k + 1, 0)

                compute(2 * b + lax.rem(core + 1 + h, 2), (k > 0) | (h > 0))

                @pl.when(h == 0)
                def _():
                    p = lax.rem(k, 2)

                    @pl.when(k > 0)
                    def _():
                        n_copy(1 - p).wait_send()
                        y_copy(1 - p).wait_send()

                    n_give[...] = n_acc[...].astype(bf16)
                    y_give[...] = y_acc[...].astype(bf16)
                    n_copy(p).start()
                    y_copy(p).start()

                @pl.when(h == 1)
                def _():
                    fold(k)

        for e in range(own_experts):
            for copy in stage_copies(e, 0):
                copy.wait()

        def loads(t, p):
            e, b = lax.rem(t, own_experts), t // own_experts
            pair = pl.ds(2 * b, 2)
            return [
                pltpu.make_async_copy(
                    lin_out.at[e, pair], g_all.at[pl.ds(4 * p, 2)], ld_sem.at[0, p]
                ),
                pltpu.make_async_copy(
                    slot_out.at[e, pair], g_all.at[pl.ds(4 * p + 2, 2)], ld_sem.at[1, p]
                ),
                pltpu.make_async_copy(hid_out.at[e, pair], hid_ld.at[p], ld_sem.at[2, p]),
            ]

        for copy in loads(jnp.int32(0), 0):
            copy.start()
        gin[...] = jnp.zeros_like(gin)
        gout[...] = jnp.zeros_like(gout)

        @pl.loop(0, chips * own_experts)
        def _(t):
            p = lax.rem(t, 2)
            for copy in loads(t, p):
                copy.wait()

            @pl.when(t + 1 < chips * own_experts)
            def _():
                for copy in loads(t + 1, 1 - p):
                    copy.start()

            e, b = lax.rem(t, own_experts), t // own_experts
            x = x_all[pl.ds(2 * b, 2)].reshape(2 * rows, width)
            lin_cot = g_all[pl.ds(4 * p, 2)].reshape(2 * rows, width)
            gin[e] += dot_tn(x, lin_cot)
            slot = g_all[pl.ds(4 * p + 2, 2)].reshape(2 * rows, width)
            gout[e] += dot_tn(slot, hid_ld[p].reshape(2 * rows, FFE))

        @pl.loop(1, chips)
        def _(k):
            for side in (-1, 1):
                away = chip + side * k

                for i in range(PIECES):

                    @pl.when((away >= 0) & (away < chips))
                    def _(side=side, away=away, i=i):
                        to_sibling(away, i).wait_send()

                        @pl.when((chip - side >= 0) & (chip - side < chips))
                        def _():
                            pass_on(away, i, me - 2 * side).wait_send()

        own_sends(lambda copy: copy.wait_send())

        def keep_of(j):
            return 2 * lax.rem(pair + 1 + j, pairs) + lax.rem(chip, 2)

        for j in range(pairs - 1):
            b = keep_of(j)
            y_hand(b).wait_recv()
            y_pre[b] = (y_pre[b].astype(f32) + y_in[j].astype(f32)).astype(bf16)
            y_leave(b, 2 + j).start()

        leaving = []
        for e in range(own_experts):
            for j in range(width // rows):
                i = e * (width // rows) + j
                x_all[i] = gin[e, j * rows : (j + 1) * rows].astype(bf16)
                g_all[i, :, :FFE] = gout[e, j * rows : (j + 1) * rows].astype(bf16)
                at = 2 * len(leaving)
                here = pl.ds(j * rows, rows)
                leaving.append(
                    (
                        pltpu.make_async_copy(
                            x_all.at[i], g_out.at[e, here, pl.ds(0, 2 * FFE)], wg_sem.at[at]
                        ),
                        pltpu.make_async_copy(
                            g_all.at[i, :, pl.ds(0, FFE)],
                            g_out.at[e, here, pl.ds(2 * FFE, FFE)],
                            wg_sem.at[at + 1],
                        ),
                    )
                )
                for copy in leaving[-1]:
                    copy.start()

        @pl.loop(1, chips)
        def _(k):
            b = order(chip, k)
            remote(
                n_mine.at[b], n_far.at[b], far_send.at[b], far_recv.at[b], 2 * b + core
            ).wait_recv()
            n_sum[...] += n_far[b].astype(f32)
            far_copy(b).wait_send()

        @pl.loop(1, devices)
        def _(k):
            block = lax.rem(me + k, devices)
            remote(
                gate_stage.at[block],
                gate_out.at[block],
                gate_send.at[block],
                gate_recv.at[block],
                block,
            ).wait_recv()
            gate_copy(block).wait_send()

        n_copy((chips - 1) % 2).wait_send()
        y_copy((chips - 1) % 2).wait_send()
        for both in leaving:
            for copy in both:
                copy.wait()
        y_leave(chip, 0).wait()
        y_leave(mate, 1).wait()
        for j in range(pairs - 1):
            y_leave(keep_of(j), 2 + j).wait()
            y_hand(keep_of(j) + mate - chip).wait_send()

        for k in range(chips):
            cot_to_sibling(k).wait_send()

    hbm = pl.BlockSpec(memory_space=pl.ANY)
    vmem = pl.BlockSpec(memory_space=pltpu.VMEM)
    block = (rows, width)
    dma = pltpu.SemaphoreType.DMA
    flops = 9 * own_experts * 2 * devices * rows * width * FFE // 1
    return pl.pallas_call(
        kernel,
        name="moe_exchange",
        out_shape=[
            jax.ShapeDtypeStruct((own_experts, devices, rows, 2 * FFE), bf16),
            jax.ShapeDtypeStruct((own_experts, devices) + block, bf16),
            jax.ShapeDtypeStruct((own_experts, devices, rows, FFE), bf16),
            jax.ShapeDtypeStruct(block, f32),
            jax.ShapeDtypeStruct((devices, gate_rows, rows), f32),
            jax.ShapeDtypeStruct((own_experts, width, 3 * FFE), bf16),
        ]
        + [jax.ShapeDtypeStruct(block, bf16)] * (1 + chips // 2),
        in_specs=[hbm] * (1 + chips) + [vmem] * 2 + [hbm],
        out_specs=[hbm] * 3 + [vmem] * 2 + [hbm] * (2 + chips // 2),
        scratch_shapes=[
            pltpu.VMEM((devices,) + block, bf16),
            pltpu.VMEM((devices,) + block, bf16),
            pltpu.VMEM((own_experts, width, 2 * FFE), bf16),
            pltpu.VMEM((own_experts, width, FFE), bf16),
            pltpu.VMEM(block, f32),
            pltpu.VMEM(block, f32),
            pltpu.VMEM((rows, LANES), f32),
            pltpu.VMEM((devices, gate_rows, rows), f32),
            pltpu.VMEM((chips,) + block, bf16),
            pltpu.VMEM((chips,) + block, bf16),
            pltpu.VMEM(block, bf16),
            pltpu.VMEM((2,) + block, bf16),
            pltpu.VMEM(block, bf16),
            pltpu.VMEM((2,) + block, bf16),
            pltpu.VMEM((chips,) + block, bf16),
            pltpu.VMEM((chips // 2 - 1,) + block, bf16),
            pltpu.VMEM((own_experts, rows, 2 * FFE), bf16),
            pltpu.VMEM((own_experts,) + block, bf16),
            pltpu.VMEM((own_experts, rows, FFE), bf16),
            pltpu.VMEM((own_experts, width, 2 * FFE), f32),
            pltpu.VMEM((own_experts, width, FFE), f32),
            pltpu.VMEM((2, 2, rows, FFE), bf16),
        ]
        + [dma]
        + [
            dma(count)
            for count in (
                (PIECES, chips + 2), (PIECES, chips), (PIECES, chips), (PIECES, chips),
                (chips,), (chips,), (chips,), (2,), (2,), (2,), (2,),
                (chips,), (chips,), (devices,), (devices,),
            )
        ]
        + [
            dma((3, own_experts)),
            dma((1 + chips // 2,)),
            dma((3, 2)),
            dma((2,)),
            dma((2 * own_experts * (width // rows),)),
            dma((chips // 2 - 1,)),
            dma((chips // 2 - 1,)),
        ],
        cost_estimate=pl.CostEstimate(
            flops=flops, bytes_accessed=40 << 20, transcendentals=devices * rows * FFE * 2
        ),
        compiler_params=pltpu.CompilerParams(
            collective_id=collective_id, has_side_effects=True, vmem_limit_bytes=63 << 20
        ),
    )(normed, *cots, mask, router, weights)


class Links:
    def __init__(self, axes):
        self.size = {axis: lax.axis_size(axis) for axis in axes}
        self.me = {axis: lax.axis_index(axis) for axis in axes}

    def barrier(self):
        sem = pltpu.get_barrier_semaphore()
        for axis, size in self.size.items():
            for k in range(1, size):
                pl.semaphore_signal(
                    sem,
                    inc=1,
                    device_id={axis: lax.rem(self.me[axis] + k, size)},
                    device_id_type=MESH,
                )
        pl.semaphore_wait(sem, sum(size - 1 for size in self.size.values()))

    def copy(self, axis, src, dst, send, recv, to):
        return pltpu.make_async_remote_copy(
            src_ref=src,
            dst_ref=dst,
            send_sem=send,
            recv_sem=recv,
            device_id={axis: to},
            device_id_type=MESH,
        )

    def swap_start(self, axis, src, dst, send, recv, local):
        me, size = self.me[axis], self.size[axis]
        pltpu.make_async_copy(src.at[me], dst.at[me], local).start()
        for k in range(1, size):
            to = lax.rem(me + k, size)
            self.copy(axis, src.at[to], dst.at[me], send.at[k - 1], recv.at[k - 1], to).start()

    def swap_wait(self, axis, src, dst, send, recv, local):
        me, size = self.me[axis], self.size[axis]
        pltpu.make_async_copy(src.at[me], dst.at[me], local).wait()
        for k in range(1, size):
            frm = lax.rem(me + size - k, size)
            self.copy(axis, src.at[frm], dst.at[frm], send.at[k - 1], recv.at[k - 1], frm).wait()


def loads(pairs, sems):
    copies = [
        pltpu.make_async_copy(src, dst, sems.at[i]) for i, (src, dst) in enumerate(pairs)
    ]
    for copy in copies:
        copy.start()
    return copies


def staged(arrays):
    return [pltpu.VMEM(x.shape, x.dtype) for x in arrays]


def swap_sems(size):
    dma = pltpu.SemaphoreType.DMA
    return [dma((size - 1,)), dma((size - 1,)), dma]


def attended_exchange(collective_id, attended_own, tokens, w_out, gain):
    devices, rows, cols = attended_own.shape
    width = tokens.shape[1]

    ins = [tokens, w_out, gain]
    outs = [
        jax.ShapeDtypeStruct((rows, width), bf16),
        jax.ShapeDtypeStruct((rows, width), f32),
        jax.ShapeDtypeStruct((rows, width), bf16),
    ]

    def kernel(att_in, *refs):
        given, results = refs[:3], refs[3:6]
        tok, w_all, gain_ref = refs[6:9]
        att_ref, mid_ref, norm_ref, got, in_sem, out_sem, *sems = refs[9:]
        links = Links(("seq",))
        arriving = loads(list(zip(given, (tok, w_all, gain_ref))), in_sem)
        links.barrier()
        links.swap_start("seq", att_in, got, *sems)
        for copy in arriving:
            copy.wait()
        links.swap_wait("seq", att_in, got, *sems)
        attended = jnp.concatenate([got[j] for j in range(devices)], axis=1)
        att_ref[...] = attended
        mid = tok[...].astype(f32) + res_mult * dot_nn(attended, w_all[...])
        mid_ref[...] = mid
        scale = lax.rsqrt(jnp.mean(mid * mid, axis=-1, keepdims=True) + norm_eps)
        norm_ref[...] = (mid * scale * gain_row(gain_ref, 1)).astype(bf16)
        for copy in loads(list(zip((att_ref, mid_ref, norm_ref), results)), out_sem):
            copy.wait()

    hbm = pl.BlockSpec(memory_space=pl.ANY)
    dma = pltpu.SemaphoreType.DMA
    return pl.pallas_call(
        kernel,
        name="attended_exchange",
        out_shape=outs,
        in_specs=[hbm] * 4,
        out_specs=[hbm] * 3,
        scratch_shapes=staged(ins)
        + staged(outs)
        + [pltpu.VMEM(attended_own.shape, bf16), dma((3,)), dma((3,))]
        + swap_sems(devices),
        compiler_params=pltpu.CompilerParams(
            collective_id=collective_id, has_side_effects=True, vmem_limit_bytes=60 << 20
        ),
    )(attended_own, *ins)


def middle_exchange(
    collective_id, moe_sum, gate_cot, normed, router, mask, mid, out_grad, gain, w_out, attended, cols
):
    devices, gate_rows, rows = gate_cot.shape
    width = normed.shape[1]
    experts = gate_rows

    ins = [moe_sum, gate_cot, normed, router, mask, mid, out_grad, gain, w_out, attended]
    outs = [
        jax.ShapeDtypeStruct((width, LANES), bf16),
        jax.ShapeDtypeStruct((rows, width), f32),
        jax.ShapeDtypeStruct((width, width), bf16),
    ]

    def kernel(*refs):
        given, heads_out, results, refs = refs[:10], refs[10], refs[11:14], refs[14:]
        (
            moe_ref, gate_ref, norm_ref, router_ref, mask_ref, mid_ref, cot_ref, gain_ref, w_all, att_ref,
            pack_out, mid_cot_out, wo_out, give, in_sem, out_sem, *sems,
        ) = refs
        links = Links(("seq",))
        arriving = loads(list(zip(given, refs[:10])), in_sem)
        links.barrier()
        for copy in arriving:
            copy.wait()
        there = mask_ref[...] > 0
        logits = jnp.where(there, dot_nn(norm_ref[...], router_ref[...]), -1e30)
        gates = jnp.where(
            there, jnp.exp(logits - jnp.max(logits, axis=1, keepdims=True)), 0.0
        )
        gates = gates / jnp.sum(gates, axis=1, keepdims=True)
        gate = gate_ref[0]
        for j in range(1, devices):
            gate = gate + gate_ref[j]
        gate = jnp.concatenate([gate, jnp.zeros((LANES - gate_rows, rows), f32)], axis=0).T
        pick_cot = gates * (gate - jnp.sum(gates * gate, axis=1, keepdims=True))
        logit_cot = pick_cot.astype(bf16)
        cot = moe_ref[...] + dot_nt(logit_cot, router_ref[...])
        mid = mid_ref[...]
        scale = lax.rsqrt(jnp.mean(mid * mid, axis=-1, keepdims=True) + norm_eps)
        gain_grad = jnp.sum(cot * mid * scale, axis=0, keepdims=True)
        weighted = cot * gain_row(gain_ref, 1)
        mid_cot = (
            cot_ref[...].astype(f32)
            + scale * weighted
            - mid * (scale * scale * scale) * jnp.mean(weighted * mid, axis=-1, keepdims=True)
        )
        mid_cot_out[...] = mid_cot
        branch_cot = (res_mult * mid_cot).astype(bf16)
        attended_cot = dot_nt(branch_cot, w_all[...]).astype(bf16)
        for j in range(devices):
            give[j] = attended_cot[:, j * cols : (j + 1) * cols]
        links.swap_start("seq", give, heads_out, *sems)
        wo_out[...] = dot_tn(att_ref[...], branch_cot).astype(bf16)
        pack = dot_tn(norm_ref[...], logit_cot)
        lane = lax.broadcasted_iota(jnp.int32, pack.shape, 1)
        pack_out[...] = jnp.where(
            lane == experts, jnp.broadcast_to(gain_grad, (LANES, width)).T, pack
        ).astype(bf16)
        for copy in loads(list(zip((pack_out, mid_cot_out, wo_out), results)), out_sem):
            copy.wait()
        links.swap_wait("seq", give, heads_out, *sems)

    hbm = pl.BlockSpec(memory_space=pl.ANY)
    dma = pltpu.SemaphoreType.DMA
    return pl.pallas_call(
        kernel,
        name="middle_exchange",
        out_shape=[jax.ShapeDtypeStruct((devices, rows, cols), bf16)] + outs,
        in_specs=[hbm] * 10,
        out_specs=[hbm] * 4,
        scratch_shapes=staged(ins)
        + staged(outs)
        + [pltpu.VMEM((devices, rows, cols), bf16), dma((10,)), dma((3,))]
        + swap_sems(devices),
        compiler_params=pltpu.CompilerParams(
            collective_id=collective_id, has_side_effects=True, vmem_limit_bytes=60 << 20
        ),
    )(*ins)


def finish(e_grads, grad_qkv, grad_wo, pack, input_grad, output, weights, gain, heads, experts):
    own_experts, e_rows, e_cols = e_grads.shape
    devices, out_rows, _ = grad_qkv.shape
    q_width = heads * HEAD_SIZE
    share = devices // KEY_VALUE_HEADS if devices > KEY_VALUE_HEADS else 1
    steps = 4
    chunk = e_rows // steps
    me = lax.axis_index("seq").astype(jnp.int32).reshape(1)

    def kernel(
        me_ref, e_ref, qkv_ref, wo_ref, pack_ref, in_ref, out_ref, wq, wk, wv, gain_ref,
        e_in, e_out, gq, gk, gv, gwo, grouter, ggain_m, ggain_a, in_grad, output_ref,
    ):
        e_in[...] = e_ref[:, :, : 2 * FFE].astype(f32)
        e_out[...] = e_ref[:, :, 2 * FFE :].astype(f32)

        @pl.when(pl.program_id(0) == 0)
        def _():
            blocks = [qkv_ref[j].astype(f32) for j in range(devices)]

            def per_head(first):
                heads_of = []
                for j in range(KEY_VALUE_HEADS):
                    part = blocks[j * share][:, first : first + HEAD_SIZE]
                    for i in range(1, share):
                        part = part + blocks[j * share + i][:, first : first + HEAD_SIZE]
                    heads_of.append(part)
                return jnp.concatenate(heads_of, axis=1)

            grad_q = jnp.concatenate([b[:, :q_width] for b in blocks], axis=1)
            grad_k = per_head(HEADS_LANES)
            grad_v = per_head(HEADS_LANES + HEAD_SIZE)
            gq[...], gk[...], gv[...] = grad_q, grad_k, grad_v

            def rounded(ref):
                return ref[...].astype(bf16).astype(f32)

            def row(column):
                return jnp.broadcast_to(column, (out_rows, LANES)).T[:1]

            gain_grad = (
                jnp.sum(rounded(wq) * grad_q, axis=1, keepdims=True)
                + jnp.sum(rounded(wk) * grad_k, axis=1, keepdims=True)
                + jnp.sum(rounded(wv) * grad_v, axis=1, keepdims=True)
            )
            own = lax.broadcasted_iota(jnp.int32, (devices, 1), 0) == me_ref[0]
            own_gain = jnp.sum(jnp.where(own, rounded(gain_ref), 0.0), axis=0, keepdims=True)
            ggain_a[...] = row(gain_grad) / own_gain
            gwo[...] = wo_ref[...]
            grouter[...] = pack_ref[...].T[:experts]
            ggain_m[...] = row(pack_ref[:, experts : experts + 1])
            in_grad[...] = in_ref[...]
            output_ref[...] = out_ref[...]

    def whole(x):
        return pl.BlockSpec(x.shape, lambda i, _: (0,) * len(x.shape))

    def own_rows(x):
        return pl.BlockSpec((out_rows, x.shape[1]), lambda i, me_ref: (me_ref[0], 0))

    def shape(*dims, dtype=f32):
        return jax.ShapeDtypeStruct(dims, dtype)

    rest = [grad_qkv, grad_wo, pack, input_grad, output]
    kv_width = KEY_VALUE_HEADS * HEAD_SIZE
    small = [
        shape(out_rows, devices * q_width),
        shape(out_rows, kv_width),
        shape(out_rows, kv_width),
        shape(*grad_wo.shape),
        shape(experts, out_rows),
        shape(1, out_rows),
        shape(1, out_rows),
        shape(*input_grad.shape, dtype=bf16),
        shape(*output.shape, dtype=bf16),
    ]
    return pl.pallas_call(
        kernel,
        name="finish",
        grid_spec=pltpu.PrefetchScalarGridSpec(
            num_scalar_prefetch=1,
            grid=(steps,),
            in_specs=[pl.BlockSpec((own_experts, chunk, e_cols), lambda i, _: (0, i, 0))]
            + [whole(x) for x in rest]
            + [own_rows(x) for x in weights]
            + [whole(gain)],
            out_specs=[
                pl.BlockSpec((own_experts, chunk, 2 * FFE), lambda i, _: (0, i, 0)),
                pl.BlockSpec((own_experts, chunk, FFE), lambda i, _: (0, i, 0)),
            ]
            + [whole(x) for x in small],
        ),
        out_shape=[
            shape(own_experts, e_rows, 2 * FFE),
            shape(own_experts, e_rows, FFE),
        ]
        + small,
        cost_estimate=pl.CostEstimate(flops=0, bytes_accessed=8 << 20, transcendentals=0),
        compiler_params=pltpu.CompilerParams(
            dimension_semantics=("arbitrary",), vmem_limit_bytes=60 << 20
        ),
    )(me, e_grads, *rest, *weights, gain)


def first_exchange(collective_id, tokens, out_grad, docs, mask, misc, gains, w_query, w_key, w_value, w_out):
    devices, parts = lax.axis_size("seq"), lax.axis_size("dp")
    w_rows, width = w_out.shape
    heads = QUERY_HEADS // devices
    q_width = heads * HEAD_SIZE
    group = QUERY_HEADS // KEY_VALUE_HEADS
    w_cols = HEADS_LANES + LANES
    weights = [w_query, w_key, w_value, w_out]

    def prepare(refs):
        given, (wq, wk, wv, wo, w_all, wo_low, sem) = refs[:4], refs[4:]
        for copy in loads(list(zip(given, (wq, wk, wv, wo))), sem):
            copy.wait()
        wo_low[...] = wo[...].astype(bf16)
        for s in range(devices):
            kv = s * heads // group * HEAD_SIZE
            pieces = [wq[:, s * q_width : (s + 1) * q_width]]
            if q_width < HEADS_LANES:
                pieces.append(jnp.zeros((w_rows, HEADS_LANES - q_width), f32))
            pieces += [wk[:, kv : kv + HEAD_SIZE], wv[:, kv : kv + HEAD_SIZE]]
            w_all[s] = jnp.concatenate(pieces, axis=1).astype(bf16)

    return exchange(
        collective_id,
        [
            ("gather", "seq", tokens, None),
            ("gather", "seq", docs, None),
            ("gather", "seq", mask, None),
            ("shift", "seq", out_grad, None),
            ("share", "dp", misc, None),
            ("gather", "dp", gains, None),
            ("gather", "dp", jax.ShapeDtypeStruct((w_rows, w_cols), bf16), 0),
            ("share", "dp", jax.ShapeDtypeStruct((w_rows, width), bf16), 1),
        ],
        prepare=prepare,
        given=weights,
        work=staged(weights)
        + [
            pltpu.VMEM((devices, w_rows, w_cols), bf16),
            pltpu.VMEM((w_rows, width), bf16),
            pltpu.SemaphoreType.DMA((4,)),
        ],
        made=lambda refs: (refs[8].at[lax.axis_index("seq")], refs[9]),
        keep=(jax.ShapeDtypeStruct((devices, w_rows, w_cols), bf16), 8),
    )


def prepare(expert_in, expert_out, picks, docs, w_router, gain_attn, gain_moe):
    own_experts, w_rows, _ = expert_in.shape
    rows, experts = picks.shape[1], w_router.shape[0]
    steps = 4
    chunk = w_rows // steps

    def kernel(
        e_in, e_out, picks_ref, docs_ref, router, gain_a, gain_m, low, mask, docs_out, misc, gains
    ):
        low[:, :, : 2 * FFE] = e_in[...].astype(bf16)
        low[:, :, 2 * FFE :] = e_out[...].astype(bf16)

        @pl.when(pl.program_id(0) == 0)
        def _():
            expert = lax.broadcasted_iota(jnp.int32, (LANES, rows), 0)
            chosen = picks_ref[:1] == expert
            for k in range(1, TOP):
                chosen = chosen | (picks_ref[k : k + 1] == expert)
            mask[...] = jnp.where(chosen, 1.0, 0.0).T.astype(bf16)
            docs_out[...] = jnp.broadcast_to(docs_ref[...], docs_out.shape)
            misc[...] = jnp.concatenate(
                [router[...], jnp.zeros((LANES - experts, w_rows), f32)], axis=0
            ).T.astype(bf16)
            upper = lax.broadcasted_iota(jnp.int32, (8, w_rows), 0) == 0
            gains[...] = jnp.where(upper, gain_a[...], gain_m[...]).astype(bf16)

    def whole(shape):
        return pl.BlockSpec(shape, lambda i: (0,) * len(shape))

    def part(x):
        return pl.BlockSpec((own_experts, chunk, x.shape[2]), lambda i: (0, i, 0))

    small = [picks, docs, w_router, gain_attn[None], gain_moe[None]]
    outs = [
        jax.ShapeDtypeStruct((rows, LANES), bf16),
        jax.ShapeDtypeStruct((8, rows), jnp.int32),
        jax.ShapeDtypeStruct((w_rows, LANES), bf16),
        jax.ShapeDtypeStruct((8, w_rows), bf16),
    ]
    return pl.pallas_call(
        kernel,
        name="prepare",
        grid=(steps,),
        out_shape=[jax.ShapeDtypeStruct((own_experts, w_rows, 3 * FFE), bf16)] + outs,
        in_specs=[part(expert_in), part(expert_out)] + [whole(x.shape) for x in small],
        out_specs=[pl.BlockSpec((own_experts, chunk, 3 * FFE), lambda i: (0, i, 0))]
        + [whole(x.shape) for x in outs],
        compiler_params=pltpu.CompilerParams(
            dimension_semantics=("arbitrary",), vmem_limit_bytes=60 << 20
        ),
    )(expert_in, expert_out, *small)


def final_exchange(
    collective_id, qkv_cot, normed, token_grads, w_full, tokens, mid_cot, gain, mid, branches
):
    devices, parts = lax.axis_size("seq"), lax.axis_size("dp")
    chips = devices // 2
    _, rows, cols = qkv_cot.shape
    width = tokens.shape[1]
    out_rows = token_grads[0].shape[2]
    gq_shape = (parts, devices, out_rows, cols)
    count = len(token_grads)
    wides = [x.shape[3] for x in token_grads]
    token_grads = [x.reshape(parts, chips, 2, out_rows, x.shape[3]) for x in token_grads]

    ins = [w_full, normed, qkv_cot, tokens, mid_cot, gain, mid, *branches]

    def kernel(*refs):
        qkv_in = refs[0]
        gt_in = refs[1 : 1 + count]
        given = refs[1 + count : 1 + count + len(ins)]
        refs = refs[1 + count + len(ins) :]
        in_grad_out, output_out, gq_out = refs[:3]
        gt_out = refs[3 : 3 + count]
        refs = refs[3 + count :]
        (
            qkv_tok, nac, gq_in, grad, gq_recv, gq_sum,
            q_send, q_recv, local, gq_send, gq_rsem, gqz_send, gqz_recv, gq_local,
        ) = refs[:14]
        work = [refs[14 + 11 * i : 25 + 11 * i] for i in range(count)]
        refs = refs[14 + 11 * count :]
        local_ins, (in_grad, output, in_sem, out_sem) = refs[: len(ins)], refs[len(ins) :]
        w_all, normed_all, qkv_all, tok_ref, mid_cot_ref, gain_ref, mid_ref, *y_refs = local_ins
        me, my = lax.axis_index("seq"), lax.axis_index("dp")
        chip, core = me // 2, lax.rem(me, 2)
        sibling = me + 1 - 2 * core
        arriving = loads(list(zip(given, local_ins)), in_sem)
        barrier = pltpu.get_barrier_semaphore()
        for axis, index, size in (("seq", me, devices), ("dp", my, parts)):
            for k in range(1, size):
                pl.semaphore_signal(
                    barrier,
                    inc=1,
                    device_id={axis: lax.rem(index + k, size)},
                    device_id_type=MESH,
                )
        pl.semaphore_wait(barrier, devices + parts - 2)

        def remote(axis, src, dst, send, recv, to):
            return pltpu.make_async_remote_copy(
                src_ref=src,
                dst_ref=dst,
                send_sem=send,
                recv_sem=recv,
                device_id={axis: to},
                device_id_type=MESH,
            )

        sent = []

        def columns(j):
            return qkv_tok.at[:, pl.ds(pl.multiple_of(j * cols, cols), cols)]

        for x, w in zip(gt_in, work):
            mine, theirs, far, near, last, sems, dp_send, dp_recv, z_send, z_recv, _ = w
            copy = remote(
                "seq", x.at[:, :, 1 - core], theirs, sems.at[0], sems.at[1], sibling
            )
            copy.start()
            sent.append(copy)
            pltpu.make_async_copy(x.at[:, :, core], mine, sems.at[2]).start()
        own = pltpu.make_async_copy(qkv_in.at[me], columns(me), local)
        own.start()
        for k in range(1, devices):
            to = lax.rem(me + k, devices)
            copy = remote(
                "seq", qkv_in.at[to], columns(me), q_send.at[k - 1], q_recv.at[k - 1], to
            )
            copy.start()
            sent.append(copy)

        for x, w in zip(gt_in, work):
            mine, theirs, far, near, last, sems, dp_send, dp_recv, z_send, z_recv, _ = w
            remote("seq", x.at[:, :, core], theirs, sems.at[0], sems.at[1], sibling).wait_recv()
            pltpu.make_async_copy(x.at[:, :, core], mine, sems.at[2]).wait()
            mine[...] = (mine[...].astype(f32) + theirs[...].astype(f32)).astype(bf16)
            for k in range(1, parts):
                to = lax.rem(my + k, parts)
                copy = remote(
                    "dp", mine.at[to], far.at[k - 1], dp_send.at[k - 1], dp_recv.at[k - 1], to
                )
                copy.start()
                sent.append(copy)

        for copy in arriving:
            copy.wait()
        grad[...] = jnp.zeros_like(grad)

        @pl.loop(0, devices)
        def _(j):
            grad[...] += dot_tn(normed_all[j], qkv_all[j])

        gq_in[...] = grad[...].astype(bf16).reshape(gq_shape)
        for k in range(1, parts):
            to = lax.rem(my + k, parts)
            copy = remote(
                "dp", gq_in.at[to], gq_recv.at[my], gq_send.at[k - 1], gq_rsem.at[k - 1], to
            )
            copy.start()
            sent.append(copy)
        own_q = pltpu.make_async_copy(gq_in.at[my], gq_recv.at[my], gq_local)
        own_q.start()
        total = y_refs[0][...].astype(f32)
        for k in range(1, len(branches)):
            total = total + y_refs[k][...].astype(f32)
        output[...] = (mid_ref[...] + res_mult * total).astype(bf16)
        leaving = [pltpu.make_async_copy(output, output_out, out_sem.at[0])]
        leaving[0].start()

        for k in range(devices):
            frm = lax.rem(me + devices - k, devices)
            if k == 0:
                own.wait()
            else:
                remote(
                    "seq", qkv_in.at[frm], columns(frm), q_send.at[k - 1], q_recv.at[k - 1], frm
                ).wait_recv()
            part = dot_nt(columns(frm)[...], w_all[frm])
            nac[...] = part if k == 0 else nac[...] + part

        resid = tok_ref[...].astype(f32)
        scale = lax.rsqrt(jnp.mean(resid * resid, axis=-1, keepdims=True) + norm_eps)
        weighted = nac[...] * gain_row(gain_ref, 0)
        in_grad[...] = (
            mid_cot_ref[...]
            + scale * weighted
            - resid
            * (scale * scale * scale)
            * jnp.mean(weighted * resid, axis=-1, keepdims=True)
        ).astype(bf16)

        leaving.append(pltpu.make_async_copy(in_grad, in_grad_out, out_sem.at[1]))
        leaving[1].start()
        own_q.wait()
        for k in range(1, parts):
            frm = lax.rem(my + parts - k, parts)
            remote(
                "dp", gq_in.at[frm], gq_recv.at[frm], gq_send.at[k - 1], gq_rsem.at[k - 1], frm
            ).wait_recv()
        summed = gq_recv[0].astype(f32)
        for p in range(1, parts):
            summed = summed + gq_recv[p].astype(f32)
        gq_sum[...] = summed.astype(bf16)
        own_z = pltpu.make_async_copy(gq_sum.at[me], gq_out.at[me], gq_local)
        own_z.start()
        for k in range(1, devices):
            to = lax.rem(me + k, devices)
            copy = remote(
                "seq", gq_sum.at[to], gq_out.at[me], gqz_send.at[k - 1], gqz_recv.at[k - 1], to
            )
            copy.start()
            sent.append(copy)
        for w in work:
            mine, theirs, far, near, last, sems, dp_send, dp_recv, z_send, z_recv, _ = w
            summed = mine[my].astype(f32)
            for k in range(1, parts):
                remote(
                    "dp", mine.at[0], far.at[k - 1], dp_send.at[k - 1], dp_recv.at[k - 1], my
                ).wait_recv()
                summed = summed + far[k - 1].astype(f32)
            near[...] = summed.astype(bf16)
            for k in range(1, chips):
                to = lax.rem(chip + k, chips)
                copy = remote(
                    "seq",
                    near.at[to],
                    last.at[k - 1],
                    z_send.at[k - 1],
                    z_recv.at[k - 1],
                    2 * to + core,
                )
                copy.start()
                sent.append(copy)

        for o, w in zip(gt_out, work):
            mine, theirs, far, near, last, sems, dp_send, dp_recv, z_send, z_recv, _ = w
            summed = near[chip].astype(f32)
            for k in range(1, chips):
                remote(
                    "seq", near.at[0], last.at[k - 1], z_send.at[k - 1], z_recv.at[k - 1], me
                ).wait_recv()
                summed = summed + last[k - 1].astype(f32)
            o[...] = summed
        own_z.wait()
        for k in range(1, devices):
            frm = lax.rem(me + devices - k, devices)
            remote(
                "seq", gq_sum.at[frm], gq_out.at[frm], gqz_send.at[k - 1], gqz_recv.at[k - 1], frm
            ).wait_recv()
        for copy in sent:
            copy.wait_send()
        for copy in leaving:
            copy.wait()

    hbm = pl.BlockSpec(memory_space=pl.ANY)
    vmem = pl.BlockSpec(memory_space=pltpu.VMEM)
    dma = pltpu.SemaphoreType.DMA
    scratch = [
        pltpu.VMEM((rows, devices * cols), bf16),
        pltpu.VMEM((rows, width), f32),
        pltpu.VMEM(gq_shape, bf16),
        pltpu.VMEM((width, cols), f32),
        pltpu.VMEM(gq_shape, bf16),
        pltpu.VMEM(gq_shape[1:], bf16),
        dma((devices - 1,)),
        dma((devices - 1,)),
        dma,
        dma((parts - 1,)),
        dma((parts - 1,)),
        dma((devices - 1,)),
        dma((devices - 1,)),
        dma,
    ]
    for wide in wides:
        piece = (out_rows, wide)
        scratch += [
            pltpu.VMEM((parts, chips) + piece, bf16),
            pltpu.VMEM((parts, chips) + piece, bf16),
            pltpu.VMEM((parts - 1, chips) + piece, bf16),
            pltpu.VMEM((chips,) + piece, bf16),
            pltpu.VMEM((chips - 1,) + piece, bf16),
            dma((3,)),
            dma((parts - 1,)),
            dma((parts - 1,)),
            dma((chips - 1,)),
            dma((chips - 1,)),
            dma,
        ]
    scratch += staged(ins) + [
        pltpu.VMEM((rows, width), bf16),
        pltpu.VMEM((rows, width), bf16),
        dma((len(ins),)),
        dma((2,)),
    ]
    return pl.pallas_call(
        kernel,
        name="final_exchange",
        out_shape=[
            jax.ShapeDtypeStruct((rows, width), bf16),
            jax.ShapeDtypeStruct((rows, width), bf16),
            jax.ShapeDtypeStruct(gq_shape[1:], bf16),
        ]
        + [jax.ShapeDtypeStruct((out_rows, wide), f32) for wide in wides],
        in_specs=[hbm] * (1 + count + len(ins)),
        out_specs=[hbm] * 3 + [vmem] * count,
        scratch_shapes=scratch,
        compiler_params=pltpu.CompilerParams(
            collective_id=collective_id, has_side_effects=True, vmem_limit_bytes=60 << 20
        ),
    )(qkv_cot, *token_grads, *ins)


def on_device(
    tokens,
    out_grad,
    doc_ids,
    expert_picks,
    w_query,
    key_weight_matrix,
    value_weight_matrix,
    w_out,
    w_router,
    gain_attn,
    gain_moe,
    expert_in,
    expert_out,
):
    devices, parts = lax.axis_size("seq"), lax.axis_size("dp")
    me = lax.axis_index("seq")
    rows, width = tokens.shape[1:]
    length = rows * devices
    experts = w_router.shape[1]
    heads = QUERY_HEADS // devices
    group = QUERY_HEADS // KEY_VALUE_HEADS
    q_width = heads * HEAD_SIZE
    w_rows = w_query.shape[0]

    w_cols = HEADS_LANES + LANES
    low, mask, doc_rows, misc, gains = prepare(
        expert_in, expert_out, expert_picks[0].T, doc_ids, w_router.T, gain_attn, gain_moe
    )
    expert_full = lax.all_gather(low, "dp", axis=1, tiled=True)
    chips = devices // 2

    def shift(x, k):
        return lax.ppermute(x, "seq", [(i, (i + 2 * k) % devices) for i in range(devices)])

    tok_all, doc_all, mask_all, middle_cot, misc_full, gains_full, w_own_all, wo_full, w_all = first_exchange(
        0,
        tokens[0],
        out_grad[0],
        doc_rows,
        mask,
        misc,
        gains,
        w_query,
        key_weight_matrix,
        value_weight_matrix,
        w_out,
    )
    w_full = lax.all_gather(w_all, "dp", axis=1, tiled=True)
    held, tok_all = lax.optimization_barrier((out_grad[0], tok_all))
    cots = [held] + [
        middle_cot if k == chips // 2 else shift(held, k) for k in range(1, chips)
    ]
    w_own_all = w_own_all.reshape(width, w_cols)
    wo_full = wo_full.reshape(width, width)
    misc_full = misc_full.reshape(width, LANES)
    table = rope_table(devices, rows)

    normed_a, q_all, kv_all, attended_own, ot, lse = attend_forward(
        tok_all, w_own_all, gains_full, table, doc_all, heads
    )
    attended, mid, normed_m = attended_exchange(
        1, attended_own, tokens[0], wo_full, gains_full
    )
    (_, _, _, moe_sum, gate_cot, e_grads, *branches) = moe_exchange(
        2, normed_m, cots, mask_all, misc_full, expert_full
    )
    e_grads = lax.psum_scatter(e_grads, "dp", scatter_dimension=1, tiled=True)
    heads_cot, router_pack, mid_cot, grad_wo = middle_exchange(
        4, moe_sum, gate_cot, normed_m, misc_full, mask, mid, out_grad[0], gains_full,
        wo_full, attended, q_width,
    )
    heads_cot, branches = lax.optimization_barrier((heads_cot, branches))
    branches = [
        branches[0],
        lax.ppermute(branches[1], "seq", [(i, i ^ 2) for i in range(devices)]),
    ] + [shift(branches[1 + k], 2 * k) for k in range(1, chips // 2)]
    qkv_cot = attend_backward(q_all, kv_all, heads_cot, ot, lse, table, doc_all, heads)
    qkv_cot, branches = lax.optimization_barrier((qkv_cot, branches))
    out_rows = w_rows // devices
    input_grad, output, grad_qkv, grad_wo, router_pack = final_exchange(
        5,
        qkv_cot,
        normed_a,
        [
            grad_wo.reshape(parts, devices, out_rows, width),
            router_pack.reshape(parts, devices, out_rows, LANES),
        ],
        w_full,
        tokens[0],
        mid_cot,
        gains_full,
        mid,
        branches,
    )

    (
        grad_e_in, grad_e_out, grad_wq, grad_wk, grad_wv, grad_wo, grad_router, grad_gain_m,
        grad_gain_a, input_grad, output,
    ) = finish(
        e_grads,
        grad_qkv,
        grad_wo,
        router_pack,
        input_grad,
        output,
        [w_query, key_weight_matrix, value_weight_matrix],
        gain_attn.reshape(devices, out_rows),
        heads,
        experts,
    )
    input_grad, output = input_grad[None], output[None]
    grad_router = grad_router.T
    grad_gain_a = grad_gain_a.reshape(out_rows)
    grad_gain_m = grad_gain_m.reshape(out_rows)
    return (
        output,
        input_grad,
        grad_wq,
        grad_wk,
        grad_wv,
        grad_wo,
        grad_router,
        grad_gain_a,
        grad_gain_m,
        grad_e_in,
        grad_e_out,
    )


def solution(mesh):
    return jax.shard_map(
        on_device,
        mesh=mesh,
        in_specs=(
            P("dp", "seq", None),
            P("dp", "seq", None),
            P("dp", "seq"),
            P("dp", "seq", None),
            P("dp", None),
            P("dp", None),
            P("dp", None),
            P("dp", None),
            P("dp", None),
            P("dp"),
            P("dp"),
            P("seq", "dp", None),
            P("seq", "dp", None),
        ),
        out_specs=(
            P("dp", "seq", None),
            P("dp", "seq", None),
            P(("dp", "seq"), None),
            P(("dp", "seq"), None),
            P(("dp", "seq"), None),
            P(("dp", "seq"), None),
            P(("dp", "seq"), None),
            P(("dp", "seq")),
            P(("dp", "seq")),
            P("seq", "dp", None),
            P("seq", "dp", None),
        ),
        check_vma=False,
    )
```
